32 devices in a mesh: row: 4 (over y, core), chan: 8 (over z, x).
Axes of the slice: x: 2, y: 2, z: 4, core: 2. Of those that a mesh axis runs over, the one named last changes fastest.
Arguments:
- inputs: bfloat16 [16, 768, 2048], P('row', 'chan'), may hold values from -6 to 6
- cotangent: bfloat16 [16, 768, 2048], P('row', 'chan'), may hold values from -6 to 6
- doc_lengths: int32 [16, 8], P('row'), may hold values from 1 to 512, 1920 in all within a row
- ema_logits: float32 [2, 768, 16], P(None, 'chan'), may hold values from -4 to 0.5
- ema_mixing: float32 [2, 768, 16], P(None, 'chan'), may hold values from -3 to 3
- ema_skip: float32 [768], P('chan'), may hold values from -4 to 4
- value_weight: float32 [768, 1536], P(('row', 'chan')), may hold values from -0.21875 to 0.21875
- base_weight: float32 [768, 3200], P(('row', 'chan')), may hold values from -0.21875 to 0.21875
- attn_weight: float32 [1536, 768], P(('row', 'chan')), may hold values from -1.25 to 1.25
- hidden_weight: float32 [768, 1536], P(('row', 'chan')), may hold values from -0.21875 to 0.21875
- output_weight: float32 [1536, 768], P(('row', 'chan')), may hold values from -0.15625 to 0.15625
- value_bias: float32 [1536], replicated, may hold values from -3 to 3
- base_bias: float32 [3200], replicated, may hold values from -3 to 3
- attn_bias: float32 [768], replicated, may hold values from -3 to 3
- hidden_bias: float32 [1536], replicated, may hold values from -3 to 3
- output_bias: float32 [768], replicated, may hold values from -3 to 3
- query_key_gain: float32 [2, 128], replicated, may hold values from -4 to 4
- query_key_shift: float32 [2, 128], replicated, may hold values from -3 to 3
- position_bias: float32 [128], replicated, may hold values from -3 to 3
- norm_gain: float32 [2, 768], replicated, may hold values from 0.5 to 1.5
- norm_bias: float32 [2, 768], replicated, may hold values from -3 to 3
Outputs:
- layer_out: bfloat16 [16, 768, 2048], P('row', 'chan')
- grad_inputs: float32 [16, 768, 2048], P('row', 'chan')
- grad_ema_logits: float32 [2, 768, 16], P(None, 'chan')
- grad_ema_mixing: float32 [2, 768, 16], P(None, 'chan')
- grad_ema_skip: float32 [768], P('chan')
- grad_value_weight: float32 [768, 1536], P(('row', 'chan'))
- grad_base_weight: float32 [768, 3200], P(('row', 'chan'))
- grad_attn_weight: float32 [1536, 768], P(('row', 'chan'))
- grad_hidden_weight: float32 [768, 1536], P(('row', 'chan'))
- grad_output_weight: float32 [1536, 768], P(('row', 'chan'))
- grad_value_bias: float32 [1536], replicated
- grad_base_bias: float32 [3200], replicated
- grad_attn_bias: float32 [768], replicated
- grad_hidden_bias: float32 [1536], replicated
- grad_output_bias: float32 [768], replicated
- grad_query_key_gain: float32 [2, 128], replicated
- grad_query_key_shift: float32 [2, 128], replicated
- grad_position_bias: float32 [128], replicated
- grad_norm_gain: float32 [2, 768], replicated
- grad_norm_bias: float32 [2, 768], replicated
The draws below stay inside these ranges and needn't reach their ends.
Inputs may be any that keep to these rules, and one draw needn't show every extreme that they name: `doc_lengths`: each row's 8 document lengths add up to 1920; the last 128 positions of the row are padding and form a segment of their own.
All inputs are finite; a program needn't handle non-finite values.
Results may differ from the reference program's by a relative error of at most 0.02.
The reference program's roundings to bfloat16 on the way count: a program that leaves them out, or rounds other values in their place, can miss the bound.
Values may be sent and summed in bfloat16 or wider, within the bound.
A program may use at most 384 MiB of HBM per device.

```python
import math
from functools import partial
import jax
import jax.numpy as jnp
import numpy as np
from jax import lax

D = 768
Z = 128
V = 1536
NDIM = 16
FF = 1536
B = 128
DOCS = 8
LEN = 2048
ROWS = 16
BASE_W = 3200


def steps_of(own_key, extent, shards, low, top_value):
    gain, own = 1.0, jax.random.fold_in(own_key, 6)
    for axis_at, shards_of in shards:
        steps = jnp.exp(jax.random.uniform(jax.random.fold_in(own, axis_at), (shards_of,), jnp.float32, low / len(shards), top_value / len(shards)))
        gain = gain * jnp.repeat(steps, extent[axis_at] // shards_of).reshape([-1 if axis == axis_at else 1 for axis in range(len(extent))])
    return gain


def profile(amount, total, most, lean):
    loads = [(1 << 20) // math.isqrt(standing ** lean) + 1 for standing in range(2, amount + 1)]
    spare, given = total - most - (amount - 1), [1] * (amount - 1)
    while spare > 0:
        candidates = [i for i in range(amount - 1) if given[i] < most]
        mass, left = sum([loads[i] for i in candidates]), spare
        for i in candidates:
            extra = min(most - given[i], max(1, left * loads[i] // mass), spare)
            given[i] = given[i] + extra
            spare = spare - extra
    return np.array([most] + given)


def ragged_sizes(rng, count, total, bound, skew):
    if count == 2:
        one = jax.random.randint(rng, (), max(1, total - bound), min(bound, total - 1) + 1)
        return jnp.stack([one, total - one])
    sizes = jnp.asarray(profile(count, total, bound, skew), jnp.int32)
    twos = (count - 1) // 2
    donor, sink = sizes[1:1 + 2 * twos:2], sizes[2:2 + 2 * twos:2]
    room = jnp.minimum(donor - 1, bound - sink)
    moved = jax.random.randint(jax.random.fold_in(rng, 1), (twos,), 0, 1 << 20) % (room + 1)
    sizes = sizes.at[1:1 + 2 * twos:2].set(donor - moved).at[2:2 + 2 * twos:2].set(sink + moved)
    return sizes[jax.random.permutation(jax.random.fold_in(rng, 2), count)]


def scatter_about(rng, shape, scale, bound, pieces=(), kind=jnp.bfloat16):
    result = scale * jax.random.normal(rng, shape, jnp.float32)
    if pieces:
        result = result * steps_of(rng, shape, pieces, -0.22, 0.18)
    return jnp.clip(result, -bound, bound).astype(kind)


def setup_inputs(seed: int = 0) -> dict:
    splits = jax.random.split(jax.random.key(seed), 22)
    return {
        "inputs": scatter_about(splits[0], (ROWS, D, LEN), 1.0, 6.0, ((0, 4), (1, 8))),
        "cotangent": scatter_about(splits[1], (ROWS, D, LEN), 1.0, 6.0, ((0, 4), (1, 8))),
        "doc_lengths": jax.vmap(lambda own: ragged_sizes(own, DOCS, LEN - B, LEN // 4, 2))(jax.random.split(splits[2], ROWS)).reshape((ROWS, DOCS)).astype(jnp.int32),
        "ema_logits": jnp.clip(-4.0 + 4.5 * jax.random.uniform(splits[3], (2, D, NDIM), jnp.float32) ** steps_of(splits[3], (2, D, NDIM), ((1, 8),), -0.2, 0.2), -4.0, 0.5),
        "ema_mixing": scatter_about(splits[4], (2, D, NDIM), 0.5, 3.0, ((1, 8),), jnp.float32),
        "ema_skip": scatter_about(splits[5], (D,), 1.0, 4.0, ((0, 8),), jnp.float32),
        "value_weight": scatter_about(splits[6], (D, V), D ** -0.5, 0.21875, ((0, 32),), jnp.float32),
        "base_weight": scatter_about(splits[7], (D, BASE_W), D ** -0.5, 0.21875, ((0, 32),), jnp.float32),
        "attn_weight": scatter_about(splits[8], (V, D), (V // 64) ** -0.5, 1.25, ((0, 32),), jnp.float32),
        "hidden_weight": scatter_about(splits[9], (D, FF), D ** -0.5, 0.21875, ((0, 32),), jnp.float32),
        "output_weight": scatter_about(splits[10], (FF, D), FF ** -0.5, 0.15625, ((0, 32),), jnp.float32),
        "value_bias": scatter_about(splits[11], (V,), 0.5, 3.0, (), jnp.float32),
        "base_bias": scatter_about(splits[12], (BASE_W,), 0.5, 3.0, (), jnp.float32),
        "attn_bias": scatter_about(splits[13], (D,), 0.5, 3.0, (), jnp.float32),
        "hidden_bias": scatter_about(splits[14], (FF,), 0.5, 3.0, (), jnp.float32),
        "output_bias": scatter_about(splits[15], (D,), 0.5, 3.0, (), jnp.float32),
        "query_key_gain": scatter_about(splits[16], (2, Z), 1.0, 4.0, (), jnp.float32),
        "query_key_shift": scatter_about(splits[17], (2, Z), 0.5, 3.0, (), jnp.float32),
        "position_bias": scatter_about(splits[18], (B,), 0.5, 3.0, (), jnp.float32),
        "norm_gain": jnp.clip(1.0 + 0.1 * jax.random.normal(splits[19], (2, D), jnp.float32), 0.5, 1.5),
        "norm_bias": scatter_about(splits[20], (2, D), 0.5, 3.0, (), jnp.float32),
    }


HIGH = lax.Precision.HIGHEST
EPSILON = 1e-05
MASKED = -1e+30

@jax.custom_vjp
def low(v):
    return lax.optimization_barrier(v.astype(jnp.bfloat16)).astype(jnp.float32)

@jax.custom_vjp
def low_back(v):
    return v

def low_keep(v):
    return (low(v), None)

def low_pass(kept, grad):
    return (grad,)

def back_keep(v):
    return (v, None)

def back_low(kept, grad):
    return (low(grad),)
low.defvjp(low_keep, low_pass)
low_back.defvjp(back_keep, back_low)

def matmul(left, right):
    return jnp.dot(left, right, precision=HIGH)

def segment_ids(lengths, positions):
    boundary = jnp.cumsum(lengths).astype(jnp.int32)
    passed = (positions[:, None] >= boundary[None, :]).astype(jnp.int32)
    return lax.optimization_barrier(jnp.sum(passed, axis=1)).astype(jnp.int32)

def layer_norm(values, scale_row, shift_row):
    center = lax.optimization_barrier(jnp.mean(values, axis=-1, keepdims=True))
    centered = values - center
    spread = lax.optimization_barrier(jnp.mean(centered * centered, axis=-1, keepdims=True))
    return centered * lax.rsqrt(spread + EPSILON) * scale_row + shift_row

def offset_table(length_block):
    offsets = jnp.arange(length_block, dtype=jnp.int32)
    distance = offsets[:, None] - offsets[None, :]
    return (distance[:, :, None] == offsets[None, None, :]).astype(jnp.float32)

def ema_step(tables, running, inputs):
    toeplitz, carry_weight, fresh_weight, final_power = tables
    state_in, previous = running
    values, segments = inputs
    same_seg = (segments[:, :, None] == segments[:, None, :]).astype(jnp.float32)
    keeping = (segments == previous[:, None]).astype(jnp.float32)
    within = jnp.einsum('cij,rij,rcj->rci', toeplitz, same_seg, values, precision=HIGH)
    carried = jnp.einsum('icn,rcn->rci', carry_weight, state_in, precision=HIGH) * keeping[:, None, :]
    closing = (segments == segments[:, -1:]).astype(jnp.float32)
    fresh_part = jnp.einsum('jcn,rcj->rcn', fresh_weight, values * closing[:, None, :], precision=HIGH)
    state_next = keeping[:, -1][:, None, None] * final_power[None] * state_in + fresh_part
    return ((state_next, segments[:, -1]), within + carried)

def ema_apply(values, segments, logits, mixing, skip_gain, length_block):
    row_count, chan_count, seq_length = values.shape
    damping = jax.nn.sigmoid(logits[0])
    decay_step = 1.0 - damping * jax.nn.sigmoid(logits[1])
    input_gain = damping * mixing[0]
    exponents = jnp.arange(length_block + 1).astype(jnp.float32)
    powers = jnp.exp(exponents[:, None, None] * jnp.log(decay_step)[None])
    kernel = lax.optimization_barrier(jnp.sum(powers[:length_block] * (input_gain * mixing[1])[None], axis=2))
    toeplitz = jnp.einsum('ijm,mc->cij', offset_table(length_block), kernel, precision=HIGH)
    tables = (toeplitz, powers[1:] * mixing[1][None], powers[:length_block][::-1] * input_gain[None], powers[length_block])
    block_count = seq_length // length_block
    blocks = values.reshape(row_count, chan_count, block_count, length_block).transpose(2, 0, 1, 3)
    block_segs = segments.reshape(row_count, block_count, length_block).transpose(1, 0, 2)
    initial = (jnp.zeros((row_count, chan_count, logits.shape[2]), jnp.float32), jnp.full((row_count,), -1, jnp.int32))
    final_carry, outputs = lax.scan(jax.checkpoint(partial(ema_step, tables)), initial, (blocks, block_segs))
    smoothed = outputs.transpose(1, 2, 0, 3).reshape(row_count, chan_count, seq_length)
    return jax.nn.silu(smoothed + skip_gain[None, :, None] * values)

def row_forward(params, row_input, row_segments):
    ema_logits, ema_mixing, ema_skip, value_weight, base_weight, attn_weight, hidden_weight, output_weight, value_bias, base_bias, attn_bias, hidden_bias, output_bias, query_key_gain, query_key_shift, position_bias, norm_gain, norm_bias = params
    averaged = ema_apply(row_input[None], row_segments[None], ema_logits, ema_mixing, ema_skip, B)[0]
    mixed = low(averaged).T
    tokens = row_input.T
    windows = LEN // B
    value_pre = low_back(matmul(tokens, low(value_weight)) + value_bias)
    value_rows = low(jax.nn.silu(value_pre)).reshape(windows, B, V)
    base_proj = low_back(matmul(mixed, low(base_weight)) + base_bias)
    update_gate = jax.nn.sigmoid(base_proj[:, :D])
    shared_z = jax.nn.silu(base_proj[:, D:D + Z])
    reset_gate = jax.nn.silu(base_proj[:, D + Z:D + Z + V])
    direct_part = base_proj[:, D + Z + V:]
    queries = low(shared_z * query_key_gain[0] + query_key_shift[0]).reshape(windows, B, Z)
    key_rows = low(shared_z * query_key_gain[1] + query_key_shift[1]).reshape(windows, B, Z)
    offsets = jnp.arange(B, dtype=jnp.int32)
    distance = offsets[:, None] - offsets[None, :]
    bias_table = jnp.take(position_bias, jnp.maximum(distance, 0), axis=0)
    window_segs = row_segments.reshape(windows, B)
    allowed = (distance >= 0)[None] & (window_segs[:, :, None] == window_segs[:, None, :])
    scores = low_back(jnp.einsum('cik,cjk->cij', queries, key_rows, precision=HIGH) * Z ** (-0.5) + bias_table[None])
    attention = low(jax.nn.softmax(jnp.where(allowed, scores, MASKED), axis=-1))
    attended = low_back(jnp.einsum('cij,cjv->civ', attention, value_rows, precision=HIGH)).reshape(LEN, V)
    mixed_att = low(attended * reset_gate)
    projected = low_back(matmul(mixed_att, low(attn_weight)))
    hidden = jax.nn.silu(direct_part + projected + attn_bias)
    out_one = tokens + update_gate * (hidden - tokens)
    normed = layer_norm(out_one, norm_gain[0], norm_bias[0])
    inner_pre = low_back(matmul(low(normed), low(hidden_weight)) + hidden_bias)
    activated = low(jax.nn.silu(inner_pre))
    outer_proj = low_back(matmul(activated, low(output_weight)))
    out_two = normed + outer_proj + output_bias
    return layer_norm(out_two, norm_gain[1], norm_bias[1]).T

def reference(inputs, cotangent, doc_lengths, ema_logits, ema_mixing, ema_skip, value_weight, base_weight, attn_weight, hidden_weight, output_weight, value_bias, base_bias, attn_bias, hidden_bias, output_bias, query_key_gain, query_key_shift, position_bias, norm_gain, norm_bias):
    params = tuple((entry.astype(jnp.float32) for entry in (ema_logits, ema_mixing, ema_skip, value_weight, base_weight, attn_weight, hidden_weight, output_weight, value_bias, base_bias, attn_bias, hidden_bias, output_bias, query_key_gain, query_key_shift, position_bias, norm_gain, norm_bias)))
    positions = jnp.arange(LEN, dtype=jnp.int32)

    def per_row(totals, row_data):
        row_input, row_grad, row_lengths = row_data
        row_segments = segment_ids(row_lengths, positions)

        def forward(param_set, row_values):
            return row_forward(param_set, row_values, row_segments)
        row_out, pullback = jax.vjp(forward, params, row_input.astype(jnp.float32))
        param_grads, input_grad = pullback(row_grad.astype(jnp.float32))
        totals = jax.tree.map(jnp.add, totals, param_grads)
        return (totals, (row_out.astype(jnp.bfloat16), input_grad))
    zeros = jax.tree.map(jnp.zeros_like, params)
    totals, (layer_out, grad_inputs) = lax.scan(per_row, zeros, (inputs, cotangent, doc_lengths))
    return (layer_out, grad_inputs, totals[0], totals[1], totals[2], totals[3], totals[4], totals[5], totals[6], totals[7], totals[8], totals[9], totals[10], totals[11], totals[12], totals[13], totals[14], totals[15], totals[16], totals[17])
```

```python
from functools import partial

import jax
import jax.numpy as jnp
from jax import lax
from jax.experimental import pallas as pl
from jax.experimental.pallas import tpu as pltpu
from jax.sharding import PartitionSpec as P

HIGH = lax.Precision.HIGHEST
EPSILON = 1e-05
MASKED = -1e30


def segment_ids(lengths, positions):
    boundary = jnp.cumsum(lengths)
    passed = (positions[:, None] >= boundary[None, :]).astype(jnp.int32)
    return jnp.sum(passed, axis=1)


def silu_slope(values):
    logistic = jax.nn.sigmoid(values)
    return logistic * (1.0 + values * (1.0 - logistic))


def layer_norm(values, scale_row, shift_row):
    center = jnp.mean(values, axis=-1, keepdims=True)
    centered = values - center
    spread = jnp.mean(centered * centered, axis=-1, keepdims=True)
    return centered * lax.rsqrt(spread + EPSILON) * scale_row + shift_row


def offset_table(length_block):
    offsets = jnp.arange(length_block, dtype=jnp.int32)
    distance = offsets[:, None] - offsets[None, :]
    return (distance[:, :, None] == offsets[None, None, :]).astype(jnp.float32)


LANES = 128
STEPS = 16


def pad_rows(block):
    short = LANES - block.shape[0]
    if short == 0:
        return block
    return jnp.concatenate([block, jnp.zeros((short, block.shape[1]), block.dtype)], axis=0)


def spread(block, slots, row, rows):
    turned = pad_rows(block).T
    slots[pl.ds(row, LANES, stride=2 * rows), :] = turned
    slots[pl.ds(row + rows, LANES, stride=2 * rows), :] = turned


def gather(slots, row, rows, chans):
    first = slots[pl.ds(row, LANES, stride=2 * rows), :]
    second = slots[pl.ds(row + rows, LANES, stride=2 * rows), :]
    return (first + second).T[:chans]


def ema_forward_kernel(x_ref, keep_ref, decay_ref, gain_ref, skip_ref, pre_ref, mixed_ref, slots, state):
    rows, chans, _ = x_ref.shape
    halves = decay_ref.shape[0]
    tall = 2 * rows

    @pl.when(pl.program_id(0) == 0)
    def _():
        state[...] = jnp.zeros_like(state)

    for row in range(rows):
        spread(x_ref[row].astype(jnp.float32), slots, row, rows)
    keep_tile = keep_ref[...]

    def group(step, carry):
        keeping, states = carry
        states = list(states)
        for inner in range(STEPS):
            at = pl.ds(pl.multiple_of((step * STEPS + inner) * tall, tall), tall)
            value = slots[at, :]
            keep = jnp.broadcast_to(keeping[:, inner : inner + 1], (tall, LANES))
            total = None
            for n in range(halves):
                states[n] = (decay_ref[n] * keep) * states[n] + gain_ref[n] * value
                total = states[n] if total is None else total + states[n]
            slots[at, :] = total
        return pltpu.roll(keeping, LANES - STEPS, axis=1), tuple(states)

    start = tuple(state[n] for n in range(halves))
    _, states = lax.fori_loop(0, LANES // STEPS, group, (keep_tile, start))
    for n in range(halves):
        state[n] = states[n]
    for row in range(rows):
        pre = gather(slots, row, rows, chans) + skip_ref[:, :1] * x_ref[row].astype(jnp.float32)
        pre_ref[row] = pre
        mixed_ref[row] = (pre * jax.nn.sigmoid(pre)).astype(jnp.bfloat16)


def ema_backward_kernel(x_ref, pre_ref, back_ref, direct_ref, keep_ref, next_ref, decay_ref, gain_ref,
                        skip_ref, skip_row_ref, grad_ref, weight_ref, power_ref, skip_out_ref,
                        slots, back_slots, state, powers, weight_sum, power_sum):
    rows, chans, _ = x_ref.shape
    halves = decay_ref.shape[0]
    tall = 2 * rows
    tiles = pl.num_programs(0) // 2
    index = pl.program_id(0)

    @pl.when(index == 0)
    def _():
        state[...] = jnp.zeros_like(state)
        powers[...] = jnp.zeros_like(powers)
        weight_sum[...] = jnp.zeros_like(weight_sum)
        power_sum[...] = jnp.zeros_like(power_sum)
        skip_out_ref[...] = jnp.zeros_like(skip_out_ref)

    @pl.when(index < tiles)
    def _():
        back_tile = back_slots.at[pl.ds(pl.multiple_of(index * (LANES * tall), LANES * tall), LANES * tall), :]
        for row in range(rows):
            values = x_ref[row].astype(jnp.float32)
            pre = pre_ref[row]
            logistic = jax.nn.sigmoid(pre)
            back = back_ref[row].astype(jnp.float32) * (logistic * (1.0 + pre * (1.0 - logistic)))
            skip_out_ref[...] += back * values
            spread(values, slots, row, rows)
            spread(back, back_tile, row, rows)

        def group(step, carry):
            keeping, states, derived, weights, sums = (carry[0], *map(list, carry[1:]))
            for inner in range(STEPS):
                at = pl.ds(pl.multiple_of((step * STEPS + inner) * tall, tall), tall)
                value = slots[at, :]
                back = back_tile[at, :]
                keep = jnp.broadcast_to(keeping[:, inner : inner + 1], (tall, LANES))
                for n in range(halves):
                    decay = decay_ref[n] * keep
                    derived[n] = decay * (derived[n] + states[n])
                    states[n] = decay * states[n] + value
                    weights[n] = weights[n] + back * states[n]
                    sums[n] = sums[n] + back * derived[n]
            return pltpu.roll(keeping, LANES - STEPS, axis=1), tuple(states), tuple(derived), tuple(weights), tuple(sums)

        refs = (state, powers, weight_sum, power_sum)
        start = tuple(tuple(ref[n] for n in range(halves)) for ref in refs)
        out = lax.fori_loop(0, LANES // STEPS, group, (keep_ref[...], *start))
        for ref, values in zip(refs, out[1:]):
            for n in range(halves):
                ref[n] = values[n]

    @pl.when(index == tiles)
    def _():
        weight_ref[...] = weight_sum[...]
        power_ref[...] = power_sum[...]
        state[...] = jnp.zeros_like(state)

    @pl.when(index >= tiles)
    def _():
        tile = 2 * tiles - 1 - index
        back_tile = back_slots.at[pl.ds(pl.multiple_of(tile * (LANES * tall), LANES * tall), LANES * tall), :]

        def group(step, carry):
            keeping, states = carry
            states = list(states)
            for inner in range(STEPS):
                at = pl.ds(pl.multiple_of((LANES - 1 - step * STEPS - inner) * tall, tall), tall)
                back = back_tile[at, :]
                keep = jnp.broadcast_to(keeping[:, LANES - 1 - inner : LANES - inner], (tall, LANES))
                total = skip_row_ref[...] * back
                for n in range(halves):
                    states[n] = (decay_ref[n] * keep) * states[n] + back
                    total = total + gain_ref[n] * states[n]
                slots[at, :] = total
            return pltpu.roll(keeping, STEPS, axis=1), tuple(states)

        start = tuple(state[n] for n in range(halves))
        _, states = lax.fori_loop(0, LANES // STEPS, group, (next_ref[...], start))
        for n in range(halves):
            state[n] = states[n]
        for row in range(rows):
            grad_ref[row] = direct_ref[row].astype(jnp.float32) + gather(slots, row, rows, chans)


def lane_table(table, rows):
    chans, count = table.shape
    spread_rows = jnp.repeat(table.T.reshape(2, count // 2, 1, chans), rows, axis=2)
    ordered = spread_rows.transpose(1, 0, 2, 3).reshape(count // 2, 2 * rows, chans)
    return jnp.pad(ordered, ((0, 0), (0, 0), (0, LANES - chans)))


def lane_sums(sums, rows, chans):
    count = sums.shape[0]
    return jnp.sum(sums.reshape(count, 2, rows, LANES), axis=2)[:, :, :chans].transpose(2, 1, 0).reshape(chans, 2 * count)


def ema_parts(logits, mixing):
    damping = jax.nn.sigmoid(logits[0])
    decay = 1.0 - damping * jax.nn.sigmoid(logits[1])
    return damping, decay, damping * mixing[0]


def keep_tables(segments):
    keeping = (segments[:, 1:] == segments[:, :-1]).astype(jnp.float32)
    edge = jnp.zeros((segments.shape[0], 1), jnp.float32)
    return (jnp.tile(jnp.concatenate([edge, keeping], axis=1), (2, 1)),
            jnp.tile(jnp.concatenate([keeping, edge], axis=1), (2, 1)))


def ema_forward(values, keep, logits, mixing, skip):
    rows, chans, length = values.shape
    _, decay, gain = ema_parts(logits, mixing)
    tables = [lane_table(decay, rows), lane_table(gain * mixing[1], rows)]
    half = tables[0].shape[0]
    tall = 2 * rows
    block = pl.BlockSpec((rows, chans, LANES), lambda i: (0, 0, i))
    whole = pl.BlockSpec((half, tall, LANES), lambda i: (0, 0, 0))
    return pl.pallas_call(
        ema_forward_kernel,
        grid=(length // LANES,),
        in_specs=[block, pl.BlockSpec((tall, LANES), lambda i: (0, i)), whole, whole,
                  pl.BlockSpec((chans, LANES), lambda i: (0, 0))],
        out_specs=[block, block],
        out_shape=[jax.ShapeDtypeStruct(values.shape, jnp.float32), jax.ShapeDtypeStruct(values.shape, jnp.bfloat16)],
        scratch_shapes=[pltpu.VMEM((LANES * tall, LANES), jnp.float32), pltpu.VMEM((half, tall, LANES), jnp.float32)],
        cost_estimate=pl.CostEstimate(flops=values.size * 80, bytes_accessed=values.size * 8, transcendentals=values.size),
    )(values, keep, *tables, jnp.broadcast_to(skip[:, None], (chans, LANES)))


def ema_backward(values, pre, back, direct, keep, keep_next, logits, mixing, skip):
    rows, chans, length = values.shape
    damping, decay, gain = ema_parts(logits, mixing)
    tables = [lane_table(decay, rows), lane_table(gain * mixing[1], rows)]
    half = tables[0].shape[0]
    tall = 2 * rows
    tiles = length // LANES
    first = lambda i: (0, 0, jnp.minimum(i, tiles - 1))
    second = lambda i: (0, 0, jnp.minimum(tiles - 1, 2 * tiles - 1 - i))
    whole = pl.BlockSpec((half, tall, LANES), lambda i: (0, 0, 0))
    flat = pl.BlockSpec((chans, LANES), lambda i: (0, 0))
    skip_row = jnp.pad(jnp.broadcast_to(skip[None], (rows, chans)), ((0, rows), (0, LANES - chans)))
    grads, weight, power, skip_sum = pl.pallas_call(
        ema_backward_kernel,
        grid=(2 * tiles,),
        in_specs=[pl.BlockSpec((rows, chans, LANES), first)] * 3
        + [pl.BlockSpec((rows, chans, LANES), second),
           pl.BlockSpec((tall, LANES), lambda i: (0, jnp.minimum(i, tiles - 1))),
           pl.BlockSpec((tall, LANES), lambda i: (0, jnp.minimum(tiles - 1, 2 * tiles - 1 - i))),
           whole, whole, flat, pl.BlockSpec((tall, LANES), lambda i: (0, 0))],
        out_specs=[pl.BlockSpec((rows, chans, LANES), second), whole, whole, flat],
        out_shape=[jax.ShapeDtypeStruct(values.shape, jnp.float32),
                   jax.ShapeDtypeStruct((half, tall, LANES), jnp.float32),
                   jax.ShapeDtypeStruct((half, tall, LANES), jnp.float32),
                   jax.ShapeDtypeStruct((chans, LANES), jnp.float32)],
        scratch_shapes=[pltpu.VMEM((LANES * tall, LANES), jnp.float32), pltpu.VMEM((length * tall, LANES), jnp.float32)]
        + [pltpu.VMEM((half, tall, LANES), jnp.float32)] * 4,
        compiler_params=pltpu.CompilerParams(vmem_limit_bytes=56 * 1024 * 1024),
        cost_estimate=pl.CostEstimate(flops=values.size * 240, bytes_accessed=values.size * 14, transcendentals=values.size),
    )(values, pre, back, direct, keep, keep_next, *tables,
      jnp.broadcast_to(skip[:, None], (chans, LANES)), skip_row)
    weight = lane_sums(weight, rows, chans)
    back_decay = gain * mixing[1] * lane_sums(power, rows, chans) / decay
    other = jax.nn.sigmoid(logits[1])
    back_damping = weight * mixing[0] * mixing[1] - back_decay * other
    grad_logits = jnp.stack([back_damping * damping * (1.0 - damping), -back_decay * damping * other * (1.0 - other)])
    grad_mixing = jnp.stack([damping * mixing[1] * weight, gain * weight])
    return grads, grad_logits, grad_mixing, jnp.sum(skip_sum, axis=1)


MESH = pl.DeviceIdType.MESH


class Place:
    def __init__(self, deep):
        self.deep = deep
        row, chan = lax.axis_index("row"), lax.axis_index("chan")
        self.y, self.core = row // 2, row % 2
        self.z, self.x = chan // 2, chan % 2
        self.row, self.chan = row, chan

    def owner(self, z, x, y, core):
        return (y * 2 + core) * (2 * self.deep) + z * 2 + x

    def over_core(self):
        return (self.row + 1 - 2 * self.core, self.chan)

    def over_x(self):
        return (self.row, self.chan + 1 - 2 * self.x)

    def over_y(self):
        return (self.row + 2 - 4 * self.y, self.chan)

    def at_z(self, z):
        return (self.row, z * 2 + self.x)

    def greet(self):
        barrier = pltpu.get_barrier_semaphore()
        others = [self.over_core(), self.over_x(), self.over_y()]
        others += [self.at_z((self.z + step) % self.deep) for step in range(1, self.deep)]
        for other in others:
            pl.semaphore_signal(barrier, inc=1, device_id=other, device_id_type=MESH)
        pl.semaphore_wait(barrier, len(others))


def gather_kernel(deep, *refs):
    count = 2
    mine, full = refs[:count], refs[count : 2 * count]
    local_sem, send_z, send_x, send_y, send_core, recv_z, recv_x, recv_y, recv_d, recv_core = refs[2 * count :]
    here = Place(deep)
    z, x, y, core = here.z, here.x, here.y, here.core
    me = here.owner(z, x, y, core)

    def piece(which, at, device, send, recv, source=None):
        spot = full[which].at[at]
        return pltpu.make_async_remote_copy(
            src_ref=spot if source is None else source, dst_ref=spot, send_sem=send, recv_sem=recv,
            device_id=device, device_id_type=MESH)

    def to_core(which, at, slot, source=None):
        return piece(which, at, here.over_core(), send_core.at[which, slot], recv_core.at[which, slot], source)

    def column(k, source=False):
        at = here.owner(k, x, y, core)
        made = []
        for which in range(count):
            origin = mine[which] if source else None
            made.append(piece(which, at, here.over_x(), send_x.at[which, k], recv_x.at[which, k], origin))
            made.append(piece(which, at, here.over_y(), send_y.at[which, k], recv_y.at[which, k], origin))
            made.append(to_core(which, at, k, origin))
        return made

    def along(k, to, side, source=False):
        at = here.owner(k, x, y, core)
        return [piece(which, at, here.at_z(to), send_z.at[which, k, side], recv_z.at[which, k],
                      mine[which] if source else None) for which in range(count)]

    def from_x(k):
        at = here.owner(k, 1 - x, y, core)
        return ([to_core(which, at, deep + k) for which in range(count)],
                [piece(which, at, here.over_y(), send_y.at[which, deep + k], recv_d.at[which, k]) for which in range(count)],
                [piece(which, at, here.over_x(), send_x.at[which, k], recv_x.at[which, k]) for which in range(count)])

    def from_y(k):
        at = here.owner(k, x, 1 - y, core)
        return ([to_core(which, at, 2 * deep + k) for which in range(count)],
                [piece(which, at, here.over_x(), send_x.at[which, deep + k], recv_d.at[which, k]) for which in range(count)],
                [piece(which, at, here.over_y(), send_y.at[which, k], recv_y.at[which, k]) for which in range(count)])

    def diagonal(k):
        at = here.owner(k, 1 - x, 1 - y, core)
        return ([to_core(which, at, 3 * deep + k) for which in range(count)],
                [piece(which, at, here.over_x(), send_x.at[which, deep + k], recv_d.at[which, k]) for which in range(count)])

    def start(copies):
        for copy in copies:
            copy.start()

    def sides(distance):
        return [z] if distance == 0 else [z - distance, z + distance]

    here.greet()
    local = [pltpu.make_async_copy(mine[which], full[which].at[me], local_sem.at[which]) for which in range(count)]
    start(local)
    for side, to in ((0, z - 1), (1, z + 1)):
        @pl.when((to >= 0) & (to < deep))
        def _():
            start(along(z, to, side, True))
    start(column(z, True))
    half = deep // 2

    def neighbours(distance):
        for k in sides(distance):
            @pl.when((k >= 0) & (k < deep))
            def _():
                cores, onward, arrived = from_x(k)
                for copy in arrived:
                    copy.wait_recv()

                @pl.when(k >= half)
                def _():
                    start(onward)
                start(cores)
                cores, onward, arrived = from_y(k)
                for copy in arrived:
                    copy.wait_recv()

                @pl.when(k < half)
                def _():
                    start(onward)
                start(cores)

    for distance in range(1, deep):
        for side, k in enumerate(sides(distance)):
            @pl.when((k >= 0) & (k < deep))
            def _():
                onward = z + 1 if side == 0 else z - 1
                for copy in along(k, z, 0):
                    copy.wait_recv()

                @pl.when((onward >= 0) & (onward < deep))
                def _():
                    start(along(k, onward, 1 - side))
                start(column(k))
        neighbours(distance - 1)
    neighbours(deep - 1)
    for k in range(deep):
        cores, arrived = diagonal(k)
        for copy in arrived:
            copy.wait_recv()
        start(cores)
    for copy in local:
        copy.wait()
    for slot, (flip_x, flip_y) in enumerate(((0, 0), (1, 0), (0, 1), (1, 1))):
        for k in range(deep):
            at = here.owner(k, x + flip_x * (1 - 2 * x), y + flip_y * (1 - 2 * y), 1 - core)
            for which in range(count):
                copy = to_core(which, at, slot * deep + k)
                copy.wait_recv()
                copy.wait_send()
    for k in range(deep):
        for copy in from_x(k)[2] + from_y(k)[2]:
            copy.wait_send()
        for copy in (from_x(k)[1] if k >= half else from_y(k)[1]):
            copy.wait_send()
        for side, valid in ((0, (k >= z) & (z > 0)), (1, (k <= z) & (z < deep - 1))):
            @pl.when(valid)
            def _():
                for copy in along(k, z, side):
                    copy.wait_send()


def gather_weights(first, second, devices, deep):
    dma = pltpu.SemaphoreType.DMA
    anywhere = pl.BlockSpec(memory_space=pl.ANY)
    return pl.pallas_call(
        partial(gather_kernel, deep),
        in_specs=[anywhere, anywhere],
        out_specs=[anywhere, anywhere],
        out_shape=[jax.ShapeDtypeStruct((devices,) + first.shape, first.dtype),
                   jax.ShapeDtypeStruct((devices,) + second.shape, second.dtype)],
        scratch_shapes=[dma((2,)), dma((2, deep, 2)), dma((2, 2 * deep)), dma((2, 2 * deep)), dma((2, 4 * deep)),
                        dma((2, deep)), dma((2, deep)), dma((2, deep)), dma((2, deep)), dma((2, 4 * deep))],
        compiler_params=pltpu.CompilerParams(collective_id=1, has_side_effects=True),
        cost_estimate=pl.CostEstimate(flops=0, bytes_accessed=first.size * devices * 4, transcendentals=0),
    )(first, second)


def both_ends(deep):
    order = []
    for k in range(deep // 2):
        order += [k, deep - 1 - k]
    return order


def reduce_kernel(deep, groups, *refs):
    total = sum(groups)
    sources, small = refs[:total], refs[total]
    outs, small_out = refs[total + 1 : total + 3], refs[total + 3]
    rest = refs[total + 4 :]
    held, from_core, from_d, from_x, from_y, from_z = (rest[2 * i : 2 * i + 2] for i in range(6))
    (small_sum, small_pair, small_deep, load_sem, core_send, core_recv, d_send, d_recv, x_send, x_recv, y_send, y_recv,
     z_send, z_recv, small_send, small_recv) = rest[12:]
    here = Place(deep)
    z, x, y, core = here.z, here.x, here.y, here.core
    half = deep // 2
    layers = both_ends(deep)
    wide = []
    first = 0
    for which, size in enumerate(groups):
        offset = 0
        for source in sources[first : first + size]:
            wide.append((which, source, offset, source.shape[2]))
            offset += source.shape[2]
        first += size

    def remote(source, target, send, recv, device):
        return pltpu.make_async_remote_copy(src_ref=source, dst_ref=target, send_sem=send, recv_sem=recv,
                                            device_id=device, device_id_type=MESH)

    def begin(index, carry):
        slot = 4 * deep - 1 - index
        k, flips = slot % deep, slot // deep
        to_x = x + (flips % 2) * (1 - 2 * x)
        to_y = y + (flips // 2) * (1 - 2 * y)
        own, other = here.owner(k, to_x, to_y, core), here.owner(k, to_x, to_y, 1 - core)
        for which, source, offset, width in wide:
            pltpu.make_async_copy(source.at[own], held[which].at[slot, :, pl.ds(offset, width)], load_sem.at[which, slot]).start()
            remote(source.at[other], from_core[which].at[slot, :, pl.ds(offset, width)],
                   core_send.at[which, slot], core_recv.at[which, slot], here.over_core()).start()
        return carry

    def ready(slot):
        for which in range(2):
            spot = held[which].at[slot]
            pltpu.make_async_copy(spot, spot, load_sem.at[which, slot]).wait()
            remote(spot, from_core[which].at[slot], core_send.at[which, slot], core_recv.at[which, slot], here.over_core()).wait_recv()
            held[which][slot] = held[which][slot] + from_core[which][slot]

    def send_d(which, k):
        side = (x_send, here.over_x()) if k < half else (y_send, here.over_y())
        return remote(held[which].at[3 * deep + k], from_d[which].at[k], d_send.at[which, k], d_recv.at[which, k], side[1])

    def send_x(which, k):
        return remote(held[which].at[deep + k], from_x[which].at[k], x_send.at[which, k], x_recv.at[which, k], here.over_x())

    def send_y(which, k):
        return remote(held[which].at[2 * deep + k], from_y[which].at[k], y_send.at[which, k], y_recv.at[which, k], here.over_y())

    def send_right(which, k):
        return remote(held[which].at[k], from_z[which].at[k], z_send.at[which, k], z_recv.at[which, k], here.at_z(z + 1))

    def send_left(which, k):
        slot = jnp.where(z - 1 == k, deep, k)
        return remote(held[which].at[k], from_z[which].at[slot], z_send.at[which, k], z_recv.at[which, slot], here.at_z(z - 1))

    def send_small(stage, device):
        return remote(small_sum.at[stage], small_pair.at[stage], small_send.at[stage], small_recv.at[stage], device)

    def send_small_deep(step):
        return remote(small_deep.at[z], small_deep.at[z], small_send.at[3 + step], small_recv.at[3 + step],
                      here.at_z((z + step) % deep))

    here.greet()
    small_sum[0] = small[...]
    send_small(0, here.over_core()).start()
    lax.fori_loop(0, 4 * deep, begin, 0)

    def small_step(stage, device):
        send_small(stage, device).wait_recv()
        small_sum[stage + 1] = small_sum[stage] + small_pair[stage]

    def pair(low, high):
        for k in (low, high):
            ready(3 * deep + k)
            for which in range(2):
                send_d(which, k).start()
        ready(deep + low)
        for which in range(2):
            send_x(which, low).start()
        ready(2 * deep + high)
        for which in range(2):
            send_y(which, high).start()
        ready(deep + high)
        for which in range(2):
            send_d(which, high).wait_recv()
            held[which][deep + high] = held[which][deep + high] + from_d[which][high]
            send_x(which, high).start()
        ready(2 * deep + low)
        for which in range(2):
            send_d(which, low).wait_recv()
            held[which][2 * deep + low] = held[which][2 * deep + low] + from_d[which][low]
            send_y(which, low).start()

    stage = 0
    devices = (here.over_core(), here.over_x(), here.over_y())
    for low in range(half):
        pair(low, deep - 1 - low)
        if stage < 2:
            small_step(stage, devices[stage])
            stage += 1
            send_small(stage, devices[stage]).start()
    while stage < 3:
        small_step(stage, devices[stage])
        stage += 1
        if stage < 3:
            send_small(stage, devices[stage]).start()
    small_deep[z] = small_sum[3]
    for step in range(1, deep):
        send_small_deep(step).start()
    for k in layers:
        ready(k)
        for which in range(2):
            send_x(which, k).wait_recv()
            send_y(which, k).wait_recv()
            held[which][k] = (held[which][k].astype(jnp.float32) + from_x[which][k].astype(jnp.float32)
                              + from_y[which][k].astype(jnp.float32)).astype(jnp.bfloat16)

        @pl.when(k > z)
        def _():
            for which in range(2):
                @pl.when(z > 0)
                def _():
                    send_right(which, k).wait_recv()
                    held[which][k] = held[which][k] + from_z[which][k]
                send_right(which, k).start()

        @pl.when(k < z)
        def _():
            for which in range(2):
                @pl.when(z < deep - 1)
                def _():
                    remote(held[which].at[k], from_z[which].at[k], z_send.at[which, k], z_recv.at[which, k], here.at_z(z - 1)).wait_recv()
                    held[which][k] = held[which][k] + from_z[which][k]
                send_left(which, k).start()

    for which in range(2):
        outs[which][...] = held[which][z].astype(jnp.float32)

        @pl.when(z > 0)
        def _():
            send_right(which, z).wait_recv()
            outs[which][...] += from_z[which][z].astype(jnp.float32)

        @pl.when(z < deep - 1)
        def _():
            remote(held[which].at[z], from_z[which].at[deep], z_send.at[which, z], z_recv.at[which, deep], here.at_z(z)).wait_recv()
            outs[which][...] += from_z[which][deep].astype(jnp.float32)
    for step in range(1, deep):
        origin = (z + deep - step) % deep
        pltpu.make_async_remote_copy(
            src_ref=small_deep.at[origin], dst_ref=small_deep.at[origin], send_sem=small_send.at[3 + step],
            recv_sem=small_recv.at[3 + step], device_id=here.at_z(origin), device_id_type=MESH).wait_recv()
    added = small_deep[0]
    for k in range(1, deep):
        added = added + small_deep[k]
    small_out[...] = added
    for stage in range(3):
        send_small(stage, devices[stage]).wait_send()
    for step in range(1, deep):
        send_small_deep(step).wait_send()
    for which in range(2):
        for slot in range(4 * deep):
            remote(held[which].at[slot], from_core[which].at[slot], core_send.at[which, slot], core_recv.at[which, slot], here.over_core()).wait_send()
        for k in range(deep):
            send_d(which, k).wait_send()
            send_x(which, k).wait_send()
            send_y(which, k).wait_send()

            @pl.when(k > z)
            def _():
                send_right(which, k).wait_send()

            @pl.when(k < z)
            def _():
                send_left(which, k).wait_send()


def reduce_weights(first, second, small, deep):
    dma = pltpu.SemaphoreType.DMA
    anywhere = pl.BlockSpec(memory_space=pl.ANY)
    vmem = pl.BlockSpec(memory_space=pltpu.VMEM)
    shapes = [(group[0].shape[1], sum(part.shape[2] for part in group)) for group in (first, second)]
    scratch = []
    for count in (4 * deep, 4 * deep, deep, deep, deep, deep + 1):
        scratch += [pltpu.VMEM((count,) + shape, jnp.bfloat16) for shape in shapes]
    scratch += [pltpu.VMEM((4,) + small.shape, jnp.float32), pltpu.VMEM((3,) + small.shape, jnp.float32),
                pltpu.VMEM((deep,) + small.shape, jnp.float32)]
    scratch += [dma((2, 4 * deep))] * 3 + [dma((2, deep))] * 6 + [dma((2, deep)), dma((2, deep + 1))] + [dma((3 + deep,))] * 2
    return pl.pallas_call(
        partial(reduce_kernel, deep, (len(first), len(second))),
        in_specs=[anywhere] * (len(first) + len(second)) + [vmem],
        out_specs=[vmem] * 3,
        out_shape=[jax.ShapeDtypeStruct(shape, jnp.float32) for shape in shapes] + [jax.ShapeDtypeStruct(small.shape, jnp.float32)],
        scratch_shapes=scratch,
        compiler_params=pltpu.CompilerParams(collective_id=2, has_side_effects=True, vmem_limit_bytes=56 * 1024 * 1024),
        cost_estimate=pl.CostEstimate(flops=0, bytes_accessed=64 * 1024 * 1024, transcendentals=0),
    )(*first, *second, small)


def whole_weights(first, second):
    if lax.axis_size("row") == 4:
        devices = lax.axis_size("row") * lax.axis_size("chan")
        return gather_weights(first, second, devices, lax.axis_size("chan") // 2)
    return [lax.all_gather(part, ("row", "chan"), axis=0) for part in (first, second)]


def owned_sums(first, second, small):
    if lax.axis_size("row") == 4:
        return reduce_weights(first, second, small, lax.axis_size("chan") // 2)
    sums = [
        [lax.psum_scatter(part, ("row", "chan"), scatter_dimension=0, tiled=True)[0] for part in group]
        for group in (first, second)
    ]
    return [jnp.concatenate(group, axis=1).astype(jnp.float32) for group in sums] + [lax.psum(small, ("row", "chan"))]


def pack(parts):
    flat = jnp.concatenate([part.reshape(-1) for part in parts])
    return jnp.pad(flat, (0, -flat.shape[0] % 1024)).reshape(-1, 128)


def unpack(packed, like):
    flat, made, offset = packed.reshape(-1), [], 0
    for part in like:
        made.append(flat[offset : offset + part.size].reshape(part.shape))
        offset += part.size
    return made


def product(left, right):
    return jnp.dot(left, right, preferred_element_type=jnp.float32)


def contract_rows(left, right):
    return lax.dot_general(
        left, right, (((0,), (0,)), ((), ())), preferred_element_type=jnp.float32
    )


def contract_cols(left, right):
    return lax.dot_general(
        left, right, (((1,), (1,)), ((), ())), preferred_element_type=jnp.float32
    )


def token_rows(blocked):
    return jnp.transpose(blocked, (0, 2, 1)).reshape(-1, blocked.shape[1])


def channel_blocks(matrix, row_count):
    return jnp.transpose(matrix.reshape(row_count, -1, matrix.shape[1]), (0, 2, 1))


def shards(
    inputs,
    cotangent,
    doc_lengths,
    ema_logits,
    ema_mixing,
    ema_skip,
    value_weight,
    base_weight,
    attn_weight,
    hidden_weight,
    output_weight,
    value_bias,
    base_bias,
    attn_bias,
    hidden_bias,
    output_bias,
    query_key_gain,
    query_key_shift,
    position_bias,
    norm_gain,
    norm_bias,
):
    row_count, chan_count, seq_length = inputs.shape
    group_count = lax.axis_size("chan")
    width = chan_count * group_count
    span_local = seq_length // group_count
    length_block = position_bias.shape[0]
    shared_width = query_key_gain.shape[1]
    value_width = value_bias.shape[0]
    token_count = row_count * span_local
    window_count = token_count // length_block
    score_scale = shared_width ** (-0.5)
    positions = jnp.arange(seq_length, dtype=jnp.int32)
    segment_rows = jax.vmap(segment_ids, (0, None))(doc_lengths, positions)

    keep, keep_next = keep_tables(segment_rows)
    pre_mix, mixed = ema_forward(inputs, keep, ema_logits, ema_mixing, ema_skip)
    first, second = whole_weights(
        jnp.concatenate([part.astype(jnp.bfloat16) for part in (value_weight, base_weight, hidden_weight)], axis=1),
        jnp.concatenate([part.astype(jnp.bfloat16) for part in (attn_weight, output_weight)], axis=1),
    )
    first, second = first.reshape(width, -1), second.reshape(value_width, -1)
    base_width = base_bias.shape[0]
    value_low = first[:, :value_width]
    base_low = first[:, value_width : value_width + base_width]
    hidden_low = first[:, value_width + base_width :]
    attn_low, output_low = second[:, :width], second[:, width:]
    token_input, token_mixed = (
        lax.all_to_all(inputs, "chan", split_axis=2, concat_axis=1, tiled=True),
        lax.all_to_all(mixed, "chan", split_axis=2, concat_axis=1, tiled=True),
    )
    input_rows = token_rows(token_input)
    mixed_rows = token_rows(token_mixed)
    local_pos = lax.axis_index("chan") * span_local + jnp.arange(span_local, dtype=jnp.int32)
    segment_local = jax.vmap(segment_ids, (0, None))(doc_lengths, local_pos).reshape(
        window_count, length_block
    )
    offset_hits = offset_table(length_block)
    bias_table = jnp.einsum("ijm,m->ij", offset_hits, position_bias, precision=HIGH)
    offsets = jnp.arange(length_block, dtype=jnp.int32)
    allowed = (offsets[:, None] >= offsets[None, :])[None] & (
        segment_local[:, :, None] == segment_local[:, None, :]
    )
    value_pre = product(input_rows, value_low) + value_bias
    value_rows = jax.nn.silu(value_pre).astype(jnp.bfloat16)
    base_proj = product(mixed_rows, base_low) + base_bias
    gate_pre = base_proj[:, :width]
    shared_pre = base_proj[:, width : width + shared_width]
    reset_pre = base_proj[:, width + shared_width : width + shared_width + value_width]
    direct_part = base_proj[:, width + shared_width + value_width :]
    update_gate = jax.nn.sigmoid(gate_pre)
    shared_z = jax.nn.silu(shared_pre)
    reset_gate = jax.nn.silu(reset_pre)
    queries = (
        (shared_z * query_key_gain[0] + query_key_shift[0])
        .astype(jnp.bfloat16)
        .reshape(window_count, length_block, shared_width)
    )
    key_rows = (
        (shared_z * query_key_gain[1] + query_key_shift[1])
        .astype(jnp.bfloat16)
        .reshape(window_count, length_block, shared_width)
    )
    value_win = value_rows.reshape(window_count, length_block, value_width)
    scores = (
        jnp.einsum("cik,cjk->cij", queries, key_rows, preferred_element_type=jnp.float32)
        * score_scale
        + bias_table[None]
    )
    attention = jax.nn.softmax(jnp.where(allowed, scores, MASKED), axis=-1)
    attention_low = attention.astype(jnp.bfloat16)
    attended = jnp.einsum(
        "cij,cjv->civ", attention_low, value_win, preferred_element_type=jnp.float32
    ).reshape(token_count, value_width)
    mixed_att = (attended * reset_gate).astype(jnp.bfloat16)
    hidden_pre = direct_part + product(mixed_att, attn_low) + attn_bias
    hidden = jax.nn.silu(hidden_pre)
    input_float = input_rows.astype(jnp.float32)
    out_one = input_float + update_gate * (hidden - input_float)
    normed, norm_back_one = jax.vjp(layer_norm, out_one, norm_gain[0], norm_bias[0])
    normed_low = normed.astype(jnp.bfloat16)
    inner_pre = product(normed_low, hidden_low) + hidden_bias
    activated = jax.nn.silu(inner_pre).astype(jnp.bfloat16)
    out_two = normed + product(activated, output_low) + output_bias
    final_rows, norm_back_two = jax.vjp(layer_norm, out_two, norm_gain[1], norm_bias[1])
    layer_out = lax.all_to_all(
        channel_blocks(final_rows.astype(jnp.bfloat16), row_count),
        "chan",
        split_axis=1,
        concat_axis=2,
        tiled=True,
    )
    token_grad = lax.all_to_all(cotangent, "chan", split_axis=2, concat_axis=1, tiled=True)
    grad_rows = token_rows(token_grad).astype(jnp.float32)
    back_two, gain_two, shift_two = norm_back_two(grad_rows)
    back_outer = back_two.astype(jnp.bfloat16)
    grad_output_weight = contract_rows(activated, back_outer)
    grad_output_bias = jnp.sum(back_two, axis=0)
    back_inner = (contract_cols(back_outer, output_low) * silu_slope(inner_pre)).astype(
        jnp.bfloat16
    )
    grad_hidden_weight = contract_rows(normed_low, back_inner)
    grad_hidden_bias = jnp.sum(back_inner.astype(jnp.float32), axis=0)
    back_normed = back_two + contract_cols(back_inner, hidden_low)
    back_one, gain_one, shift_one = norm_back_one(back_normed)
    back_hidden = back_one * update_gate * silu_slope(hidden_pre)
    back_proj = back_hidden.astype(jnp.bfloat16)
    grad_attn_weight = contract_rows(mixed_att, back_proj)
    grad_attn_bias = jnp.sum(back_hidden, axis=0)
    back_mix = contract_cols(back_proj, attn_low)
    back_attended = (back_mix * reset_gate).astype(jnp.bfloat16)
    back_reset = back_mix * attended
    back_att_win = back_attended.reshape(window_count, length_block, value_width)
    back_attention = jnp.einsum(
        "civ,cjv->cij", back_att_win, value_win, preferred_element_type=jnp.float32
    )
    back_values = jnp.einsum(
        "cij,civ->cjv", attention_low, back_att_win, preferred_element_type=jnp.float32
    ).reshape(token_count, value_width)
    back_scores = (
        attention * (back_attention - jnp.sum(attention * back_attention, axis=-1, keepdims=True))
    ).astype(jnp.bfloat16)
    grad_position = jnp.einsum(
        "ijm,ij->m", offset_hits, jnp.sum(back_scores.astype(jnp.float32), axis=0), precision=HIGH
    )
    back_queries = (
        jnp.einsum(
            "cij,cjk->cik", back_scores, key_rows, preferred_element_type=jnp.float32
        ).reshape(token_count, shared_width)
        * score_scale
    )
    back_keys = (
        jnp.einsum(
            "cij,cik->cjk", back_scores, queries, preferred_element_type=jnp.float32
        ).reshape(token_count, shared_width)
        * score_scale
    )
    back_shared = back_queries * query_key_gain[0] + back_keys * query_key_gain[1]
    grad_key_gain = jnp.stack(
        [jnp.sum(back_queries * shared_z, axis=0), jnp.sum(back_keys * shared_z, axis=0)]
    )
    grad_key_shift = jnp.stack([jnp.sum(back_queries, axis=0), jnp.sum(back_keys, axis=0)])
    back_value = (back_values * silu_slope(value_pre)).astype(jnp.bfloat16)
    grad_value_weight = contract_rows(input_rows, back_value)
    grad_value_bias = jnp.sum(back_value.astype(jnp.float32), axis=0)
    back_base = jnp.concatenate(
        [
            back_one * (hidden - input_float) * update_gate * (1.0 - update_gate),
            back_shared * silu_slope(shared_pre),
            back_reset * silu_slope(reset_pre),
            back_hidden,
        ],
        axis=1,
    ).astype(jnp.bfloat16)
    grad_base_weight = contract_rows(mixed_rows, back_base)
    grad_base_bias = jnp.sum(back_base.astype(jnp.float32), axis=0)
    back_mixed_rows = contract_cols(back_base, base_low)
    back_direct = back_one * (1.0 - update_gate) + contract_cols(back_value, value_low)
    back_input, back_mixed = (
        lax.all_to_all(
            channel_blocks(back_direct, row_count).astype(jnp.bfloat16),
            "chan",
            split_axis=1,
            concat_axis=2,
            tiled=True,
        ),
        lax.all_to_all(
            channel_blocks(back_mixed_rows, row_count).astype(jnp.bfloat16),
            "chan",
            split_axis=1,
            concat_axis=2,
            tiled=True,
        ),
    )
    grad_inputs, grad_logits, grad_mixing, grad_skip = ema_backward(
        inputs, pre_mix, back_mixed, back_input, keep, keep_next, ema_logits, ema_mixing, ema_skip
    )
    grad_logits, grad_mixing, grad_skip = lax.psum((grad_logits, grad_mixing, grad_skip), "row")
    grad_norm_gain = jnp.stack([gain_one, gain_two])
    grad_norm_bias = jnp.stack([shift_one, shift_two])
    small = (
        grad_value_bias,
        grad_base_bias,
        grad_attn_bias,
        grad_hidden_bias,
        grad_output_bias,
        grad_key_gain,
        grad_key_shift,
        grad_position,
        grad_norm_gain,
        grad_norm_bias,
    )

    def owners(terms):
        devices = lax.axis_size("row") * group_count
        return terms.astype(jnp.bfloat16).reshape(devices, -1, terms.shape[1])

    first_sum, second_sum, small_sum = owned_sums(
        [owners(grad_value_weight), owners(grad_base_weight), owners(grad_hidden_weight)],
        [owners(grad_attn_weight), owners(grad_output_weight)],
        pack(small),
    )
    (
        sum_value_bias,
        sum_base_bias,
        sum_attn_bias,
        sum_hidden_bias,
        sum_output_bias,
        sum_key_gain,
        sum_key_shift,
        sum_position,
        sum_norm_gain,
        sum_norm_bias,
    ) = unpack(small_sum, small)
    owner_value = first_sum[:, :value_width]
    owner_base = first_sum[:, value_width : value_width + base_width]
    owner_hidden = first_sum[:, value_width + base_width :]
    owner_attn, owner_output = second_sum[:, :width], second_sum[:, width:]
    return (
        layer_out,
        grad_inputs,
        grad_logits,
        grad_mixing,
        grad_skip,
        owner_value,
        owner_base,
        owner_attn,
        owner_hidden,
        owner_output,
        sum_value_bias,
        sum_base_bias,
        sum_attn_bias,
        sum_hidden_bias,
        sum_output_bias,
        sum_key_gain,
        sum_key_shift,
        sum_position,
        sum_norm_gain,
        sum_norm_bias,
    )


def solution(mesh):
    in_specs = (
        P("row", "chan", None),
        P("row", "chan", None),
        P("row", None),
        P(None, "chan", None),
        P(None, "chan", None),
        P("chan"),
        P(("row", "chan"), None),
        P(("row", "chan"), None),
        P(("row", "chan"), None),
        P(("row", "chan"), None),
        P(("row", "chan"), None),
        P(),
        P(),
        P(),
        P(),
        P(),
        P(),
        P(),
        P(),
        P(),
        P(),
    )
    out_specs = (
        P("row", "chan", None),
        P("row", "chan", None),
        P(None, "chan", None),
        P(None, "chan", None),
        P("chan"),
        P(("row", "chan"), None),
        P(("row", "chan"), None),
        P(("row", "chan"), None),
        P(("row", "chan"), None),
        P(("row", "chan"), None),
        P(),
        P(),
        P(),
        P(),
        P(),
        P(),
        P(),
        P(),
        P(),
        P(),
    )
    return jax.shard_map(shards, mesh=mesh, in_specs=in_specs, out_specs=out_specs, check_vma=False)
```

```python
from functools import partial

import jax
import jax.numpy as jnp
from jax import lax
from jax.experimental import pallas as pl
from jax.experimental.pallas import tpu as pltpu
from jax.sharding import PartitionSpec as P

HIGH = lax.Precision.HIGHEST
EPSILON = 1e-05
MASKED = -1e30


def segment_ids(lengths, positions):
    boundary = jnp.cumsum(lengths)
    passed = (positions[:, None] >= boundary[None, :]).astype(jnp.int32)
    return jnp.sum(passed, axis=1)


def silu_slope(values):
    logistic = jax.nn.sigmoid(values)
    return logistic * (1.0 + values * (1.0 - logistic))


def layer_norm(values, scale_row, shift_row):
    center = jnp.mean(values, axis=-1, keepdims=True)
    centered = values - center
    spread = jnp.mean(centered * centered, axis=-1, keepdims=True)
    return centered * lax.rsqrt(spread + EPSILON) * scale_row + shift_row


def offset_table(length_block):
    offsets = jnp.arange(length_block, dtype=jnp.int32)
    distance = offsets[:, None] - offsets[None, :]
    return (distance[:, :, None] == offsets[None, None, :]).astype(jnp.float32)


LANES = 128
STEPS = 16
MESH = pl.DeviceIdType.MESH


def pad_rows(block):
    short = LANES - block.shape[0]
    if short == 0:
        return block
    return jnp.concatenate([block, jnp.zeros((short, block.shape[1]), block.dtype)], axis=0)


def spread(block, slots, row, rows):
    turned = pad_rows(block).T
    slots[pl.ds(row, LANES, stride=2 * rows), :] = turned
    slots[pl.ds(row + rows, LANES, stride=2 * rows), :] = turned


def gather(slots, row, rows, chans):
    first = slots[pl.ds(row, LANES, stride=2 * rows), :]
    second = slots[pl.ds(row + rows, LANES, stride=2 * rows), :]
    return (first + second).T[:chans]


def tile_of(ref, tile):
    return ref.at[:, :, pl.ds(pl.multiple_of(tile * LANES, LANES), LANES)]


def lanes_of(ref, tile):
    return ref[:, pl.ds(pl.multiple_of(tile * LANES, LANES), LANES)]


def slot_at(step, tall):
    return pl.ds(pl.multiple_of(step * tall, tall), tall)


def average_tile(x_tile, keep_tile, decay_ref, gain_ref, skip_ref, pre_tile, mixed_tile, slots, state):
    rows, chans, _ = x_tile.shape
    halves = decay_ref.shape[0]
    tall = 2 * rows
    for row in range(rows):
        spread(x_tile[row].astype(jnp.float32), slots, row, rows)

    def group(step, carry):
        keeping, states = carry
        states = list(states)
        for inner in range(STEPS):
            at = slot_at(step * STEPS + inner, tall)
            value = slots[at, :]
            keep = jnp.broadcast_to(keeping[:, inner : inner + 1], (tall, LANES))
            total = None
            for n in range(halves):
                states[n] = (decay_ref[n] * keep) * states[n] + gain_ref[n] * value
                total = states[n] if total is None else total + states[n]
            slots[at, :] = total
        return pltpu.roll(keeping, LANES - STEPS, axis=1), tuple(states)

    start = tuple(state[n] for n in range(halves))
    _, states = lax.fori_loop(0, LANES // STEPS, group, (keep_tile, start))
    for n in range(halves):
        state[n] = states[n]
    for row in range(rows):
        pre = gather(slots, row, rows, chans) + skip_ref[:, :1] * x_tile[row].astype(jnp.float32)
        pre_tile[row] = pre
        mixed_tile[row] = (pre * jax.nn.sigmoid(pre)).astype(jnp.bfloat16)


def back_tile_of(back_slots, tile, tall):
    return back_slots.at[pl.ds(pl.multiple_of(tile * (LANES * tall), LANES * tall), LANES * tall), :]


def weigh_tile(x_tile, pre_tile, back_mixed_tile, keep_tile, decay_ref, skip_sum, slots, back_tile, state, powers, weight_sum, power_sum):
    rows = x_tile.shape[0]
    halves = decay_ref.shape[0]
    tall = 2 * rows
    for row in range(rows):
        values = x_tile[row].astype(jnp.float32)
        pre = pre_tile[row]
        logistic = jax.nn.sigmoid(pre)
        back = back_mixed_tile[row].astype(jnp.float32) * (logistic * (1.0 + pre * (1.0 - logistic)))
        skip_sum[...] += back * values
        spread(values, slots, row, rows)
        spread(back, back_tile, row, rows)

    def group(step, carry):
        keeping, states, derived, weights, sums = (carry[0], *map(list, carry[1:]))
        for inner in range(STEPS):
            at = slot_at(step * STEPS + inner, tall)
            value = slots[at, :]
            back = back_tile[at, :]
            keep = jnp.broadcast_to(keeping[:, inner : inner + 1], (tall, LANES))
            for n in range(halves):
                decay = decay_ref[n] * keep
                derived[n] = decay * (derived[n] + states[n])
                states[n] = decay * states[n] + value
                weights[n] = weights[n] + back * states[n]
                sums[n] = sums[n] + back * derived[n]
        return pltpu.roll(keeping, LANES - STEPS, axis=1), tuple(states), tuple(derived), tuple(weights), tuple(sums)

    refs = (state, powers, weight_sum, power_sum)
    start = tuple(tuple(ref[n] for n in range(halves)) for ref in refs)
    out = lax.fori_loop(0, LANES // STEPS, group, (keep_tile, *start))
    for ref, values in zip(refs, out[1:]):
        for n in range(halves):
            ref[n] = values[n]


def adjoint_tile(direct_tile, next_tile, decay_ref, gain_ref, skip_row_ref, grad_tile, slots, back_tile, state):
    rows, chans, _ = direct_tile.shape
    halves = decay_ref.shape[0]
    tall = 2 * rows

    def group(step, carry):
        keeping, states = carry
        states = list(states)
        for inner in range(STEPS):
            at = slot_at(LANES - 1 - step * STEPS - inner, tall)
            back = back_tile[at, :]
            keep = jnp.broadcast_to(keeping[:, LANES - 1 - inner : LANES - inner], (tall, LANES))
            total = skip_row_ref[...] * back
            for n in range(halves):
                states[n] = (decay_ref[n] * keep) * states[n] + back
                total = total + gain_ref[n] * states[n]
            slots[at, :] = total
        return pltpu.roll(keeping, STEPS, axis=1), tuple(states)

    start = tuple(state[n] for n in range(halves))
    _, states = lax.fori_loop(0, LANES // STEPS, group, (next_tile, start))
    for n in range(halves):
        state[n] = states[n]
    for row in range(rows):
        grad_tile[row] = direct_tile[row].astype(jnp.float32) + gather(slots, row, rows, chans)


class Place:
    def __init__(self, deep):
        self.deep = deep
        row, chan = lax.axis_index("row"), lax.axis_index("chan")
        self.y, self.core = row // 2, row % 2
        self.z, self.x = chan // 2, chan % 2
        self.row, self.chan = row, chan

    def owner(self, z, x, y, core):
        return (y * 2 + core) * (2 * self.deep) + z * 2 + x

    def over_core(self):
        return (self.row + 1 - 2 * self.core, self.chan)

    def over_x(self):
        return (self.row, self.chan + 1 - 2 * self.x)

    def over_y(self):
        return (self.row + 2 - 4 * self.y, self.chan)

    def at_z(self, z):
        return (self.row, z * 2 + self.x)

    def at_chan(self, step):
        chan = (self.chan + step) % (2 * self.deep)
        return chan, (self.row, chan)

    def greet(self):
        barrier = pltpu.get_barrier_semaphore()
        others = [self.over_core(), self.over_y()]
        others += [self.at_chan(step)[1] for step in range(1, 2 * self.deep)]
        for other in others:
            pl.semaphore_signal(barrier, inc=1, device_id=other, device_id_type=MESH)
        pl.semaphore_wait(barrier, len(others))


def remote(source, target, send, recv, device):
    return pltpu.make_async_remote_copy(src_ref=source, dst_ref=target, send_sem=send, recv_sem=recv,
                                        device_id=device, device_id_type=MESH)


def start(copies):
    for copy in copies:
        copy.start()


class ToTokens:
    def __init__(self, here, source, target, send, recv, keep):
        self.here, self.source, self.target = here, source, target
        self.send, self.recv, self.keep = send, recv, keep
        self.chans, self.span = source.shape[1], target.shape[2]

    def block(self, chan):
        return self.source.at[:, :, pl.ds(pl.multiple_of(chan * self.span, LANES), self.span)]

    def spot(self, chan):
        return self.target.at[:, pl.ds(pl.multiple_of(chan * self.chans, 8), self.chans), :]

    def own(self):
        return pltpu.make_async_copy(self.block(self.here.chan), self.spot(self.here.chan), self.keep)

    def out(self, chan):
        return remote(self.block(chan), self.spot(self.here.chan), self.send.at[chan], self.recv.at[self.here.chan], (self.here.row, chan))

    def arrival(self, chan):
        return remote(self.block(chan), self.spot(chan), self.send.at[chan], self.recv.at[chan], (self.here.row, chan))

    def begin(self):
        for step in range(1, 2 * self.here.deep):
            self.out(self.here.at_chan(step)[0]).start()
        self.own().start()

    def begin_one(self, chan):
        @pl.when(chan == self.here.chan)
        def _():
            self.own().start()

        @pl.when(chan != self.here.chan)
        def _():
            self.out(chan).start()

    def arrive(self):
        self.own().wait()
        for step in range(1, 2 * self.here.deep):
            self.arrival(self.here.at_chan(step)[0]).wait_recv()

    def finish(self):
        for step in range(1, 2 * self.here.deep):
            self.out(self.here.at_chan(step)[0]).wait_send()


class ToChannels(ToTokens):
    def __init__(self, here, source, target, send, recv, keep):
        super().__init__(here, source, target, send, recv, keep)
        self.chans, self.span = target.shape[1], source.shape[2]

    def block(self, chan):
        return self.source.at[:, pl.ds(pl.multiple_of(chan * self.chans, 8), self.chans), :]

    def spot(self, chan):
        return self.target.at[:, :, pl.ds(pl.multiple_of(chan * self.span, LANES), self.span)]


def forward_kernel(deep, first, second, x_ref, keep_ref, decay_ref, gain_ref, skip_ref,
                   first_full, second_full, token_x, token_mixed, pre_ref,
                   mixed, slots, state, local_sem, send_z, send_x, send_y, send_core, recv_z, recv_x, recv_y, recv_d, recv_core,
                   a_send, a_recv, b_send, b_recv):
    count = 2
    mine, full = (first, second), (first_full, second_full)
    here = Place(deep)
    z, x, y, core = here.z, here.x, here.y, here.core
    me = here.owner(z, x, y, core)
    layers = range(deep)

    def piece(which, at, device, send, recv, source=None):
        spot = full[which].at[at]
        return remote(spot if source is None else source, spot, send, recv, device)

    def to_core(at, slot, source=False):
        return [piece(which, at, here.over_core(), send_core.at[which, slot], recv_core.at[which, slot],
                      mine[which] if source else None) for which in range(count)]

    def own_x(k, source=False):
        at = here.owner(k, x, y, core)
        return [piece(which, at, here.over_x(), send_x.at[which, k], recv_x.at[which, k],
                      mine[which] if source else None) for which in range(count)]

    def own_y(k, source=False):
        at = here.owner(k, x, y, core)
        return [piece(which, at, here.over_y(), send_y.at[which, k], recv_y.at[which, k],
                      mine[which] if source else None) for which in range(count)]

    def column(k, source=False):
        start(own_x(k, source))
        start(own_y(k, source))
        start(to_core(here.owner(k, x, y, core), k, source))

    def along(k, to, side, source=False):
        at = here.owner(k, x, y, core)
        return [piece(which, at, here.at_z(to), send_z.at[which, k, side], recv_z.at[which, k],
                      mine[which] if source else None) for which in range(count)]

    def onward(k):
        at = here.owner(k, 1 - x, y, core)
        return [piece(which, at, here.over_y(), send_y.at[which, deep + k], recv_d.at[which, k]) for which in range(count)]

    def wait_from(at, recv, k, device):
        for which in range(count):
            piece(which, at, device, send_x.at[which, 0], recv.at[which, k]).wait_recv()

    def sides(distance):
        return [z] if distance == 0 else [z - distance, z + distance]

    def neighbours(distance):
        for k in sides(distance):
            @pl.when((k >= 0) & (k < deep))
            def _():
                at = here.owner(k, 1 - x, y, core)
                wait_from(at, recv_x, k, here.over_x())
                start(onward(k))
                start(to_core(at, deep + k))
                at = here.owner(k, x, 1 - y, core)
                wait_from(at, recv_y, k, here.over_y())
                start(to_core(at, 2 * deep + k))

    def layer_step(distance):
        for side, k in enumerate(sides(distance)):
            @pl.when((k >= 0) & (k < deep))
            def _():
                to = z + 1 if side == 0 else z - 1
                wait_from(here.owner(k, x, y, core), recv_z, k, here.at_z(z))

                @pl.when((to >= 0) & (to < deep))
                def _():
                    start(along(k, to, 1 - side))
                column(k)

    here.greet()
    tokens_x = ToTokens(here, x_ref, token_x, a_send, a_recv, local_sem.at[2])
    tokens_mixed = ToTokens(here, mixed, token_mixed, b_send, b_recv, local_sem.at[3])
    local = [pltpu.make_async_copy(mine[which], full[which].at[me], local_sem.at[which]) for which in range(count)]
    start(local)
    for side, to in ((0, z - 1), (1, z + 1)):
        @pl.when((to >= 0) & (to < deep))
        def _():
            start(along(z, to, side, True))
    column(z, True)
    tokens_x.begin()
    state[...] = jnp.zeros_like(state)
    tiles = x_ref.shape[2] // LANES
    each = tokens_x.span // LANES

    def tile_step(tile, carry):
        average_tile(tile_of(x_ref, tile), lanes_of(keep_ref, tile), decay_ref, gain_ref, skip_ref,
                     tile_of(pre_ref, tile), tile_of(mixed, tile), slots, state)

        @pl.when(tile % each == each - 1)
        def _():
            tokens_mixed.begin_one(tile // each)

        @pl.when(tile == tiles // 2 - 1)
        def _():
            layer_step(1)
        return carry

    lax.fori_loop(0, tiles, tile_step, 0)
    neighbours(0)
    for distance in range(2, deep):
        layer_step(distance)
        neighbours(distance - 1)
    neighbours(deep - 1)
    for k in layers:
        at = here.owner(k, 1 - x, 1 - y, core)
        wait_from(at, recv_d, k, here.over_y())
        start(to_core(at, 3 * deep + k))
    for copy in local:
        copy.wait()
    tokens_x.arrive()
    tokens_mixed.arrive()
    for slot, (flip_x, flip_y) in enumerate(((0, 0), (1, 0), (0, 1), (1, 1))):
        for k in layers:
            at = here.owner(k, x + flip_x * (1 - 2 * x), y + flip_y * (1 - 2 * y), 1 - core)
            for copy in to_core(at, slot * deep + k):
                copy.wait_recv()
                copy.wait_send()
    for k in layers:
        for copy in own_x(k) + own_y(k) + onward(k):
            copy.wait_send()
        for side, valid in ((0, (k >= z) & (z > 0)), (1, (k <= z) & (z < deep - 1))):
            @pl.when(valid)
            def _():
                for copy in along(k, z, side):
                    copy.wait_send()
    tokens_x.finish()
    tokens_mixed.finish()


def both_ends(deep):
    order = []
    for k in range(deep // 2):
        order += [k, deep - 1 - k]
    return order


def backward_kernel(deep, groups, *refs):
    total = sum(groups)
    sources = refs[:total]
    (small, x_ref, pre_ref, mixed_rows, direct_rows, keep_ref, next_ref, decay_ref, gain_ref, skip_row_ref) = refs[total : total + 10]
    refs = refs[total + 10 :]
    first_out, second_out, small_out, grad_ref, sums_out, skips_out = refs[:6]
    outs = (first_out, second_out)
    rest = refs[6:]
    held, from_core, from_d, from_x, from_y, from_z = (rest[2 * i : 2 * i + 2] for i in range(6))
    (small_sum, small_pair, small_deep, load_sem, core_send, core_recv, d_send, d_recv, x_send, x_recv, y_send, y_recv,
     z_send, z_recv, small_send, small_recv, back_mixed, direct, slots, back_slots, state, powers, sums, sums_pair,
     skips, skips_pair,     local_sem, a_send, a_recv, b_send, b_recv, sums_send, sums_recv) = rest[12:]
    here = Place(deep)
    z, x, y, core = here.z, here.x, here.y, here.core
    rows, chans, length = x_ref.shape
    halves = decay_ref.shape[0]
    tall = 2 * rows
    tiles = length // LANES
    wide = []
    first = 0
    for which, size in enumerate(groups):
        offset = 0
        for source in sources[first : first + size]:
            wide.append((which, source, offset, source.shape[2]))
            offset += source.shape[2]
        first += size

    def begin(index, carry):
        slot = 4 * deep - 1 - index
        k, flips = slot % deep, slot // deep
        to_x = x + (flips % 2) * (1 - 2 * x)
        to_y = y + (flips // 2) * (1 - 2 * y)
        own, other = here.owner(k, to_x, to_y, core), here.owner(k, to_x, to_y, 1 - core)
        for which, source, offset, width in wide:
            pltpu.make_async_copy(source.at[own], held[which].at[slot, :, pl.ds(offset, width)], load_sem.at[which, slot]).start()
            remote(source.at[other], from_core[which].at[slot, :, pl.ds(offset, width)],
                   core_send.at[which, slot], core_recv.at[which, slot], here.over_core()).start()
        return carry

    def ready(slot):
        for which in range(2):
            spot = held[which].at[slot]
            pltpu.make_async_copy(spot, spot, load_sem.at[which, slot]).wait()
            remote(spot, from_core[which].at[slot], core_send.at[which, slot], core_recv.at[which, slot], here.over_core()).wait_recv()
            held[which][slot] = held[which][slot] + from_core[which][slot]

    def send_d(which, k):
        return remote(held[which].at[3 * deep + k], from_d[which].at[k], d_send.at[which, k], d_recv.at[which, k], here.over_y())

    def send_x(which, k):
        return remote(held[which].at[deep + k], from_x[which].at[k], x_send.at[which, k], x_recv.at[which, k], here.over_x())

    def send_y(which, k):
        return remote(held[which].at[2 * deep + k], from_y[which].at[k], y_send.at[which, k], y_recv.at[which, k], here.over_y())

    def send_right(which, k):
        return remote(held[which].at[k], from_z[which].at[k], z_send.at[which, k], z_recv.at[which, k], here.at_z(z + 1))

    def send_left(which, k):
        slot = jnp.where(z - 1 == k, deep, k)
        return remote(held[which].at[k], from_z[which].at[slot], z_send.at[which, k], z_recv.at[which, slot], here.at_z(z - 1))

    def from_right(which, k, slot):
        return remote(held[which].at[k], from_z[which].at[slot], z_send.at[which, k], z_recv.at[which, slot], here.at_z(z + 1))

    def send_small(stage):
        device = (here.over_core(), here.over_x(), here.over_y())[stage]
        return remote(small_sum.at[stage], small_pair.at[stage], small_send.at[stage], small_recv.at[stage], device)

    def send_small_deep(step):
        return remote(small_deep.at[z], small_deep.at[z], small_send.at[3 + step], small_recv.at[3 + step],
                      here.at_z((z + step) % deep))

    def send_sums(stage):
        device = (here.over_core(), here.over_y())[stage]
        return [remote(sums.at[stage], sums_pair.at[stage], sums_send.at[0, stage], sums_recv.at[0, stage], device),
                remote(skips.at[stage], skips_pair.at[stage], sums_send.at[1, stage], sums_recv.at[1, stage], device)]

    def sums_step(stage):
        for copy in send_sums(stage):
            copy.wait_recv()
        sums[stage + 1] = sums[stage] + sums_pair[stage]
        skips[stage + 1] = skips[stage] + skips_pair[stage]

    here.greet()
    mixed_back = ToChannels(here, mixed_rows, back_mixed, a_send, a_recv, local_sem.at[0])
    direct_back = ToChannels(here, direct_rows, direct, b_send, b_recv, local_sem.at[1])
    mixed_back.begin()
    direct_back.begin()
    small_sum[0] = small[...]
    send_small(0).start()
    lax.fori_loop(0, 4 * deep, begin, 0)

    def small_step(stage):
        send_small(stage).wait_recv()
        small_sum[stage + 1] = small_sum[stage] + small_pair[stage]
        if stage < 2:
            send_small(stage + 1).start()

    layers = both_ends(deep)
    for k in layers:
        ready(3 * deep + k)
        for which in range(2):
            send_d(which, k).start()
    small_step(0)
    for k in layers:
        ready(2 * deep + k)
        for which in range(2):
            send_y(which, k).start()
    small_step(1)
    for k in layers:
        ready(deep + k)
        for which in range(2):
            send_d(which, k).wait_recv()
            held[which][deep + k] = held[which][deep + k] + from_d[which][k]
            send_x(which, k).start()
    small_step(2)
    small_deep[z] = small_sum[3]
    for step in range(1, deep):
        send_small_deep(step).start()
    for k in layers:
        ready(k)

    state[...] = jnp.zeros_like(state)
    powers[...] = jnp.zeros_like(powers)
    sums[0] = jnp.zeros_like(sums[0])
    skips[0] = jnp.zeros_like(skips[0])
    own_sums = sums.at[0]
    weight_sum, power_sum = own_sums.at[pl.ds(0, halves)], own_sums.at[pl.ds(halves, halves)]
    mixed_back.arrive()

    def layer_step(k):
        for which in range(2):
            send_x(which, k).wait_recv()
            send_y(which, k).wait_recv()
            held[which][k] = (held[which][k].astype(jnp.float32) + from_x[which][k].astype(jnp.float32)
                              + from_y[which][k].astype(jnp.float32)).astype(jnp.bfloat16)

        @pl.when(k > z)
        def _():
            for which in range(2):
                @pl.when(z > 0)
                def _():
                    send_right(which, k).wait_recv()
                    held[which][k] = held[which][k] + from_z[which][k]
                send_right(which, k).start()

        @pl.when(k < z)
        def _():
            for which in range(2):
                @pl.when(z < deep - 1)
                def _():
                    from_right(which, k, k).wait_recv()
                    held[which][k] = held[which][k] + from_z[which][k]
                send_left(which, k).start()

    def weigh_step(tile, carry):
        weigh_tile(tile_of(x_ref, tile), tile_of(pre_ref, tile), tile_of(back_mixed, tile), lanes_of(keep_ref, tile), decay_ref,
                   skips.at[0], slots, back_tile_of(back_slots, tile, tall), state, powers, weight_sum, power_sum)
        return carry

    lax.fori_loop(0, tiles, weigh_step, 0)
    for copy in send_sums(0):
        copy.start()
    state[...] = jnp.zeros_like(state)
    direct_back.arrive()
    acts = {0: layers[:1], tiles // 3: layers[1:2], 2 * tiles // 3: layers[2:3]}

    def adjoint_step(step, carry):
        tile = tiles - 1 - step
        adjoint_tile(tile_of(direct, tile), lanes_of(next_ref, tile), decay_ref, gain_ref, skip_row_ref, tile_of(grad_ref, tile),
                     slots, back_tile_of(back_slots, tile, tall), state)
        for at, chosen in acts.items():
            @pl.when(step == at)
            def _():
                for k in chosen:
                    layer_step(k)

        @pl.when(step == tiles // 2)
        def _():
            sums_step(0)
            for copy in send_sums(1):
                copy.start()
        return carry

    lax.fori_loop(0, tiles, adjoint_step, 0)
    sums_step(1)
    sums_out[...] = sums[2]
    skips_out[...] = skips[2]
    for k in layers[3:]:
        layer_step(k)
    for which in range(2):
        outs[which][...] = held[which][z].astype(jnp.float32)

        @pl.when(z > 0)
        def _():
            send_right(which, z).wait_recv()
            outs[which][...] += from_z[which][z].astype(jnp.float32)

        @pl.when(z < deep - 1)
        def _():
            from_right(which, z, deep).wait_recv()
            outs[which][...] += from_z[which][deep].astype(jnp.float32)
    for step in range(1, deep):
        origin = (z + deep - step) % deep
        remote(small_deep.at[origin], small_deep.at[origin], small_send.at[3 + step], small_recv.at[3 + step], here.at_z(origin)).wait_recv()
    added = small_deep[0]
    for k in range(1, deep):
        added = added + small_deep[k]
    small_out[...] = added
    for stage in range(3):
        send_small(stage).wait_send()
    for stage in range(2):
        for copy in send_sums(stage):
            copy.wait_send()
    for step in range(1, deep):
        send_small_deep(step).wait_send()
    mixed_back.finish()
    direct_back.finish()
    for which in range(2):
        for slot in range(4 * deep):
            remote(held[which].at[slot], from_core[which].at[slot], core_send.at[which, slot], core_recv.at[which, slot], here.over_core()).wait_send()
        for k in range(deep):
            send_d(which, k).wait_send()
            send_x(which, k).wait_send()
            send_y(which, k).wait_send()

            @pl.when(k > z)
            def _():
                send_right(which, k).wait_send()

            @pl.when(k < z)
            def _():
                send_left(which, k).wait_send()


def ema_parts(logits, mixing):
    damping = jax.nn.sigmoid(logits[0])
    decay = 1.0 - damping * jax.nn.sigmoid(logits[1])
    return damping, decay, damping * mixing[0]


def keep_tables(segments):
    keeping = (segments[:, 1:] == segments[:, :-1]).astype(jnp.float32)
    edge = jnp.zeros((segments.shape[0], 1), jnp.float32)
    return (jnp.tile(jnp.concatenate([edge, keeping], axis=1), (2, 1)),
            jnp.tile(jnp.concatenate([keeping, edge], axis=1), (2, 1)))


def lane_table(table, rows):
    chans, count = table.shape
    spread_rows = jnp.repeat(table.T.reshape(2, count // 2, 1, chans), rows, axis=2)
    ordered = spread_rows.transpose(1, 0, 2, 3).reshape(count // 2, 2 * rows, chans)
    return jnp.pad(ordered, ((0, 0), (0, 0), (0, LANES - chans)))


def lane_sums(sums, rows, chans):
    count = sums.shape[0]
    return jnp.sum(sums.reshape(count, 2, rows, LANES), axis=2)[:, :, :chans].transpose(2, 1, 0).reshape(chans, 2 * count)


def ema_tables(logits, mixing, rows):
    _, decay, gain = ema_parts(logits, mixing)
    return [lane_table(decay, rows), lane_table(gain * mixing[1], rows)]


def ema_grads(weight, power, skips, logits, mixing, rows, chans):
    damping, decay, gain = ema_parts(logits, mixing)
    weight = lane_sums(weight, rows, chans)
    back_decay = gain * mixing[1] * lane_sums(power, rows, chans) / decay
    other = jax.nn.sigmoid(logits[1])
    back_damping = weight * mixing[0] * mixing[1] - back_decay * other
    grad_logits = jnp.stack([back_damping * damping * (1.0 - damping), -back_decay * damping * other * (1.0 - other)])
    grad_mixing = jnp.stack([damping * mixing[1] * weight, gain * weight])
    return grad_logits, grad_mixing, jnp.sum(skips, axis=1)


def dma(*shape):
    return pltpu.SemaphoreType.DMA(shape)


ANYWHERE = pl.BlockSpec(memory_space=pl.ANY)
NEAR = pl.BlockSpec(memory_space=pltpu.VMEM)
ROOM = 60 * 1024 * 1024


def forward_exchange(first, second, values, keep, tables, skip, devices, deep):
    rows, chans, length = values.shape
    half, tall, _ = tables[0].shape
    tokens = (rows, chans * 2 * deep, length // (2 * deep))
    return pl.pallas_call(
        partial(forward_kernel, deep),
        in_specs=[ANYWHERE, ANYWHERE] + [NEAR] * 5,
        out_specs=[ANYWHERE] * 4 + [NEAR],
        out_shape=[jax.ShapeDtypeStruct((devices,) + first.shape, first.dtype),
                   jax.ShapeDtypeStruct((devices,) + second.shape, second.dtype),
                   jax.ShapeDtypeStruct(tokens, jnp.bfloat16), jax.ShapeDtypeStruct(tokens, jnp.bfloat16),
                   jax.ShapeDtypeStruct(values.shape, jnp.float32)],
        scratch_shapes=[pltpu.VMEM(values.shape, jnp.bfloat16), pltpu.VMEM((LANES * tall, LANES), jnp.float32),
                        pltpu.VMEM((half, tall, LANES), jnp.float32),
                        dma(4), dma(2, deep, 2), dma(2, deep), dma(2, 2 * deep), dma(2, 4 * deep),
                        dma(2, deep), dma(2, deep), dma(2, deep), dma(2, deep), dma(2, 4 * deep)] + [dma(2 * deep)] * 4,
        compiler_params=pltpu.CompilerParams(collective_id=1, has_side_effects=True, vmem_limit_bytes=ROOM),
        cost_estimate=pl.CostEstimate(flops=values.size * 80, bytes_accessed=first.size * devices * 4, transcendentals=values.size),
    )(first, second, values, keep, *tables, jnp.broadcast_to(skip[:, None], (chans, LANES)))


def backward_exchange(first, second, small, values, pre, mixed_rows, direct_rows, keep, keep_next, tables, skip, deep):
    rows, chans, length = values.shape
    half, tall, _ = tables[0].shape
    skip_row = jnp.pad(jnp.broadcast_to(skip[None], (rows, chans)), ((0, rows), (0, LANES - chans)))
    shapes = [(group[0].shape[1], sum(part.shape[2] for part in group)) for group in (first, second)]
    scratch = []
    for count in (4 * deep, 4 * deep, deep, deep, deep, deep + 1):
        scratch += [pltpu.VMEM((count,) + shape, jnp.bfloat16) for shape in shapes]
    scratch += [pltpu.VMEM((4,) + small.shape, jnp.float32), pltpu.VMEM((3,) + small.shape, jnp.float32),
                pltpu.VMEM((deep,) + small.shape, jnp.float32)]
    scratch += [dma(2, 4 * deep)] * 3 + [dma(2, deep)] * 6 + [dma(2, deep), dma(2, deep + 1)] + [dma(3 + deep)] * 2
    scratch += [pltpu.VMEM(values.shape, jnp.bfloat16)] * 2
    scratch += [pltpu.VMEM((LANES * tall, LANES), jnp.float32), pltpu.VMEM((length * tall, LANES), jnp.float32)]
    scratch += [pltpu.VMEM((half, tall, LANES), jnp.float32)] * 2
    scratch += [pltpu.VMEM((3, 2 * half, tall, LANES), jnp.float32), pltpu.VMEM((2, 2 * half, tall, LANES), jnp.float32)]
    scratch += [pltpu.VMEM((3, chans, LANES), jnp.float32), pltpu.VMEM((2, chans, LANES), jnp.float32)]
    scratch += [dma(2)] + [dma(2 * deep)] * 4 + [dma(2, 2)] * 2
    return pl.pallas_call(
        partial(backward_kernel, deep, (len(first), len(second))),
        in_specs=[ANYWHERE] * (len(first) + len(second)) + [NEAR] * 3 + [ANYWHERE] * 2 + [NEAR] * 5,
        out_specs=[NEAR] * 6,
        out_shape=[jax.ShapeDtypeStruct(shape, jnp.float32) for shape in shapes]
        + [jax.ShapeDtypeStruct(small.shape, jnp.float32), jax.ShapeDtypeStruct(values.shape, jnp.float32),
           jax.ShapeDtypeStruct((2 * half, tall, LANES), jnp.float32), jax.ShapeDtypeStruct((chans, LANES), jnp.float32)],
        scratch_shapes=scratch,
        compiler_params=pltpu.CompilerParams(collective_id=2, has_side_effects=True, vmem_limit_bytes=ROOM),
        cost_estimate=pl.CostEstimate(flops=values.size * 240, bytes_accessed=64 * 1024 * 1024, transcendentals=values.size),
    )(*first, *second, small, values, pre, mixed_rows, direct_rows, keep, keep_next, *tables, skip_row)


def pack(parts):
    flat = jnp.concatenate([part.reshape(-1) for part in parts])
    return jnp.pad(flat, (0, -flat.shape[0] % 1024)).reshape(-1, 128)


def unpack(packed, like):
    flat, made, offset = packed.reshape(-1), [], 0
    for part in like:
        made.append(flat[offset : offset + part.size].reshape(part.shape))
        offset += part.size
    return made


def plain_forward_kernel(x_ref, keep_ref, decay_ref, gain_ref, skip_ref, pre_ref, mixed_ref, slots, state):
    @pl.when(pl.program_id(0) == 0)
    def _():
        state[...] = jnp.zeros_like(state)

    average_tile(x_ref, keep_ref[...], decay_ref, gain_ref, skip_ref, pre_ref, mixed_ref, slots, state)


def plain_backward_kernel(x_ref, pre_ref, back_ref, direct_ref, keep_ref, next_ref, decay_ref, gain_ref, skip_row_ref,
                          grad_ref, sums_ref, skips_ref, slots, back_slots, state, powers):
    halves, tall, _ = decay_ref.shape
    tiles = pl.num_programs(0) // 2
    index = pl.program_id(0)

    @pl.when(index == 0)
    def _():
        state[...] = jnp.zeros_like(state)
        powers[...] = jnp.zeros_like(powers)
        sums_ref[...] = jnp.zeros_like(sums_ref)
        skips_ref[...] = jnp.zeros_like(skips_ref)

    @pl.when(index < tiles)
    def _():
        weigh_tile(x_ref, pre_ref, back_ref, keep_ref[...], decay_ref, skips_ref, slots, back_tile_of(back_slots, index, tall),
                   state, powers, sums_ref.at[pl.ds(0, halves)], sums_ref.at[pl.ds(halves, halves)])

    @pl.when(index == tiles)
    def _():
        state[...] = jnp.zeros_like(state)

    @pl.when(index >= tiles)
    def _():
        adjoint_tile(direct_ref, next_ref[...], decay_ref, gain_ref, skip_row_ref, grad_ref, slots,
                     back_tile_of(back_slots, 2 * tiles - 1 - index, tall), state)


def gathered(part):
    return lax.all_gather(part, ("row", "chan"), axis=0)


def plain_forward(first, second, values, keep, tables, skip):
    rows, chans, length = values.shape
    half, tall, _ = tables[0].shape
    block = pl.BlockSpec((rows, chans, LANES), lambda i: (0, 0, i))
    whole = pl.BlockSpec((half, tall, LANES), lambda i: (0, 0, 0))
    pre, mixed = pl.pallas_call(
        plain_forward_kernel,
        grid=(length // LANES,),
        in_specs=[block, pl.BlockSpec((tall, LANES), lambda i: (0, i)), whole, whole, pl.BlockSpec((chans, LANES), lambda i: (0, 0))],
        out_specs=[block, block],
        out_shape=[jax.ShapeDtypeStruct(values.shape, jnp.float32), jax.ShapeDtypeStruct(values.shape, jnp.bfloat16)],
        scratch_shapes=[pltpu.VMEM((LANES * tall, LANES), jnp.float32), pltpu.VMEM((half, tall, LANES), jnp.float32)],
    )(values, keep, *tables, jnp.broadcast_to(skip[:, None], (chans, LANES)))
    moved = [lax.all_to_all(part, "chan", split_axis=2, concat_axis=1, tiled=True) for part in (values, mixed)]
    return gathered(first), gathered(second), *moved, pre


def plain_backward(first, second, small, values, pre, mixed_rows, direct_rows, keep, keep_next, tables, skip):
    rows, chans, length = values.shape
    back, direct = [lax.all_to_all(part, "chan", split_axis=1, concat_axis=2, tiled=True) for part in (mixed_rows, direct_rows)]
    half, tall, _ = tables[0].shape
    tiles = length // LANES
    skip_row = jnp.pad(jnp.broadcast_to(skip[None], (rows, chans)), ((0, rows), (0, LANES - chans)))
    ahead = pl.BlockSpec((rows, chans, LANES), lambda i: (0, 0, jnp.minimum(i, tiles - 1)))
    behind = pl.BlockSpec((rows, chans, LANES), lambda i: (0, 0, jnp.minimum(tiles - 1, 2 * tiles - 1 - i)))
    whole = pl.BlockSpec((half, tall, LANES), lambda i: (0, 0, 0))
    grads, sums, skips = pl.pallas_call(
        plain_backward_kernel,
        grid=(2 * tiles,),
        in_specs=[ahead] * 3 + [behind, pl.BlockSpec((tall, LANES), lambda i: (0, jnp.minimum(i, tiles - 1))),
                                pl.BlockSpec((tall, LANES), lambda i: (0, jnp.minimum(tiles - 1, 2 * tiles - 1 - i))),
                                whole, whole, pl.BlockSpec((tall, LANES), lambda i: (0, 0))],
        out_specs=[behind, pl.BlockSpec((2 * half, tall, LANES), lambda i: (0, 0, 0)), pl.BlockSpec((chans, LANES), lambda i: (0, 0))],
        out_shape=[jax.ShapeDtypeStruct(values.shape, jnp.float32), jax.ShapeDtypeStruct((2 * half, tall, LANES), jnp.float32),
                   jax.ShapeDtypeStruct((chans, LANES), jnp.float32)],
        scratch_shapes=[pltpu.VMEM((LANES * tall, LANES), jnp.float32), pltpu.VMEM((length * tall, LANES), jnp.float32)]
        + [pltpu.VMEM((half, tall, LANES), jnp.float32)] * 2,
        compiler_params=pltpu.CompilerParams(vmem_limit_bytes=ROOM),
    )(values, pre, back, direct, keep, keep_next, *tables, skip_row)
    sums, skips, small = lax.psum((sums, skips), "row") + (lax.psum(small, ("row", "chan")),)
    owned = [
        jnp.concatenate([lax.psum_scatter(part, ("row", "chan"), scatter_dimension=0, tiled=True)[0] for part in group], axis=1)
        for group in (first, second)
    ]
    return *[part.astype(jnp.float32) for part in owned], small, grads, sums, skips


def product(left, right):
    return jnp.dot(left, right, preferred_element_type=jnp.float32)


def contract_rows(left, right):
    return lax.dot_general(
        left, right, (((0,), (0,)), ((), ())), preferred_element_type=jnp.float32
    )


def contract_cols(left, right):
    return lax.dot_general(
        left, right, (((1,), (1,)), ((), ())), preferred_element_type=jnp.float32
    )


def token_rows(blocked):
    return jnp.transpose(blocked, (0, 2, 1)).reshape(-1, blocked.shape[1])


def channel_blocks(matrix, row_count):
    return jnp.transpose(matrix.reshape(row_count, -1, matrix.shape[1]), (0, 2, 1))


def shards(
    inputs,
    cotangent,
    doc_lengths,
    ema_logits,
    ema_mixing,
    ema_skip,
    value_weight,
    base_weight,
    attn_weight,
    hidden_weight,
    output_weight,
    value_bias,
    base_bias,
    attn_bias,
    hidden_bias,
    output_bias,
    query_key_gain,
    query_key_shift,
    position_bias,
    norm_gain,
    norm_bias,
):
    row_count, chan_count, seq_length = inputs.shape
    group_count = lax.axis_size("chan")
    width = chan_count * group_count
    span_local = seq_length // group_count
    length_block = position_bias.shape[0]
    shared_width = query_key_gain.shape[1]
    value_width = value_bias.shape[0]
    token_count = row_count * span_local
    window_count = token_count // length_block
    score_scale = shared_width ** (-0.5)
    positions = jnp.arange(seq_length, dtype=jnp.int32)
    segment_rows = jax.vmap(segment_ids, (0, None))(doc_lengths, positions)

    keep, keep_next = keep_tables(segment_rows)
    tables = ema_tables(ema_logits, ema_mixing, row_count)
    on_four = lax.axis_size("row") == 4
    devices, deep = lax.axis_size("row") * group_count, group_count // 2
    first = jnp.concatenate([part.astype(jnp.bfloat16) for part in (value_weight, base_weight, hidden_weight)], axis=1)
    second = jnp.concatenate([part.astype(jnp.bfloat16) for part in (attn_weight, output_weight)], axis=1)
    exchange = partial(forward_exchange, devices=devices, deep=deep) if on_four else plain_forward
    first, second, token_input, token_mixed, pre_mix = exchange(first, second, inputs, keep, tables, ema_skip)
    cotangent, first = lax.optimization_barrier((cotangent, first))
    first, second = first.reshape(width, -1), second.reshape(value_width, -1)
    base_width = base_bias.shape[0]
    value_low = first[:, :value_width]
    base_low = first[:, value_width : value_width + base_width]
    hidden_low = first[:, value_width + base_width :]
    attn_low, output_low = second[:, :width], second[:, width:]
    input_rows = token_rows(token_input)
    mixed_rows = token_rows(token_mixed)
    local_pos = lax.axis_index("chan") * span_local + jnp.arange(span_local, dtype=jnp.int32)
    segment_local = jax.vmap(segment_ids, (0, None))(doc_lengths, local_pos).reshape(
        window_count, length_block
    )
    offset_hits = offset_table(length_block)
    bias_table = jnp.einsum("ijm,m->ij", offset_hits, position_bias, precision=HIGH)
    offsets = jnp.arange(length_block, dtype=jnp.int32)
    allowed = (offsets[:, None] >= offsets[None, :])[None] & (
        segment_local[:, :, None] == segment_local[:, None, :]
    )
    value_pre = product(input_rows, value_low) + value_bias
    value_rows = jax.nn.silu(value_pre).astype(jnp.bfloat16)
    base_proj = product(mixed_rows, base_low) + base_bias
    gate_pre = base_proj[:, :width]
    shared_pre = base_proj[:, width : width + shared_width]
    reset_pre = base_proj[:, width + shared_width : width + shared_width + value_width]
    direct_part = base_proj[:, width + shared_width + value_width :]
    update_gate = jax.nn.sigmoid(gate_pre)
    shared_z = jax.nn.silu(shared_pre)
    reset_gate = jax.nn.silu(reset_pre)
    queries = (
        (shared_z * query_key_gain[0] + query_key_shift[0])
        .astype(jnp.bfloat16)
        .reshape(window_count, length_block, shared_width)
    )
    key_rows = (
        (shared_z * query_key_gain[1] + query_key_shift[1])
        .astype(jnp.bfloat16)
        .reshape(window_count, length_block, shared_width)
    )
    value_win = value_rows.reshape(window_count, length_block, value_width)
    scores = (
        jnp.einsum("cik,cjk->cij", queries, key_rows, preferred_element_type=jnp.float32)
        * score_scale
        + bias_table[None]
    )
    attention = jax.nn.softmax(jnp.where(allowed, scores, MASKED), axis=-1)
    attention_low = attention.astype(jnp.bfloat16)
    attended = jnp.einsum(
        "cij,cjv->civ", attention_low, value_win, preferred_element_type=jnp.float32
    ).reshape(token_count, value_width)
    mixed_att = (attended * reset_gate).astype(jnp.bfloat16)
    hidden_pre = direct_part + product(mixed_att, attn_low) + attn_bias
    hidden = jax.nn.silu(hidden_pre)
    input_float = input_rows.astype(jnp.float32)
    out_one = input_float + update_gate * (hidden - input_float)
    normed, norm_back_one = jax.vjp(layer_norm, out_one, norm_gain[0], norm_bias[0])
    normed_low = normed.astype(jnp.bfloat16)
    inner_pre = product(normed_low, hidden_low) + hidden_bias
    activated = jax.nn.silu(inner_pre).astype(jnp.bfloat16)
    out_two = normed + product(activated, output_low) + output_bias
    final_rows, norm_back_two = jax.vjp(layer_norm, out_two, norm_gain[1], norm_bias[1])
    layer_out = lax.all_to_all(
        channel_blocks(final_rows.astype(jnp.bfloat16), row_count),
        "chan",
        split_axis=1,
        concat_axis=2,
        tiled=True,
    )
    token_grad = lax.all_to_all(cotangent, "chan", split_axis=2, concat_axis=1, tiled=True)
    grad_rows = token_rows(token_grad).astype(jnp.float32)
    back_two, gain_two, shift_two = norm_back_two(grad_rows)
    back_outer = back_two.astype(jnp.bfloat16)
    grad_output_weight = contract_rows(activated, back_outer)
    grad_output_bias = jnp.sum(back_two, axis=0)
    back_inner = (contract_cols(back_outer, output_low) * silu_slope(inner_pre)).astype(
        jnp.bfloat16
    )
    grad_hidden_weight = contract_rows(normed_low, back_inner)
    grad_hidden_bias = jnp.sum(back_inner.astype(jnp.float32), axis=0)
    back_normed = back_two + contract_cols(back_inner, hidden_low)
    back_one, gain_one, shift_one = norm_back_one(back_normed)
    back_hidden = back_one * update_gate * silu_slope(hidden_pre)
    back_proj = back_hidden.astype(jnp.bfloat16)
    grad_attn_weight = contract_rows(mixed_att, back_proj)
    grad_attn_bias = jnp.sum(back_hidden, axis=0)
    back_mix = contract_cols(back_proj, attn_low)
    back_attended = (back_mix * reset_gate).astype(jnp.bfloat16)
    back_reset = back_mix * attended
    back_att_win = back_attended.reshape(window_count, length_block, value_width)
    back_attention = jnp.einsum(
        "civ,cjv->cij", back_att_win, value_win, preferred_element_type=jnp.float32
    )
    back_values = jnp.einsum(
        "cij,civ->cjv", attention_low, back_att_win, preferred_element_type=jnp.float32
    ).reshape(token_count, value_width)
    back_scores = (
        attention * (back_attention - jnp.sum(attention * back_attention, axis=-1, keepdims=True))
    ).astype(jnp.bfloat16)
    grad_position = jnp.einsum(
        "ijm,ij->m", offset_hits, jnp.sum(back_scores.astype(jnp.float32), axis=0), precision=HIGH
    )
    back_queries = (
        jnp.einsum(
            "cij,cjk->cik", back_scores, key_rows, preferred_element_type=jnp.float32
        ).reshape(token_count, shared_width)
        * score_scale
    )
    back_keys = (
        jnp.einsum(
            "cij,cik->cjk", back_scores, queries, preferred_element_type=jnp.float32
        ).reshape(token_count, shared_width)
        * score_scale
    )
    back_shared = back_queries * query_key_gain[0] + back_keys * query_key_gain[1]
    grad_key_gain = jnp.stack(
        [jnp.sum(back_queries * shared_z, axis=0), jnp.sum(back_keys * shared_z, axis=0)]
    )
    grad_key_shift = jnp.stack([jnp.sum(back_queries, axis=0), jnp.sum(back_keys, axis=0)])
    back_value = (back_values * silu_slope(value_pre)).astype(jnp.bfloat16)
    grad_value_weight = contract_rows(input_rows, back_value)
    grad_value_bias = jnp.sum(back_value.astype(jnp.float32), axis=0)
    back_base = jnp.concatenate(
        [
            back_one * (hidden - input_float) * update_gate * (1.0 - update_gate),
            back_shared * silu_slope(shared_pre),
            back_reset * silu_slope(reset_pre),
            back_hidden,
        ],
        axis=1,
    ).astype(jnp.bfloat16)
    grad_base_weight = contract_rows(mixed_rows, back_base)
    grad_base_bias = jnp.sum(back_base.astype(jnp.float32), axis=0)
    back_mixed_rows = contract_cols(back_base, base_low)
    back_direct = back_one * (1.0 - update_gate) + contract_cols(back_value, value_low)
    grad_norm_gain = jnp.stack([gain_one, gain_two])
    grad_norm_bias = jnp.stack([shift_one, shift_two])
    small = (
        grad_value_bias,
        grad_base_bias,
        grad_attn_bias,
        grad_hidden_bias,
        grad_output_bias,
        grad_key_gain,
        grad_key_shift,
        grad_position,
        grad_norm_gain,
        grad_norm_bias,
    )

    def owners(terms):
        return terms.astype(jnp.bfloat16).reshape(devices, -1, terms.shape[1])

    pre_mix, layer_out = lax.optimization_barrier((pre_mix, layer_out))
    exchange = partial(backward_exchange, deep=deep) if on_four else plain_backward
    first_sum, second_sum, small_sum, grad_inputs, sums, skips = exchange(
        [owners(grad_value_weight), owners(grad_base_weight), owners(grad_hidden_weight)],
        [owners(grad_attn_weight), owners(grad_output_weight)],
        pack(small),
        inputs,
        pre_mix,
        channel_blocks(back_mixed_rows, row_count).astype(jnp.bfloat16),
        channel_blocks(back_direct, row_count).astype(jnp.bfloat16),
        keep,
        keep_next,
        tables,
        ema_skip,
    )
    states = sums.shape[0] // 2
    grad_logits, grad_mixing, grad_skip = ema_grads(
        sums[:states], sums[states:], skips, ema_logits, ema_mixing, row_count, chan_count
    )
    (
        sum_value_bias,
        sum_base_bias,
        sum_attn_bias,
        sum_hidden_bias,
        sum_output_bias,
        sum_key_gain,
        sum_key_shift,
        sum_position,
        sum_norm_gain,
        sum_norm_bias,
    ) = unpack(small_sum, small)
    owner_value = first_sum[:, :value_width]
    owner_base = first_sum[:, value_width : value_width + base_width]
    owner_hidden = first_sum[:, value_width + base_width :]
    owner_attn, owner_output = second_sum[:, :width], second_sum[:, width:]
    return (
        layer_out,
        grad_inputs,
        grad_logits,
        grad_mixing,
        grad_skip,
        owner_value,
        owner_base,
        owner_attn,
        owner_hidden,
        owner_output,
        sum_value_bias,
        sum_base_bias,
        sum_attn_bias,
        sum_hidden_bias,
        sum_output_bias,
        sum_key_gain,
        sum_key_shift,
        sum_position,
        sum_norm_gain,
        sum_norm_bias,
    )


def solution(mesh):
    in_specs = (
        P("row", "chan", None),
        P("row", "chan", None),
        P("row", None),
        P(None, "chan", None),
        P(None, "chan", None),
        P("chan"),
        P(("row", "chan"), None),
        P(("row", "chan"), None),
        P(("row", "chan"), None),
        P(("row", "chan"), None),
        P(("row", "chan"), None),
        P(),
        P(),
        P(),
        P(),
        P(),
        P(),
        P(),
        P(),
        P(),
        P(),
    )
    out_specs = (
        P("row", "chan", None),
        P("row", "chan", None),
        P(None, "chan", None),
        P(None, "chan", None),
        P("chan"),
        P(("row", "chan"), None),
        P(("row", "chan"), None),
        P(("row", "chan"), None),
        P(("row", "chan"), None),
        P(("row", "chan"), None),
        P(),
        P(),
        P(),
        P(),
        P(),
        P(),
        P(),
        P(),
        P(),
        P(),
    )
    return jax.shard_map(shards, mesh=mesh, in_specs=in_specs, out_specs=out_specs, check_vma=False)
```

```python
from functools import partial

import jax
import jax.numpy as jnp
from jax import lax
from jax.experimental import pallas as pl
from jax.experimental.pallas import tpu as pltpu
from jax.sharding import PartitionSpec as P

HIGH = lax.Precision.HIGHEST
EPSILON = 1e-05
MASKED = -1e30


def segment_ids(lengths, positions):
    boundary = jnp.cumsum(lengths)
    passed = (positions[:, None] >= boundary[None, :]).astype(jnp.int32)
    return jnp.sum(passed, axis=1)


def silu_slope(values):
    logistic = jax.nn.sigmoid(values)
    return logistic * (1.0 + values * (1.0 - logistic))


def layer_norm(values, scale_row, shift_row):
    center = jnp.mean(values, axis=-1, keepdims=True)
    centered = values - center
    spread = jnp.mean(centered * centered, axis=-1, keepdims=True)
    return centered * lax.rsqrt(spread + EPSILON) * scale_row + shift_row


def offset_table(length_block):
    offsets = jnp.arange(length_block, dtype=jnp.int32)
    distance = offsets[:, None] - offsets[None, :]
    return (distance[:, :, None] == offsets[None, None, :]).astype(jnp.float32)


LANES = 128
STEPS = 16
MESH = pl.DeviceIdType.MESH


def pad_rows(block):
    short = LANES - block.shape[0]
    if short == 0:
        return block
    return jnp.concatenate([block, jnp.zeros((short, block.shape[1]), block.dtype)], axis=0)


def spread(block, slots, row, rows):
    turned = pad_rows(block).T
    slots[pl.ds(row, LANES, stride=2 * rows), :] = turned
    slots[pl.ds(row + rows, LANES, stride=2 * rows), :] = turned


def gather(slots, row, rows, chans):
    first = slots[pl.ds(row, LANES, stride=2 * rows), :]
    second = slots[pl.ds(row + rows, LANES, stride=2 * rows), :]
    return (first + second).T[:chans]


def tile_of(ref, tile):
    return ref.at[:, :, pl.ds(pl.multiple_of(tile * LANES, LANES), LANES)]


def lanes_of(ref, tile):
    return ref[:, pl.ds(pl.multiple_of(tile * LANES, LANES), LANES)]


def slot_at(step, tall):
    return pl.ds(pl.multiple_of(step * tall, tall), tall)


def average_tile(x_tile, keep_tile, decay_ref, gain_ref, skip_ref, pre_tile, mixed_tile, slots, state):
    rows, chans, _ = x_tile.shape
    halves = decay_ref.shape[0]
    tall = 2 * rows
    for row in range(rows):
        spread(x_tile[row].astype(jnp.float32), slots, row, rows)

    def group(step, carry):
        keeping, states = carry
        states = list(states)
        for inner in range(STEPS):
            at = slot_at(step * STEPS + inner, tall)
            value = slots[at, :]
            keep = jnp.broadcast_to(keeping[:, inner : inner + 1], (tall, LANES))
            total = None
            for n in range(halves):
                states[n] = (decay_ref[n] * keep) * states[n] + gain_ref[n] * value
                total = states[n] if total is None else total + states[n]
            slots[at, :] = total
        return pltpu.roll(keeping, LANES - STEPS, axis=1), tuple(states)

    start = tuple(state[n] for n in range(halves))
    _, states = lax.fori_loop(0, LANES // STEPS, group, (keep_tile, start))
    for n in range(halves):
        state[n] = states[n]
    for row in range(rows):
        pre = gather(slots, row, rows, chans) + skip_ref[:, :1] * x_tile[row].astype(jnp.float32)
        pre_tile[row] = pre
        mixed_tile[row] = (pre * jax.nn.sigmoid(pre)).astype(jnp.bfloat16)


def back_tile_of(back_slots, tile, tall):
    return back_slots.at[pl.ds(pl.multiple_of(tile * (LANES * tall), LANES * tall), LANES * tall), :]


def weigh_tile(x_tile, pre_tile, back_mixed_tile, keep_tile, decay_ref, skip_sum, slots, back_tile, state, powers, weight_sum, power_sum):
    rows = x_tile.shape[0]
    halves = decay_ref.shape[0]
    tall = 2 * rows
    for row in range(rows):
        values = x_tile[row].astype(jnp.float32)
        pre = pre_tile[row]
        logistic = jax.nn.sigmoid(pre)
        back = back_mixed_tile[row].astype(jnp.float32) * (logistic * (1.0 + pre * (1.0 - logistic)))
        skip_sum[...] += back * values
        spread(values, slots, row, rows)
        spread(back, back_tile, row, rows)

    def group(step, carry):
        keeping, states, derived, weights, sums = (carry[0], *map(list, carry[1:]))
        for inner in range(STEPS):
            at = slot_at(step * STEPS + inner, tall)
            value = slots[at, :]
            back = back_tile[at, :]
            keep = jnp.broadcast_to(keeping[:, inner : inner + 1], (tall, LANES))
            for n in range(halves):
                decay = decay_ref[n] * keep
                derived[n] = decay * (derived[n] + states[n])
                states[n] = decay * states[n] + value
                weights[n] = weights[n] + back * states[n]
                sums[n] = sums[n] + back * derived[n]
        return pltpu.roll(keeping, LANES - STEPS, axis=1), tuple(states), tuple(derived), tuple(weights), tuple(sums)

    refs = (state, powers, weight_sum, power_sum)
    start = tuple(tuple(ref[n] for n in range(halves)) for ref in refs)
    out = lax.fori_loop(0, LANES // STEPS, group, (keep_tile, *start))
    for ref, values in zip(refs, out[1:]):
        for n in range(halves):
            ref[n] = values[n]


def adjoint_tile(next_tile, decay_ref, gain_ref, skip_row_ref, grad_tile, slots, back_tile, state):
    rows, chans, _ = grad_tile.shape
    halves = decay_ref.shape[0]
    tall = 2 * rows

    def group(step, carry):
        keeping, states = carry
        states = list(states)
        for inner in range(STEPS):
            at = slot_at(LANES - 1 - step * STEPS - inner, tall)
            back = back_tile[at, :]
            keep = jnp.broadcast_to(keeping[:, LANES - 1 - inner : LANES - inner], (tall, LANES))
            total = skip_row_ref[...] * back
            for n in range(halves):
                states[n] = (decay_ref[n] * keep) * states[n] + back
                total = total + gain_ref[n] * states[n]
            slots[at, :] = total
        return pltpu.roll(keeping, STEPS, axis=1), tuple(states)

    start = tuple(state[n] for n in range(halves))
    _, states = lax.fori_loop(0, LANES // STEPS, group, (next_tile, start))
    for n in range(halves):
        state[n] = states[n]
    for row in range(rows):
        grad_tile[row] = gather(slots, row, rows, chans)


class Place:
    def __init__(self, deep):
        self.deep = deep
        row, chan = lax.axis_index("row"), lax.axis_index("chan")
        self.y, self.core = row // 2, row % 2
        self.z, self.x = chan // 2, chan % 2
        self.row, self.chan = row, chan

    def owner(self, z, x, y, core):
        return (y * 2 + core) * (2 * self.deep) + z * 2 + x

    def over_core(self):
        return (self.row + 1 - 2 * self.core, self.chan)

    def over_x(self):
        return (self.row, self.chan + 1 - 2 * self.x)

    def over_y(self):
        return (self.row + 2 - 4 * self.y, self.chan)

    def at_z(self, z):
        return (self.row, z * 2 + self.x)

    def at_chan(self, step):
        chan = (self.chan + step) % (2 * self.deep)
        return chan, (self.row, chan)

    def greet(self):
        barrier = pltpu.get_barrier_semaphore()
        others = [self.over_core(), self.over_y()]
        others += [self.at_chan(step)[1] for step in range(1, 2 * self.deep)]
        for other in others:
            pl.semaphore_signal(barrier, inc=1, device_id=other, device_id_type=MESH)
        pl.semaphore_wait(barrier, len(others))


def remote(source, target, send, recv, device):
    return pltpu.make_async_remote_copy(src_ref=source, dst_ref=target, send_sem=send, recv_sem=recv,
                                        device_id=device, device_id_type=MESH)


def start(copies):
    for copy in copies:
        copy.start()


class ToTokens:
    def __init__(self, here, source, target, send, recv, keep):
        self.here, self.source, self.target = here, source, target
        self.send, self.recv, self.keep = send, recv, keep
        self.chans, self.span = source.shape[1], target.shape[2]

    def block(self, chan):
        return self.source.at[:, :, pl.ds(pl.multiple_of(chan * self.span, LANES), self.span)]

    def spot(self, chan):
        return self.target.at[:, pl.ds(pl.multiple_of(chan * self.chans, 8), self.chans), :]

    def own(self):
        return pltpu.make_async_copy(self.block(self.here.chan), self.spot(self.here.chan), self.keep)

    def out(self, chan):
        return remote(self.block(chan), self.spot(self.here.chan), self.send.at[chan], self.recv.at[self.here.chan], (self.here.row, chan))

    def arrival(self, chan):
        return remote(self.block(chan), self.spot(chan), self.send.at[chan], self.recv.at[chan], (self.here.row, chan))

    def begin_same(self):
        for step in range(2, 2 * self.here.deep, 2):
            self.out(self.here.at_chan(step)[0]).start()
        self.own().start()

    def begin_cross(self):
        for step in range(1, 2 * self.here.deep, 2):
            self.out(self.here.at_chan(step)[0]).start()

    def begin(self):
        self.begin_cross()
        self.begin_same()

    def begin_one(self, chan):
        @pl.when(chan == self.here.chan)
        def _():
            self.own().start()

        @pl.when(chan != self.here.chan)
        def _():
            self.out(chan).start()

    def arrive(self):
        self.own().wait()
        for step in range(1, 2 * self.here.deep):
            self.arrival(self.here.at_chan(step)[0]).wait_recv()

    def finish(self):
        for step in range(1, 2 * self.here.deep):
            self.out(self.here.at_chan(step)[0]).wait_send()


class ToChannels(ToTokens):
    def __init__(self, here, source, target, send, recv, keep):
        super().__init__(here, source, target, send, recv, keep)
        self.chans, self.span = target.shape[1], source.shape[2]

    def block(self, chan):
        return self.source.at[:, pl.ds(pl.multiple_of(chan * self.chans, 8), self.chans), :]

    def spot(self, chan):
        return self.target.at[:, :, pl.ds(pl.multiple_of(chan * self.span, LANES), self.span)]


def forward_kernel(deep, first, second, x_ref, keep_ref, decay_ref, gain_ref, skip_ref,
                   first_full, second_full, token_x, token_mixed, pre_ref,
                   mixed, slots, state, local_sem, send_z, send_x, send_y, send_d, send_core, recv_z, recv_x, recv_y, recv_d, recv_core,
                   a_send, a_recv, b_send, b_recv):
    count = 2
    mine, full = (first, second), (first_full, second_full)
    here = Place(deep)
    z, x, y, core = here.z, here.x, here.y, here.core
    me = here.owner(z, x, y, core)
    layers = range(deep)

    def piece(which, at, device, send, recv, source=None):
        spot = full[which].at[at]
        return remote(spot if source is None else source, spot, send, recv, device)

    def to_core(at, slot, source=False):
        return [piece(which, at, here.over_core(), send_core.at[which, slot], recv_core.at[which, slot],
                      mine[which] if source else None) for which in range(count)]

    def own_x(k, source=False):
        at = here.owner(k, x, y, core)
        return [piece(which, at, here.over_x(), send_x.at[which, k], recv_x.at[which, k],
                      mine[which] if source else None) for which in range(count)]

    def own_y(k, source=False):
        at = here.owner(k, x, y, core)
        return [piece(which, at, here.over_y(), send_y.at[which, k], recv_y.at[which, k],
                      mine[which] if source else None) for which in range(count)]

    def column(k, source=False):
        start(own_x(k, source))
        start(own_y(k, source))
        start(to_core(here.owner(k, x, y, core), k, source))

    def along(k, to, side, source=False):
        at = here.owner(k, x, y, core)
        return [piece(which, at, here.at_z(to), send_z.at[which, k, side], recv_z.at[which, k],
                      mine[which] if source else None) for which in range(count)]

    via_x = 1

    def onward_y(k):
        at = here.owner(k, 1 - x, y, core)
        return [piece(which, at, here.over_y(), send_d.at[which, k], recv_d.at[which, k]) for which in range(count)]

    def onward_x(k):
        at = here.owner(k, x, 1 - y, core)
        return [piece(which, at, here.over_x(), send_d.at[which, k], recv_d.at[which, k]) for which in range(count)]

    def wait_from(at, recv, k, device):
        for which in range(count):
            piece(which, at, device, send_x.at[which, 0], recv.at[which, k]).wait_recv()

    def sides(distance):
        return [z] if distance == 0 else [z - distance, z + distance]

    def neighbours(distance):
        for k in sides(distance):
            @pl.when((k >= 0) & (k < deep))
            def _():
                at = here.owner(k, 1 - x, y, core)
                wait_from(at, recv_x, k, here.over_x())

                @pl.when(k >= via_x)
                def _():
                    start(onward_y(k))
                start(to_core(at, deep + k))
                at = here.owner(k, x, 1 - y, core)
                wait_from(at, recv_y, k, here.over_y())

                @pl.when(k < via_x)
                def _():
                    start(onward_x(k))
                start(to_core(at, 2 * deep + k))

    def layer_step(distance):
        for side, k in enumerate(sides(distance)):
            @pl.when((k >= 0) & (k < deep))
            def _():
                to = z + 1 if side == 0 else z - 1
                wait_from(here.owner(k, x, y, core), recv_z, k, here.at_z(z))

                @pl.when((to >= 0) & (to < deep))
                def _():
                    start(along(k, to, 1 - side))
                column(k)

    here.greet()
    tokens_x = ToTokens(here, x_ref, token_x, a_send, a_recv, local_sem.at[2])
    tokens_mixed = ToTokens(here, mixed, token_mixed, b_send, b_recv, local_sem.at[3])
    local = [pltpu.make_async_copy(mine[which], full[which].at[me], local_sem.at[which]) for which in range(count)]
    start(local)
    for side, to in ((0, z - 1), (1, z + 1)):
        @pl.when((to >= 0) & (to < deep))
        def _():
            start(along(z, to, side, True))
    column(z, True)
    state[...] = jnp.zeros_like(state)
    tiles = x_ref.shape[2] // LANES
    each = tokens_x.span // LANES

    def tile_step(tile, carry):
        average_tile(tile_of(x_ref, tile), lanes_of(keep_ref, tile), decay_ref, gain_ref, skip_ref,
                     tile_of(pre_ref, tile), tile_of(mixed, tile), slots, state)

        @pl.when(tile == 5)
        def _():
            layer_step(1)

        @pl.when(tile == 8)
        def _():
            neighbours(0)

        @pl.when(tile == 12)
        def _():
            layer_step(2)

        @pl.when(tile == 15)
        def _():
            layer_step(3)
            tokens_x.begin()
        return carry

    lax.fori_loop(0, tiles, tile_step, 0)
    tokens_mixed.begin()
    neighbours(1)
    neighbours(2)
    neighbours(deep - 1)
    for k in layers:
        at = here.owner(k, 1 - x, 1 - y, core)
        wait_from(at, recv_d, k, here.over_y())
        start(to_core(at, 3 * deep + k))
    for copy in local:
        copy.wait()
    tokens_x.arrive()
    tokens_mixed.arrive()
    for slot, (flip_x, flip_y) in enumerate(((0, 0), (1, 0), (0, 1), (1, 1))):
        for k in layers:
            at = here.owner(k, x + flip_x * (1 - 2 * x), y + flip_y * (1 - 2 * y), 1 - core)
            for copy in to_core(at, slot * deep + k):
                copy.wait_recv()
                copy.wait_send()
    for k in layers:
        for copy in own_x(k) + own_y(k) + (onward_x(k) if k < via_x else onward_y(k)):
            copy.wait_send()
        for side, valid in ((0, (k >= z) & (z > 0)), (1, (k <= z) & (z < deep - 1))):
            @pl.when(valid)
            def _():
                for copy in along(k, z, side):
                    copy.wait_send()
    tokens_x.finish()
    tokens_mixed.finish()


LAYER_TIMES = ((3, 11), (0, 12), (2, 16), (1, 20))
LAYER_GAP = 4


def backward_kernel(deep, groups, *refs):
    total = sum(groups)
    sources = refs[:total]
    (small, x_ref, pre_ref, mixed_rows, direct_rows, keep_ref, next_ref, decay_ref, gain_ref, skip_row_ref) = refs[total : total + 10]
    refs = refs[total + 10 :]
    first_out, second_out, small_out, grad_ref, sums_out, skips_out = refs[:6]
    outs = (first_out, second_out)
    rest = refs[6:]
    held, from_core, from_d, from_x, from_y, from_z = (rest[2 * i : 2 * i + 2] for i in range(6))
    (small_sum, small_pair, small_deep, load_sem, core_send, core_recv, d_send, d_recv, x_send, x_recv, y_send, y_recv,
     z_send, z_recv, small_send, small_recv, back_mixed, direct, slots, back_slots, state, powers, sums, sums_pair,
     skips, skips_pair,     local_sem, a_send, a_recv, b_send, b_recv, sums_send, sums_recv) = rest[12:]
    here = Place(deep)
    z, x, y, core = here.z, here.x, here.y, here.core
    rows, chans, length = x_ref.shape
    halves = decay_ref.shape[0]
    tall = 2 * rows
    tiles = length // LANES
    wide = []
    first = 0
    for which, size in enumerate(groups):
        offset = 0
        for source in sources[first : first + size]:
            wide.append((which, source, offset, source.shape[2]))
            offset += source.shape[2]
        first += size

    def begin(index, carry):
        slot = 4 * deep - 1 - index
        k, flips = slot % deep, slot // deep
        to_x = x + (flips % 2) * (1 - 2 * x)
        to_y = y + (flips // 2) * (1 - 2 * y)
        own, other = here.owner(k, to_x, to_y, core), here.owner(k, to_x, to_y, 1 - core)
        for which, source, offset, width in wide:
            pltpu.make_async_copy(source.at[own], held[which].at[slot, :, pl.ds(offset, width)], load_sem.at[which, slot]).start()
            remote(source.at[other], from_core[which].at[slot, :, pl.ds(offset, width)],
                   core_send.at[which, slot], core_recv.at[which, slot], here.over_core()).start()
        return carry

    def ready(slot):
        for which in range(2):
            spot = held[which].at[slot]
            pltpu.make_async_copy(spot, spot, load_sem.at[which, slot]).wait()
            remote(spot, from_core[which].at[slot], core_send.at[which, slot], core_recv.at[which, slot], here.over_core()).wait_recv()
            held[which][slot] = held[which][slot] + from_core[which][slot]

    via_x = 1

    def send_d(which, k):
        device = here.over_x() if k < via_x else here.over_y()
        return remote(held[which].at[3 * deep + k], from_d[which].at[k], d_send.at[which, k], d_recv.at[which, k], device)

    def send_x(which, k):
        return remote(held[which].at[deep + k], from_x[which].at[k], x_send.at[which, k], x_recv.at[which, k], here.over_x())

    def send_y(which, k):
        return remote(held[which].at[2 * deep + k], from_y[which].at[k], y_send.at[which, k], y_recv.at[which, k], here.over_y())

    def send_right(which, k):
        return remote(held[which].at[k], from_z[which].at[k], z_send.at[which, k], z_recv.at[which, k], here.at_z(z + 1))

    def send_left(which, k):
        slot = jnp.where(z - 1 == k, deep, k)
        return remote(held[which].at[k], from_z[which].at[slot], z_send.at[which, k], z_recv.at[which, slot], here.at_z(z - 1))

    def from_right(which, k, slot):
        return remote(held[which].at[k], from_z[which].at[slot], z_send.at[which, k], z_recv.at[which, slot], here.at_z(z + 1))

    def send_small(stage):
        device = (here.over_core(), here.over_y(), here.over_x())[stage]
        return remote(small_sum.at[stage], small_pair.at[stage], small_send.at[stage], small_recv.at[stage], device)

    def send_small_deep(step):
        return remote(small_deep.at[z], small_deep.at[z], small_send.at[3 + step], small_recv.at[3 + step],
                      here.at_z((z + step) % deep))

    def send_sums(stage):
        device = (here.over_core(), here.over_y())[stage]
        return [remote(sums.at[stage], sums_pair.at[stage], sums_send.at[0, stage], sums_recv.at[0, stage], device),
                remote(skips.at[stage], skips_pair.at[stage], sums_send.at[1, stage], sums_recv.at[1, stage], device)]

    def sums_step(stage):
        for copy in send_sums(stage):
            copy.wait_recv()
        sums[stage + 1] = sums[stage] + sums_pair[stage]
        skips[stage + 1] = skips[stage] + skips_pair[stage]

    here.greet()
    mixed_back = ToChannels(here, mixed_rows, back_mixed, a_send, a_recv, local_sem.at[0])
    direct_back = ToChannels(here, direct_rows, direct, b_send, b_recv, local_sem.at[1])
    mixed_back.begin()
    small_sum[0] = small[...]
    send_small(0).start()
    lax.fori_loop(0, 4 * deep, begin, 0)

    def small_step(stage):
        send_small(stage).wait_recv()
        small_sum[stage + 1] = small_sum[stage] + small_pair[stage]
        if stage < 2:
            send_small(stage + 1).start()

    def diagonal(k):
        ready(3 * deep + k)
        for which in range(2):
            send_d(which, k).start()

    def side(slot, send, k, waits):
        ready(slot * deep + k)
        for which in range(2):
            if waits:
                send_d(which, k).wait_recv()
                held[which][slot * deep + k] = held[which][slot * deep + k] + from_d[which][k]
            send(which, k).start()

    def x_side(k):
        side(1, send_x, k, k >= via_x)

    def y_side(k):
        side(2, send_y, k, k < via_x)

    diagonal(3)
    small_step(0)
    y_side(3)
    diagonal(0)
    x_side(0)
    diagonal(2)
    diagonal(1)
    small_step(1)
    direct_back.begin_same()
    x_side(3)
    y_side(0)
    y_side(2)
    x_side(2)
    y_side(1)
    for k in range(deep):
        ready(k)
    x_side(1)
    small_step(2)
    small_deep[z] = small_sum[3]
    for step in range(1, deep):
        send_small_deep(step).start()

    state[...] = jnp.zeros_like(state)
    powers[...] = jnp.zeros_like(powers)
    sums[0] = jnp.zeros_like(sums[0])
    skips[0] = jnp.zeros_like(skips[0])
    own_sums = sums.at[0]
    weight_sum, power_sum = own_sums.at[pl.ds(0, halves)], own_sums.at[pl.ds(halves, halves)]
    mixed_back.arrive()
    direct_back.begin_cross()

    def layer_sums(k):
        for which in range(2):
            send_x(which, k).wait_recv()
            send_y(which, k).wait_recv()
            held[which][k] = (held[which][k].astype(jnp.float32) + from_x[which][k].astype(jnp.float32)
                              + from_y[which][k].astype(jnp.float32)).astype(jnp.bfloat16)

    def layer_step(k):
        layer_sums(k)

        @pl.when(k > z)
        def _():
            for which in range(2):
                @pl.when(z > 0)
                def _():
                    send_right(which, k).wait_recv()
                    held[which][k] = held[which][k] + from_z[which][k]
                send_right(which, k).start()

        @pl.when(k < z)
        def _():
            for which in range(2):
                @pl.when(z < deep - 1)
                def _():
                    from_right(which, k, k).wait_recv()
                    held[which][k] = held[which][k] + from_z[which][k]
                send_left(which, k).start()

    def layer_steps(index):
        for k, base in LAYER_TIMES:
            hop = jnp.where(k > z, z, deep - 1 - z)

            @pl.when((index == base + LAYER_GAP * hop) & (k != z))
            def _():
                layer_step(k)

    def weigh_step(tile, carry):
        weigh_tile(tile_of(x_ref, tile), tile_of(pre_ref, tile), tile_of(back_mixed, tile), lanes_of(keep_ref, tile), decay_ref,
                   skips.at[0], slots, back_tile_of(back_slots, tile, tall), state, powers, weight_sum, power_sum)
        layer_steps(tile)
        return carry

    lax.fori_loop(0, tiles, weigh_step, 0)
    for copy in send_sums(0):
        copy.start()
    state[...] = jnp.zeros_like(state)

    def adjoint_step(step, carry):
        tile = tiles - 1 - step
        adjoint_tile(lanes_of(next_ref, tile), decay_ref, gain_ref, skip_row_ref, tile_of(grad_ref, tile),
                     slots, back_tile_of(back_slots, tile, tall), state)
        layer_steps(tiles + step)

        @pl.when(step == tiles // 2)
        def _():
            sums_step(0)
            for copy in send_sums(1):
                copy.start()
        return carry

    lax.fori_loop(0, tiles, adjoint_step, 0)
    layer_sums(z)
    direct_back.arrive()

    def direct_step(tile, carry):
        grads, addend = tile_of(grad_ref, tile), tile_of(direct, tile)
        for row in range(rows):
            grads[row] = grads[row] + addend[row].astype(jnp.float32)
        return carry

    lax.fori_loop(0, tiles, direct_step, 0)
    sums_step(1)
    sums_out[...] = sums[2]
    skips_out[...] = skips[2]
    for which in range(2):
        outs[which][...] = held[which][z].astype(jnp.float32)

        @pl.when(z > 0)
        def _():
            send_right(which, z).wait_recv()
            outs[which][...] += from_z[which][z].astype(jnp.float32)

        @pl.when(z < deep - 1)
        def _():
            from_right(which, z, deep).wait_recv()
            outs[which][...] += from_z[which][deep].astype(jnp.float32)
    for step in range(1, deep):
        origin = (z + deep - step) % deep
        remote(small_deep.at[origin], small_deep.at[origin], small_send.at[3 + step], small_recv.at[3 + step], here.at_z(origin)).wait_recv()
    added = small_deep[0]
    for k in range(1, deep):
        added = added + small_deep[k]
    small_out[...] = added
    for stage in range(3):
        send_small(stage).wait_send()
    for stage in range(2):
        for copy in send_sums(stage):
            copy.wait_send()
    for step in range(1, deep):
        send_small_deep(step).wait_send()
    mixed_back.finish()
    direct_back.finish()
    for which in range(2):
        for slot in range(4 * deep):
            remote(held[which].at[slot], from_core[which].at[slot], core_send.at[which, slot], core_recv.at[which, slot], here.over_core()).wait_send()
        for k in range(deep):
            send_d(which, k).wait_send()
            send_x(which, k).wait_send()
            send_y(which, k).wait_send()

            @pl.when(k > z)
            def _():
                send_right(which, k).wait_send()

            @pl.when(k < z)
            def _():
                send_left(which, k).wait_send()


def ema_parts(logits, mixing):
    damping = jax.nn.sigmoid(logits[0])
    decay = 1.0 - damping * jax.nn.sigmoid(logits[1])
    return damping, decay, damping * mixing[0]


def keep_tables(segments):
    keeping = (segments[:, 1:] == segments[:, :-1]).astype(jnp.float32)
    edge = jnp.zeros((segments.shape[0], 1), jnp.float32)
    return (jnp.tile(jnp.concatenate([edge, keeping], axis=1), (2, 1)),
            jnp.tile(jnp.concatenate([keeping, edge], axis=1), (2, 1)))


def lane_table(table, rows):
    chans, count = table.shape
    spread_rows = jnp.repeat(table.T.reshape(2, count // 2, 1, chans), rows, axis=2)
    ordered = spread_rows.transpose(1, 0, 2, 3).reshape(count // 2, 2 * rows, chans)
    return jnp.pad(ordered, ((0, 0), (0, 0), (0, LANES - chans)))


def lane_sums(sums, rows, chans):
    count = sums.shape[0]
    return jnp.sum(sums.reshape(count, 2, rows, LANES), axis=2)[:, :, :chans].transpose(2, 1, 0).reshape(chans, 2 * count)


def ema_tables(logits, mixing, rows):
    _, decay, gain = ema_parts(logits, mixing)
    return [lane_table(decay, rows), lane_table(gain * mixing[1], rows)]


def ema_grads(weight, power, skips, logits, mixing, rows, chans):
    damping, decay, gain = ema_parts(logits, mixing)
    weight = lane_sums(weight, rows, chans)
    back_decay = gain * mixing[1] * lane_sums(power, rows, chans) / decay
    other = jax.nn.sigmoid(logits[1])
    back_damping = weight * mixing[0] * mixing[1] - back_decay * other
    grad_logits = jnp.stack([back_damping * damping * (1.0 - damping), -back_decay * damping * other * (1.0 - other)])
    grad_mixing = jnp.stack([damping * mixing[1] * weight, gain * weight])
    return grad_logits, grad_mixing, jnp.sum(skips, axis=1)


def dma(*shape):
    return pltpu.SemaphoreType.DMA(shape)


ANYWHERE = pl.BlockSpec(memory_space=pl.ANY)
NEAR = pl.BlockSpec(memory_space=pltpu.VMEM)
ROOM = 60 * 1024 * 1024


def forward_exchange(first, second, values, keep, tables, skip, devices, deep):
    rows, chans, length = values.shape
    half, tall, _ = tables[0].shape
    tokens = (rows, chans * 2 * deep, length // (2 * deep))
    return pl.pallas_call(
        partial(forward_kernel, deep),
        in_specs=[ANYWHERE, ANYWHERE] + [NEAR] * 5,
        out_specs=[ANYWHERE] * 4 + [NEAR],
        out_shape=[jax.ShapeDtypeStruct((devices,) + first.shape, first.dtype),
                   jax.ShapeDtypeStruct((devices,) + second.shape, second.dtype),
                   jax.ShapeDtypeStruct(tokens, jnp.bfloat16), jax.ShapeDtypeStruct(tokens, jnp.bfloat16),
                   jax.ShapeDtypeStruct(values.shape, jnp.float32)],
        scratch_shapes=[pltpu.VMEM(values.shape, jnp.bfloat16), pltpu.VMEM((LANES * tall, LANES), jnp.float32),
                        pltpu.VMEM((half, tall, LANES), jnp.float32),
                        dma(4), dma(2, deep, 2), dma(2, deep), dma(2, deep), dma(2, deep), dma(2, 4 * deep),
                        dma(2, deep), dma(2, deep), dma(2, deep), dma(2, deep), dma(2, 4 * deep)] + [dma(2 * deep)] * 4,
        compiler_params=pltpu.CompilerParams(collective_id=1, has_side_effects=True, vmem_limit_bytes=ROOM),
        cost_estimate=pl.CostEstimate(flops=values.size * 80, bytes_accessed=first.size * devices * 4, transcendentals=values.size),
    )(first, second, values, keep, *tables, jnp.broadcast_to(skip[:, None], (chans, LANES)))


def backward_exchange(first, second, small, values, pre, mixed_rows, direct_rows, keep, keep_next, tables, skip, deep):
    rows, chans, length = values.shape
    half, tall, _ = tables[0].shape
    skip_row = jnp.pad(jnp.broadcast_to(skip[None], (rows, chans)), ((0, rows), (0, LANES - chans)))
    shapes = [(group[0].shape[1], sum(part.shape[2] for part in group)) for group in (first, second)]
    scratch = []
    for count in (4 * deep, 4 * deep, deep, deep, deep, deep + 1):
        scratch += [pltpu.VMEM((count,) + shape, jnp.bfloat16) for shape in shapes]
    scratch += [pltpu.VMEM((4,) + small.shape, jnp.float32), pltpu.VMEM((3,) + small.shape, jnp.float32),
                pltpu.VMEM((deep,) + small.shape, jnp.float32)]
    scratch += [dma(2, 4 * deep)] * 3 + [dma(2, deep)] * 6 + [dma(2, deep), dma(2, deep + 1)] + [dma(3 + deep)] * 2
    scratch += [pltpu.VMEM(values.shape, jnp.bfloat16)] * 2
    scratch += [pltpu.VMEM((LANES * tall, LANES), jnp.float32), pltpu.VMEM((length * tall, LANES), jnp.float32)]
    scratch += [pltpu.VMEM((half, tall, LANES), jnp.float32)] * 2
    scratch += [pltpu.VMEM((3, 2 * half, tall, LANES), jnp.float32), pltpu.VMEM((2, 2 * half, tall, LANES), jnp.float32)]
    scratch += [pltpu.VMEM((3, chans, LANES), jnp.float32), pltpu.VMEM((2, chans, LANES), jnp.float32)]
    scratch += [dma(2)] + [dma(2 * deep)] * 4 + [dma(2, 2)] * 2
    return pl.pallas_call(
        partial(backward_kernel, deep, (len(first), len(second))),
        in_specs=[ANYWHERE] * (len(first) + len(second)) + [NEAR] * 3 + [ANYWHERE] * 2 + [NEAR] * 5,
        out_specs=[NEAR] * 6,
        out_shape=[jax.ShapeDtypeStruct(shape, jnp.float32) for shape in shapes]
        + [jax.ShapeDtypeStruct(small.shape, jnp.float32), jax.ShapeDtypeStruct(values.shape, jnp.float32),
           jax.ShapeDtypeStruct((2 * half, tall, LANES), jnp.float32), jax.ShapeDtypeStruct((chans, LANES), jnp.float32)],
        scratch_shapes=scratch,
        compiler_params=pltpu.CompilerParams(collective_id=2, has_side_effects=True, vmem_limit_bytes=ROOM),
        cost_estimate=pl.CostEstimate(flops=values.size * 240, bytes_accessed=64 * 1024 * 1024, transcendentals=values.size),
    )(*first, *second, small, values, pre, mixed_rows, direct_rows, keep, keep_next, *tables, skip_row)


def pack(parts):
    flat = jnp.concatenate([part.reshape(-1) for part in parts])
    return jnp.pad(flat, (0, -flat.shape[0] % 1024)).reshape(-1, 128)


def unpack(packed, like):
    flat, made, offset = packed.reshape(-1), [], 0
    for part in like:
        made.append(flat[offset : offset + part.size].reshape(part.shape))
        offset += part.size
    return made


def plain_forward_kernel(x_ref, keep_ref, decay_ref, gain_ref, skip_ref, pre_ref, mixed_ref, slots, state):
    @pl.when(pl.program_id(0) == 0)
    def _():
        state[...] = jnp.zeros_like(state)

    average_tile(x_ref, keep_ref[...], decay_ref, gain_ref, skip_ref, pre_ref, mixed_ref, slots, state)


def plain_backward_kernel(x_ref, pre_ref, back_ref, direct_ref, keep_ref, next_ref, decay_ref, gain_ref, skip_row_ref,
                          grad_ref, sums_ref, skips_ref, slots, back_slots, state, powers):
    halves, tall, _ = decay_ref.shape
    tiles = pl.num_programs(0) // 2
    index = pl.program_id(0)

    @pl.when(index == 0)
    def _():
        state[...] = jnp.zeros_like(state)
        powers[...] = jnp.zeros_like(powers)
        sums_ref[...] = jnp.zeros_like(sums_ref)
        skips_ref[...] = jnp.zeros_like(skips_ref)

    @pl.when(index < tiles)
    def _():
        weigh_tile(x_ref, pre_ref, back_ref, keep_ref[...], decay_ref, skips_ref, slots, back_tile_of(back_slots, index, tall),
                   state, powers, sums_ref.at[pl.ds(0, halves)], sums_ref.at[pl.ds(halves, halves)])

    @pl.when(index == tiles)
    def _():
        state[...] = jnp.zeros_like(state)

    @pl.when(index >= tiles)
    def _():
        adjoint_tile(next_ref[...], decay_ref, gain_ref, skip_row_ref, grad_ref, slots,
                     back_tile_of(back_slots, 2 * tiles - 1 - index, tall), state)
        for row in range(grad_ref.shape[0]):
            grad_ref[row] = grad_ref[row] + direct_ref[row].astype(jnp.float32)


def gathered(part):
    return lax.all_gather(part, ("row", "chan"), axis=0)


def plain_forward(first, second, values, keep, tables, skip):
    rows, chans, length = values.shape
    half, tall, _ = tables[0].shape
    block = pl.BlockSpec((rows, chans, LANES), lambda i: (0, 0, i))
    whole = pl.BlockSpec((half, tall, LANES), lambda i: (0, 0, 0))
    pre, mixed = pl.pallas_call(
        plain_forward_kernel,
        grid=(length // LANES,),
        in_specs=[block, pl.BlockSpec((tall, LANES), lambda i: (0, i)), whole, whole, pl.BlockSpec((chans, LANES), lambda i: (0, 0))],
        out_specs=[block, block],
        out_shape=[jax.ShapeDtypeStruct(values.shape, jnp.float32), jax.ShapeDtypeStruct(values.shape, jnp.bfloat16)],
        scratch_shapes=[pltpu.VMEM((LANES * tall, LANES), jnp.float32), pltpu.VMEM((half, tall, LANES), jnp.float32)],
    )(values, keep, *tables, jnp.broadcast_to(skip[:, None], (chans, LANES)))
    moved = [lax.all_to_all(part, "chan", split_axis=2, concat_axis=1, tiled=True) for part in (values, mixed)]
    return gathered(first), gathered(second), *moved, pre


def plain_backward(first, second, small, values, pre, mixed_rows, direct_rows, keep, keep_next, tables, skip):
    rows, chans, length = values.shape
    back, direct = [lax.all_to_all(part, "chan", split_axis=1, concat_axis=2, tiled=True) for part in (mixed_rows, direct_rows)]
    half, tall, _ = tables[0].shape
    tiles = length // LANES
    skip_row = jnp.pad(jnp.broadcast_to(skip[None], (rows, chans)), ((0, rows), (0, LANES - chans)))
    ahead = pl.BlockSpec((rows, chans, LANES), lambda i: (0, 0, jnp.minimum(i, tiles - 1)))
    behind = pl.BlockSpec((rows, chans, LANES), lambda i: (0, 0, jnp.minimum(tiles - 1, 2 * tiles - 1 - i)))
    whole = pl.BlockSpec((half, tall, LANES), lambda i: (0, 0, 0))
    grads, sums, skips = pl.pallas_call(
        plain_backward_kernel,
        grid=(2 * tiles,),
        in_specs=[ahead] * 3 + [behind, pl.BlockSpec((tall, LANES), lambda i: (0, jnp.minimum(i, tiles - 1))),
                                pl.BlockSpec((tall, LANES), lambda i: (0, jnp.minimum(tiles - 1, 2 * tiles - 1 - i))),
                                whole, whole, pl.BlockSpec((tall, LANES), lambda i: (0, 0))],
        out_specs=[behind, pl.BlockSpec((2 * half, tall, LANES), lambda i: (0, 0, 0)), pl.BlockSpec((chans, LANES), lambda i: (0, 0))],
        out_shape=[jax.ShapeDtypeStruct(values.shape, jnp.float32), jax.ShapeDtypeStruct((2 * half, tall, LANES), jnp.float32),
                   jax.ShapeDtypeStruct((chans, LANES), jnp.float32)],
        scratch_shapes=[pltpu.VMEM((LANES * tall, LANES), jnp.float32), pltpu.VMEM((length * tall, LANES), jnp.float32)]
        + [pltpu.VMEM((half, tall, LANES), jnp.float32)] * 2,
        compiler_params=pltpu.CompilerParams(vmem_limit_bytes=ROOM),
    )(values, pre, back, direct, keep, keep_next, *tables, skip_row)
    sums, skips, small = lax.psum((sums, skips), "row") + (lax.psum(small, ("row", "chan")),)
    owned = [
        jnp.concatenate([lax.psum_scatter(part, ("row", "chan"), scatter_dimension=0, tiled=True)[0] for part in group], axis=1)
        for group in (first, second)
    ]
    return *[part.astype(jnp.float32) for part in owned], small, grads, sums, skips


def product(left, right):
    return jnp.dot(left, right, preferred_element_type=jnp.float32)


def contract_rows(left, right):
    return lax.dot_general(
        left, right, (((0,), (0,)), ((), ())), preferred_element_type=jnp.float32
    )


def contract_cols(left, right):
    return lax.dot_general(
        left, right, (((1,), (1,)), ((), ())), preferred_element_type=jnp.float32
    )


def token_rows(blocked):
    return jnp.transpose(blocked, (0, 2, 1)).reshape(-1, blocked.shape[1])


def channel_blocks(matrix, row_count):
    return jnp.transpose(matrix.reshape(row_count, -1, matrix.shape[1]), (0, 2, 1))


def shards(
    inputs,
    cotangent,
    doc_lengths,
    ema_logits,
    ema_mixing,
    ema_skip,
    value_weight,
    base_weight,
    attn_weight,
    hidden_weight,
    output_weight,
    value_bias,
    base_bias,
    attn_bias,
    hidden_bias,
    output_bias,
    query_key_gain,
    query_key_shift,
    position_bias,
    norm_gain,
    norm_bias,
):
    row_count, chan_count, seq_length = inputs.shape
    group_count = lax.axis_size("chan")
    width = chan_count * group_count
    span_local = seq_length // group_count
    length_block = position_bias.shape[0]
    shared_width = query_key_gain.shape[1]
    value_width = value_bias.shape[0]
    token_count = row_count * span_local
    window_count = token_count // length_block
    score_scale = shared_width ** (-0.5)
    positions = jnp.arange(seq_length, dtype=jnp.int32)
    segment_rows = jax.vmap(segment_ids, (0, None))(doc_lengths, positions)

    keep, keep_next = keep_tables(segment_rows)
    tables = ema_tables(ema_logits, ema_mixing, row_count)
    on_four = lax.axis_size("row") == 4 and group_count == 8
    devices, deep = lax.axis_size("row") * group_count, group_count // 2
    first = jnp.concatenate([part.astype(jnp.bfloat16) for part in (value_weight, base_weight, hidden_weight)], axis=1)
    second = jnp.concatenate([part.astype(jnp.bfloat16) for part in (attn_weight, output_weight)], axis=1)
    exchange = partial(forward_exchange, devices=devices, deep=deep) if on_four else plain_forward
    first, second, token_input, token_mixed, pre_mix = exchange(first, second, inputs, keep, tables, ema_skip)
    cotangent, first = lax.optimization_barrier((cotangent, first))
    first, second = first.reshape(width, -1), second.reshape(value_width, -1)
    base_width = base_bias.shape[0]
    value_low = first[:, :value_width]
    base_low = first[:, value_width : value_width + base_width]
    hidden_low = first[:, value_width + base_width :]
    attn_low, output_low = second[:, :width], second[:, width:]
    input_rows = token_rows(token_input)
    mixed_rows = token_rows(token_mixed)
    local_pos = lax.axis_index("chan") * span_local + jnp.arange(span_local, dtype=jnp.int32)
    segment_local = jax.vmap(segment_ids, (0, None))(doc_lengths, local_pos).reshape(
        window_count, length_block
    )
    offset_hits = offset_table(length_block)
    bias_table = jnp.einsum("ijm,m->ij", offset_hits, position_bias, precision=HIGH)
    offsets = jnp.arange(length_block, dtype=jnp.int32)
    allowed = (offsets[:, None] >= offsets[None, :])[None] & (
        segment_local[:, :, None] == segment_local[:, None, :]
    )
    value_pre = product(input_rows, value_low) + value_bias
    value_rows = jax.nn.silu(value_pre).astype(jnp.bfloat16)
    base_proj = product(mixed_rows, base_low) + base_bias
    gate_pre = base_proj[:, :width]
    shared_pre = base_proj[:, width : width + shared_width]
    reset_pre = base_proj[:, width + shared_width : width + shared_width + value_width]
    direct_part = base_proj[:, width + shared_width + value_width :]
    update_gate = jax.nn.sigmoid(gate_pre)
    shared_z = jax.nn.silu(shared_pre)
    reset_gate = jax.nn.silu(reset_pre)
    queries = (
        (shared_z * query_key_gain[0] + query_key_shift[0])
        .astype(jnp.bfloat16)
        .reshape(window_count, length_block, shared_width)
    )
    key_rows = (
        (shared_z * query_key_gain[1] + query_key_shift[1])
        .astype(jnp.bfloat16)
        .reshape(window_count, length_block, shared_width)
    )
    value_win = value_rows.reshape(window_count, length_block, value_width)
    scores = (
        jnp.einsum("cik,cjk->cij", queries, key_rows, preferred_element_type=jnp.float32)
        * score_scale
        + bias_table[None]
    )
    attention = jax.nn.softmax(jnp.where(allowed, scores, MASKED), axis=-1)
    attention_low = attention.astype(jnp.bfloat16)
    attended = jnp.einsum(
        "cij,cjv->civ", attention_low, value_win, preferred_element_type=jnp.float32
    ).reshape(token_count, value_width)
    mixed_att = (attended * reset_gate).astype(jnp.bfloat16)
    hidden_pre = direct_part + product(mixed_att, attn_low) + attn_bias
    hidden = jax.nn.silu(hidden_pre)
    input_float = input_rows.astype(jnp.float32)
    out_one = input_float + update_gate * (hidden - input_float)
    normed, norm_back_one = jax.vjp(layer_norm, out_one, norm_gain[0], norm_bias[0])
    normed_low = normed.astype(jnp.bfloat16)
    inner_pre = product(normed_low, hidden_low) + hidden_bias
    activated = jax.nn.silu(inner_pre).astype(jnp.bfloat16)
    out_two = normed + product(activated, output_low) + output_bias
    final_rows, norm_back_two = jax.vjp(layer_norm, out_two, norm_gain[1], norm_bias[1])
    layer_out = lax.all_to_all(
        channel_blocks(final_rows.astype(jnp.bfloat16), row_count),
        "chan",
        split_axis=1,
        concat_axis=2,
        tiled=True,
    )
    token_grad = lax.all_to_all(cotangent, "chan", split_axis=2, concat_axis=1, tiled=True)
    grad_rows = token_rows(token_grad).astype(jnp.float32)
    back_two, gain_two, shift_two = norm_back_two(grad_rows)
    back_outer = back_two.astype(jnp.bfloat16)
    grad_output_weight = contract_rows(activated, back_outer)
    grad_output_bias = jnp.sum(back_two, axis=0)
    back_inner = (contract_cols(back_outer, output_low) * silu_slope(inner_pre)).astype(
        jnp.bfloat16
    )
    grad_hidden_weight = contract_rows(normed_low, back_inner)
    grad_hidden_bias = jnp.sum(back_inner.astype(jnp.float32), axis=0)
    back_normed = back_two + contract_cols(back_inner, hidden_low)
    back_one, gain_one, shift_one = norm_back_one(back_normed)
    back_hidden = back_one * update_gate * silu_slope(hidden_pre)
    back_proj = back_hidden.astype(jnp.bfloat16)
    grad_attn_weight = contract_rows(mixed_att, back_proj)
    grad_attn_bias = jnp.sum(back_hidden, axis=0)
    back_mix = contract_cols(back_proj, attn_low)
    back_mix, layer_out = lax.optimization_barrier((back_mix, layer_out))
    back_attended = (back_mix * reset_gate).astype(jnp.bfloat16)
    back_reset = back_mix * attended
    back_att_win = back_attended.reshape(window_count, length_block, value_width)
    back_attention = jnp.einsum(
        "civ,cjv->cij", back_att_win, value_win, preferred_element_type=jnp.float32
    )
    back_values = jnp.einsum(
        "cij,civ->cjv", attention_low, back_att_win, preferred_element_type=jnp.float32
    ).reshape(token_count, value_width)
    back_scores = (
        attention * (back_attention - jnp.sum(attention * back_attention, axis=-1, keepdims=True))
    ).astype(jnp.bfloat16)
    grad_position = jnp.einsum(
        "ijm,ij->m", offset_hits, jnp.sum(back_scores.astype(jnp.float32), axis=0), precision=HIGH
    )
    back_queries = (
        jnp.einsum(
            "cij,cjk->cik", back_scores, key_rows, preferred_element_type=jnp.float32
        ).reshape(token_count, shared_width)
        * score_scale
    )
    back_keys = (
        jnp.einsum(
            "cij,cik->cjk", back_scores, queries, preferred_element_type=jnp.float32
        ).reshape(token_count, shared_width)
        * score_scale
    )
    back_shared = back_queries * query_key_gain[0] + back_keys * query_key_gain[1]
    grad_key_gain = jnp.stack(
        [jnp.sum(back_queries * shared_z, axis=0), jnp.sum(back_keys * shared_z, axis=0)]
    )
    grad_key_shift = jnp.stack([jnp.sum(back_queries, axis=0), jnp.sum(back_keys, axis=0)])
    back_value = (back_values * silu_slope(value_pre)).astype(jnp.bfloat16)
    grad_value_weight = contract_rows(input_rows, back_value)
    grad_value_bias = jnp.sum(back_value.astype(jnp.float32), axis=0)
    back_base = jnp.concatenate(
        [
            back_one * (hidden - input_float) * update_gate * (1.0 - update_gate),
            back_shared * silu_slope(shared_pre),
            back_reset * silu_slope(reset_pre),
            back_hidden,
        ],
        axis=1,
    ).astype(jnp.bfloat16)
    grad_base_weight = contract_rows(mixed_rows, back_base)
    grad_base_bias = jnp.sum(back_base.astype(jnp.float32), axis=0)
    back_mixed_rows = contract_cols(back_base, base_low)
    back_direct = back_one * (1.0 - update_gate) + contract_cols(back_value, value_low)
    grad_norm_gain = jnp.stack([gain_one, gain_two])
    grad_norm_bias = jnp.stack([shift_one, shift_two])
    small = (
        grad_value_bias,
        grad_base_bias,
        grad_attn_bias,
        grad_hidden_bias,
        grad_output_bias,
        grad_key_gain,
        grad_key_shift,
        grad_position,
        grad_norm_gain,
        grad_norm_bias,
    )

    def owners(terms):
        return terms.astype(jnp.bfloat16).reshape(devices, -1, terms.shape[1])

    exchange = partial(backward_exchange, deep=deep) if on_four else plain_backward
    first_sum, second_sum, small_sum, grad_inputs, sums, skips = exchange(
        [owners(grad_value_weight), owners(grad_base_weight), owners(grad_hidden_weight)],
        [owners(grad_attn_weight), owners(grad_output_weight)],
        pack(small),
        inputs,
        pre_mix,
        channel_blocks(back_mixed_rows, row_count).astype(jnp.bfloat16),
        channel_blocks(back_direct, row_count).astype(jnp.bfloat16),
        keep,
        keep_next,
        tables,
        ema_skip,
    )
    states = sums.shape[0] // 2
    grad_logits, grad_mixing, grad_skip = ema_grads(
        sums[:states], sums[states:], skips, ema_logits, ema_mixing, row_count, chan_count
    )
    (
        sum_value_bias,
        sum_base_bias,
        sum_attn_bias,
        sum_hidden_bias,
        sum_output_bias,
        sum_key_gain,
        sum_key_shift,
        sum_position,
        sum_norm_gain,
        sum_norm_bias,
    ) = unpack(small_sum, small)
    owner_value = first_sum[:, :value_width]
    owner_base = first_sum[:, value_width : value_width + base_width]
    owner_hidden = first_sum[:, value_width + base_width :]
    owner_attn, owner_output = second_sum[:, :width], second_sum[:, width:]
    return (
        layer_out,
        grad_inputs,
        grad_logits,
        grad_mixing,
        grad_skip,
        owner_value,
        owner_base,
        owner_attn,
        owner_hidden,
        owner_output,
        sum_value_bias,
        sum_base_bias,
        sum_attn_bias,
        sum_hidden_bias,
        sum_output_bias,
        sum_key_gain,
        sum_key_shift,
        sum_position,
        sum_norm_gain,
        sum_norm_bias,
    )


def solution(mesh):
    in_specs = (
        P("row", "chan", None),
        P("row", "chan", None),
        P("row", None),
        P(None, "chan", None),
        P(None, "chan", None),
        P("chan"),
        P(("row", "chan"), None),
        P(("row", "chan"), None),
        P(("row", "chan"), None),
        P(("row", "chan"), None),
        P(("row", "chan"), None),
        P(),
        P(),
        P(),
        P(),
        P(),
        P(),
        P(),
        P(),
        P(),
        P(),
    )
    out_specs = (
        P("row", "chan", None),
        P("row", "chan", None),
        P(None, "chan", None),
        P(None, "chan", None),
        P("chan"),
        P(("row", "chan"), None),
        P(("row", "chan"), None),
        P(("row", "chan"), None),
        P(("row", "chan"), None),
        P(("row", "chan"), None),
        P(),
        P(),
        P(),
        P(),
        P(),
        P(),
        P(),
        P(),
        P(),
        P(),
    )
    return jax.shard_map(shards, mesh=mesh, in_specs=in_specs, out_specs=out_specs, check_vma=False)
```

```python
from functools import partial

import jax
import jax.numpy as jnp
from jax import lax
from jax.experimental import pallas as pl
from jax.experimental.pallas import tpu as pltpu
from jax.sharding import PartitionSpec as P

HIGH = lax.Precision.HIGHEST
EPSILON = 1e-05
MASKED = -1e30


def segment_ids(lengths, positions):
    boundary = jnp.cumsum(lengths)
    passed = (positions[:, None] >= boundary[None, :]).astype(jnp.int32)
    return jnp.sum(passed, axis=1)


LANES = 128
STEPS = 16
MESH = pl.DeviceIdType.MESH


def pad_rows(block):
    short = LANES - block.shape[0]
    if short == 0:
        return block
    return jnp.concatenate([block, jnp.zeros((short, block.shape[1]), block.dtype)], axis=0)


def spread(block, slots, row, rows):
    turned = pad_rows(block).T
    slots[pl.ds(row, LANES, stride=2 * rows), :] = turned
    slots[pl.ds(row + rows, LANES, stride=2 * rows), :] = turned


def gather(slots, row, rows, chans):
    first = slots[pl.ds(row, LANES, stride=2 * rows), :]
    second = slots[pl.ds(row + rows, LANES, stride=2 * rows), :]
    return (first + second).T[:chans]


def tile_of(ref, tile):
    return ref.at[:, :, pl.ds(pl.multiple_of(tile * LANES, LANES), LANES)]


def lanes_of(ref, tile):
    return ref[:, pl.ds(pl.multiple_of(tile * LANES, LANES), LANES)]


def slot_at(step, tall):
    return pl.ds(pl.multiple_of(step * tall, tall), tall)


def average_tile(x_tile, keep_tile, decay_ref, gain_ref, skip_ref, pre_tile, mixed_tile, slots, state):
    rows, chans, _ = x_tile.shape
    halves = decay_ref.shape[0]
    tall = 2 * rows
    for row in range(rows):
        spread(x_tile[row].astype(jnp.float32), slots, row, rows)

    def group(step, carry):
        keeping, states = carry
        states = list(states)
        for inner in range(STEPS):
            at = slot_at(step * STEPS + inner, tall)
            value = slots[at, :]
            keep = jnp.broadcast_to(keeping[:, inner : inner + 1], (tall, LANES))
            total = None
            for n in range(halves):
                states[n] = (decay_ref[n] * keep) * states[n] + gain_ref[n] * value
                total = states[n] if total is None else total + states[n]
            slots[at, :] = total
        return pltpu.roll(keeping, LANES - STEPS, axis=1), tuple(states)

    start = tuple(state[n] for n in range(halves))
    _, states = lax.fori_loop(0, LANES // STEPS, group, (keep_tile, start))
    for n in range(halves):
        state[n] = states[n]
    for row in range(rows):
        pre = gather(slots, row, rows, chans) + skip_ref[:, :1] * x_tile[row].astype(jnp.float32)
        pre_tile[row] = pre
        mixed_tile[row] = (pre * jax.nn.sigmoid(pre)).astype(jnp.bfloat16)


def back_tile_of(back_slots, tile, tall):
    return back_slots.at[pl.ds(pl.multiple_of(tile * (LANES * tall), LANES * tall), LANES * tall), :]


def weigh_tile(x_tile, pre_tile, back_mixed_tile, keep_tile, decay_ref, skip_sum, slots, back_tile, state, powers, weight_sum, power_sum):
    rows = x_tile.shape[0]
    halves = decay_ref.shape[0]
    tall = 2 * rows
    for row in range(rows):
        values = x_tile[row].astype(jnp.float32)
        pre = pre_tile[row]
        logistic = jax.nn.sigmoid(pre)
        back = back_mixed_tile[row].astype(jnp.float32) * (logistic * (1.0 + pre * (1.0 - logistic)))
        skip_sum[...] += back * values
        spread(values, slots, row, rows)
        spread(back, back_tile, row, rows)

    def group(step, carry):
        keeping, states, derived, weights, sums = (carry[0], *map(list, carry[1:]))
        for inner in range(STEPS):
            at = slot_at(step * STEPS + inner, tall)
            value = slots[at, :]
            back = back_tile[at, :]
            keep = jnp.broadcast_to(keeping[:, inner : inner + 1], (tall, LANES))
            for n in range(halves):
                decay = decay_ref[n] * keep
                derived[n] = decay * (derived[n] + states[n])
                states[n] = decay * states[n] + value
                weights[n] = weights[n] + back * states[n]
                sums[n] = sums[n] + back * derived[n]
        return pltpu.roll(keeping, LANES - STEPS, axis=1), tuple(states), tuple(derived), tuple(weights), tuple(sums)

    refs = (state, powers, weight_sum, power_sum)
    start = tuple(tuple(ref[n] for n in range(halves)) for ref in refs)
    out = lax.fori_loop(0, LANES // STEPS, group, (keep_tile, *start))
    for ref, values in zip(refs, out[1:]):
        for n in range(halves):
            ref[n] = values[n]


def adjoint_tile(next_tile, decay_ref, gain_ref, skip_row_ref, grad_tile, slots, back_tile, state):
    rows, chans, _ = grad_tile.shape
    halves = decay_ref.shape[0]
    tall = 2 * rows

    def group(step, carry):
        keeping, states = carry
        states = list(states)
        for inner in range(STEPS):
            at = slot_at(LANES - 1 - step * STEPS - inner, tall)
            back = back_tile[at, :]
            keep = jnp.broadcast_to(keeping[:, LANES - 1 - inner : LANES - inner], (tall, LANES))
            total = skip_row_ref[...] * back
            for n in range(halves):
                states[n] = (decay_ref[n] * keep) * states[n] + back
                total = total + gain_ref[n] * states[n]
            slots[at, :] = total
        return pltpu.roll(keeping, STEPS, axis=1), tuple(states)

    start = tuple(state[n] for n in range(halves))
    _, states = lax.fori_loop(0, LANES // STEPS, group, (next_tile, start))
    for n in range(halves):
        state[n] = states[n]
    for row in range(rows):
        grad_tile[row] = gather(slots, row, rows, chans)


class Place:
    def __init__(self, deep):
        self.deep = deep
        row, chan = lax.axis_index("row"), lax.axis_index("chan")
        self.y, self.core = row // 2, row % 2
        self.z, self.x = chan // 2, chan % 2
        self.row, self.chan = row, chan

    def owner(self, z, x, y, core):
        return (y * 2 + core) * (2 * self.deep) + z * 2 + x

    def over_core(self):
        return (self.row + 1 - 2 * self.core, self.chan)

    def over_x(self):
        return (self.row, self.chan + 1 - 2 * self.x)

    def over_y(self):
        return (self.row + 2 - 4 * self.y, self.chan)

    def at_z(self, z):
        return (self.row, z * 2 + self.x)

    def at_chan(self, step):
        chan = (self.chan + step) % (2 * self.deep)
        return chan, (self.row, chan)

    def greet(self):
        barrier = pltpu.get_barrier_semaphore()
        others = [self.over_core(), self.over_y()]
        others += [self.at_chan(step)[1] for step in range(1, 2 * self.deep)]
        for other in others:
            pl.semaphore_signal(barrier, inc=1, device_id=other, device_id_type=MESH)
        pl.semaphore_wait(barrier, len(others))

    def greet_line(self):
        barrier = pltpu.get_barrier_semaphore()
        for step in range(1, 2 * self.deep):
            pl.semaphore_signal(barrier, inc=1, device_id=self.at_chan(step)[1], device_id_type=MESH)
        pl.semaphore_wait(barrier, 2 * self.deep - 1)


def remote(source, target, send, recv, device):
    return pltpu.make_async_remote_copy(src_ref=source, dst_ref=target, send_sem=send, recv_sem=recv,
                                        device_id=device, device_id_type=MESH)


def start(copies):
    for copy in copies:
        copy.start()


class ToTokens:
    def __init__(self, here, source, target, send, recv, keep):
        self.here, self.source, self.target = here, source, target
        self.send, self.recv, self.keep = send, recv, keep
        self.chans, self.span = source.shape[1], target.shape[2]

    def block(self, chan):
        return self.source.at[:, :, pl.ds(pl.multiple_of(chan * self.span, LANES), self.span)]

    def spot(self, chan):
        return self.target.at[:, pl.ds(pl.multiple_of(chan * self.chans, 8), self.chans), :]

    def own(self):
        return pltpu.make_async_copy(self.block(self.here.chan), self.spot(self.here.chan), self.keep)

    def out(self, chan):
        return remote(self.block(chan), self.spot(self.here.chan), self.send.at[chan], self.recv.at[self.here.chan], (self.here.row, chan))

    def arrival(self, chan):
        return remote(self.block(chan), self.spot(chan), self.send.at[chan], self.recv.at[chan], (self.here.row, chan))

    def begin_same(self):
        for step in range(2, 2 * self.here.deep, 2):
            self.out(self.here.at_chan(step)[0]).start()
        self.own().start()

    def begin_cross(self):
        for step in range(1, 2 * self.here.deep, 2):
            self.out(self.here.at_chan(step)[0]).start()

    def begin(self):
        self.begin_cross()
        self.begin_same()

    def begin_one(self, chan):
        @pl.when(chan == self.here.chan)
        def _():
            self.own().start()

        @pl.when(chan != self.here.chan)
        def _():
            self.out(chan).start()

    def arrive(self):
        self.own().wait()
        for step in range(1, 2 * self.here.deep):
            self.arrival(self.here.at_chan(step)[0]).wait_recv()

    def finish(self):
        for step in range(1, 2 * self.here.deep):
            self.out(self.here.at_chan(step)[0]).wait_send()


class ToChannels(ToTokens):
    def __init__(self, here, source, target, send, recv, keep):
        super().__init__(here, source, target, send, recv, keep)
        self.chans, self.span = target.shape[1], source.shape[2]

    def block(self, chan):
        return self.source.at[:, pl.ds(pl.multiple_of(chan * self.chans, 8), self.chans), :]

    def spot(self, chan):
        return self.target.at[:, :, pl.ds(pl.multiple_of(chan * self.span, LANES), self.span)]


def forward_kernel(deep, groups, *refs):
    total = sum(groups)
    forward_body(deep, groups, refs[:total], *refs[total:])


def forward_body(deep, groups, shards_in, x_ref, keep_ref, decay_ref, gain_ref, skip_ref,
                   first_full, second_full, token_x, token_mixed, pre_ref,
                   first, second, mixed, slots, state, local_sem, send_z, send_x, send_y, send_d, send_core, recv_z, recv_x, recv_y, recv_d, recv_core,
                   a_send, a_recv, b_send, b_recv):
    count = 2
    mine, full = (first, second), (first_full, second_full)
    here = Place(deep)
    z, x, y, core = here.z, here.x, here.y, here.core
    me = here.owner(z, x, y, core)
    layers = range(deep)

    def piece(which, at, device, send, recv, source=None):
        spot = full[which].at[at]
        return remote(spot if source is None else source, spot, send, recv, device)

    def to_core(at, slot, source=False):
        return [piece(which, at, here.over_core(), send_core.at[which, slot], recv_core.at[which, slot],
                      mine[which] if source else None) for which in range(count)]

    def own_x(k, source=False):
        at = here.owner(k, x, y, core)
        return [piece(which, at, here.over_x(), send_x.at[which, k], recv_x.at[which, k],
                      mine[which] if source else None) for which in range(count)]

    def own_y(k, source=False):
        at = here.owner(k, x, y, core)
        return [piece(which, at, here.over_y(), send_y.at[which, k], recv_y.at[which, k],
                      mine[which] if source else None) for which in range(count)]

    def column(k, source=False):
        start(own_x(k, source))
        start(own_y(k, source))
        start(to_core(here.owner(k, x, y, core), k, source))

    def along(k, to, side, source=False):
        at = here.owner(k, x, y, core)
        return [piece(which, at, here.at_z(to), send_z.at[which, k, side], recv_z.at[which, k],
                      mine[which] if source else None) for which in range(count)]

    via_x = 1

    def onward_y(k):
        at = here.owner(k, 1 - x, y, core)
        return [piece(which, at, here.over_y(), send_d.at[which, k], recv_d.at[which, k]) for which in range(count)]

    def onward_x(k):
        at = here.owner(k, x, 1 - y, core)
        return [piece(which, at, here.over_x(), send_d.at[which, k], recv_d.at[which, k]) for which in range(count)]

    def wait_from(at, recv, k, device):
        for which in range(count):
            piece(which, at, device, send_x.at[which, 0], recv.at[which, k]).wait_recv()

    def sides(distance):
        return [z] if distance == 0 else [z - distance, z + distance]

    def neighbours(distance):
        for k in sides(distance):
            @pl.when((k >= 0) & (k < deep))
            def _():
                at = here.owner(k, 1 - x, y, core)
                wait_from(at, recv_x, k, here.over_x())

                @pl.when(k >= via_x)
                def _():
                    start(onward_y(k))
                start(to_core(at, deep + k))
                at = here.owner(k, x, 1 - y, core)
                wait_from(at, recv_y, k, here.over_y())

                @pl.when(k < via_x)
                def _():
                    start(onward_x(k))
                start(to_core(at, 2 * deep + k))

    def layer_step(distance):
        for side, k in enumerate(sides(distance)):
            @pl.when((k >= 0) & (k < deep))
            def _():
                to = z + 1 if side == 0 else z - 1
                wait_from(here.owner(k, x, y, core), recv_z, k, here.at_z(z))

                @pl.when((to >= 0) & (to < deep))
                def _():
                    start(along(k, to, 1 - side))
                column(k)

    at_shard = 0
    for target, size in zip(mine, groups):
        offset = 0
        for shard in shards_in[at_shard : at_shard + size]:
            target[:, pl.ds(offset, shard.shape[1])] = shard[...].astype(jnp.bfloat16)
            offset += shard.shape[1]
        at_shard += size
    here.greet()
    tokens_x = ToTokens(here, x_ref, token_x, a_send, a_recv, local_sem.at[2])
    tokens_mixed = ToTokens(here, mixed, token_mixed, b_send, b_recv, local_sem.at[3])
    local = [pltpu.make_async_copy(mine[which], full[which].at[me], local_sem.at[which]) for which in range(count)]
    start(local)
    for side, to in ((0, z - 1), (1, z + 1)):
        @pl.when((to >= 0) & (to < deep))
        def _():
            start(along(z, to, side, True))
    column(z, True)
    state[...] = jnp.zeros_like(state)
    tiles = x_ref.shape[2] // LANES
    each = tokens_x.span // LANES

    def tile_step(tile, carry):
        average_tile(tile_of(x_ref, tile), lanes_of(keep_ref, tile), decay_ref, gain_ref, skip_ref,
                     tile_of(pre_ref, tile), tile_of(mixed, tile), slots, state)

        @pl.when(tile == 5)
        def _():
            layer_step(1)

        @pl.when(tile == 8)
        def _():
            neighbours(0)

        @pl.when(tile == 12)
        def _():
            layer_step(2)

        @pl.when(tile == 15)
        def _():
            layer_step(3)
            tokens_x.begin()
        return carry

    lax.fori_loop(0, tiles, tile_step, 0)
    tokens_mixed.begin()
    neighbours(1)
    neighbours(2)
    neighbours(deep - 1)
    for k in layers:
        at = here.owner(k, 1 - x, 1 - y, core)
        wait_from(at, recv_d, k, here.over_y())
        start(to_core(at, 3 * deep + k))
    for copy in local:
        copy.wait()
    tokens_x.arrive()
    tokens_mixed.arrive()
    for slot, (flip_x, flip_y) in enumerate(((0, 0), (1, 0), (0, 1), (1, 1))):
        for k in layers:
            at = here.owner(k, x + flip_x * (1 - 2 * x), y + flip_y * (1 - 2 * y), 1 - core)
            for copy in to_core(at, slot * deep + k):
                copy.wait_recv()
                copy.wait_send()
    for k in layers:
        for copy in own_x(k) + own_y(k) + (onward_x(k) if k < via_x else onward_y(k)):
            copy.wait_send()
        for side, valid in ((0, (k >= z) & (z > 0)), (1, (k <= z) & (z < deep - 1))):
            @pl.when(valid)
            def _():
                for copy in along(k, z, side):
                    copy.wait_send()
    tokens_x.finish()
    tokens_mixed.finish()


LAYER_TIMES = ((3, 11), (0, 12), (2, 16), (1, 20))
LAYER_GAP = 4


def backward_kernel(deep, groups, *refs):
    total = sum(groups)
    sources = refs[:total]
    (small, x_ref, pre_ref, mixed_rows, direct_rows, keep_ref, next_ref, decay_ref, gain_ref, skip_row_ref) = refs[total : total + 10]
    refs = refs[total + 10 :]
    outs, (small_out, grad_ref, direct, sums_out, skips_out) = refs[:total], refs[total : total + 5]
    rest = refs[total + 5 :]
    held, from_core, from_d, from_x, from_y, from_z = (rest[2 * i : 2 * i + 2] for i in range(6))
    (small_sum, small_pair, small_deep, load_sem, core_send, core_recv, d_send, d_recv, x_send, x_recv, y_send, y_recv,
     z_send, z_recv, small_send, small_recv, back_mixed, slots, back_slots, state, powers, sums, sums_pair,
     skips, skips_pair,     local_sem, a_send, a_recv, b_send, b_recv, sums_send, sums_recv) = rest[12:]
    here = Place(deep)
    z, x, y, core = here.z, here.x, here.y, here.core
    rows, chans, length = x_ref.shape
    halves = decay_ref.shape[0]
    tall = 2 * rows
    tiles = length // LANES
    wide = []
    first = 0
    for which, size in enumerate(groups):
        offset = 0
        for source in sources[first : first + size]:
            wide.append((which, source, offset, source.shape[2]))
            offset += source.shape[2]
        first += size

    def begin(index, carry):
        slot = 4 * deep - 1 - index
        k, flips = slot % deep, slot // deep
        to_x = x + (flips % 2) * (1 - 2 * x)
        to_y = y + (flips // 2) * (1 - 2 * y)
        own, other = here.owner(k, to_x, to_y, core), here.owner(k, to_x, to_y, 1 - core)
        for which, source, offset, width in wide:
            pltpu.make_async_copy(source.at[own], held[which].at[slot, :, pl.ds(offset, width)], load_sem.at[which, slot]).start()
            remote(source.at[other], from_core[which].at[slot, :, pl.ds(offset, width)],
                   core_send.at[which, slot], core_recv.at[which, slot], here.over_core()).start()
        return carry

    def ready(slot):
        for which in range(2):
            spot = held[which].at[slot]
            pltpu.make_async_copy(spot, spot, load_sem.at[which, slot]).wait()
            remote(spot, from_core[which].at[slot], core_send.at[which, slot], core_recv.at[which, slot], here.over_core()).wait_recv()
            held[which][slot] = held[which][slot] + from_core[which][slot]

    via_x = 1

    def send_d(which, k):
        device = here.over_x() if k < via_x else here.over_y()
        return remote(held[which].at[3 * deep + k], from_d[which].at[k], d_send.at[which, k], d_recv.at[which, k], device)

    def send_x(which, k):
        return remote(held[which].at[deep + k], from_x[which].at[k], x_send.at[which, k], x_recv.at[which, k], here.over_x())

    def send_y(which, k):
        return remote(held[which].at[2 * deep + k], from_y[which].at[k], y_send.at[which, k], y_recv.at[which, k], here.over_y())

    def send_right(which, k):
        return remote(held[which].at[k], from_z[which].at[k], z_send.at[which, k], z_recv.at[which, k], here.at_z(z + 1))

    def send_left(which, k):
        slot = jnp.where(z - 1 == k, deep, k)
        return remote(held[which].at[k], from_z[which].at[slot], z_send.at[which, k], z_recv.at[which, slot], here.at_z(z - 1))

    def from_right(which, k, slot):
        return remote(held[which].at[k], from_z[which].at[slot], z_send.at[which, k], z_recv.at[which, slot], here.at_z(z + 1))

    def send_small(stage):
        device = (here.over_core(), here.over_y(), here.over_x())[stage]
        return remote(small_sum.at[stage], small_pair.at[stage], small_send.at[stage], small_recv.at[stage], device)

    def send_small_deep(step):
        return remote(small_deep.at[z], small_deep.at[z], small_send.at[3 + step], small_recv.at[3 + step],
                      here.at_z((z + step) % deep))

    def send_sums(stage):
        device = (here.over_core(), here.over_y())[stage]
        return [remote(sums.at[stage], sums_pair.at[stage], sums_send.at[0, stage], sums_recv.at[0, stage], device),
                remote(skips.at[stage], skips_pair.at[stage], sums_send.at[1, stage], sums_recv.at[1, stage], device)]

    def sums_step(stage):
        for copy in send_sums(stage):
            copy.wait_recv()
        sums[stage + 1] = sums[stage] + sums_pair[stage]
        skips[stage + 1] = skips[stage] + skips_pair[stage]

    here.greet()
    mixed_back = ToChannels(here, mixed_rows, back_mixed, a_send, a_recv, local_sem.at[0])
    direct_back = ToChannels(here, direct_rows, direct, b_send, b_recv, local_sem.at[1])
    mixed_back.begin()
    small_sum[0] = small[...]
    send_small(0).start()
    lax.fori_loop(0, 4 * deep, begin, 0)

    def small_step(stage):
        send_small(stage).wait_recv()
        small_sum[stage + 1] = small_sum[stage] + small_pair[stage]
        if stage < 2:
            send_small(stage + 1).start()

    def diagonal(k):
        ready(3 * deep + k)
        for which in range(2):
            send_d(which, k).start()

    def side(slot, send, k, waits):
        ready(slot * deep + k)
        for which in range(2):
            if waits:
                send_d(which, k).wait_recv()
                held[which][slot * deep + k] = held[which][slot * deep + k] + from_d[which][k]
            send(which, k).start()

    def x_side(k):
        side(1, send_x, k, k >= via_x)

    def y_side(k):
        side(2, send_y, k, k < via_x)

    diagonal(3)
    small_step(0)
    y_side(3)
    diagonal(0)
    x_side(0)
    diagonal(2)
    diagonal(1)
    small_step(1)
    direct_back.begin_same()
    x_side(3)
    y_side(0)
    y_side(2)
    x_side(2)
    y_side(1)
    for k in range(deep):
        ready(k)
    x_side(1)
    small_step(2)
    small_deep[z] = small_sum[3]
    for step in range(1, deep):
        send_small_deep(step).start()

    state[...] = jnp.zeros_like(state)
    powers[...] = jnp.zeros_like(powers)
    sums[0] = jnp.zeros_like(sums[0])
    skips[0] = jnp.zeros_like(skips[0])
    own_sums = sums.at[0]
    weight_sum, power_sum = own_sums.at[pl.ds(0, halves)], own_sums.at[pl.ds(halves, halves)]
    mixed_back.arrive()
    direct_back.begin_cross()

    def layer_sums(k):
        for which in range(2):
            send_x(which, k).wait_recv()
            send_y(which, k).wait_recv()
            held[which][k] = (held[which][k].astype(jnp.float32) + from_x[which][k].astype(jnp.float32)
                              + from_y[which][k].astype(jnp.float32)).astype(jnp.bfloat16)

    def layer_step(k):
        layer_sums(k)

        @pl.when(k > z)
        def _():
            for which in range(2):
                @pl.when(z > 0)
                def _():
                    send_right(which, k).wait_recv()
                    held[which][k] = held[which][k] + from_z[which][k]
                send_right(which, k).start()

        @pl.when(k < z)
        def _():
            for which in range(2):
                @pl.when(z < deep - 1)
                def _():
                    from_right(which, k, k).wait_recv()
                    held[which][k] = held[which][k] + from_z[which][k]
                send_left(which, k).start()

    def layer_steps(index):
        for k, base in LAYER_TIMES:
            hop = jnp.where(k > z, z, deep - 1 - z)

            @pl.when((index == base + LAYER_GAP * hop) & (k != z))
            def _():
                layer_step(k)

    def weigh_step(tile, carry):
        weigh_tile(tile_of(x_ref, tile), tile_of(pre_ref, tile), tile_of(back_mixed, tile), lanes_of(keep_ref, tile), decay_ref,
                   skips.at[0], slots, back_tile_of(back_slots, tile, tall), state, powers, weight_sum, power_sum)
        layer_steps(tile)
        return carry

    lax.fori_loop(0, tiles, weigh_step, 0)
    for copy in send_sums(0):
        copy.start()
    state[...] = jnp.zeros_like(state)

    def adjoint_step(step, carry):
        tile = tiles - 1 - step
        adjoint_tile(lanes_of(next_ref, tile), decay_ref, gain_ref, skip_row_ref, tile_of(grad_ref, tile),
                     slots, back_tile_of(back_slots, tile, tall), state)
        layer_steps(tiles + step)

        @pl.when(step == tiles // 2)
        def _():
            sums_step(0)
            for copy in send_sums(1):
                copy.start()
        return carry

    lax.fori_loop(0, tiles, adjoint_step, 0)
    layer_sums(z)
    sums_step(1)
    sums_out[...] = sums[2]
    skips_out[...] = skips[2]
    for which in range(2):
        @pl.when(z > 0)
        def _():
            send_right(which, z).wait_recv()

        @pl.when(z < deep - 1)
        def _():
            from_right(which, z, deep).wait_recv()
    for out, (which, _, offset, width) in zip(outs, wide):
        columns = pl.ds(offset, width)
        out[...] = held[which][z, :, columns].astype(jnp.float32)

        @pl.when(z > 0)
        def _():
            out[...] += from_z[which][z, :, columns].astype(jnp.float32)

        @pl.when(z < deep - 1)
        def _():
            out[...] += from_z[which][deep, :, columns].astype(jnp.float32)
    direct_back.arrive()
    for step in range(1, deep):
        origin = (z + deep - step) % deep
        remote(small_deep.at[origin], small_deep.at[origin], small_send.at[3 + step], small_recv.at[3 + step], here.at_z(origin)).wait_recv()
    added = small_deep[0]
    for k in range(1, deep):
        added = added + small_deep[k]
    small_out[...] = added
    for stage in range(3):
        send_small(stage).wait_send()
    for stage in range(2):
        for copy in send_sums(stage):
            copy.wait_send()
    for step in range(1, deep):
        send_small_deep(step).wait_send()
    mixed_back.finish()
    direct_back.finish()
    for which in range(2):
        for slot in range(4 * deep):
            remote(held[which].at[slot], from_core[which].at[slot], core_send.at[which, slot], core_recv.at[which, slot], here.over_core()).wait_send()
        for k in range(deep):
            send_d(which, k).wait_send()
            send_x(which, k).wait_send()
            send_y(which, k).wait_send()

            @pl.when(k > z)
            def _():
                send_right(which, k).wait_send()

            @pl.when(k < z)
            def _():
                send_left(which, k).wait_send()


def ema_parts(logits, mixing):
    damping = jax.nn.sigmoid(logits[0])
    decay = 1.0 - damping * jax.nn.sigmoid(logits[1])
    return damping, decay, damping * mixing[0]


def keep_tables(lengths, length):
    rows, count = lengths.shape
    earlier = jnp.tril(jnp.ones((count, count), jnp.int32))
    begins = jnp.sum(lengths[:, None, :] * earlier[None], axis=2)
    positions = jnp.arange(length, dtype=jnp.int32)

    def continues(at):
        hit = jnp.any(at[None, :, None] == begins[:, None, :], axis=2) | ((at == 0) | (at == length))[None]
        return jnp.tile(1.0 - hit.astype(jnp.float32), (2, 1))

    return continues(positions), continues(positions + 1)


def lane_table(table, rows):
    chans, count = table.shape
    spread_rows = jnp.repeat(table.T.reshape(2, count // 2, 1, chans), rows, axis=2)
    ordered = spread_rows.transpose(1, 0, 2, 3).reshape(count // 2, 2 * rows, chans)
    return jnp.pad(ordered, ((0, 0), (0, 0), (0, LANES - chans)))


def lane_sums(sums, rows, chans):
    count = sums.shape[0]
    return jnp.sum(sums.reshape(count, 2, rows, LANES), axis=2)[:, :, :chans].transpose(2, 1, 0).reshape(chans, 2 * count)


def ema_tables(logits, mixing, rows):
    _, decay, gain = ema_parts(logits, mixing)
    return [lane_table(decay, rows), lane_table(gain * mixing[1], rows)]


def ema_grads(weight, power, skips, logits, mixing, rows, chans):
    damping, decay, gain = ema_parts(logits, mixing)
    weight = lane_sums(weight, rows, chans)
    back_decay = gain * mixing[1] * lane_sums(power, rows, chans) / decay
    other = jax.nn.sigmoid(logits[1])
    back_damping = weight * mixing[0] * mixing[1] - back_decay * other
    grad_logits = jnp.stack([back_damping * damping * (1.0 - damping), -back_decay * damping * other * (1.0 - other)])
    grad_mixing = jnp.stack([damping * mixing[1] * weight, gain * weight])
    return grad_logits, grad_mixing, jnp.sum(skips, axis=1)


def dma(*shape):
    return pltpu.SemaphoreType.DMA(shape)


ANYWHERE = pl.BlockSpec(memory_space=pl.ANY)
NEAR = pl.BlockSpec(memory_space=pltpu.VMEM)
ROOM = 60 * 1024 * 1024


def forward_exchange(first, second, values, keep, tables, skip, devices, deep):
    rows, chans, length = values.shape
    shapes = [(group[0].shape[0], sum(part.shape[1] for part in group)) for group in (first, second)]
    low = jnp.bfloat16
    half, tall, _ = tables[0].shape
    tokens = (rows, chans * 2 * deep, length // (2 * deep))
    return pl.pallas_call(
        partial(forward_kernel, deep, (len(first), len(second))),
        in_specs=[NEAR] * (len(first) + len(second) + 5),
        out_specs=[ANYWHERE] * 4 + [NEAR],
        out_shape=[jax.ShapeDtypeStruct((devices,) + shape, low) for shape in shapes] + [
                   jax.ShapeDtypeStruct(tokens, jnp.bfloat16), jax.ShapeDtypeStruct(tokens, jnp.bfloat16),
                   jax.ShapeDtypeStruct(values.shape, jnp.float32)],
        scratch_shapes=[pltpu.VMEM(shape, low) for shape in shapes] + [pltpu.VMEM(values.shape, jnp.bfloat16), pltpu.VMEM((LANES * tall, LANES), jnp.float32),
                        pltpu.VMEM((half, tall, LANES), jnp.float32),
                        dma(4), dma(2, deep, 2), dma(2, deep), dma(2, deep), dma(2, deep), dma(2, 4 * deep),
                        dma(2, deep), dma(2, deep), dma(2, deep), dma(2, deep), dma(2, 4 * deep)] + [dma(2 * deep)] * 4,
        compiler_params=pltpu.CompilerParams(collective_id=1, has_side_effects=True, vmem_limit_bytes=ROOM),
        cost_estimate=pl.CostEstimate(flops=values.size * 80, bytes_accessed=48 * 1024 * 1024, transcendentals=values.size),
    )(*first, *second, values, keep, *tables, jnp.broadcast_to(skip[:, None], (chans, LANES)))


def backward_exchange(first, second, small, values, pre, mixed_rows, direct_rows, keep, keep_next, tables, skip, deep):
    rows, chans, length = values.shape
    half, tall, _ = tables[0].shape
    skip_row = jnp.pad(jnp.broadcast_to(skip[None], (rows, chans)), ((0, rows), (0, LANES - chans)))
    shapes = [(group[0].shape[1], sum(part.shape[2] for part in group)) for group in (first, second)]
    scratch = []
    for count in (4 * deep, 4 * deep, deep, deep, deep, deep + 1):
        scratch += [pltpu.VMEM((count,) + shape, jnp.bfloat16) for shape in shapes]
    scratch += [pltpu.VMEM((4,) + small.shape, jnp.float32), pltpu.VMEM((3,) + small.shape, jnp.float32),
                pltpu.VMEM((deep,) + small.shape, jnp.float32)]
    scratch += [dma(2, 4 * deep)] * 3 + [dma(2, deep)] * 6 + [dma(2, deep), dma(2, deep + 1)] + [dma(3 + deep)] * 2
    scratch += [pltpu.VMEM(values.shape, jnp.bfloat16)]
    scratch += [pltpu.VMEM((LANES * tall, LANES), jnp.float32), pltpu.VMEM((length * tall, LANES), jnp.float32)]
    scratch += [pltpu.VMEM((half, tall, LANES), jnp.float32)] * 2
    scratch += [pltpu.VMEM((3, 2 * half, tall, LANES), jnp.float32), pltpu.VMEM((2, 2 * half, tall, LANES), jnp.float32)]
    scratch += [pltpu.VMEM((3, chans, LANES), jnp.float32), pltpu.VMEM((2, chans, LANES), jnp.float32)]
    scratch += [dma(2)] + [dma(2 * deep)] * 4 + [dma(2, 2)] * 2
    return pl.pallas_call(
        partial(backward_kernel, deep, (len(first), len(second))),
        in_specs=[ANYWHERE] * (len(first) + len(second)) + [NEAR] * 3 + [ANYWHERE] * 2 + [NEAR] * 5,
        out_specs=[NEAR] * (len(first) + len(second) + 2) + [ANYWHERE] + [NEAR] * 2,
        out_shape=[jax.ShapeDtypeStruct(part.shape[1:], jnp.float32) for part in (*first, *second)]
        + [jax.ShapeDtypeStruct(small.shape, jnp.float32), jax.ShapeDtypeStruct(values.shape, jnp.float32),
           jax.ShapeDtypeStruct(values.shape, jnp.bfloat16),
           jax.ShapeDtypeStruct((2 * half, tall, LANES), jnp.float32), jax.ShapeDtypeStruct((chans, LANES), jnp.float32)],
        scratch_shapes=scratch,
        compiler_params=pltpu.CompilerParams(collective_id=2, has_side_effects=True, vmem_limit_bytes=ROOM),
        cost_estimate=pl.CostEstimate(flops=values.size * 240, bytes_accessed=64 * 1024 * 1024, transcendentals=values.size),
    )(*first, *second, small, values, pre, mixed_rows, direct_rows, keep, keep_next, *tables, skip_row)


def plain_forward_kernel(x_ref, keep_ref, decay_ref, gain_ref, skip_ref, pre_ref, mixed_ref, slots, state):
    @pl.when(pl.program_id(0) == 0)
    def _():
        state[...] = jnp.zeros_like(state)

    average_tile(x_ref, keep_ref[...], decay_ref, gain_ref, skip_ref, pre_ref, mixed_ref, slots, state)


def plain_backward_kernel(x_ref, pre_ref, back_ref, keep_ref, next_ref, decay_ref, gain_ref, skip_row_ref,
                          grad_ref, sums_ref, skips_ref, slots, back_slots, state, powers):
    halves, tall, _ = decay_ref.shape
    tiles = pl.num_programs(0) // 2
    index = pl.program_id(0)

    @pl.when(index == 0)
    def _():
        state[...] = jnp.zeros_like(state)
        powers[...] = jnp.zeros_like(powers)
        sums_ref[...] = jnp.zeros_like(sums_ref)
        skips_ref[...] = jnp.zeros_like(skips_ref)

    @pl.when(index < tiles)
    def _():
        weigh_tile(x_ref, pre_ref, back_ref, keep_ref[...], decay_ref, skips_ref, slots, back_tile_of(back_slots, index, tall),
                   state, powers, sums_ref.at[pl.ds(0, halves)], sums_ref.at[pl.ds(halves, halves)])

    @pl.when(index == tiles)
    def _():
        state[...] = jnp.zeros_like(state)

    @pl.when(index >= tiles)
    def _():
        adjoint_tile(next_ref[...], decay_ref, gain_ref, skip_row_ref, grad_ref, slots,
                     back_tile_of(back_slots, 2 * tiles - 1 - index, tall), state)


def gathered(part):
    return lax.all_gather(part, ("row", "chan"), axis=0)


def plain_forward(first, second, values, keep, tables, skip):
    rows, chans, length = values.shape
    half, tall, _ = tables[0].shape
    first, second = (jnp.concatenate([part.astype(jnp.bfloat16) for part in group], axis=1) for group in (first, second))
    block = pl.BlockSpec((rows, chans, LANES), lambda i: (0, 0, i))
    whole = pl.BlockSpec((half, tall, LANES), lambda i: (0, 0, 0))
    pre, mixed = pl.pallas_call(
        plain_forward_kernel,
        grid=(length // LANES,),
        in_specs=[block, pl.BlockSpec((tall, LANES), lambda i: (0, i)), whole, whole, pl.BlockSpec((chans, LANES), lambda i: (0, 0))],
        out_specs=[block, block],
        out_shape=[jax.ShapeDtypeStruct(values.shape, jnp.float32), jax.ShapeDtypeStruct(values.shape, jnp.bfloat16)],
        scratch_shapes=[pltpu.VMEM((LANES * tall, LANES), jnp.float32), pltpu.VMEM((half, tall, LANES), jnp.float32)],
    )(values, keep, *tables, jnp.broadcast_to(skip[:, None], (chans, LANES)))
    moved = [lax.all_to_all(part, "chan", split_axis=2, concat_axis=1, tiled=True) for part in (values, mixed)]
    return gathered(first), gathered(second), *moved, pre


def plain_backward(first, second, small, values, pre, mixed_rows, direct_rows, keep, keep_next, tables, skip):
    rows, chans, length = values.shape
    back, direct = [lax.all_to_all(part, "chan", split_axis=1, concat_axis=2, tiled=True) for part in (mixed_rows, direct_rows)]
    half, tall, _ = tables[0].shape
    tiles = length // LANES
    skip_row = jnp.pad(jnp.broadcast_to(skip[None], (rows, chans)), ((0, rows), (0, LANES - chans)))
    ahead = pl.BlockSpec((rows, chans, LANES), lambda i: (0, 0, jnp.minimum(i, tiles - 1)))
    behind = pl.BlockSpec((rows, chans, LANES), lambda i: (0, 0, jnp.minimum(tiles - 1, 2 * tiles - 1 - i)))
    whole = pl.BlockSpec((half, tall, LANES), lambda i: (0, 0, 0))
    grads, sums, skips = pl.pallas_call(
        plain_backward_kernel,
        grid=(2 * tiles,),
        in_specs=[ahead] * 3 + [pl.BlockSpec((tall, LANES), lambda i: (0, jnp.minimum(i, tiles - 1))),
                                pl.BlockSpec((tall, LANES), lambda i: (0, jnp.minimum(tiles - 1, 2 * tiles - 1 - i))),
                                whole, whole, pl.BlockSpec((tall, LANES), lambda i: (0, 0))],
        out_specs=[behind, pl.BlockSpec((2 * half, tall, LANES), lambda i: (0, 0, 0)), pl.BlockSpec((chans, LANES), lambda i: (0, 0))],
        out_shape=[jax.ShapeDtypeStruct(values.shape, jnp.float32), jax.ShapeDtypeStruct((2 * half, tall, LANES), jnp.float32),
                   jax.ShapeDtypeStruct((chans, LANES), jnp.float32)],
        scratch_shapes=[pltpu.VMEM((LANES * tall, LANES), jnp.float32), pltpu.VMEM((length * tall, LANES), jnp.float32)]
        + [pltpu.VMEM((half, tall, LANES), jnp.float32)] * 2,
        compiler_params=pltpu.CompilerParams(vmem_limit_bytes=ROOM),
    )(values, pre, back, keep, keep_next, *tables, skip_row)
    sums, skips, small = lax.psum((sums, skips), "row") + (lax.psum(small, ("row", "chan")),)
    owned = [
        lax.psum_scatter(part, ("row", "chan"), scatter_dimension=0, tiled=True)[0].astype(jnp.float32) for part in (*first, *second)
    ]
    return *owned, small, grads, direct, sums, skips


PIECE = 256


def over_pieces(width, body):
    for at in range(0, width, PIECE):
        body(at)


def times(left, right):
    return jnp.dot(left, right, preferred_element_type=jnp.float32)


def times_turned(left, right):
    return lax.dot_general(left, right, (((1,), (1,)), ((), ())), preferred_element_type=jnp.float32)


def turned_times(left, right):
    return lax.dot_general(left, right, (((0,), (0,)), ((), ())), preferred_element_type=jnp.float32)


def silu_and_slope(values):
    logistic = jax.nn.sigmoid(values)
    return values * logistic, logistic * (1.0 + values * (1.0 - logistic))


def normalize(values):
    center = jnp.mean(values, axis=-1, keepdims=True)
    centered = values - center
    scale = lax.rsqrt(jnp.mean(centered * centered, axis=-1, keepdims=True) + EPSILON)
    return centered * scale, scale


def normalize_back(grads, normal, scale):
    return (grads - jnp.mean(grads, axis=-1, keepdims=True) - normal * jnp.mean(grads * normal, axis=-1, keepdims=True)) * scale


def shear(table, step):
    side = table.shape[1]
    index = lax.broadcasted_iota(jnp.int32, table.shape, 0)
    bit = 1
    while bit < side:
        table = jnp.where((index // bit) % 2 == 1, pltpu.roll(table, bit if step == 1 else side - bit, axis=1), table)
        bit *= 2
    return table


def parts_of(ref, widths):
    made, offset = [], 0
    for width in widths:
        made.append(ref.at[:, pl.ds(offset, width)])
        offset += width
    return made


def token_forward_kernel(sizes, deep, *refs):
    width, shared_width, value_width, inner_width, block = sizes
    input_ref, mixed_ref, segments_ref, position_ref, first, second, biases, gain, shift, norm_gain, norm_bias = refs[:11]
    base_width = 2 * width + shared_width + value_width
    value_bias, base_bias, attn_bias, hidden_bias, output_bias = parts_of(biases, (value_width, base_width, width, inner_width, width))
    if deep:
        cotangent, token_grad = refs[11], refs[35]
        local_sem, send_sem, recv_sem = refs[40:43]
        refs = refs[12:35] + refs[36:40]
        here = Place(deep)
        moved = ToTokens(here, cotangent, token_grad, send_sem, recv_sem, local_sem.at[0])

        @pl.when(pl.program_id(0) == 0)
        def _():
            here.greet_line()
            moved.begin()
    else:
        refs = refs[11:]
    token_forward_body(sizes, input_ref, mixed_ref, segments_ref, position_ref, first, second, value_bias, base_bias, attn_bias,
                       hidden_bias, output_bias, gain, shift, norm_gain, norm_bias, *refs)
    if deep:
        @pl.when(pl.program_id(0) == pl.num_programs(0) - 1)
        def _():
            moved.arrive()
            moved.finish()


def token_forward_body(
    sizes, input_ref, mixed_ref, segments_ref, position_ref, first, second, value_bias, base_bias, attn_bias, hidden_bias, output_bias,
    gain, shift, norm_gain, norm_bias,
    layer_ref, x_rows, mixed_rows, values, value_slope, reset, reset_back, attention, queries, keys, shared, shared_slope,
    mixed_att, hidden_back, gate_back, gate, normal_one, scale_one, normed_low, activated, inner_slope, normal_two, scale_two,
    reset_slope, wide, row_values, table,
):
    width, shared_width, value_width, inner_width, block = sizes
    low = jnp.bfloat16
    base_at = value_width
    reset_at = width + shared_width
    direct_at = reset_at + value_width
    hidden_at = base_at + direct_at + width

    @pl.when(pl.program_id(0) == 0)
    def _():
        table[...] = shear(jnp.broadcast_to(position_ref[...], (block, block)), 1)

    x_float = input_ref[0].astype(jnp.float32).T
    row_values[...] = x_float
    x_rows[...] = x_float.astype(low)
    mixed_rows[...] = mixed_ref[0].astype(jnp.float32).T.astype(low)

    def value_piece(at):
        out, slope = silu_and_slope(times(x_rows[...], first[:, pl.ds(at, PIECE)]) + value_bias[:, pl.ds(at, PIECE)])
        values[:, pl.ds(at, PIECE)] = out.astype(low)
        value_slope[:, pl.ds(at, PIECE)] = slope.astype(low)

    over_pieces(value_width, value_piece)

    def base(at, size):
        return times(mixed_rows[...], first[:, pl.ds(base_at + at, size)]) + base_bias[:, pl.ds(at, size)]

    shared_value, slope = silu_and_slope(base(width, shared_width))
    shared[...] = shared_value
    shared_slope[...] = slope
    queries[...] = (shared_value * gain[0:1, :] + shift[0:1, :]).astype(low)
    keys[...] = (shared_value * gain[1:2, :] + shift[1:2, :]).astype(low)

    def reset_piece(at):
        out, slope = silu_and_slope(base(reset_at + at, PIECE))
        reset[:, pl.ds(at, PIECE)] = out.astype(low)
        wide[:, pl.ds(at, PIECE)] = out
        reset_slope[:, pl.ds(at, PIECE)] = slope

    over_pieces(value_width, reset_piece)
    for window in range(x_rows.shape[0] // block):
        rows = pl.ds(window * block, block)
        across = jnp.broadcast_to(segments_ref[0, :, pl.ds(window * block, block)], (block, block))
        earlier = lax.broadcasted_iota(jnp.int32, (block, block), 0) >= lax.broadcasted_iota(jnp.int32, (block, block), 1)
        allowed = earlier & (across == across.T)
        scores = times_turned(queries[rows, :], keys[rows, :]) * shared_width ** (-0.5) + table[...]
        scores = jnp.where(allowed, scores, MASKED)
        raised = jnp.exp(scores - jnp.max(scores, axis=-1, keepdims=True))
        weights = raised / jnp.sum(raised, axis=-1, keepdims=True)
        attention[window] = weights
        weights_low = weights.astype(low)

        def attended_piece(at):
            columns = pl.ds(at, PIECE)
            attended = times(weights_low, values[rows, columns])
            mixed_att[rows, columns] = (attended * wide[rows, columns]).astype(low)
            reset_back[rows, columns] = (attended * reset_slope[rows, columns]).astype(low)

        over_pieces(value_width, attended_piece)

    def hidden_piece(at):
        columns = pl.ds(at, PIECE)
        update = jax.nn.sigmoid(base(at, PIECE))
        pre = base(direct_at + at, PIECE) + times(mixed_att[...], second[:, columns]) + attn_bias[:, columns]
        hidden, slope = silu_and_slope(pre)
        value = row_values[:, columns]
        change = hidden - value
        gate[:, columns] = update.astype(low)
        hidden_back[:, columns] = (update * slope).astype(low)
        gate_back[:, columns] = (change * update * (1.0 - update)).astype(low)
        row_values[:, columns] = value + update * change

    over_pieces(width, hidden_piece)
    normal, scale = normalize(row_values[...])
    normal_one[...] = normal
    scale_one[...] = jnp.broadcast_to(scale, scale_one.shape)
    normed = normal * norm_gain[0:1, :] + norm_bias[0:1, :]
    normed_low[...] = normed.astype(low)
    row_values[...] = normed

    def inner_piece(at):
        columns = pl.ds(at, PIECE)
        out, slope = silu_and_slope(times(normed_low[...], first[:, pl.ds(hidden_at + at, PIECE)]) + hidden_bias[:, columns])
        activated[:, columns] = out.astype(low)
        inner_slope[:, columns] = slope.astype(low)

    over_pieces(inner_width, inner_piece)

    def outer_piece(at):
        columns = pl.ds(at, PIECE)
        row_values[:, columns] += times(activated[...], second[:, pl.ds(width + at, PIECE)]) + output_bias[:, columns]

    over_pieces(width, outer_piece)
    normal, scale = normalize(row_values[...])
    normal_two[...] = normal
    scale_two[...] = jnp.broadcast_to(scale, scale_two.shape)
    layer_ref[0] = (normal * norm_gain[1:2, :] + norm_bias[1:2, :]).T.astype(low)


def token_forward(token_input, token_mixed, segments, position, first, second, vectors, sizes, cotangent, deep):
    rows, width, span = token_input.shape
    _, shared_width, value_width, inner_width, block = sizes
    tokens = rows * span
    low, full = jnp.bfloat16, jnp.float32
    windows = span // block

    def by_rows(columns, kind):
        return jax.ShapeDtypeStruct((tokens, columns), kind), pl.BlockSpec((span, columns), lambda i: (i, 0))

    def whole(part):
        return pl.BlockSpec(part.shape, lambda i: (0,) * part.ndim, pipeline_mode=pl.Buffered(1))

    turned = pl.BlockSpec((1, width, span), lambda i: (i, 0, 0))
    tables = pl.BlockSpec((windows, block, block), lambda i: (i, 0, 0))
    outs = [
        (jax.ShapeDtypeStruct((rows, width, span), low), turned),
        by_rows(width, low), by_rows(width, low), by_rows(value_width, low), by_rows(value_width, low),
        by_rows(value_width, low), by_rows(value_width, low),
        (jax.ShapeDtypeStruct((rows * windows, block, block), full), tables),
        by_rows(shared_width, low), by_rows(shared_width, low), by_rows(shared_width, full), by_rows(shared_width, full),
        by_rows(value_width, low), by_rows(width, low), by_rows(width, low), by_rows(width, low),
        by_rows(width, full), by_rows(128, full), by_rows(width, low), by_rows(inner_width, low), by_rows(inner_width, low),
        by_rows(width, full), by_rows(128, full),
    ]
    if deep:
        outs.append((jax.ShapeDtypeStruct((rows, width, span), low), ANYWHERE))
    made = pl.pallas_call(
        partial(token_forward_kernel, sizes, deep),
        grid=(rows,),
        in_specs=[turned, turned, pl.BlockSpec((1, 1, span), lambda i: (i, 0, 0))] + [whole(part) for part in (position, first, second, *vectors)] + [ANYWHERE] * bool(deep),
        out_specs=[spec for _, spec in outs],
        out_shape=[shape for shape, _ in outs],
        scratch_shapes=[pltpu.VMEM((span, value_width), full), pltpu.VMEM((span, value_width), full), pltpu.VMEM((span, width), full),
                        pltpu.VMEM((block, block), full)] + ([dma(1), dma(2 * deep), dma(2 * deep)] if deep else []),
        compiler_params=(pltpu.CompilerParams(collective_id=3, has_side_effects=True, vmem_limit_bytes=ROOM) if deep
                         else pltpu.CompilerParams(vmem_limit_bytes=ROOM)),
        cost_estimate=pl.CostEstimate(flops=2 * tokens * (first.size + second.size), bytes_accessed=60 * 1024 * 1024, transcendentals=tokens * 8192),
    )(token_input, token_mixed, segments, position, first, second, *vectors, *([cotangent] if deep else []))
    if not deep:
        made = [*made, lax.all_to_all(cotangent, "chan", split_axis=2, concat_axis=1, tiled=True)]
    return made


def small_widths(sizes):
    width, shared_width, value_width, inner_width, block = sizes
    base_width = 2 * width + shared_width + value_width
    return (value_width, base_width, width, inner_width, width) + (shared_width,) * 4 + (width,) * 4 + (block,)


def token_backward_kernel(sizes, deep, *refs):
    if deep:
        layer_blocks, layer_out = refs[22], refs[30]
        local_sem, send_sem, recv_sem = refs[34:37]
        refs = refs[:22] + refs[23:30] + refs[31:34]
        here = Place(deep)
        moved = ToChannels(here, layer_blocks, layer_out, send_sem, recv_sem, local_sem.at[0])

        @pl.when(pl.program_id(0) == 0)
        def _():
            here.greet_line()
            moved.begin()
    token_backward_body(sizes, *refs)
    if deep:
        @pl.when(pl.program_id(0) == pl.num_programs(0) - 1)
        def _():
            moved.arrive()
            moved.finish()


def token_backward_body(
    sizes, grad_ref, first, second, gain, norm_gain,
    values, value_slope, reset, reset_back, attention, queries, keys, shared, shared_slope,
    hidden_back, gate_back, gate, normal_one, scale_one, inner_slope, normal_two, scale_two,
    mixed_out, direct_out, back_outer, back_inner, back_base, back_value,
    small, row_values, back_attended, score_sum,
):
    width, shared_width, value_width, inner_width, block = sizes
    low = jnp.bfloat16
    base_at = value_width
    reset_at = width + shared_width
    direct_at = reset_at + value_width
    base_width = direct_at + width
    hidden_at = base_at + base_width
    scale = shared_width ** (-0.5)
    (value_sum, base_sum, attn_sum, hidden_sum, output_sum, query_gain, key_gain, query_shift, key_shift,
     gain_one, gain_two, shift_one, shift_two, position_sum) = parts_of(small, small_widths(sizes))

    @pl.when(pl.program_id(0) == 0)
    def _():
        small[...] = jnp.zeros_like(small)
        score_sum[...] = jnp.zeros_like(score_sum)

    def total(part):
        return jnp.sum(part, axis=0, keepdims=True)

    grads = grad_ref[0].astype(jnp.float32).T
    normal = normal_two[...]
    gain_two[...] += total(grads * normal)
    shift_two[...] += total(grads)
    back_two = normalize_back(grads * norm_gain[1:2, :], normal, scale_two[:, :1])
    row_values[...] = back_two
    output_sum[...] += total(back_two)
    back_outer[...] = back_two.astype(low)

    def inner_piece(at):
        columns = pl.ds(at, PIECE)
        back = (times_turned(back_outer[...], second[columns, pl.ds(width, width)]) * inner_slope[:, columns].astype(jnp.float32)).astype(low)
        back_inner[:, columns] = back
        hidden_sum[:, columns] += total(back.astype(jnp.float32))

    over_pieces(inner_width, inner_piece)

    def normed_piece(at):
        columns = pl.ds(at, PIECE)
        row_values[:, columns] += times_turned(back_inner[...], first[columns, pl.ds(hidden_at, inner_width)])

    over_pieces(width, normed_piece)
    back_normed = row_values[...]
    normal = normal_one[...]
    gain_one[...] += total(back_normed * normal)
    shift_one[...] += total(back_normed)
    back_one = normalize_back(back_normed * norm_gain[0:1, :], normal, scale_one[:, :1])
    back_hidden = back_one * hidden_back[...].astype(jnp.float32)
    attn_sum[...] += total(back_hidden)
    back_base[:, direct_at:base_width] = back_hidden.astype(low)
    back_base[:, 0:width] = (back_one * gate_back[...].astype(jnp.float32)).astype(low)
    row_values[...] = back_one * (1.0 - gate[...].astype(jnp.float32))

    def mix_piece(at):
        columns = pl.ds(at, PIECE)
        back = times_turned(back_base[:, direct_at:base_width], second[columns, pl.ds(0, width)])
        back_attended[:, columns] = (back * reset[:, columns].astype(jnp.float32)).astype(low)
        back_base[:, pl.ds(reset_at + at, PIECE)] = (back * reset_back[:, columns].astype(jnp.float32)).astype(low)

    over_pieces(value_width, mix_piece)
    for window in range(grads.shape[0] // block):
        rows = pl.ds(window * block, block)
        weights = attention[window]
        back_weights = times_turned(back_attended[rows, :], values[rows, :])
        back_scores = (weights * (back_weights - jnp.sum(weights * back_weights, axis=-1, keepdims=True))).astype(low)
        score_sum[...] += back_scores.astype(jnp.float32)
        back_queries = times(back_scores, keys[rows, :]) * scale
        back_keys = turned_times(back_scores, queries[rows, :]) * scale
        shared_rows = shared[rows, :]
        query_gain[...] += total(back_queries * shared_rows)
        key_gain[...] += total(back_keys * shared_rows)
        query_shift[...] += total(back_queries)
        key_shift[...] += total(back_keys)
        back_shared = back_queries * gain[0:1, :] + back_keys * gain[1:2, :]
        back_base[rows, width:reset_at] = (back_shared * shared_slope[rows, :]).astype(low)
        weights_turned = weights.T.astype(low)

        def value_piece(at):
            columns = pl.ds(at, PIECE)
            back = times(weights_turned, back_attended[rows, columns]) * value_slope[rows, columns].astype(jnp.float32)
            back_value[rows, columns] = back.astype(low)

        over_pieces(value_width, value_piece)
    value_sum[...] += total(back_value[...].astype(jnp.float32))
    base_sum[...] += total(back_base[...].astype(jnp.float32))

    def out_piece(at):
        rows = pl.ds(at, PIECE)
        mixed_out[0, rows, :] = times_turned(first[rows, pl.ds(base_at, base_width)], back_base[...]).astype(low)
        direct_out[0, rows, :] = (times_turned(first[rows, pl.ds(0, value_width)], back_value[...]) + row_values[:, rows].T).astype(low)

    over_pieces(width, out_piece)

    @pl.when(pl.program_id(0) == pl.num_programs(0) - 1)
    def _():
        position_sum[...] = total(shear(score_sum[...], -1))


def token_backward(token_grad, first, second, gain, norm_gain, kept, sizes, layer_blocks, deep):
    rows, width, span = token_grad.shape
    _, shared_width, value_width, inner_width, block = sizes
    tokens = rows * span
    low, full = jnp.bfloat16, jnp.float32
    base_width = 2 * width + shared_width + value_width

    def by_rows(columns, kind):
        return jax.ShapeDtypeStruct((tokens, columns), kind), pl.BlockSpec((span, columns), lambda i: (i, 0))

    def whole(part):
        return pl.BlockSpec(part.shape, lambda i: (0,) * len(part.shape), pipeline_mode=pl.Buffered(1))

    def sums(*shape):
        return jax.ShapeDtypeStruct(shape, full), pl.BlockSpec(shape, lambda i: (0, 0))

    def rows_of(part):
        if part.ndim == 3:
            return pl.BlockSpec((span // block, block, block), lambda i: (i, 0, 0))
        return pl.BlockSpec((span, part.shape[1]), lambda i: (i, 0))

    turned = pl.BlockSpec((1, width, span), lambda i: (i, 0, 0))
    outs = [
        (jax.ShapeDtypeStruct((rows, width, span), low), turned), (jax.ShapeDtypeStruct((rows, width, span), low), turned),
        by_rows(width, low), by_rows(inner_width, low), by_rows(base_width, low), by_rows(value_width, low),
        sums(1, sum(small_widths(sizes))),
    ]
    if deep:
        outs.append((jax.ShapeDtypeStruct((rows, width // (2 * deep), span * 2 * deep), low), ANYWHERE))
    made = pl.pallas_call(
        partial(token_backward_kernel, sizes, deep),
        grid=(rows,),
        in_specs=[turned, whole(first), whole(second), whole(gain), whole(norm_gain)] + [rows_of(part) for part in kept] + [ANYWHERE] * bool(deep),
        out_specs=[spec for _, spec in outs],
        out_shape=[shape for shape, _ in outs],
        scratch_shapes=[pltpu.VMEM((span, width), full), pltpu.VMEM((span, value_width), low), pltpu.VMEM((block, block), full)]
        + ([dma(1), dma(2 * deep), dma(2 * deep)] if deep else []),
        compiler_params=(pltpu.CompilerParams(collective_id=4, has_side_effects=True, vmem_limit_bytes=ROOM) if deep
                         else pltpu.CompilerParams(vmem_limit_bytes=ROOM)),
        cost_estimate=pl.CostEstimate(flops=2 * tokens * (first.size + second.size), bytes_accessed=60 * 1024 * 1024, transcendentals=0),
    )(token_grad, first, second, gain, norm_gain, *kept, *([layer_blocks] if deep else []))
    if not deep:
        made = [*made, lax.all_to_all(layer_blocks, "chan", split_axis=1, concat_axis=2, tiled=True)]
    return made


def contract_rows(left, right):
    return lax.dot_general(
        left, right, (((0,), (0,)), ((), ())), preferred_element_type=jnp.float32
    )


def shards(
    inputs,
    cotangent,
    doc_lengths,
    ema_logits,
    ema_mixing,
    ema_skip,
    value_weight,
    base_weight,
    attn_weight,
    hidden_weight,
    output_weight,
    value_bias,
    base_bias,
    attn_bias,
    hidden_bias,
    output_bias,
    query_key_gain,
    query_key_shift,
    position_bias,
    norm_gain,
    norm_bias,
):
    row_count, chan_count, seq_length = inputs.shape
    group_count = lax.axis_size("chan")
    width = chan_count * group_count
    span_local = seq_length // group_count
    length_block = position_bias.shape[0]
    shared_width = query_key_gain.shape[1]
    value_width = value_bias.shape[0]
    keep, keep_next = keep_tables(doc_lengths, seq_length)
    tables = ema_tables(ema_logits, ema_mixing, row_count)
    on_four = lax.axis_size("row") == 4 and group_count == 8
    devices, deep = lax.axis_size("row") * group_count, group_count // 2
    exchange = partial(forward_exchange, devices=devices, deep=deep) if on_four else plain_forward
    first, second, token_input, token_mixed, pre_mix = exchange(
        [value_weight, base_weight, hidden_weight], [attn_weight, output_weight], inputs, keep, tables, ema_skip
    )
    first, second = first.reshape(width, -1), second.reshape(value_width, -1)
    base_width = base_bias.shape[0]
    local_pos = lax.axis_index("chan") * span_local + jnp.arange(span_local, dtype=jnp.int32)
    segments = jax.vmap(segment_ids, (0, None))(doc_lengths, local_pos).astype(jnp.float32)[:, None]
    turned_bias = jnp.roll(position_bias[::-1], 1)[None]
    sizes = (width, shared_width, value_width, hidden_bias.shape[0], length_block)
    biases = jnp.concatenate([value_bias, base_bias, attn_bias, hidden_bias, output_bias])[None]
    vectors = [biases, query_key_gain, query_key_shift, norm_gain, norm_bias]
    reach = deep if on_four else 0
    (
        layer_blocks,
        input_rows,
        mixed_rows,
        values,
        value_slope,
        reset,
        reset_back,
        attention,
        queries,
        keys,
        shared,
        shared_slope,
        mixed_att,
        hidden_back,
        gate_back,
        gate,
        normal_one,
        scale_one,
        normed_low,
        activated,
        inner_slope,
        normal_two,
        scale_two,
        token_grad,
    ) = token_forward(token_input, token_mixed, segments, turned_bias, first, second, vectors, sizes, cotangent, reach)
    kept = [values, value_slope, reset, reset_back, attention, queries, keys, shared, shared_slope]
    kept += [hidden_back, gate_back, gate, normal_one, scale_one, inner_slope, normal_two, scale_two]
    (
        back_mixed_blocks,
        back_direct_blocks,
        back_outer,
        back_inner,
        back_base,
        back_value,
        small,
        layer_out,
    ) = token_backward(token_grad, first, second, query_key_gain, norm_gain, kept, sizes, layer_blocks, reach)
    back_proj = back_base[:, base_width - width :]
    grad_output_weight = contract_rows(activated, back_outer)
    grad_hidden_weight = contract_rows(normed_low, back_inner)
    grad_attn_weight = contract_rows(mixed_att, back_proj)
    grad_value_weight = contract_rows(input_rows, back_value)
    grad_base_weight = contract_rows(mixed_rows, back_base)
    def owners(terms):
        return terms.astype(jnp.bfloat16).reshape(devices, -1, terms.shape[1])

    exchange = partial(backward_exchange, deep=deep) if on_four else plain_backward
    owner_value, owner_base, owner_hidden, owner_attn, owner_output, small, grad_ema, direct, sums, skips = exchange(
        [owners(grad_value_weight), owners(grad_base_weight), owners(grad_hidden_weight)],
        [owners(grad_attn_weight), owners(grad_output_weight)],
        small,
        inputs,
        pre_mix,
        back_mixed_blocks,
        back_direct_blocks,
        keep,
        keep_next,
        tables,
        ema_skip,
    )
    grad_inputs = grad_ema + direct.astype(jnp.float32)
    states = sums.shape[0] // 2
    grad_logits, grad_mixing, grad_skip = ema_grads(
        sums[:states], sums[states:], skips, ema_logits, ema_mixing, row_count, chan_count
    )
    offset, summed = 0, []
    for size in small_widths(sizes):
        summed.append(small[0, offset : offset + size])
        offset += size
    sum_value_bias, sum_base_bias, sum_attn_bias, sum_hidden_bias, sum_output_bias = summed[:5]
    sum_key_gain, sum_key_shift, sum_norm_gain, sum_norm_bias = (jnp.stack(summed[at : at + 2]) for at in (5, 7, 9, 11))
    sum_position = jnp.roll(summed[13][::-1], 1)
    return (
        layer_out,
        grad_inputs,
        grad_logits,
        grad_mixing,
        grad_skip,
        owner_value,
        owner_base,
        owner_attn,
        owner_hidden,
        owner_output,
        sum_value_bias,
        sum_base_bias,
        sum_attn_bias,
        sum_hidden_bias,
        sum_output_bias,
        sum_key_gain,
        sum_key_shift,
        sum_position,
        sum_norm_gain,
        sum_norm_bias,
    )


def solution(mesh):
    in_specs = (
        P("row", "chan", None),
        P("row", "chan", None),
        P("row", None),
        P(None, "chan", None),
        P(None, "chan", None),
        P("chan"),
        P(("row", "chan"), None),
        P(("row", "chan"), None),
        P(("row", "chan"), None),
        P(("row", "chan"), None),
        P(("row", "chan"), None),
        P(),
        P(),
        P(),
        P(),
        P(),
        P(),
        P(),
        P(),
        P(),
        P(),
    )
    out_specs = (
        P("row", "chan", None),
        P("row", "chan", None),
        P(None, "chan", None),
        P(None, "chan", None),
        P("chan"),
        P(("row", "chan"), None),
        P(("row", "chan"), None),
        P(("row", "chan"), None),
        P(("row", "chan"), None),
        P(("row", "chan"), None),
        P(),
        P(),
        P(),
        P(),
        P(),
        P(),
        P(),
        P(),
        P(),
        P(),
    )
    return jax.shard_map(shards, mesh=mesh, in_specs=in_specs, out_specs=out_specs, check_vma=False)
```

```python
from functools import partial

import jax
import jax.numpy as jnp
from jax import lax
from jax.experimental import pallas as pl
from jax.experimental.pallas import tpu as pltpu
from jax.sharding import PartitionSpec as P

HIGH = lax.Precision.HIGHEST
EPSILON = 1e-05
MASKED = -1e30


def segment_ids(lengths, positions):
    boundary = jnp.cumsum(lengths)
    passed = (positions[:, None] >= boundary[None, :]).astype(jnp.int32)
    return jnp.sum(passed, axis=1)


LANES = 128
STEPS = 16
MESH = pl.DeviceIdType.MESH


def pad_rows(block):
    short = LANES - block.shape[0]
    if short == 0:
        return block
    return jnp.concatenate([block, jnp.zeros((short, block.shape[1]), block.dtype)], axis=0)


def spread(block, slots, row, rows):
    turned = pad_rows(block).T
    slots[pl.ds(row, LANES, stride=2 * rows), :] = turned
    slots[pl.ds(row + rows, LANES, stride=2 * rows), :] = turned


def gather(slots, row, rows, chans):
    first = slots[pl.ds(row, LANES, stride=2 * rows), :]
    second = slots[pl.ds(row + rows, LANES, stride=2 * rows), :]
    return (first + second).T[:chans]


def tile_of(ref, tile):
    return ref.at[:, :, pl.ds(pl.multiple_of(tile * LANES, LANES), LANES)]


def lanes_of(ref, tile):
    return ref[:, pl.ds(pl.multiple_of(tile * LANES, LANES), LANES)]


def slot_at(step, tall):
    return pl.ds(pl.multiple_of(step * tall, tall), tall)


TABLE_ROWS = 40


def fill_tables(compact, decay_ref, gain_ref, skip_row_ref):
    halves, tall, _ = decay_ref.shape
    upper = lax.broadcasted_iota(jnp.int32, (tall, LANES), 0) < tall // 2
    for target, at in ((decay_ref, 0), (gain_ref, 2 * halves)):
        for n in range(halves):
            low, high = compact[at + n : at + n + 1, :], compact[at + halves + n : at + halves + n + 1, :]
            target[n] = jnp.where(upper, jnp.broadcast_to(low, (tall, LANES)), jnp.broadcast_to(high, (tall, LANES)))
    skip = compact[4 * halves : 4 * halves + 1, :]
    skip_row_ref[...] = jnp.where(upper, jnp.broadcast_to(skip, (tall, LANES)), 0.0)


def average_tile(x_tile, keep_tile, decay_ref, gain_ref, skip_row_ref, pre_tile, mixed_tile, slots, state):
    rows, chans, _ = x_tile.shape
    halves = decay_ref.shape[0]
    tall = 2 * rows
    for row in range(rows):
        spread(x_tile[row].astype(jnp.float32), slots, row, rows)

    def group(step, carry):
        keeping, states = carry
        states = list(states)
        for inner in range(STEPS):
            at = slot_at(step * STEPS + inner, tall)
            value = slots[at, :]
            keep = jnp.broadcast_to(keeping[:, inner : inner + 1], (tall, LANES))
            total = skip_row_ref[...] * value
            for n in range(halves):
                states[n] = (decay_ref[n] * keep) * states[n] + gain_ref[n] * value
                total = total + states[n]
            slots[at, :] = total
        return pltpu.roll(keeping, LANES - STEPS, axis=1), tuple(states)

    start = tuple(state[n] for n in range(halves))
    _, states = lax.fori_loop(0, LANES // STEPS, group, (keep_tile, start))
    for n in range(halves):
        state[n] = states[n]
    for row in range(rows):
        pre = gather(slots, row, rows, chans)
        if pre_tile is not None:
            pre_tile[row] = pre
        mixed_tile[row] = (pre * jax.nn.sigmoid(pre)).astype(jnp.bfloat16)


def back_tile_of(back_slots, tile, tall):
    return back_slots.at[pl.ds(pl.multiple_of(tile * (LANES * tall), LANES * tall), LANES * tall), :]


def weigh_tile(x_tile, pre_tile, back_mixed_tile, keep_tile, decay_ref, skip_sum, slots, back_tile, state, powers, weight_sum, power_sum):
    rows = x_tile.shape[0]
    halves = decay_ref.shape[0]
    tall = 2 * rows
    for row in range(rows):
        values = x_tile[row].astype(jnp.float32)
        pre = pre_tile[row]
        logistic = jax.nn.sigmoid(pre)
        back = back_mixed_tile[row].astype(jnp.float32) * (logistic * (1.0 + pre * (1.0 - logistic)))
        skip_sum[...] += back * values
        spread(values, slots, row, rows)
        spread(back, back_tile, row, rows)

    def group(step, carry):
        keeping, states, derived, weights, sums = (carry[0], *map(list, carry[1:]))
        for inner in range(STEPS):
            at = slot_at(step * STEPS + inner, tall)
            value = slots[at, :]
            back = back_tile[at, :]
            keep = jnp.broadcast_to(keeping[:, inner : inner + 1], (tall, LANES))
            for n in range(halves):
                decay = decay_ref[n] * keep
                derived[n] = decay * (derived[n] + states[n])
                states[n] = decay * states[n] + value
                weights[n] = weights[n] + back * states[n]
                sums[n] = sums[n] + back * derived[n]
        return pltpu.roll(keeping, LANES - STEPS, axis=1), tuple(states), tuple(derived), tuple(weights), tuple(sums)

    refs = (state, powers, weight_sum, power_sum)
    start = tuple(tuple(ref[n] for n in range(halves)) for ref in refs)
    out = lax.fori_loop(0, LANES // STEPS, group, (keep_tile, *start))
    for ref, values in zip(refs, out[1:]):
        for n in range(halves):
            ref[n] = values[n]


def adjoint_tile(next_tile, decay_ref, gain_ref, skip_row_ref, grad_tile, slots, back_tile, state):
    rows, chans, _ = grad_tile.shape
    halves = decay_ref.shape[0]
    tall = 2 * rows

    def group(step, carry):
        keeping, states = carry
        states = list(states)
        for inner in range(STEPS):
            at = slot_at(LANES - 1 - step * STEPS - inner, tall)
            back = back_tile[at, :]
            keep = jnp.broadcast_to(keeping[:, LANES - 1 - inner : LANES - inner], (tall, LANES))
            total = skip_row_ref[...] * back
            for n in range(halves):
                states[n] = (decay_ref[n] * keep) * states[n] + back
                total = total + gain_ref[n] * states[n]
            slots[at, :] = total
        return pltpu.roll(keeping, STEPS, axis=1), tuple(states)

    start = tuple(state[n] for n in range(halves))
    _, states = lax.fori_loop(0, LANES // STEPS, group, (next_tile, start))
    for n in range(halves):
        state[n] = states[n]
    for row in range(rows):
        grad_tile[row] = gather(slots, row, rows, chans)


class Place:
    def __init__(self, deep):
        self.deep = deep
        row, chan = lax.axis_index("row"), lax.axis_index("chan")
        self.y, self.core = row // 2, row % 2
        self.z, self.x = chan // 2, chan % 2
        self.row, self.chan = row, chan

    def owner(self, z, x, y, core):
        return (y * 2 + core) * (2 * self.deep) + z * 2 + x

    def over_core(self):
        return (self.row + 1 - 2 * self.core, self.chan)

    def over_x(self):
        return (self.row, self.chan + 1 - 2 * self.x)

    def over_y(self):
        return (self.row + 2 - 4 * self.y, self.chan)

    def at_z(self, z):
        return (self.row, z * 2 + self.x)

    def at_chan(self, step):
        chan = (self.chan + step) % (2 * self.deep)
        return chan, (self.row, chan)

    def greet(self):
        barrier = pltpu.get_barrier_semaphore()
        others = [self.over_core(), self.over_y()]
        others += [self.at_chan(step)[1] for step in range(1, 2 * self.deep)]
        for other in others:
            pl.semaphore_signal(barrier, inc=1, device_id=other, device_id_type=MESH)
        pl.semaphore_wait(barrier, len(others))

    def greet_line(self):
        barrier = pltpu.get_barrier_semaphore()
        for step in range(1, 2 * self.deep):
            pl.semaphore_signal(barrier, inc=1, device_id=self.at_chan(step)[1], device_id_type=MESH)
        pl.semaphore_wait(barrier, 2 * self.deep - 1)


def remote(source, target, send, recv, device):
    return pltpu.make_async_remote_copy(src_ref=source, dst_ref=target, send_sem=send, recv_sem=recv,
                                        device_id=device, device_id_type=MESH)


def start(copies):
    for copy in copies:
        copy.start()


class ToTokens:
    def __init__(self, here, source, target, send, recv, keep):
        self.here, self.source, self.target = here, source, target
        self.send, self.recv, self.keep = send, recv, keep
        self.chans, self.span = source.shape[1], target.shape[2]

    def block(self, chan):
        return self.source.at[:, :, pl.ds(pl.multiple_of(chan * self.span, LANES), self.span)]

    def spot(self, chan):
        return self.target.at[:, pl.ds(pl.multiple_of(chan * self.chans, 8), self.chans), :]

    def own(self):
        return pltpu.make_async_copy(self.block(self.here.chan), self.spot(self.here.chan), self.keep)

    def out(self, chan):
        return remote(self.block(chan), self.spot(self.here.chan), self.send.at[chan], self.recv.at[self.here.chan], (self.here.row, chan))

    def arrival(self, chan):
        return remote(self.block(chan), self.spot(chan), self.send.at[chan], self.recv.at[chan], (self.here.row, chan))

    def begin_same(self):
        for step in range(2, 2 * self.here.deep, 2):
            self.out(self.here.at_chan(step)[0]).start()
        self.own().start()

    def begin_cross(self):
        for step in range(1, 2 * self.here.deep, 2):
            self.out(self.here.at_chan(step)[0]).start()

    def begin(self):
        self.begin_cross()
        self.begin_same()

    def begin_one(self, chan):
        @pl.when(chan == self.here.chan)
        def _():
            self.own().start()

        @pl.when(chan != self.here.chan)
        def _():
            self.out(chan).start()

    def arrive(self):
        self.own().wait()
        for step in range(1, 2 * self.here.deep):
            self.arrival(self.here.at_chan(step)[0]).wait_recv()

    def finish(self):
        for step in range(1, 2 * self.here.deep):
            self.out(self.here.at_chan(step)[0]).wait_send()


class ToChannels(ToTokens):
    def __init__(self, here, source, target, send, recv, keep):
        super().__init__(here, source, target, send, recv, keep)
        self.chans, self.span = target.shape[1], source.shape[2]

    def block(self, chan):
        return self.source.at[:, pl.ds(pl.multiple_of(chan * self.chans, 8), self.chans), :]

    def spot(self, chan):
        return self.target.at[:, :, pl.ds(pl.multiple_of(chan * self.span, LANES), self.span)]


def forward_kernel(deep, groups, *refs):
    total = sum(groups)
    forward_body(deep, groups, refs[:total], *refs[total:])


def forward_body(deep, groups, shards_in, x_ref, keep_ref, compact_ref,
                   first_full, second_full, token_x, token_mixed, pre_ref,
                   first, second, mixed, slots, state, decay_ref, gain_ref, skip_row_ref, local_sem, send_z, send_x, send_y, send_d, send_core, recv_z, recv_x, recv_y, recv_d, recv_core,
                   a_send, a_recv, b_send, b_recv):
    count = 2
    mine, full = (first, second), (first_full, second_full)
    here = Place(deep)
    z, x, y, core = here.z, here.x, here.y, here.core
    me = here.owner(z, x, y, core)
    layers = range(deep)

    def piece(which, at, device, send, recv, source=None):
        spot = full[which].at[at]
        return remote(spot if source is None else source, spot, send, recv, device)

    def to_core(at, slot, source=False):
        return [piece(which, at, here.over_core(), send_core.at[which, slot], recv_core.at[which, slot],
                      mine[which] if source else None) for which in range(count)]

    def own_x(k, source=False):
        at = here.owner(k, x, y, core)
        return [piece(which, at, here.over_x(), send_x.at[which, k], recv_x.at[which, k],
                      mine[which] if source else None) for which in range(count)]

    def own_y(k, source=False):
        at = here.owner(k, x, y, core)
        return [piece(which, at, here.over_y(), send_y.at[which, k], recv_y.at[which, k],
                      mine[which] if source else None) for which in range(count)]

    def column(k, source=False):
        start(own_x(k, source))
        start(own_y(k, source))
        start(to_core(here.owner(k, x, y, core), k, source))

    def along(k, to, side, source=False):
        at = here.owner(k, x, y, core)
        return [piece(which, at, here.at_z(to), send_z.at[which, k, side], recv_z.at[which, k],
                      mine[which] if source else None) for which in range(count)]

    via_x = 1

    def onward_y(k):
        at = here.owner(k, 1 - x, y, core)
        return [piece(which, at, here.over_y(), send_d.at[which, k], recv_d.at[which, k]) for which in range(count)]

    def onward_x(k):
        at = here.owner(k, x, 1 - y, core)
        return [piece(which, at, here.over_x(), send_d.at[which, k], recv_d.at[which, k]) for which in range(count)]

    def wait_from(at, recv, k, device):
        for which in range(count):
            piece(which, at, device, send_x.at[which, 0], recv.at[which, k]).wait_recv()

    def sides(distance):
        return [z] if distance == 0 else [z - distance, z + distance]

    def neighbours(distance):
        for k in sides(distance):
            @pl.when((k >= 0) & (k < deep))
            def _():
                at = here.owner(k, 1 - x, y, core)
                wait_from(at, recv_x, k, here.over_x())

                @pl.when(k >= via_x)
                def _():
                    start(onward_y(k))
                start(to_core(at, deep + k))
                at = here.owner(k, x, 1 - y, core)
                wait_from(at, recv_y, k, here.over_y())

                @pl.when(k < via_x)
                def _():
                    start(onward_x(k))
                start(to_core(at, 2 * deep + k))

    def layer_step(distance):
        for side, k in enumerate(sides(distance)):
            @pl.when((k >= 0) & (k < deep))
            def _():
                to = z + 1 if side == 0 else z - 1
                wait_from(here.owner(k, x, y, core), recv_z, k, here.at_z(z))

                @pl.when((to >= 0) & (to < deep))
                def _():
                    start(along(k, to, 1 - side))
                column(k)

    at_shard = 0
    for target, size in zip(mine, groups):
        offset = 0
        for shard in shards_in[at_shard : at_shard + size]:
            target[:, pl.ds(offset, shard.shape[1])] = shard[...].astype(jnp.bfloat16)
            offset += shard.shape[1]
        at_shard += size
    here.greet()
    tokens_x = ToTokens(here, x_ref, token_x, a_send, a_recv, local_sem.at[2])
    tokens_mixed = ToTokens(here, mixed, token_mixed, b_send, b_recv, local_sem.at[3])
    local = [pltpu.make_async_copy(mine[which], full[which].at[me], local_sem.at[which]) for which in range(count)]
    start(local)
    for side, to in ((0, z - 1), (1, z + 1)):
        @pl.when((to >= 0) & (to < deep))
        def _():
            start(along(z, to, side, True))
    column(z, True)
    fill_tables(compact_ref, decay_ref, gain_ref, skip_row_ref)
    state[...] = jnp.zeros_like(state)
    tiles = x_ref.shape[2] // LANES
    each = tokens_x.span // LANES

    def tile_step(tile, carry):
        average_tile(tile_of(x_ref, tile), lanes_of(keep_ref, tile), decay_ref, gain_ref, skip_row_ref,
                     tile_of(pre_ref, tile), tile_of(mixed, tile), slots, state)

        @pl.when(tile == 5)
        def _():
            layer_step(1)

        @pl.when(tile == 8)
        def _():
            neighbours(0)

        @pl.when(tile == 12)
        def _():
            layer_step(2)

        @pl.when(tile == 15)
        def _():
            layer_step(3)
            tokens_x.begin()
        return carry

    lax.fori_loop(0, tiles, tile_step, 0)
    tokens_mixed.begin()
    neighbours(1)
    neighbours(2)
    neighbours(deep - 1)
    for k in layers:
        at = here.owner(k, 1 - x, 1 - y, core)
        wait_from(at, recv_d, k, here.over_y())
        start(to_core(at, 3 * deep + k))
    for copy in local:
        copy.wait()
    tokens_x.arrive()
    tokens_mixed.arrive()
    for slot, (flip_x, flip_y) in enumerate(((0, 0), (1, 0), (0, 1), (1, 1))):
        for k in layers:
            at = here.owner(k, x + flip_x * (1 - 2 * x), y + flip_y * (1 - 2 * y), 1 - core)
            for copy in to_core(at, slot * deep + k):
                copy.wait_recv()
                copy.wait_send()
    for k in layers:
        for copy in own_x(k) + own_y(k) + (onward_x(k) if k < via_x else onward_y(k)):
            copy.wait_send()
        for side, valid in ((0, (k >= z) & (z > 0)), (1, (k <= z) & (z < deep - 1))):
            @pl.when(valid)
            def _():
                for copy in along(k, z, side):
                    copy.wait_send()
    tokens_x.finish()
    tokens_mixed.finish()


LAYER_TIMES = ((3, 11), (0, 12), (2, 16), (1, 20))
LAYER_GAP = 4


def backward_kernel(deep, groups, *refs):
    total = sum(groups)
    sources = refs[:total]
    (small, x_ref, pre_ref, mixed_rows, direct_rows, keep_ref, next_ref, compact_ref) = refs[total : total + 8]
    refs = refs[total + 8 :]
    outs, (small_out, grad_ref, direct, sums_out, skips_out) = refs[:total], refs[total : total + 5]
    rest = refs[total + 5 :]
    held, from_core, from_d, from_x, from_y, from_z = (rest[2 * i : 2 * i + 2] for i in range(6))
    (small_sum, small_pair, small_deep, load_sem, core_send, core_recv, d_send, d_recv, x_send, x_recv, y_send, y_recv,
     z_send, z_recv, small_send, small_recv, back_mixed, slots, back_slots, state, powers, sums, sums_pair,
     skips, skips_pair,     local_sem, a_send, a_recv, b_send, b_recv, sums_send, sums_recv, decay_ref, gain_ref, skip_row_ref) = rest[12:]
    here = Place(deep)
    z, x, y, core = here.z, here.x, here.y, here.core
    rows, chans, length = x_ref.shape
    halves = decay_ref.shape[0]
    tall = 2 * rows
    tiles = length // LANES
    wide = []
    first = 0
    for which, size in enumerate(groups):
        offset = 0
        for source in sources[first : first + size]:
            wide.append((which, source, offset, source.shape[2]))
            offset += source.shape[2]
        first += size

    def begin(index, carry):
        slot = 4 * deep - 1 - index
        k, flips = slot % deep, slot // deep
        to_x = x + (flips % 2) * (1 - 2 * x)
        to_y = y + (flips // 2) * (1 - 2 * y)
        own, other = here.owner(k, to_x, to_y, core), here.owner(k, to_x, to_y, 1 - core)
        for which, source, offset, width in wide:
            pltpu.make_async_copy(source.at[own], held[which].at[slot, :, pl.ds(offset, width)], load_sem.at[which, slot]).start()
            remote(source.at[other], from_core[which].at[slot, :, pl.ds(offset, width)],
                   core_send.at[which, slot], core_recv.at[which, slot], here.over_core()).start()
        return carry

    def ready(slot):
        for which in range(2):
            spot = held[which].at[slot]
            pltpu.make_async_copy(spot, spot, load_sem.at[which, slot]).wait()
            remote(spot, from_core[which].at[slot], core_send.at[which, slot], core_recv.at[which, slot], here.over_core()).wait_recv()
            held[which][slot] = held[which][slot] + from_core[which][slot]

    via_x = 1

    def send_d(which, k):
        device = here.over_x() if k < via_x else here.over_y()
        return remote(held[which].at[3 * deep + k], from_d[which].at[k], d_send.at[which, k], d_recv.at[which, k], device)

    def send_x(which, k):
        return remote(held[which].at[deep + k], from_x[which].at[k], x_send.at[which, k], x_recv.at[which, k], here.over_x())

    def send_y(which, k):
        return remote(held[which].at[2 * deep + k], from_y[which].at[k], y_send.at[which, k], y_recv.at[which, k], here.over_y())

    def send_right(which, k):
        return remote(held[which].at[k], from_z[which].at[k], z_send.at[which, k], z_recv.at[which, k], here.at_z(z + 1))

    def send_left(which, k):
        slot = jnp.where(z - 1 == k, deep, k)
        return remote(held[which].at[k], from_z[which].at[slot], z_send.at[which, k], z_recv.at[which, slot], here.at_z(z - 1))

    def from_right(which, k, slot):
        return remote(held[which].at[k], from_z[which].at[slot], z_send.at[which, k], z_recv.at[which, slot], here.at_z(z + 1))

    def send_small(stage):
        device = (here.over_core(), here.over_y(), here.over_x())[stage]
        return remote(small_sum.at[stage], small_pair.at[stage], small_send.at[stage], small_recv.at[stage], device)

    def send_small_deep(step):
        return remote(small_deep.at[z], small_deep.at[z], small_send.at[3 + step], small_recv.at[3 + step],
                      here.at_z((z + step) % deep))

    def send_sums(stage):
        device = (here.over_core(), here.over_y())[stage]
        return [remote(sums.at[stage], sums_pair.at[stage], sums_send.at[0, stage], sums_recv.at[0, stage], device),
                remote(skips.at[stage], skips_pair.at[stage], sums_send.at[1, stage], sums_recv.at[1, stage], device)]

    def sums_step(stage):
        for copy in send_sums(stage):
            copy.wait_recv()
        sums[stage + 1] = sums[stage] + sums_pair[stage]
        skips[stage + 1] = skips[stage] + skips_pair[stage]

    here.greet()
    mixed_back = ToChannels(here, mixed_rows, back_mixed, a_send, a_recv, local_sem.at[0])
    direct_back = ToChannels(here, direct_rows, direct, b_send, b_recv, local_sem.at[1])
    mixed_back.begin()
    small_sum[0] = small[...]
    send_small(0).start()
    lax.fori_loop(0, 4 * deep, begin, 0)

    def small_step(stage):
        send_small(stage).wait_recv()
        small_sum[stage + 1] = small_sum[stage] + small_pair[stage]
        if stage < 2:
            send_small(stage + 1).start()

    def diagonal(k):
        ready(3 * deep + k)
        for which in range(2):
            send_d(which, k).start()

    def side(slot, send, k, waits):
        ready(slot * deep + k)
        for which in range(2):
            if waits:
                send_d(which, k).wait_recv()
                held[which][slot * deep + k] = held[which][slot * deep + k] + from_d[which][k]
            send(which, k).start()

    def x_side(k):
        side(1, send_x, k, k >= via_x)

    def y_side(k):
        side(2, send_y, k, k < via_x)

    diagonal(3)
    small_step(0)
    y_side(3)
    diagonal(0)
    x_side(0)
    diagonal(2)
    diagonal(1)
    small_step(1)
    direct_back.begin_same()
    x_side(3)
    y_side(0)
    y_side(2)
    x_side(2)
    y_side(1)
    for k in range(deep):
        ready(k)
    x_side(1)
    small_step(2)
    small_deep[z] = small_sum[3]
    for step in range(1, deep):
        send_small_deep(step).start()

    fill_tables(compact_ref, decay_ref, gain_ref, skip_row_ref)
    state[...] = jnp.zeros_like(state)
    powers[...] = jnp.zeros_like(powers)
    sums[0] = jnp.zeros_like(sums[0])
    skips[0] = jnp.zeros_like(skips[0])
    own_sums = sums.at[0]
    weight_sum, power_sum = own_sums.at[pl.ds(0, halves)], own_sums.at[pl.ds(halves, halves)]
    mixed_back.arrive()
    direct_back.begin_cross()

    def layer_sums(k):
        for which in range(2):
            send_x(which, k).wait_recv()
            send_y(which, k).wait_recv()
            held[which][k] = (held[which][k].astype(jnp.float32) + from_x[which][k].astype(jnp.float32)
                              + from_y[which][k].astype(jnp.float32)).astype(jnp.bfloat16)

    def layer_step(k):
        layer_sums(k)

        @pl.when(k > z)
        def _():
            for which in range(2):
                @pl.when(z > 0)
                def _():
                    send_right(which, k).wait_recv()
                    held[which][k] = held[which][k] + from_z[which][k]
                send_right(which, k).start()

        @pl.when(k < z)
        def _():
            for which in range(2):
                @pl.when(z < deep - 1)
                def _():
                    from_right(which, k, k).wait_recv()
                    held[which][k] = held[which][k] + from_z[which][k]
                send_left(which, k).start()

    def layer_steps(index):
        for k, base in LAYER_TIMES:
            hop = jnp.where(k > z, z, deep - 1 - z)

            @pl.when((index == base + LAYER_GAP * hop) & (k != z))
            def _():
                layer_step(k)

    def weigh_step(tile, carry):
        weigh_tile(tile_of(x_ref, tile), tile_of(pre_ref, tile), tile_of(back_mixed, tile), lanes_of(keep_ref, tile), decay_ref,
                   skips.at[0], slots, back_tile_of(back_slots, tile, tall), state, powers, weight_sum, power_sum)
        layer_steps(tile)
        return carry

    lax.fori_loop(0, tiles, weigh_step, 0)
    for copy in send_sums(0):
        copy.start()
    state[...] = jnp.zeros_like(state)

    def adjoint_step(step, carry):
        tile = tiles - 1 - step
        adjoint_tile(lanes_of(next_ref, tile), decay_ref, gain_ref, skip_row_ref, tile_of(grad_ref, tile),
                     slots, back_tile_of(back_slots, tile, tall), state)
        layer_steps(tiles + step)

        @pl.when(step == tiles // 2)
        def _():
            sums_step(0)
            for copy in send_sums(1):
                copy.start()
        return carry

    lax.fori_loop(0, tiles, adjoint_step, 0)
    layer_sums(z)
    sums_step(1)
    sums_out[...] = sums[2]
    skips_out[...] = skips[2]
    for which in range(2):
        @pl.when(z > 0)
        def _():
            send_right(which, z).wait_recv()

        @pl.when(z < deep - 1)
        def _():
            from_right(which, z, deep).wait_recv()
    for out, (which, _, offset, width) in zip(outs, wide):
        columns = pl.ds(offset, width)
        out[...] = held[which][z, :, columns].astype(jnp.float32)

        @pl.when(z > 0)
        def _():
            out[...] += from_z[which][z, :, columns].astype(jnp.float32)

        @pl.when(z < deep - 1)
        def _():
            out[...] += from_z[which][deep, :, columns].astype(jnp.float32)
    direct_back.arrive()
    for step in range(1, deep):
        origin = (z + deep - step) % deep
        remote(small_deep.at[origin], small_deep.at[origin], small_send.at[3 + step], small_recv.at[3 + step], here.at_z(origin)).wait_recv()
    added = small_deep[0]
    for k in range(1, deep):
        added = added + small_deep[k]
    small_out[...] = added
    for stage in range(3):
        send_small(stage).wait_send()
    for stage in range(2):
        for copy in send_sums(stage):
            copy.wait_send()
    for step in range(1, deep):
        send_small_deep(step).wait_send()
    mixed_back.finish()
    direct_back.finish()
    for which in range(2):
        for slot in range(4 * deep):
            remote(held[which].at[slot], from_core[which].at[slot], core_send.at[which, slot], core_recv.at[which, slot], here.over_core()).wait_send()
        for k in range(deep):
            send_d(which, k).wait_send()
            send_x(which, k).wait_send()
            send_y(which, k).wait_send()

            @pl.when(k > z)
            def _():
                send_right(which, k).wait_send()

            @pl.when(k < z)
            def _():
                send_left(which, k).wait_send()


def ema_parts(logits, mixing):
    damping = jax.nn.sigmoid(logits[0])
    decay = 1.0 - damping * jax.nn.sigmoid(logits[1])
    return damping, decay, damping * mixing[0]


def keep_tables(lengths, length):
    rows, count = lengths.shape
    earlier = jnp.tril(jnp.ones((count, count), jnp.int32))
    begins = jnp.sum(lengths[:, None, :] * earlier[None], axis=2)
    positions = jnp.arange(length, dtype=jnp.int32)

    def continues(at):
        hit = jnp.any(at[None, :, None] == begins[:, None, :], axis=2) | ((at == 0) | (at == length))[None]
        return jnp.tile(1.0 - hit.astype(jnp.float32), (2, 1))

    return continues(positions), continues(positions + 1)


def lane_sums(sums, rows, chans):
    count = sums.shape[0]
    return jnp.sum(sums.reshape(count, 2, rows, LANES), axis=2)[:, :, :chans].transpose(2, 1, 0).reshape(chans, 2 * count)


def ema_table(logits, mixing, skip):
    _, decay, gain = ema_parts(logits, mixing)
    rows = jnp.concatenate([decay.T, (gain * mixing[1]).T, skip[None]], axis=0)
    return jnp.pad(rows, ((0, TABLE_ROWS - rows.shape[0]), (0, LANES - rows.shape[1])))


def ema_grads(weight, power, skips, logits, mixing, rows, chans):
    damping, decay, gain = ema_parts(logits, mixing)
    weight = lane_sums(weight, rows, chans)
    back_decay = gain * mixing[1] * lane_sums(power, rows, chans) / decay
    other = jax.nn.sigmoid(logits[1])
    back_damping = weight * mixing[0] * mixing[1] - back_decay * other
    grad_logits = jnp.stack([back_damping * damping * (1.0 - damping), -back_decay * damping * other * (1.0 - other)])
    grad_mixing = jnp.stack([damping * mixing[1] * weight, gain * weight])
    return grad_logits, grad_mixing, jnp.sum(skips, axis=1)


def dma(*shape):
    return pltpu.SemaphoreType.DMA(shape)


ANYWHERE = pl.BlockSpec(memory_space=pl.ANY)
NEAR = pl.BlockSpec(memory_space=pltpu.VMEM)
ROOM = 60 * 1024 * 1024


def forward_exchange(first, second, values, keep, compact, devices, deep):
    rows, chans, length = values.shape
    shapes = [(group[0].shape[0], sum(part.shape[1] for part in group)) for group in (first, second)]
    low, full = jnp.bfloat16, jnp.float32
    half, tall = (TABLE_ROWS - 8) // 4, 2 * rows
    tokens = (rows, chans * 2 * deep, length // (2 * deep))
    table = pltpu.VMEM((half, tall, LANES), full)
    return pl.pallas_call(
        partial(forward_kernel, deep, (len(first), len(second))),
        in_specs=[NEAR] * (len(first) + len(second) + 3),
        out_specs=[ANYWHERE] * 4 + [NEAR],
        out_shape=[jax.ShapeDtypeStruct((devices,) + shape, low) for shape in shapes]
        + [jax.ShapeDtypeStruct(tokens, low), jax.ShapeDtypeStruct(tokens, low), jax.ShapeDtypeStruct(values.shape, full)],
        scratch_shapes=[pltpu.VMEM(shape, low) for shape in shapes]
        + [pltpu.VMEM(values.shape, low), pltpu.VMEM((LANES * tall, LANES), full), table, table, table, pltpu.VMEM((tall, LANES), full),
           dma(4), dma(2, deep, 2), dma(2, deep), dma(2, deep), dma(2, deep), dma(2, 4 * deep),
           dma(2, deep), dma(2, deep), dma(2, deep), dma(2, deep), dma(2, 4 * deep)] + [dma(2 * deep)] * 4,
        compiler_params=pltpu.CompilerParams(collective_id=1, has_side_effects=True, vmem_limit_bytes=ROOM),
        cost_estimate=pl.CostEstimate(flops=values.size * 160, bytes_accessed=48 * 1024 * 1024, transcendentals=values.size),
    )(*first, *second, values, keep, compact)


def backward_exchange(first, second, small, values, pre, mixed_rows, direct_rows, keep, keep_next, compact, deep):
    rows, chans, length = values.shape
    half, tall = (TABLE_ROWS - 8) // 4, 2 * rows
    shapes = [(group[0].shape[1], sum(part.shape[2] for part in group)) for group in (first, second)]
    scratch = []
    for count in (4 * deep, 4 * deep, deep, deep, deep, deep + 1):
        scratch += [pltpu.VMEM((count,) + shape, jnp.bfloat16) for shape in shapes]
    scratch += [pltpu.VMEM((4,) + small.shape, jnp.float32), pltpu.VMEM((3,) + small.shape, jnp.float32),
                pltpu.VMEM((deep,) + small.shape, jnp.float32)]
    scratch += [dma(2, 4 * deep)] * 3 + [dma(2, deep)] * 6 + [dma(2, deep), dma(2, deep + 1)] + [dma(3 + deep)] * 2
    scratch += [pltpu.VMEM(values.shape, jnp.bfloat16)]
    scratch += [pltpu.VMEM((LANES * tall, LANES), jnp.float32), pltpu.VMEM((length * tall, LANES), jnp.float32)]
    scratch += [pltpu.VMEM((half, tall, LANES), jnp.float32)] * 2
    scratch += [pltpu.VMEM((3, 2 * half, tall, LANES), jnp.float32), pltpu.VMEM((2, 2 * half, tall, LANES), jnp.float32)]
    scratch += [pltpu.VMEM((3, chans, LANES), jnp.float32), pltpu.VMEM((2, chans, LANES), jnp.float32)]
    scratch += [dma(2)] + [dma(2 * deep)] * 4 + [dma(2, 2)] * 2
    scratch += [pltpu.VMEM((half, tall, LANES), jnp.float32)] * 2 + [pltpu.VMEM((tall, LANES), jnp.float32)]
    return pl.pallas_call(
        partial(backward_kernel, deep, (len(first), len(second))),
        in_specs=[ANYWHERE] * (len(first) + len(second)) + [NEAR] * 3 + [ANYWHERE] * 2 + [NEAR] * 3,
        out_specs=[NEAR] * (len(first) + len(second) + 2) + [ANYWHERE] + [NEAR] * 2,
        out_shape=[jax.ShapeDtypeStruct(part.shape[1:], jnp.float32) for part in (*first, *second)]
        + [jax.ShapeDtypeStruct(small.shape, jnp.float32), jax.ShapeDtypeStruct(values.shape, jnp.float32),
           jax.ShapeDtypeStruct(values.shape, jnp.bfloat16),
           jax.ShapeDtypeStruct((2 * half, tall, LANES), jnp.float32), jax.ShapeDtypeStruct((chans, LANES), jnp.float32)],
        scratch_shapes=scratch,
        compiler_params=pltpu.CompilerParams(collective_id=2, has_side_effects=True, vmem_limit_bytes=ROOM),
        cost_estimate=pl.CostEstimate(flops=values.size * 240, bytes_accessed=64 * 1024 * 1024, transcendentals=values.size),
    )(*first, *second, small, values, pre, mixed_rows, direct_rows, keep, keep_next, compact)


def plain_forward_kernel(x_ref, keep_ref, compact_ref, pre_ref, mixed_ref, slots, state, decay_ref, gain_ref, skip_row_ref):
    @pl.when(pl.program_id(0) == 0)
    def _():
        state[...] = jnp.zeros_like(state)
        fill_tables(compact_ref, decay_ref, gain_ref, skip_row_ref)

    average_tile(x_ref, keep_ref[...], decay_ref, gain_ref, skip_row_ref, pre_ref, mixed_ref, slots, state)


def plain_backward_kernel(x_ref, pre_ref, back_ref, keep_ref, next_ref, compact_ref, grad_ref, sums_ref, skips_ref,
                          slots, back_slots, state, powers, decay_ref, gain_ref, skip_row_ref):
    halves, tall, _ = decay_ref.shape
    tiles = pl.num_programs(0) // 2
    index = pl.program_id(0)

    @pl.when(index == 0)
    def _():
        fill_tables(compact_ref, decay_ref, gain_ref, skip_row_ref)
        state[...] = jnp.zeros_like(state)
        powers[...] = jnp.zeros_like(powers)
        sums_ref[...] = jnp.zeros_like(sums_ref)
        skips_ref[...] = jnp.zeros_like(skips_ref)

    @pl.when(index < tiles)
    def _():
        weigh_tile(x_ref, pre_ref, back_ref, keep_ref[...], decay_ref, skips_ref, slots, back_tile_of(back_slots, index, tall),
                   state, powers, sums_ref.at[pl.ds(0, halves)], sums_ref.at[pl.ds(halves, halves)])

    @pl.when(index == tiles)
    def _():
        state[...] = jnp.zeros_like(state)

    @pl.when(index >= tiles)
    def _():
        adjoint_tile(next_ref[...], decay_ref, gain_ref, skip_row_ref, grad_ref, slots,
                     back_tile_of(back_slots, 2 * tiles - 1 - index, tall), state)


def gathered(part):
    return lax.all_gather(part, ("row", "chan"), axis=0)


def plain_forward(first, second, values, keep, compact):
    rows, chans, length = values.shape
    half, tall = (TABLE_ROWS - 8) // 4, 2 * rows
    first, second = (jnp.concatenate([part.astype(jnp.bfloat16) for part in group], axis=1) for group in (first, second))
    block = pl.BlockSpec((rows, chans, LANES), lambda i: (0, 0, i))
    table = pl.BlockSpec((TABLE_ROWS, LANES), lambda i: (0, 0))
    spread_tables = [pltpu.VMEM((half, tall, LANES), jnp.float32)] * 2 + [pltpu.VMEM((tall, LANES), jnp.float32)]
    pre, mixed = pl.pallas_call(
        plain_forward_kernel,
        grid=(length // LANES,),
        in_specs=[block, pl.BlockSpec((tall, LANES), lambda i: (0, i)), table],
        out_specs=[block, block],
        out_shape=[jax.ShapeDtypeStruct(values.shape, jnp.float32), jax.ShapeDtypeStruct(values.shape, jnp.bfloat16)],
        scratch_shapes=[pltpu.VMEM((LANES * tall, LANES), jnp.float32), pltpu.VMEM((half, tall, LANES), jnp.float32)] + spread_tables,
    )(values, keep, compact)
    moved = [lax.all_to_all(part, "chan", split_axis=2, concat_axis=1, tiled=True) for part in (values, mixed)]
    return gathered(first), gathered(second), *moved, pre


def plain_backward(first, second, small, values, pre, mixed_rows, direct_rows, keep, keep_next, compact):
    rows, chans, length = values.shape
    back, direct = [lax.all_to_all(part, "chan", split_axis=1, concat_axis=2, tiled=True) for part in (mixed_rows, direct_rows)]
    half, tall = (TABLE_ROWS - 8) // 4, 2 * rows
    tiles = length // LANES
    ahead = pl.BlockSpec((rows, chans, LANES), lambda i: (0, 0, jnp.minimum(i, tiles - 1)))
    behind = pl.BlockSpec((rows, chans, LANES), lambda i: (0, 0, jnp.minimum(tiles - 1, 2 * tiles - 1 - i)))
    table = pl.BlockSpec((TABLE_ROWS, LANES), lambda i: (0, 0))
    spread_tables = [pltpu.VMEM((half, tall, LANES), jnp.float32)] * 2 + [pltpu.VMEM((tall, LANES), jnp.float32)]
    grads, sums, skips = pl.pallas_call(
        plain_backward_kernel,
        grid=(2 * tiles,),
        in_specs=[ahead] * 3 + [pl.BlockSpec((tall, LANES), lambda i: (0, jnp.minimum(i, tiles - 1))),
                                pl.BlockSpec((tall, LANES), lambda i: (0, jnp.minimum(tiles - 1, 2 * tiles - 1 - i))),
                                table],
        out_specs=[behind, pl.BlockSpec((2 * half, tall, LANES), lambda i: (0, 0, 0)), pl.BlockSpec((chans, LANES), lambda i: (0, 0))],
        out_shape=[jax.ShapeDtypeStruct(values.shape, jnp.float32), jax.ShapeDtypeStruct((2 * half, tall, LANES), jnp.float32),
                   jax.ShapeDtypeStruct((chans, LANES), jnp.float32)],
        scratch_shapes=[pltpu.VMEM((LANES * tall, LANES), jnp.float32), pltpu.VMEM((length * tall, LANES), jnp.float32)]
        + [pltpu.VMEM((half, tall, LANES), jnp.float32)] * 2 + spread_tables,
        compiler_params=pltpu.CompilerParams(vmem_limit_bytes=ROOM),
    )(values, pre, back, keep, keep_next, compact)
    sums, skips, small = lax.psum((sums, skips), "row") + (lax.psum(small, ("row", "chan")),)
    owned = [
        lax.psum_scatter(part, ("row", "chan"), scatter_dimension=0, tiled=True)[0].astype(jnp.float32) for part in (*first, *second)
    ]
    return *owned, small, grads, direct, sums, skips


PIECE = 256


def over_pieces(width, body):
    for at in range(0, width, PIECE):
        body(at)


def times(left, right):
    return jnp.dot(left, right, preferred_element_type=jnp.float32)


def times_turned(left, right):
    return lax.dot_general(left, right, (((1,), (1,)), ((), ())), preferred_element_type=jnp.float32)


def turned_times(left, right):
    return lax.dot_general(left, right, (((0,), (0,)), ((), ())), preferred_element_type=jnp.float32)


def silu_and_slope(values):
    logistic = jax.nn.sigmoid(values)
    return values * logistic, logistic * (1.0 + values * (1.0 - logistic))


def normalize(values):
    center = jnp.mean(values, axis=-1, keepdims=True)
    centered = values - center
    scale = lax.rsqrt(jnp.mean(centered * centered, axis=-1, keepdims=True) + EPSILON)
    return centered * scale, scale


def normalize_back(grads, normal, scale):
    return (grads - jnp.mean(grads, axis=-1, keepdims=True) - normal * jnp.mean(grads * normal, axis=-1, keepdims=True)) * scale


def shear(table, step):
    side = table.shape[1]
    index = lax.broadcasted_iota(jnp.int32, table.shape, 0)
    bit = 1
    while bit < side:
        table = jnp.where((index // bit) % 2 == 1, pltpu.roll(table, bit if step == 1 else side - bit, axis=1), table)
        bit *= 2
    return table


def wait_first(load):
    @pl.when(pl.program_id(0) == 0)
    def _():
        load.wait()


def parts_of(ref, widths):
    made, offset = [], 0
    for width in widths:
        made.append(ref.at[:, pl.ds(offset, width)])
        offset += width
    return made


def token_forward_kernel(sizes, deep, *refs):
    width, shared_width, value_width, inner_width, block = sizes
    input_ref, mixed_ref, segments_ref, position_ref, first_far, second_far, biases, gain, shift, norm_gain, norm_bias = refs[:11]
    refs, (first, second, load_sem) = refs[:-3], refs[-3:]
    loads = [pltpu.make_async_copy(far, near, load_sem.at[at]) for at, (far, near) in enumerate(((first_far, first), (second_far, second)))]

    @pl.when(pl.program_id(0) == 0)
    def _():
        start(loads)

    base_width = 2 * width + shared_width + value_width
    value_bias, base_bias, attn_bias, hidden_bias, output_bias = parts_of(biases, (value_width, base_width, width, inner_width, width))
    if deep:
        cotangent, token_grad = refs[11], refs[35]
        local_sem, send_sem, recv_sem = refs[40:43]
        refs = refs[12:35] + refs[36:40]
        here = Place(deep)
        moved = ToTokens(here, cotangent, token_grad, send_sem, recv_sem, local_sem.at[0])

        @pl.when(pl.program_id(0) == 0)
        def _():
            here.greet_line()
            moved.begin()
    else:
        refs = refs[11:]
    token_forward_body(sizes, loads, input_ref, mixed_ref, segments_ref, position_ref, first, second, value_bias, base_bias, attn_bias,
                       hidden_bias, output_bias, gain, shift, norm_gain, norm_bias, *refs)
    if deep:
        @pl.when(pl.program_id(0) == pl.num_programs(0) - 1)
        def _():
            moved.arrive()
            moved.finish()


def token_forward_body(
    sizes, loads, input_ref, mixed_ref, segments_ref, position_ref, first, second, value_bias, base_bias, attn_bias, hidden_bias, output_bias,
    gain, shift, norm_gain, norm_bias,
    layer_ref, x_rows, mixed_rows, values, value_slope, reset, reset_back, attention, queries, keys, shared, shared_slope,
    mixed_att, hidden_back, gate_back, gate, normal_one, scale_one, normed_low, activated, inner_slope, normal_two, scale_two,
    reset_slope, wide, row_values, table,
):
    width, shared_width, value_width, inner_width, block = sizes
    low = jnp.bfloat16
    base_at = value_width
    reset_at = width + shared_width
    direct_at = reset_at + value_width
    hidden_at = base_at + direct_at + width

    @pl.when(pl.program_id(0) == 0)
    def _():
        table[...] = shear(jnp.broadcast_to(position_ref[...], (block, block)), 1)

    x_float = input_ref[0].astype(jnp.float32).T
    row_values[...] = x_float
    x_rows[...] = x_float.astype(low)
    mixed_rows[...] = mixed_ref[0].astype(jnp.float32).T.astype(low)

    wait_first(loads[0])

    def value_piece(at):
        out, slope = silu_and_slope(times(x_rows[...], first[:, pl.ds(at, PIECE)]) + value_bias[:, pl.ds(at, PIECE)])
        values[:, pl.ds(at, PIECE)] = out.astype(low)
        value_slope[:, pl.ds(at, PIECE)] = slope.astype(low)

    over_pieces(value_width, value_piece)

    def base(at, size):
        return times(mixed_rows[...], first[:, pl.ds(base_at + at, size)]) + base_bias[:, pl.ds(at, size)]

    shared_value, slope = silu_and_slope(base(width, shared_width))
    shared[...] = shared_value
    shared_slope[...] = slope
    queries[...] = (shared_value * gain[0:1, :] + shift[0:1, :]).astype(low)
    keys[...] = (shared_value * gain[1:2, :] + shift[1:2, :]).astype(low)

    def reset_piece(at):
        out, slope = silu_and_slope(base(reset_at + at, PIECE))
        reset[:, pl.ds(at, PIECE)] = out.astype(low)
        wide[:, pl.ds(at, PIECE)] = out
        reset_slope[:, pl.ds(at, PIECE)] = slope

    over_pieces(value_width, reset_piece)
    for window in range(x_rows.shape[0] // block):
        rows = pl.ds(window * block, block)
        across = jnp.broadcast_to(segments_ref[0, :, pl.ds(window * block, block)], (block, block))
        earlier = lax.broadcasted_iota(jnp.int32, (block, block), 0) >= lax.broadcasted_iota(jnp.int32, (block, block), 1)
        allowed = earlier & (across == across.T)
        scores = times_turned(queries[rows, :], keys[rows, :]) * shared_width ** (-0.5) + table[...]
        scores = jnp.where(allowed, scores, MASKED)
        raised = jnp.exp(scores - jnp.max(scores, axis=-1, keepdims=True))
        weights = raised / jnp.sum(raised, axis=-1, keepdims=True)
        attention[window] = weights
        weights_low = weights.astype(low)

        def attended_piece(at):
            columns = pl.ds(at, PIECE)
            attended = times(weights_low, values[rows, columns])
            mixed_att[rows, columns] = (attended * wide[rows, columns]).astype(low)
            reset_back[rows, columns] = (attended * reset_slope[rows, columns]).astype(low)

        over_pieces(value_width, attended_piece)

    wait_first(loads[1])

    def hidden_piece(at):
        columns = pl.ds(at, PIECE)
        update = jax.nn.sigmoid(base(at, PIECE))
        pre = base(direct_at + at, PIECE) + times(mixed_att[...], second[:, columns]) + attn_bias[:, columns]
        hidden, slope = silu_and_slope(pre)
        value = row_values[:, columns]
        change = hidden - value
        gate[:, columns] = update.astype(low)
        hidden_back[:, columns] = (update * slope).astype(low)
        gate_back[:, columns] = (change * update * (1.0 - update)).astype(low)
        row_values[:, columns] = value + update * change

    over_pieces(width, hidden_piece)
    normal, scale = normalize(row_values[...])
    normal_one[...] = normal
    scale_one[...] = jnp.broadcast_to(scale, scale_one.shape)
    normed = normal * norm_gain[0:1, :] + norm_bias[0:1, :]
    normed_low[...] = normed.astype(low)
    row_values[...] = normed

    def inner_piece(at):
        columns = pl.ds(at, PIECE)
        out, slope = silu_and_slope(times(normed_low[...], first[:, pl.ds(hidden_at + at, PIECE)]) + hidden_bias[:, columns])
        activated[:, columns] = out.astype(low)
        inner_slope[:, columns] = slope.astype(low)

    over_pieces(inner_width, inner_piece)

    def outer_piece(at):
        columns = pl.ds(at, PIECE)
        row_values[:, columns] += times(activated[...], second[:, pl.ds(width + at, PIECE)]) + output_bias[:, columns]

    over_pieces(width, outer_piece)
    normal, scale = normalize(row_values[...])
    normal_two[...] = normal
    scale_two[...] = jnp.broadcast_to(scale, scale_two.shape)
    layer_ref[0] = (normal * norm_gain[1:2, :] + norm_bias[1:2, :]).T.astype(low)


def token_forward(token_input, token_mixed, segments, position, first, second, vectors, sizes, cotangent, deep):
    rows, width, span = token_input.shape
    _, shared_width, value_width, inner_width, block = sizes
    tokens = rows * span
    low, full = jnp.bfloat16, jnp.float32
    windows = span // block

    def by_rows(columns, kind):
        return jax.ShapeDtypeStruct((tokens, columns), kind), pl.BlockSpec((span, columns), lambda i: (i, 0))

    def whole(part):
        return pl.BlockSpec(part.shape, lambda i: (0,) * part.ndim, pipeline_mode=pl.Buffered(1))

    turned = pl.BlockSpec((1, width, span), lambda i: (i, 0, 0))
    tables = pl.BlockSpec((windows, block, block), lambda i: (i, 0, 0))
    outs = [
        (jax.ShapeDtypeStruct((rows, width, span), low), turned),
        by_rows(width, low), by_rows(width, low), by_rows(value_width, low), by_rows(value_width, low),
        by_rows(value_width, low), by_rows(value_width, low),
        (jax.ShapeDtypeStruct((rows * windows, block, block), full), tables),
        by_rows(shared_width, low), by_rows(shared_width, low), by_rows(shared_width, full), by_rows(shared_width, full),
        by_rows(value_width, low), by_rows(width, low), by_rows(width, low), by_rows(width, low),
        by_rows(width, full), by_rows(128, full), by_rows(width, low), by_rows(inner_width, low), by_rows(inner_width, low),
        by_rows(width, full), by_rows(128, full),
    ]
    if deep:
        outs.append((jax.ShapeDtypeStruct((rows, width, span), low), ANYWHERE))
    made = pl.pallas_call(
        partial(token_forward_kernel, sizes, deep),
        grid=(rows,),
        in_specs=[turned, turned, pl.BlockSpec((1, 1, span), lambda i: (i, 0, 0))] + [whole(position), ANYWHERE, ANYWHERE] + [whole(part) for part in vectors] + [ANYWHERE] * bool(deep),
        out_specs=[spec for _, spec in outs],
        out_shape=[shape for shape, _ in outs],
        scratch_shapes=[pltpu.VMEM((span, value_width), full), pltpu.VMEM((span, value_width), full), pltpu.VMEM((span, width), full),
                        pltpu.VMEM((block, block), full)] + ([dma(1), dma(2 * deep), dma(2 * deep)] if deep else [])
        + [pltpu.VMEM(first.shape, low), pltpu.VMEM(second.shape, low), dma(2)],
        compiler_params=(pltpu.CompilerParams(collective_id=3, has_side_effects=True, vmem_limit_bytes=ROOM) if deep
                         else pltpu.CompilerParams(vmem_limit_bytes=ROOM)),
        cost_estimate=pl.CostEstimate(flops=2 * tokens * (first.size + second.size), bytes_accessed=60 * 1024 * 1024, transcendentals=tokens * 8192),
    )(token_input, token_mixed, segments, position, first, second, *vectors, *([cotangent] if deep else []))
    if not deep:
        made = [*made, lax.all_to_all(cotangent, "chan", split_axis=2, concat_axis=1, tiled=True)]
    return made


def small_widths(sizes):
    width, shared_width, value_width, inner_width, block = sizes
    base_width = 2 * width + shared_width + value_width
    return (value_width, base_width, width, inner_width, width) + (shared_width,) * 4 + (width,) * 4 + (block,)


def token_backward_kernel(sizes, deep, *refs):
    refs, (first, second, load_sem) = refs[:-3], refs[-3:]
    loads = [pltpu.make_async_copy(far, near, load_sem.at[at]) for at, (far, near) in enumerate(((refs[1], first), (refs[2], second)))]

    @pl.when(pl.program_id(0) == 0)
    def _():
        start(loads[::-1])

    refs = (refs[0], first, second) + refs[3:]
    if deep:
        layer_blocks, layer_out = refs[22], refs[30]
        local_sem, send_sem, recv_sem = refs[34:37]
        refs = refs[:22] + refs[23:30] + refs[31:34]
        here = Place(deep)
        moved = ToChannels(here, layer_blocks, layer_out, send_sem, recv_sem, local_sem.at[0])

        @pl.when(pl.program_id(0) == 0)
        def _():
            here.greet_line()
            moved.begin()
    token_backward_body(sizes, loads, *refs)
    if deep:
        @pl.when(pl.program_id(0) == pl.num_programs(0) - 1)
        def _():
            moved.arrive()
            moved.finish()


def token_backward_body(
    sizes, loads, grad_ref, first, second, gain, norm_gain,
    values, value_slope, reset, reset_back, attention, queries, keys, shared, shared_slope,
    hidden_back, gate_back, gate, normal_one, scale_one, inner_slope, normal_two, scale_two,
    mixed_out, direct_out, back_outer, back_inner, back_base, back_value,
    small, row_values, back_attended, score_sum,
):
    width, shared_width, value_width, inner_width, block = sizes
    low = jnp.bfloat16
    base_at = value_width
    reset_at = width + shared_width
    direct_at = reset_at + value_width
    base_width = direct_at + width
    hidden_at = base_at + base_width
    scale = shared_width ** (-0.5)
    (value_sum, base_sum, attn_sum, hidden_sum, output_sum, query_gain, key_gain, query_shift, key_shift,
     gain_one, gain_two, shift_one, shift_two, position_sum) = parts_of(small, small_widths(sizes))

    @pl.when(pl.program_id(0) == 0)
    def _():
        small[...] = jnp.zeros_like(small)
        score_sum[...] = jnp.zeros_like(score_sum)

    def total(part):
        return jnp.sum(part, axis=0, keepdims=True)

    grads = grad_ref[0].astype(jnp.float32).T
    normal = normal_two[...]
    gain_two[...] += total(grads * normal)
    shift_two[...] += total(grads)
    back_two = normalize_back(grads * norm_gain[1:2, :], normal, scale_two[:, :1])
    row_values[...] = back_two
    output_sum[...] += total(back_two)
    back_outer[...] = back_two.astype(low)

    wait_first(loads[1])

    def inner_piece(at):
        columns = pl.ds(at, PIECE)
        back = (times_turned(back_outer[...], second[columns, pl.ds(width, width)]) * inner_slope[:, columns].astype(jnp.float32)).astype(low)
        back_inner[:, columns] = back
        hidden_sum[:, columns] += total(back.astype(jnp.float32))

    over_pieces(inner_width, inner_piece)

    wait_first(loads[0])

    def normed_piece(at):
        columns = pl.ds(at, PIECE)
        row_values[:, columns] += times_turned(back_inner[...], first[columns, pl.ds(hidden_at, inner_width)])

    over_pieces(width, normed_piece)
    back_normed = row_values[...]
    normal = normal_one[...]
    gain_one[...] += total(back_normed * normal)
    shift_one[...] += total(back_normed)
    back_one = normalize_back(back_normed * norm_gain[0:1, :], normal, scale_one[:, :1])
    back_hidden = back_one * hidden_back[...].astype(jnp.float32)
    attn_sum[...] += total(back_hidden)
    back_base[:, direct_at:base_width] = back_hidden.astype(low)
    back_base[:, 0:width] = (back_one * gate_back[...].astype(jnp.float32)).astype(low)
    row_values[...] = back_one * (1.0 - gate[...].astype(jnp.float32))

    def mix_piece(at):
        columns = pl.ds(at, PIECE)
        back = times_turned(back_base[:, direct_at:base_width], second[columns, pl.ds(0, width)])
        back_attended[:, columns] = (back * reset[:, columns].astype(jnp.float32)).astype(low)
        back_base[:, pl.ds(reset_at + at, PIECE)] = (back * reset_back[:, columns].astype(jnp.float32)).astype(low)

    over_pieces(value_width, mix_piece)
    for window in range(grads.shape[0] // block):
        rows = pl.ds(window * block, block)
        weights = attention[window]
        back_weights = times_turned(back_attended[rows, :], values[rows, :])
        back_scores = (weights * (back_weights - jnp.sum(weights * back_weights, axis=-1, keepdims=True))).astype(low)
        score_sum[...] += back_scores.astype(jnp.float32)
        back_queries = times(back_scores, keys[rows, :]) * scale
        back_keys = turned_times(back_scores, queries[rows, :]) * scale
        shared_rows = shared[rows, :]
        query_gain[...] += total(back_queries * shared_rows)
        key_gain[...] += total(back_keys * shared_rows)
        query_shift[...] += total(back_queries)
        key_shift[...] += total(back_keys)
        back_shared = back_queries * gain[0:1, :] + back_keys * gain[1:2, :]
        back_base[rows, width:reset_at] = (back_shared * shared_slope[rows, :]).astype(low)
        weights_turned = weights.T.astype(low)

        def value_piece(at):
            columns = pl.ds(at, PIECE)
            back = times(weights_turned, back_attended[rows, columns]) * value_slope[rows, columns].astype(jnp.float32)
            back_value[rows, columns] = back.astype(low)

        over_pieces(value_width, value_piece)
    value_sum[...] += total(back_value[...].astype(jnp.float32))
    base_sum[...] += total(back_base[...].astype(jnp.float32))

    def out_piece(at):
        rows = pl.ds(at, PIECE)
        mixed_out[0, rows, :] = times_turned(first[rows, pl.ds(base_at, base_width)], back_base[...]).astype(low)
        direct_out[0, rows, :] = (times_turned(first[rows, pl.ds(0, value_width)], back_value[...]) + row_values[:, rows].T).astype(low)

    over_pieces(width, out_piece)

    @pl.when(pl.program_id(0) == pl.num_programs(0) - 1)
    def _():
        position_sum[...] = total(shear(score_sum[...], -1))


def token_backward(token_grad, first, second, gain, norm_gain, kept, sizes, layer_blocks, deep):
    rows, width, span = token_grad.shape
    _, shared_width, value_width, inner_width, block = sizes
    tokens = rows * span
    low, full = jnp.bfloat16, jnp.float32
    base_width = 2 * width + shared_width + value_width

    def by_rows(columns, kind):
        return jax.ShapeDtypeStruct((tokens, columns), kind), pl.BlockSpec((span, columns), lambda i: (i, 0))

    def whole(part):
        return pl.BlockSpec(part.shape, lambda i: (0,) * len(part.shape), pipeline_mode=pl.Buffered(1))

    def sums(*shape):
        return jax.ShapeDtypeStruct(shape, full), pl.BlockSpec(shape, lambda i: (0, 0))

    def rows_of(part):
        if part.ndim == 3:
            return pl.BlockSpec((span // block, block, block), lambda i: (i, 0, 0))
        return pl.BlockSpec((span, part.shape[1]), lambda i: (i, 0))

    turned = pl.BlockSpec((1, width, span), lambda i: (i, 0, 0))
    outs = [
        (jax.ShapeDtypeStruct((rows, width, span), low), turned), (jax.ShapeDtypeStruct((rows, width, span), low), turned),
        by_rows(width, low), by_rows(inner_width, low), by_rows(base_width, low), by_rows(value_width, low),
        sums(1, sum(small_widths(sizes))),
    ]
    if deep:
        outs.append((jax.ShapeDtypeStruct((rows, width // (2 * deep), span * 2 * deep), low), ANYWHERE))
    made = pl.pallas_call(
        partial(token_backward_kernel, sizes, deep),
        grid=(rows,),
        in_specs=[turned, ANYWHERE, ANYWHERE, whole(gain), whole(norm_gain)] + [rows_of(part) for part in kept] + [ANYWHERE] * bool(deep),
        out_specs=[spec for _, spec in outs],
        out_shape=[shape for shape, _ in outs],
        scratch_shapes=[pltpu.VMEM((span, width), full), pltpu.VMEM((span, value_width), low), pltpu.VMEM((block, block), full)]
        + ([dma(1), dma(2 * deep), dma(2 * deep)] if deep else []) + [pltpu.VMEM(first.shape, low), pltpu.VMEM(second.shape, low), dma(2)],
        compiler_params=(pltpu.CompilerParams(collective_id=4, has_side_effects=True, vmem_limit_bytes=ROOM) if deep
                         else pltpu.CompilerParams(vmem_limit_bytes=ROOM)),
        cost_estimate=pl.CostEstimate(flops=2 * tokens * (first.size + second.size), bytes_accessed=60 * 1024 * 1024, transcendentals=0),
    )(token_grad, first, second, gain, norm_gain, *kept, *([layer_blocks] if deep else []))
    if not deep:
        made = [*made, lax.all_to_all(layer_blocks, "chan", split_axis=1, concat_axis=2, tiled=True)]
    return made


def contract_rows(left, right):
    return lax.dot_general(
        left, right, (((0,), (0,)), ((), ())), preferred_element_type=jnp.float32
    )


def shards(
    inputs,
    cotangent,
    doc_lengths,
    ema_logits,
    ema_mixing,
    ema_skip,
    value_weight,
    base_weight,
    attn_weight,
    hidden_weight,
    output_weight,
    value_bias,
    base_bias,
    attn_bias,
    hidden_bias,
    output_bias,
    query_key_gain,
    query_key_shift,
    position_bias,
    norm_gain,
    norm_bias,
):
    row_count, chan_count, seq_length = inputs.shape
    group_count = lax.axis_size("chan")
    width = chan_count * group_count
    span_local = seq_length // group_count
    length_block = position_bias.shape[0]
    shared_width = query_key_gain.shape[1]
    value_width = value_bias.shape[0]
    keep, keep_next = keep_tables(doc_lengths, seq_length)
    compact = ema_table(ema_logits, ema_mixing, ema_skip)
    on_four = lax.axis_size("row") == 4 and group_count == 8
    devices, deep = lax.axis_size("row") * group_count, group_count // 2
    exchange = partial(forward_exchange, devices=devices, deep=deep) if on_four else plain_forward
    first, second, token_input, token_mixed, pre_mix = exchange(
        [value_weight, base_weight, hidden_weight], [attn_weight, output_weight], inputs, keep, compact
    )
    first, second = first.reshape(width, -1), second.reshape(value_width, -1)
    base_width = base_bias.shape[0]
    local_pos = lax.axis_index("chan") * span_local + jnp.arange(span_local, dtype=jnp.int32)
    segments = jax.vmap(segment_ids, (0, None))(doc_lengths, local_pos).astype(jnp.float32)[:, None]
    turned_bias = jnp.roll(position_bias[::-1], 1)[None]
    sizes = (width, shared_width, value_width, hidden_bias.shape[0], length_block)
    biases = jnp.concatenate([value_bias, base_bias, attn_bias, hidden_bias, output_bias])[None]
    vectors = [biases, query_key_gain, query_key_shift, norm_gain, norm_bias]
    reach = deep if on_four else 0
    (
        layer_blocks,
        input_rows,
        mixed_rows,
        values,
        value_slope,
        reset,
        reset_back,
        attention,
        queries,
        keys,
        shared,
        shared_slope,
        mixed_att,
        hidden_back,
        gate_back,
        gate,
        normal_one,
        scale_one,
        normed_low,
        activated,
        inner_slope,
        normal_two,
        scale_two,
        token_grad,
    ) = token_forward(token_input, token_mixed, segments, turned_bias, first, second, vectors, sizes, cotangent, reach)
    kept = [values, value_slope, reset, reset_back, attention, queries, keys, shared, shared_slope]
    kept += [hidden_back, gate_back, gate, normal_one, scale_one, inner_slope, normal_two, scale_two]
    (
        back_mixed_blocks,
        back_direct_blocks,
        back_outer,
        back_inner,
        back_base,
        back_value,
        small,
        layer_out,
    ) = token_backward(token_grad, first, second, query_key_gain, norm_gain, kept, sizes, layer_blocks, reach)
    back_proj = back_base[:, base_width - width :]
    grad_output_weight = contract_rows(activated, back_outer)
    grad_hidden_weight = contract_rows(normed_low, back_inner)
    grad_attn_weight = contract_rows(mixed_att, back_proj)
    grad_value_weight = contract_rows(input_rows, back_value)
    grad_base_weight = contract_rows(mixed_rows, back_base)
    def owners(terms):
        return terms.astype(jnp.bfloat16).reshape(devices, -1, terms.shape[1])

    exchange = partial(backward_exchange, deep=deep) if on_four else plain_backward
    owner_value, owner_base, owner_hidden, owner_attn, owner_output, small, grad_ema, direct, sums, skips = exchange(
        [owners(grad_value_weight), owners(grad_base_weight), owners(grad_hidden_weight)],
        [owners(grad_attn_weight), owners(grad_output_weight)],
        small,
        inputs,
        pre_mix,
        back_mixed_blocks,
        back_direct_blocks,
        keep,
        keep_next,
        compact,
    )
    grad_inputs = grad_ema + direct.astype(jnp.float32)
    states = sums.shape[0] // 2
    grad_logits, grad_mixing, grad_skip = ema_grads(
        sums[:states], sums[states:], skips, ema_logits, ema_mixing, row_count, chan_count
    )
    offset, summed = 0, []
    for count, size in ((1, value_width), (1, base_width), (1, width), (1, hidden_bias.shape[0]), (1, width),
                        (2, shared_width), (2, shared_width), (2, width), (2, width), (1, length_block)):
        part = small[0, offset : offset + count * size]
        summed.append(part if count == 1 else part.reshape(count, size))
        offset += count * size
    summed.insert(7, jnp.roll(summed.pop()[::-1], 1))
    return (
        layer_out,
        grad_inputs,
        grad_logits,
        grad_mixing,
        grad_skip,
        owner_value,
        owner_base,
        owner_attn,
        owner_hidden,
        owner_output,
        *summed,
    )


def solution(mesh):
    in_specs = (
        P("row", "chan", None),
        P("row", "chan", None),
        P("row", None),
        P(None, "chan", None),
        P(None, "chan", None),
        P("chan"),
        P(("row", "chan"), None),
        P(("row", "chan"), None),
        P(("row", "chan"), None),
        P(("row", "chan"), None),
        P(("row", "chan"), None),
        P(),
        P(),
        P(),
        P(),
        P(),
        P(),
        P(),
        P(),
        P(),
        P(),
    )
    out_specs = (
        P("row", "chan", None),
        P("row", "chan", None),
        P(None, "chan", None),
        P(None, "chan", None),
        P("chan"),
        P(("row", "chan"), None),
        P(("row", "chan"), None),
        P(("row", "chan"), None),
        P(("row", "chan"), None),
        P(("row", "chan"), None),
        P(),
        P(),
        P(),
        P(),
        P(),
        P(),
        P(),
        P(),
        P(),
        P(),
    )
    return jax.shard_map(shards, mesh=mesh, in_specs=in_specs, out_specs=out_specs, check_vma=False)
```

```python
from functools import partial

import jax
import jax.numpy as jnp
from jax import lax
from jax.experimental import pallas as pl
from jax.experimental.pallas import tpu as pltpu
from jax.sharding import PartitionSpec as P

HIGH = lax.Precision.HIGHEST
EPSILON = 1e-05
MASKED = -1e30


def segment_ids(lengths, positions):
    boundary = jnp.cumsum(lengths)
    passed = (positions[:, None] >= boundary[None, :]).astype(jnp.int32)
    return jnp.sum(passed, axis=1)


LANES = 128
STEPS = 16
MESH = pl.DeviceIdType.MESH


def pad_rows(block):
    short = LANES - block.shape[0]
    if short == 0:
        return block
    return jnp.concatenate([block, jnp.zeros((short, block.shape[1]), block.dtype)], axis=0)


def spread(block, slots, row, rows):
    turned = pad_rows(block).T
    slots[pl.ds(row, LANES, stride=2 * rows), :] = turned
    slots[pl.ds(row + rows, LANES, stride=2 * rows), :] = turned


def gather(slots, row, rows, chans):
    first = slots[pl.ds(row, LANES, stride=2 * rows), :]
    second = slots[pl.ds(row + rows, LANES, stride=2 * rows), :]
    return (first + second).T[:chans]


def tile_of(ref, tile):
    return ref.at[:, :, pl.ds(pl.multiple_of(tile * LANES, LANES), LANES)]


def lanes_of(ref, tile):
    return ref[:, pl.ds(pl.multiple_of(tile * LANES, LANES), LANES)]


def slot_at(step, tall):
    return pl.ds(pl.multiple_of(step * tall, tall), tall)


TABLE_ROWS = 40


def fill_tables(compact, decay_ref, gain_ref, skip_row_ref):
    halves, tall, _ = decay_ref.shape
    upper = lax.broadcasted_iota(jnp.int32, (tall, LANES), 0) < tall // 2
    for target, at in ((decay_ref, 0), (gain_ref, 2 * halves)):
        for n in range(halves):
            low, high = compact[at + n : at + n + 1, :], compact[at + halves + n : at + halves + n + 1, :]
            target[n] = jnp.where(upper, jnp.broadcast_to(low, (tall, LANES)), jnp.broadcast_to(high, (tall, LANES)))
    skip = compact[4 * halves : 4 * halves + 1, :]
    skip_row_ref[...] = jnp.where(upper, jnp.broadcast_to(skip, (tall, LANES)), 0.0)


def average_tile(x_tile, keep_tile, decay_ref, gain_ref, skip_row_ref, pre_tile, mixed_tile, slots, state):
    rows, chans, _ = x_tile.shape
    halves = decay_ref.shape[0]
    tall = 2 * rows
    for row in range(rows):
        spread(x_tile[row].astype(jnp.float32), slots, row, rows)

    def group(step, carry):
        keeping, states = carry
        states = list(states)
        for inner in range(STEPS):
            at = slot_at(step * STEPS + inner, tall)
            value = slots[at, :]
            keep = jnp.broadcast_to(keeping[:, inner : inner + 1], (tall, LANES))
            total = skip_row_ref[...] * value
            for n in range(halves):
                states[n] = (decay_ref[n] * keep) * states[n] + gain_ref[n] * value
                total = total + states[n]
            slots[at, :] = total
        return pltpu.roll(keeping, LANES - STEPS, axis=1), tuple(states)

    start = tuple(state[n] for n in range(halves))
    _, states = lax.fori_loop(0, LANES // STEPS, group, (keep_tile, start))
    for n in range(halves):
        state[n] = states[n]
    for row in range(rows):
        pre = gather(slots, row, rows, chans)
        if pre_tile is not None:
            pre_tile[row] = pre
        mixed_tile[row] = (pre * jax.nn.sigmoid(pre)).astype(jnp.bfloat16)


def back_tile_of(back_slots, tile, tall):
    return back_slots.at[pl.ds(pl.multiple_of(tile * (LANES * tall), LANES * tall), LANES * tall), :]


def weigh_tile(x_tile, pre_tile, back_mixed_tile, keep_tile, decay_ref, skip_sum, slots, back_tile, state, powers, weight_sum, power_sum):
    rows = x_tile.shape[0]
    halves = decay_ref.shape[0]
    tall = 2 * rows
    for row in range(rows):
        values = x_tile[row].astype(jnp.float32)
        pre = pre_tile[row]
        logistic = jax.nn.sigmoid(pre)
        back = back_mixed_tile[row].astype(jnp.float32) * (logistic * (1.0 + pre * (1.0 - logistic)))
        skip_sum[...] += back * values
        spread(values, slots, row, rows)
        spread(back, back_tile, row, rows)

    def group(step, carry):
        keeping, states, derived, weights, sums = (carry[0], *map(list, carry[1:]))
        for inner in range(STEPS):
            at = slot_at(step * STEPS + inner, tall)
            value = slots[at, :]
            back = back_tile[at, :]
            keep = jnp.broadcast_to(keeping[:, inner : inner + 1], (tall, LANES))
            for n in range(halves):
                decay = decay_ref[n] * keep
                derived[n] = decay * (derived[n] + states[n])
                states[n] = decay * states[n] + value
                weights[n] = weights[n] + back * states[n]
                sums[n] = sums[n] + back * derived[n]
        return pltpu.roll(keeping, LANES - STEPS, axis=1), tuple(states), tuple(derived), tuple(weights), tuple(sums)

    refs = (state, powers, weight_sum, power_sum)
    start = tuple(tuple(ref[n] for n in range(halves)) for ref in refs)
    out = lax.fori_loop(0, LANES // STEPS, group, (keep_tile, *start))
    for ref, values in zip(refs, out[1:]):
        for n in range(halves):
            ref[n] = values[n]


def adjoint_tile(next_tile, decay_ref, gain_ref, skip_row_ref, grad_tile, slots, back_tile, state):
    rows, chans, _ = grad_tile.shape
    halves = decay_ref.shape[0]
    tall = 2 * rows

    def group(step, carry):
        keeping, states = carry
        states = list(states)
        for inner in range(STEPS):
            at = slot_at(LANES - 1 - step * STEPS - inner, tall)
            back = back_tile[at, :]
            keep = jnp.broadcast_to(keeping[:, LANES - 1 - inner : LANES - inner], (tall, LANES))
            total = skip_row_ref[...] * back
            for n in range(halves):
                states[n] = (decay_ref[n] * keep) * states[n] + back
                total = total + gain_ref[n] * states[n]
            slots[at, :] = total
        return pltpu.roll(keeping, STEPS, axis=1), tuple(states)

    start = tuple(state[n] for n in range(halves))
    _, states = lax.fori_loop(0, LANES // STEPS, group, (next_tile, start))
    for n in range(halves):
        state[n] = states[n]
    for row in range(rows):
        grad_tile[row] = gather(slots, row, rows, chans)


class Place:
    def __init__(self, deep):
        self.deep = deep
        row, chan = lax.axis_index("row"), lax.axis_index("chan")
        self.y, self.core = row // 2, row % 2
        self.z, self.x = chan // 2, chan % 2
        self.row, self.chan = row, chan

    def owner(self, z, x, y, core):
        return (y * 2 + core) * (2 * self.deep) + z * 2 + x

    def over_core(self):
        return (self.row + 1 - 2 * self.core, self.chan)

    def over_x(self):
        return (self.row, self.chan + 1 - 2 * self.x)

    def over_y(self):
        return (self.row + 2 - 4 * self.y, self.chan)

    def at_z(self, z):
        return (self.row, z * 2 + self.x)

    def at_chan(self, step):
        chan = (self.chan + step) % (2 * self.deep)
        return chan, (self.row, chan)

    def greet(self):
        barrier = pltpu.get_barrier_semaphore()
        others = [self.over_core(), self.over_y()]
        others += [self.at_chan(step)[1] for step in range(1, 2 * self.deep)]
        for other in others:
            pl.semaphore_signal(barrier, inc=1, device_id=other, device_id_type=MESH)
        pl.semaphore_wait(barrier, len(others))

    def greet_line(self):
        barrier = pltpu.get_barrier_semaphore()
        for step in range(1, 2 * self.deep):
            pl.semaphore_signal(barrier, inc=1, device_id=self.at_chan(step)[1], device_id_type=MESH)
        pl.semaphore_wait(barrier, 2 * self.deep - 1)


def remote(source, target, send, recv, device):
    return pltpu.make_async_remote_copy(src_ref=source, dst_ref=target, send_sem=send, recv_sem=recv,
                                        device_id=device, device_id_type=MESH)


def start(copies):
    for copy in copies:
        copy.start()


class ToTokens:
    def __init__(self, here, source, target, send, recv, keep):
        self.here, self.source, self.target = here, source, target
        self.send, self.recv, self.keep = send, recv, keep
        self.chans, self.span = source.shape[1], target.shape[2]

    def block(self, chan):
        return self.source.at[:, :, pl.ds(pl.multiple_of(chan * self.span, LANES), self.span)]

    def spot(self, chan):
        return self.target.at[:, pl.ds(pl.multiple_of(chan * self.chans, 8), self.chans), :]

    def own(self):
        return pltpu.make_async_copy(self.block(self.here.chan), self.spot(self.here.chan), self.keep)

    def out(self, chan):
        return remote(self.block(chan), self.spot(self.here.chan), self.send.at[chan], self.recv.at[self.here.chan], (self.here.row, chan))

    def arrival(self, chan):
        return remote(self.block(chan), self.spot(chan), self.send.at[chan], self.recv.at[chan], (self.here.row, chan))

    def begin_same(self):
        for step in range(2, 2 * self.here.deep, 2):
            self.out(self.here.at_chan(step)[0]).start()
        self.own().start()

    def begin_cross(self):
        for step in range(1, 2 * self.here.deep, 2):
            self.out(self.here.at_chan(step)[0]).start()

    def begin(self):
        self.begin_cross()
        self.begin_same()

    def begin_one(self, chan):
        @pl.when(chan == self.here.chan)
        def _():
            self.own().start()

        @pl.when(chan != self.here.chan)
        def _():
            self.out(chan).start()

    def arrive(self):
        self.own().wait()
        for step in range(1, 2 * self.here.deep):
            self.arrival(self.here.at_chan(step)[0]).wait_recv()

    def finish(self):
        for step in range(1, 2 * self.here.deep):
            self.out(self.here.at_chan(step)[0]).wait_send()


class ToChannels(ToTokens):
    def __init__(self, here, source, target, send, recv, keep):
        super().__init__(here, source, target, send, recv, keep)
        self.chans, self.span = target.shape[1], source.shape[2]

    def block(self, chan):
        return self.source.at[:, pl.ds(pl.multiple_of(chan * self.chans, 8), self.chans), :]

    def spot(self, chan):
        return self.target.at[:, :, pl.ds(pl.multiple_of(chan * self.span, LANES), self.span)]


def forward_kernel(deep, groups, *refs):
    total = sum(groups)
    forward_body(deep, groups, refs[:total], *refs[total:])


def forward_body(deep, groups, shards_in, x_ref, keep_ref, compact_ref,
                   first_full, second_full, token_x, token_mixed, pre_ref,
                   first, second, mixed, slots, state, decay_ref, gain_ref, skip_row_ref, local_sem, send_z, send_x, send_y, send_d, send_core, recv_z, recv_x, recv_y, recv_d, recv_core,
                   a_send, a_recv, b_send, b_recv):
    count = 2
    mine, full = (first, second), (first_full, second_full)
    here = Place(deep)
    z, x, y, core = here.z, here.x, here.y, here.core
    me = here.owner(z, x, y, core)
    layers = range(deep)

    def piece(which, at, device, send, recv, source=None):
        spot = full[which].at[at]
        return remote(spot if source is None else source, spot, send, recv, device)

    def to_core(at, slot, source=False):
        return [piece(which, at, here.over_core(), send_core.at[which, slot], recv_core.at[which, slot],
                      mine[which] if source else None) for which in range(count)]

    def own_x(k, source=False):
        at = here.owner(k, x, y, core)
        return [piece(which, at, here.over_x(), send_x.at[which, k], recv_x.at[which, k],
                      mine[which] if source else None) for which in range(count)]

    def own_y(k, source=False):
        at = here.owner(k, x, y, core)
        return [piece(which, at, here.over_y(), send_y.at[which, k], recv_y.at[which, k],
                      mine[which] if source else None) for which in range(count)]

    def column(k, source=False):
        start(own_x(k, source))
        start(own_y(k, source))
        start(to_core(here.owner(k, x, y, core), k, source))

    def along(k, to, side, source=False):
        at = here.owner(k, x, y, core)
        return [piece(which, at, here.at_z(to), send_z.at[which, k, side], recv_z.at[which, k],
                      mine[which] if source else None) for which in range(count)]

    via_x = 1

    def onward_y(k):
        at = here.owner(k, 1 - x, y, core)
        return [piece(which, at, here.over_y(), send_d.at[which, k], recv_d.at[which, k]) for which in range(count)]

    def onward_x(k):
        at = here.owner(k, x, 1 - y, core)
        return [piece(which, at, here.over_x(), send_d.at[which, k], recv_d.at[which, k]) for which in range(count)]

    def wait_from(at, recv, k, device):
        for which in range(count):
            piece(which, at, device, send_x.at[which, 0], recv.at[which, k]).wait_recv()

    def sides(distance):
        return [z] if distance == 0 else [z - distance, z + distance]

    def neighbours(distance):
        for k in sides(distance):
            @pl.when((k >= 0) & (k < deep))
            def _():
                at = here.owner(k, 1 - x, y, core)
                wait_from(at, recv_x, k, here.over_x())

                @pl.when(k >= via_x)
                def _():
                    start(onward_y(k))
                start(to_core(at, deep + k))
                at = here.owner(k, x, 1 - y, core)
                wait_from(at, recv_y, k, here.over_y())

                @pl.when(k < via_x)
                def _():
                    start(onward_x(k))
                start(to_core(at, 2 * deep + k))

    def layer_step(distance):
        for side, k in enumerate(sides(distance)):
            @pl.when((k >= 0) & (k < deep))
            def _():
                to = z + 1 if side == 0 else z - 1
                wait_from(here.owner(k, x, y, core), recv_z, k, here.at_z(z))

                @pl.when((to >= 0) & (to < deep))
                def _():
                    start(along(k, to, 1 - side))
                column(k)

    at_shard = 0
    for target, size in zip(mine, groups):
        offset = 0
        for shard in shards_in[at_shard : at_shard + size]:
            target[:, pl.ds(offset, shard.shape[1])] = shard[...].astype(jnp.bfloat16)
            offset += shard.shape[1]
        at_shard += size
    here.greet()
    tokens_x = ToTokens(here, x_ref, token_x, a_send, a_recv, local_sem.at[2])
    tokens_mixed = ToTokens(here, mixed, token_mixed, b_send, b_recv, local_sem.at[3])
    local = [pltpu.make_async_copy(mine[which], full[which].at[me], local_sem.at[which]) for which in range(count)]
    start(local)
    for side, to in ((0, z - 1), (1, z + 1)):
        @pl.when((to >= 0) & (to < deep))
        def _():
            start(along(z, to, side, True))
    column(z, True)
    fill_tables(compact_ref, decay_ref, gain_ref, skip_row_ref)
    state[...] = jnp.zeros_like(state)
    tiles = x_ref.shape[2] // LANES
    each = tokens_x.span // LANES

    def tile_step(tile, carry):
        average_tile(tile_of(x_ref, tile), lanes_of(keep_ref, tile), decay_ref, gain_ref, skip_row_ref,
                     tile_of(pre_ref, tile), tile_of(mixed, tile), slots, state)

        @pl.when(tile == 5)
        def _():
            layer_step(1)

        @pl.when(tile == 8)
        def _():
            neighbours(0)

        @pl.when(tile == 12)
        def _():
            layer_step(2)

        @pl.when(tile == 15)
        def _():
            layer_step(3)
            tokens_x.begin()
        return carry

    lax.fori_loop(0, tiles, tile_step, 0)
    tokens_mixed.begin()
    neighbours(1)
    neighbours(2)
    neighbours(deep - 1)
    for k in layers:
        at = here.owner(k, 1 - x, 1 - y, core)
        wait_from(at, recv_d, k, here.over_y())
        start(to_core(at, 3 * deep + k))
    for copy in local:
        copy.wait()
    tokens_x.arrive()
    tokens_mixed.arrive()
    for slot, (flip_x, flip_y) in enumerate(((0, 0), (1, 0), (0, 1), (1, 1))):
        for k in layers:
            at = here.owner(k, x + flip_x * (1 - 2 * x), y + flip_y * (1 - 2 * y), 1 - core)
            for copy in to_core(at, slot * deep + k):
                copy.wait_recv()
                copy.wait_send()
    for k in layers:
        for copy in own_x(k) + own_y(k) + (onward_x(k) if k < via_x else onward_y(k)):
            copy.wait_send()
        for side, valid in ((0, (k >= z) & (z > 0)), (1, (k <= z) & (z < deep - 1))):
            @pl.when(valid)
            def _():
                for copy in along(k, z, side):
                    copy.wait_send()
    tokens_x.finish()
    tokens_mixed.finish()


LAYER_TIMES = ((3, 11), (0, 12), (2, 16), (1, 20))
LAYER_GAP = 4


def backward_kernel(deep, groups, *refs):
    total = sum(groups)
    sources = refs[:total]
    (small, x_ref, pre_ref, mixed_rows, direct_rows, keep_ref, next_ref, compact_ref) = refs[total : total + 8]
    refs = refs[total + 8 :]
    outs, (small_out, grad_ref, direct, sums_out, skips_out) = refs[:total], refs[total : total + 5]
    rest = refs[total + 5 :]
    held, from_core, from_d, from_x, from_y, from_z = (rest[2 * i : 2 * i + 2] for i in range(6))
    (small_sum, small_pair, small_deep, load_sem, core_send, core_recv, d_send, d_recv, x_send, x_recv, y_send, y_recv,
     z_send, z_recv, small_send, small_recv, back_mixed, slots, back_slots, state, powers, sums, sums_pair,
     skips, skips_pair,     local_sem, a_send, a_recv, b_send, b_recv, sums_send, sums_recv, decay_ref, gain_ref, skip_row_ref) = rest[12:]
    here = Place(deep)
    z, x, y, core = here.z, here.x, here.y, here.core
    rows, chans, length = x_ref.shape
    halves = decay_ref.shape[0]
    tall = 2 * rows
    tiles = length // LANES
    wide = []
    first = 0
    for which, size in enumerate(groups):
        offset = 0
        for source in sources[first : first + size]:
            wide.append((which, source, offset, source.shape[2]))
            offset += source.shape[2]
        first += size

    def begin(index, carry):
        slot = 4 * deep - 1 - index
        k, flips = slot % deep, slot // deep
        to_x = x + (flips % 2) * (1 - 2 * x)
        to_y = y + (flips // 2) * (1 - 2 * y)
        own, other = here.owner(k, to_x, to_y, core), here.owner(k, to_x, to_y, 1 - core)
        for which, source, offset, width in wide:
            pltpu.make_async_copy(source.at[own], held[which].at[slot, :, pl.ds(offset, width)], load_sem.at[which, slot]).start()
            remote(source.at[other], from_core[which].at[slot, :, pl.ds(offset, width)],
                   core_send.at[which, slot], core_recv.at[which, slot], here.over_core()).start()
        return carry

    def ready(slot):
        for which in range(2):
            spot = held[which].at[slot]
            pltpu.make_async_copy(spot, spot, load_sem.at[which, slot]).wait()
            remote(spot, from_core[which].at[slot], core_send.at[which, slot], core_recv.at[which, slot], here.over_core()).wait_recv()
            held[which][slot] = held[which][slot] + from_core[which][slot]

    via_x = 1

    def send_d(which, k):
        device = here.over_x() if k < via_x else here.over_y()
        return remote(held[which].at[3 * deep + k], from_d[which].at[k], d_send.at[which, k], d_recv.at[which, k], device)

    def send_x(which, k):
        return remote(held[which].at[deep + k], from_x[which].at[k], x_send.at[which, k], x_recv.at[which, k], here.over_x())

    def send_y(which, k):
        return remote(held[which].at[2 * deep + k], from_y[which].at[k], y_send.at[which, k], y_recv.at[which, k], here.over_y())

    def send_right(which, k):
        return remote(held[which].at[k], from_z[which].at[k], z_send.at[which, k], z_recv.at[which, k], here.at_z(z + 1))

    def send_left(which, k):
        slot = jnp.where(z - 1 == k, deep, k)
        return remote(held[which].at[k], from_z[which].at[slot], z_send.at[which, k], z_recv.at[which, slot], here.at_z(z - 1))

    def from_right(which, k, slot):
        return remote(held[which].at[k], from_z[which].at[slot], z_send.at[which, k], z_recv.at[which, slot], here.at_z(z + 1))

    def send_small(stage):
        device = (here.over_core(), here.over_y(), here.over_x())[stage]
        return remote(small_sum.at[stage], small_pair.at[stage], small_send.at[stage], small_recv.at[stage], device)

    def send_small_deep(step):
        return remote(small_deep.at[z], small_deep.at[z], small_send.at[3 + step], small_recv.at[3 + step],
                      here.at_z((z + step) % deep))

    def send_sums(stage):
        device = (here.over_core(), here.over_y())[stage]
        return [remote(sums.at[stage], sums_pair.at[stage], sums_send.at[0, stage], sums_recv.at[0, stage], device),
                remote(skips.at[stage], skips_pair.at[stage], sums_send.at[1, stage], sums_recv.at[1, stage], device)]

    def sums_step(stage):
        for copy in send_sums(stage):
            copy.wait_recv()
        sums[stage + 1] = sums[stage] + sums_pair[stage]
        skips[stage + 1] = skips[stage] + skips_pair[stage]

    here.greet()
    mixed_back = ToChannels(here, mixed_rows, back_mixed, a_send, a_recv, local_sem.at[0])
    direct_back = ToChannels(here, direct_rows, direct, b_send, b_recv, local_sem.at[1])
    mixed_back.begin()
    small_sum[0] = small[...]
    send_small(0).start()
    lax.fori_loop(0, 4 * deep, begin, 0)

    def small_step(stage):
        send_small(stage).wait_recv()
        small_sum[stage + 1] = small_sum[stage] + small_pair[stage]
        if stage < 2:
            send_small(stage + 1).start()

    def diagonal(k):
        ready(3 * deep + k)
        for which in range(2):
            send_d(which, k).start()

    def side(slot, send, k, waits):
        ready(slot * deep + k)
        for which in range(2):
            if waits:
                send_d(which, k).wait_recv()
                held[which][slot * deep + k] = held[which][slot * deep + k] + from_d[which][k]
            send(which, k).start()

    def x_side(k):
        side(1, send_x, k, k >= via_x)

    def y_side(k):
        side(2, send_y, k, k < via_x)

    diagonal(3)
    small_step(0)
    y_side(3)
    diagonal(0)
    x_side(0)
    diagonal(2)
    diagonal(1)
    small_step(1)
    direct_back.begin_same()
    x_side(3)
    y_side(0)
    y_side(2)
    x_side(2)
    y_side(1)
    for k in range(deep):
        ready(k)
    x_side(1)
    small_step(2)
    small_deep[z] = small_sum[3]
    for step in range(1, deep):
        send_small_deep(step).start()

    fill_tables(compact_ref, decay_ref, gain_ref, skip_row_ref)
    state[...] = jnp.zeros_like(state)
    powers[...] = jnp.zeros_like(powers)
    sums[0] = jnp.zeros_like(sums[0])
    skips[0] = jnp.zeros_like(skips[0])
    own_sums = sums.at[0]
    weight_sum, power_sum = own_sums.at[pl.ds(0, halves)], own_sums.at[pl.ds(halves, halves)]
    mixed_back.arrive()
    direct_back.begin_cross()

    def layer_sums(k):
        for which in range(2):
            send_x(which, k).wait_recv()
            send_y(which, k).wait_recv()
            held[which][k] = (held[which][k].astype(jnp.float32) + from_x[which][k].astype(jnp.float32)
                              + from_y[which][k].astype(jnp.float32)).astype(jnp.bfloat16)

    def layer_step(k):
        layer_sums(k)

        @pl.when(k > z)
        def _():
            for which in range(2):
                @pl.when(z > 0)
                def _():
                    send_right(which, k).wait_recv()
                    held[which][k] = held[which][k] + from_z[which][k]
                send_right(which, k).start()

        @pl.when(k < z)
        def _():
            for which in range(2):
                @pl.when(z < deep - 1)
                def _():
                    from_right(which, k, k).wait_recv()
                    held[which][k] = held[which][k] + from_z[which][k]
                send_left(which, k).start()

    def layer_steps(index):
        for k, base in LAYER_TIMES:
            hop = jnp.where(k > z, z, deep - 1 - z)

            @pl.when((index == base + LAYER_GAP * hop) & (k != z))
            def _():
                layer_step(k)

    def weigh_step(tile, carry):
        weigh_tile(tile_of(x_ref, tile), tile_of(pre_ref, tile), tile_of(back_mixed, tile), lanes_of(keep_ref, tile), decay_ref,
                   skips.at[0], slots, back_tile_of(back_slots, tile, tall), state, powers, weight_sum, power_sum)
        layer_steps(tile)
        return carry

    lax.fori_loop(0, tiles, weigh_step, 0)
    for copy in send_sums(0):
        copy.start()
    state[...] = jnp.zeros_like(state)

    def adjoint_step(step, carry):
        tile = tiles - 1 - step
        adjoint_tile(lanes_of(next_ref, tile), decay_ref, gain_ref, skip_row_ref, tile_of(grad_ref, tile),
                     slots, back_tile_of(back_slots, tile, tall), state)
        layer_steps(tiles + step)

        @pl.when(step == tiles // 2)
        def _():
            sums_step(0)
            for copy in send_sums(1):
                copy.start()
        return carry

    lax.fori_loop(0, tiles, adjoint_step, 0)
    layer_sums(z)
    sums_step(1)
    sums_out[...] = sums[2]
    skips_out[...] = skips[2]
    for which in range(2):
        @pl.when(z > 0)
        def _():
            send_right(which, z).wait_recv()

        @pl.when(z < deep - 1)
        def _():
            from_right(which, z, deep).wait_recv()
    for out, (which, _, offset, width) in zip(outs, wide):
        columns = pl.ds(offset, width)
        out[...] = held[which][z, :, columns].astype(jnp.float32)

        @pl.when(z > 0)
        def _():
            out[...] += from_z[which][z, :, columns].astype(jnp.float32)

        @pl.when(z < deep - 1)
        def _():
            out[...] += from_z[which][deep, :, columns].astype(jnp.float32)
    direct_back.arrive()
    for step in range(1, deep):
        origin = (z + deep - step) % deep
        remote(small_deep.at[origin], small_deep.at[origin], small_send.at[3 + step], small_recv.at[3 + step], here.at_z(origin)).wait_recv()
    added = small_deep[0]
    for k in range(1, deep):
        added = added + small_deep[k]
    small_out[...] = added
    for stage in range(3):
        send_small(stage).wait_send()
    for stage in range(2):
        for copy in send_sums(stage):
            copy.wait_send()
    for step in range(1, deep):
        send_small_deep(step).wait_send()
    mixed_back.finish()
    direct_back.finish()
    for which in range(2):
        for slot in range(4 * deep):
            remote(held[which].at[slot], from_core[which].at[slot], core_send.at[which, slot], core_recv.at[which, slot], here.over_core()).wait_send()
        for k in range(deep):
            send_d(which, k).wait_send()
            send_x(which, k).wait_send()
            send_y(which, k).wait_send()

            @pl.when(k > z)
            def _():
                send_right(which, k).wait_send()

            @pl.when(k < z)
            def _():
                send_left(which, k).wait_send()


def ema_parts(logits, mixing):
    damping = jax.nn.sigmoid(logits[0])
    decay = 1.0 - damping * jax.nn.sigmoid(logits[1])
    return damping, decay, damping * mixing[0]


def keep_tables(lengths, length):
    rows, count = lengths.shape
    earlier = jnp.tril(jnp.ones((count, count), jnp.int32))
    begins = jnp.sum(lengths[:, None, :] * earlier[None], axis=2)
    positions = jnp.arange(length, dtype=jnp.int32)

    def continues(at):
        hit = jnp.any(at[None, :, None] == begins[:, None, :], axis=2) | ((at == 0) | (at == length))[None]
        return jnp.tile(1.0 - hit.astype(jnp.float32), (2, 1))

    return continues(positions), continues(positions + 1)


def lane_sums(sums, rows, chans):
    count = sums.shape[0]
    return jnp.sum(sums.reshape(count, 2, rows, LANES), axis=2)[:, :, :chans].transpose(2, 1, 0).reshape(chans, 2 * count)


def ema_table(logits, mixing, skip):
    _, decay, gain = ema_parts(logits, mixing)
    rows = jnp.concatenate([decay.T, (gain * mixing[1]).T, skip[None]], axis=0)
    return jnp.pad(rows, ((0, TABLE_ROWS - rows.shape[0]), (0, LANES - rows.shape[1])))


def ema_grads(weight, power, skips, logits, mixing, rows, chans):
    damping, decay, gain = ema_parts(logits, mixing)
    weight = lane_sums(weight, rows, chans)
    back_decay = gain * mixing[1] * lane_sums(power, rows, chans) / decay
    other = jax.nn.sigmoid(logits[1])
    back_damping = weight * mixing[0] * mixing[1] - back_decay * other
    grad_logits = jnp.stack([back_damping * damping * (1.0 - damping), -back_decay * damping * other * (1.0 - other)])
    grad_mixing = jnp.stack([damping * mixing[1] * weight, gain * weight])
    return grad_logits, grad_mixing, jnp.sum(skips, axis=1)


def dma(*shape):
    return pltpu.SemaphoreType.DMA(shape)


ANYWHERE = pl.BlockSpec(memory_space=pl.ANY)
NEAR = pl.BlockSpec(memory_space=pltpu.VMEM)
ROOM = 60 * 1024 * 1024


def forward_exchange(first, second, values, keep, compact, devices, deep):
    rows, chans, length = values.shape
    shapes = [(group[0].shape[0], sum(part.shape[1] for part in group)) for group in (first, second)]
    low, full = jnp.bfloat16, jnp.float32
    half, tall = (TABLE_ROWS - 8) // 4, 2 * rows
    tokens = (rows, chans * 2 * deep, length // (2 * deep))
    table = pltpu.VMEM((half, tall, LANES), full)
    return pl.pallas_call(
        partial(forward_kernel, deep, (len(first), len(second))),
        in_specs=[NEAR] * (len(first) + len(second) + 3),
        out_specs=[ANYWHERE] * 4 + [NEAR],
        out_shape=[jax.ShapeDtypeStruct((devices,) + shape, low) for shape in shapes]
        + [jax.ShapeDtypeStruct(tokens, low), jax.ShapeDtypeStruct(tokens, low), jax.ShapeDtypeStruct(values.shape, full)],
        scratch_shapes=[pltpu.VMEM(shape, low) for shape in shapes]
        + [pltpu.VMEM(values.shape, low), pltpu.VMEM((LANES * tall, LANES), full), table, table, table, pltpu.VMEM((tall, LANES), full),
           dma(4), dma(2, deep, 2), dma(2, deep), dma(2, deep), dma(2, deep), dma(2, 4 * deep),
           dma(2, deep), dma(2, deep), dma(2, deep), dma(2, deep), dma(2, 4 * deep)] + [dma(2 * deep)] * 4,
        compiler_params=pltpu.CompilerParams(collective_id=1, has_side_effects=True, vmem_limit_bytes=ROOM),
        cost_estimate=pl.CostEstimate(flops=values.size * 160, bytes_accessed=48 * 1024 * 1024, transcendentals=values.size),
    )(*first, *second, values, keep, compact)


def backward_exchange(first, second, small, values, pre, mixed_rows, direct_rows, keep, keep_next, compact, deep):
    rows, chans, length = values.shape
    half, tall = (TABLE_ROWS - 8) // 4, 2 * rows
    shapes = [(group[0].shape[1], sum(part.shape[2] for part in group)) for group in (first, second)]
    scratch = []
    for count in (4 * deep, 4 * deep, deep, deep, deep, deep + 1):
        scratch += [pltpu.VMEM((count,) + shape, jnp.bfloat16) for shape in shapes]
    scratch += [pltpu.VMEM((4,) + small.shape, jnp.float32), pltpu.VMEM((3,) + small.shape, jnp.float32),
                pltpu.VMEM((deep,) + small.shape, jnp.float32)]
    scratch += [dma(2, 4 * deep)] * 3 + [dma(2, deep)] * 6 + [dma(2, deep), dma(2, deep + 1)] + [dma(3 + deep)] * 2
    scratch += [pltpu.VMEM(values.shape, jnp.bfloat16)]
    scratch += [pltpu.VMEM((LANES * tall, LANES), jnp.float32), pltpu.VMEM((length * tall, LANES), jnp.float32)]
    scratch += [pltpu.VMEM((half, tall, LANES), jnp.float32)] * 2
    scratch += [pltpu.VMEM((3, 2 * half, tall, LANES), jnp.float32), pltpu.VMEM((2, 2 * half, tall, LANES), jnp.float32)]
    scratch += [pltpu.VMEM((3, chans, LANES), jnp.float32), pltpu.VMEM((2, chans, LANES), jnp.float32)]
    scratch += [dma(2)] + [dma(2 * deep)] * 4 + [dma(2, 2)] * 2
    scratch += [pltpu.VMEM((half, tall, LANES), jnp.float32)] * 2 + [pltpu.VMEM((tall, LANES), jnp.float32)]
    return pl.pallas_call(
        partial(backward_kernel, deep, (len(first), len(second))),
        in_specs=[ANYWHERE] * (len(first) + len(second)) + [NEAR] * 3 + [ANYWHERE] * 2 + [NEAR] * 3,
        out_specs=[NEAR] * (len(first) + len(second) + 2) + [ANYWHERE] + [NEAR] * 2,
        out_shape=[jax.ShapeDtypeStruct(part.shape[1:], jnp.float32) for part in (*first, *second)]
        + [jax.ShapeDtypeStruct(small.shape, jnp.float32), jax.ShapeDtypeStruct(values.shape, jnp.float32),
           jax.ShapeDtypeStruct(values.shape, jnp.bfloat16),
           jax.ShapeDtypeStruct((2 * half, tall, LANES), jnp.float32), jax.ShapeDtypeStruct((chans, LANES), jnp.float32)],
        scratch_shapes=scratch,
        compiler_params=pltpu.CompilerParams(collective_id=2, has_side_effects=True, vmem_limit_bytes=ROOM),
        cost_estimate=pl.CostEstimate(flops=values.size * 240, bytes_accessed=64 * 1024 * 1024, transcendentals=values.size),
    )(*first, *second, small, values, pre, mixed_rows, direct_rows, keep, keep_next, compact)


def plain_forward_kernel(x_ref, keep_ref, compact_ref, pre_ref, mixed_ref, slots, state, decay_ref, gain_ref, skip_row_ref):
    @pl.when(pl.program_id(0) == 0)
    def _():
        state[...] = jnp.zeros_like(state)
        fill_tables(compact_ref, decay_ref, gain_ref, skip_row_ref)

    average_tile(x_ref, keep_ref[...], decay_ref, gain_ref, skip_row_ref, pre_ref, mixed_ref, slots, state)


def plain_backward_kernel(x_ref, pre_ref, back_ref, keep_ref, next_ref, compact_ref, grad_ref, sums_ref, skips_ref,
                          slots, back_slots, state, powers, decay_ref, gain_ref, skip_row_ref):
    halves, tall, _ = decay_ref.shape
    tiles = pl.num_programs(0) // 2
    index = pl.program_id(0)

    @pl.when(index == 0)
    def _():
        fill_tables(compact_ref, decay_ref, gain_ref, skip_row_ref)
        state[...] = jnp.zeros_like(state)
        powers[...] = jnp.zeros_like(powers)
        sums_ref[...] = jnp.zeros_like(sums_ref)
        skips_ref[...] = jnp.zeros_like(skips_ref)

    @pl.when(index < tiles)
    def _():
        weigh_tile(x_ref, pre_ref, back_ref, keep_ref[...], decay_ref, skips_ref, slots, back_tile_of(back_slots, index, tall),
                   state, powers, sums_ref.at[pl.ds(0, halves)], sums_ref.at[pl.ds(halves, halves)])

    @pl.when(index == tiles)
    def _():
        state[...] = jnp.zeros_like(state)

    @pl.when(index >= tiles)
    def _():
        adjoint_tile(next_ref[...], decay_ref, gain_ref, skip_row_ref, grad_ref, slots,
                     back_tile_of(back_slots, 2 * tiles - 1 - index, tall), state)


def gathered(part):
    return lax.all_gather(part, ("row", "chan"), axis=0)


def plain_forward(first, second, values, keep, compact):
    rows, chans, length = values.shape
    half, tall = (TABLE_ROWS - 8) // 4, 2 * rows
    first, second = (jnp.concatenate([part.astype(jnp.bfloat16) for part in group], axis=1) for group in (first, second))
    block = pl.BlockSpec((rows, chans, LANES), lambda i: (0, 0, i))
    table = pl.BlockSpec((TABLE_ROWS, LANES), lambda i: (0, 0))
    spread_tables = [pltpu.VMEM((half, tall, LANES), jnp.float32)] * 2 + [pltpu.VMEM((tall, LANES), jnp.float32)]
    pre, mixed = pl.pallas_call(
        plain_forward_kernel,
        grid=(length // LANES,),
        in_specs=[block, pl.BlockSpec((tall, LANES), lambda i: (0, i)), table],
        out_specs=[block, block],
        out_shape=[jax.ShapeDtypeStruct(values.shape, jnp.float32), jax.ShapeDtypeStruct(values.shape, jnp.bfloat16)],
        scratch_shapes=[pltpu.VMEM((LANES * tall, LANES), jnp.float32), pltpu.VMEM((half, tall, LANES), jnp.float32)] + spread_tables,
    )(values, keep, compact)
    moved = [lax.all_to_all(part, "chan", split_axis=2, concat_axis=1, tiled=True) for part in (values, mixed)]
    return gathered(first), gathered(second), *moved, pre


def plain_backward(first, second, small, values, pre, mixed_rows, direct_rows, keep, keep_next, compact):
    rows, chans, length = values.shape
    back, direct = [lax.all_to_all(part, "chan", split_axis=1, concat_axis=2, tiled=True) for part in (mixed_rows, direct_rows)]
    half, tall = (TABLE_ROWS - 8) // 4, 2 * rows
    tiles = length // LANES
    ahead = pl.BlockSpec((rows, chans, LANES), lambda i: (0, 0, jnp.minimum(i, tiles - 1)))
    behind = pl.BlockSpec((rows, chans, LANES), lambda i: (0, 0, jnp.minimum(tiles - 1, 2 * tiles - 1 - i)))
    table = pl.BlockSpec((TABLE_ROWS, LANES), lambda i: (0, 0))
    spread_tables = [pltpu.VMEM((half, tall, LANES), jnp.float32)] * 2 + [pltpu.VMEM((tall, LANES), jnp.float32)]
    grads, sums, skips = pl.pallas_call(
        plain_backward_kernel,
        grid=(2 * tiles,),
        in_specs=[ahead] * 3 + [pl.BlockSpec((tall, LANES), lambda i: (0, jnp.minimum(i, tiles - 1))),
                                pl.BlockSpec((tall, LANES), lambda i: (0, jnp.minimum(tiles - 1, 2 * tiles - 1 - i))),
                                table],
        out_specs=[behind, pl.BlockSpec((2 * half, tall, LANES), lambda i: (0, 0, 0)), pl.BlockSpec((chans, LANES), lambda i: (0, 0))],
        out_shape=[jax.ShapeDtypeStruct(values.shape, jnp.float32), jax.ShapeDtypeStruct((2 * half, tall, LANES), jnp.float32),
                   jax.ShapeDtypeStruct((chans, LANES), jnp.float32)],
        scratch_shapes=[pltpu.VMEM((LANES * tall, LANES), jnp.float32), pltpu.VMEM((length * tall, LANES), jnp.float32)]
        + [pltpu.VMEM((half, tall, LANES), jnp.float32)] * 2 + spread_tables,
        compiler_params=pltpu.CompilerParams(vmem_limit_bytes=ROOM),
    )(values, pre, back, keep, keep_next, compact)
    sums, skips, small = lax.psum((sums, skips), "row") + (lax.psum(small, ("row", "chan")),)
    owned = [
        lax.psum_scatter(part, ("row", "chan"), scatter_dimension=0, tiled=True)[0].astype(jnp.float32) for part in (*first, *second)
    ]
    return *owned, small, grads, direct, sums, skips


PIECE = 256


def over_pieces(width, body):
    for at in range(0, width, PIECE):
        body(at)


def times(left, right):
    return jnp.dot(left, right, preferred_element_type=jnp.float32)


def times_turned(left, right):
    return lax.dot_general(left, right, (((1,), (1,)), ((), ())), preferred_element_type=jnp.float32)


def turned_times(left, right):
    return lax.dot_general(left, right, (((0,), (0,)), ((), ())), preferred_element_type=jnp.float32)


def silu_and_slope(values):
    logistic = jax.nn.sigmoid(values)
    return values * logistic, logistic * (1.0 + values * (1.0 - logistic))


def normalize(values):
    center = jnp.mean(values, axis=-1, keepdims=True)
    centered = values - center
    scale = lax.rsqrt(jnp.mean(centered * centered, axis=-1, keepdims=True) + EPSILON)
    return centered * scale, scale


def normalize_back(grads, normal, scale):
    return (grads - jnp.mean(grads, axis=-1, keepdims=True) - normal * jnp.mean(grads * normal, axis=-1, keepdims=True)) * scale


def shear(table, step):
    side = table.shape[1]
    index = lax.broadcasted_iota(jnp.int32, table.shape, 0)
    bit = 1
    while bit < side:
        table = jnp.where((index // bit) % 2 == 1, pltpu.roll(table, bit if step == 1 else side - bit, axis=1), table)
        bit *= 2
    return table


def row_of(ref, at, size):
    return ref[pl.ds(at, size)].reshape(1, size)


def wait_first(load):
    @pl.when(pl.program_id(0) == 0)
    def _():
        load.wait()


def parts_of(ref, widths):
    made, offset = [], 0
    for width in widths:
        made.append(ref.at[:, pl.ds(offset, width)])
        offset += width
    return made


def token_forward_kernel(sizes, deep, *refs):
    width, shared_width, value_width, inner_width, block = sizes
    input_ref, mixed_ref, segments_ref, position_ref, first_far, second_far = refs[:6]
    value_bias, base_bias, attn_bias, hidden_bias, output_bias, gain, shift, norm_gain, norm_bias = refs[6:15]
    refs = refs[4:]
    refs, (first, second, load_sem) = refs[:-3], refs[-3:]
    loads = [pltpu.make_async_copy(far, near, load_sem.at[at]) for at, (far, near) in enumerate(((first_far, first), (second_far, second)))]

    @pl.when(pl.program_id(0) == 0)
    def _():
        start(loads)
    if deep:
        cotangent, token_grad = refs[11], refs[35]
        local_sem, send_sem, recv_sem = refs[40:43]
        refs = refs[12:35] + refs[36:40]
        here = Place(deep)
        moved = ToTokens(here, cotangent, token_grad, send_sem, recv_sem, local_sem.at[0])

        @pl.when(pl.program_id(0) == 0)
        def _():
            here.greet_line()
            moved.begin()
    else:
        refs = refs[11:]
    token_forward_body(sizes, loads, input_ref, mixed_ref, segments_ref, position_ref, first, second, value_bias, base_bias, attn_bias,
                       hidden_bias, output_bias, gain, shift, norm_gain, norm_bias, *refs)
    if deep:
        @pl.when(pl.program_id(0) == pl.num_programs(0) - 1)
        def _():
            moved.arrive()
            moved.finish()


def token_forward_body(
    sizes, loads, input_ref, mixed_ref, segments_ref, position_ref, first, second, value_bias, base_bias, attn_bias, hidden_bias, output_bias,
    gain, shift, norm_gain, norm_bias,
    layer_ref, x_rows, mixed_rows, values, value_slope, reset, reset_back, attention, queries, keys, shared, shared_slope,
    mixed_att, hidden_back, gate_back, gate, normal_one, scale_one, normed_low, activated, inner_slope, normal_two, scale_two,
    reset_slope, wide, row_values, table,
):
    width, shared_width, value_width, inner_width, block = sizes
    low = jnp.bfloat16
    base_at = value_width
    reset_at = width + shared_width
    direct_at = reset_at + value_width
    hidden_at = base_at + direct_at + width

    @pl.when(pl.program_id(0) == 0)
    def _():
        table[...] = shear(jnp.broadcast_to(position_ref[...], (block, block)), 1)

    x_float = input_ref[0].astype(jnp.float32).T
    row_values[...] = x_float
    x_rows[...] = x_float.astype(low)
    mixed_rows[...] = mixed_ref[0].astype(jnp.float32).T.astype(low)

    wait_first(loads[0])

    def value_piece(at):
        out, slope = silu_and_slope(times(x_rows[...], first[:, pl.ds(at, PIECE)]) + row_of(value_bias, at, PIECE))
        values[:, pl.ds(at, PIECE)] = out.astype(low)
        value_slope[:, pl.ds(at, PIECE)] = slope.astype(low)

    over_pieces(value_width, value_piece)

    def base(at, size):
        return times(mixed_rows[...], first[:, pl.ds(base_at + at, size)]) + row_of(base_bias, at, size)

    shared_value, slope = silu_and_slope(base(width, shared_width))
    shared[...] = shared_value
    shared_slope[...] = slope
    queries[...] = (shared_value * gain[0:1, :] + shift[0:1, :]).astype(low)
    keys[...] = (shared_value * gain[1:2, :] + shift[1:2, :]).astype(low)

    def reset_piece(at):
        out, slope = silu_and_slope(base(reset_at + at, PIECE))
        reset[:, pl.ds(at, PIECE)] = out.astype(low)
        wide[:, pl.ds(at, PIECE)] = out
        reset_slope[:, pl.ds(at, PIECE)] = slope

    over_pieces(value_width, reset_piece)
    for window in range(x_rows.shape[0] // block):
        rows = pl.ds(window * block, block)
        across = jnp.broadcast_to(segments_ref[0, :, pl.ds(window * block, block)], (block, block))
        earlier = lax.broadcasted_iota(jnp.int32, (block, block), 0) >= lax.broadcasted_iota(jnp.int32, (block, block), 1)
        allowed = earlier & (across == across.T)
        scores = times_turned(queries[rows, :], keys[rows, :]) * shared_width ** (-0.5) + table[...]
        scores = jnp.where(allowed, scores, MASKED)
        raised = jnp.exp(scores - jnp.max(scores, axis=-1, keepdims=True))
        weights = raised / jnp.sum(raised, axis=-1, keepdims=True)
        attention[window] = weights
        weights_low = weights.astype(low)

        def attended_piece(at):
            columns = pl.ds(at, PIECE)
            attended = times(weights_low, values[rows, columns])
            mixed_att[rows, columns] = (attended * wide[rows, columns]).astype(low)
            reset_back[rows, columns] = (attended * reset_slope[rows, columns]).astype(low)

        over_pieces(value_width, attended_piece)

    wait_first(loads[1])

    def hidden_piece(at):
        columns = pl.ds(at, PIECE)
        update = jax.nn.sigmoid(base(at, PIECE))
        pre = base(direct_at + at, PIECE) + times(mixed_att[...], second[:, columns]) + row_of(attn_bias, at, PIECE)
        hidden, slope = silu_and_slope(pre)
        value = row_values[:, columns]
        change = hidden - value
        gate[:, columns] = update.astype(low)
        hidden_back[:, columns] = (update * slope).astype(low)
        gate_back[:, columns] = (change * update * (1.0 - update)).astype(low)
        row_values[:, columns] = value + update * change

    over_pieces(width, hidden_piece)
    normal, scale = normalize(row_values[...])
    normal_one[...] = normal
    scale_one[...] = jnp.broadcast_to(scale, scale_one.shape)
    normed = normal * norm_gain[0:1, :] + norm_bias[0:1, :]
    normed_low[...] = normed.astype(low)
    row_values[...] = normed

    def inner_piece(at):
        columns = pl.ds(at, PIECE)
        out, slope = silu_and_slope(times(normed_low[...], first[:, pl.ds(hidden_at + at, PIECE)]) + row_of(hidden_bias, at, PIECE))
        activated[:, columns] = out.astype(low)
        inner_slope[:, columns] = slope.astype(low)

    over_pieces(inner_width, inner_piece)

    def outer_piece(at):
        columns = pl.ds(at, PIECE)
        row_values[:, columns] += times(activated[...], second[:, pl.ds(width + at, PIECE)]) + row_of(output_bias, at, PIECE)

    over_pieces(width, outer_piece)
    normal, scale = normalize(row_values[...])
    normal_two[...] = normal
    scale_two[...] = jnp.broadcast_to(scale, scale_two.shape)
    layer_ref[0] = (normal * norm_gain[1:2, :] + norm_bias[1:2, :]).T.astype(low)


def token_forward(token_input, token_mixed, segments, position, first, second, vectors, sizes, cotangent, deep):
    rows, width, span = token_input.shape
    _, shared_width, value_width, inner_width, block = sizes
    tokens = rows * span
    low, full = jnp.bfloat16, jnp.float32
    windows = span // block

    def by_rows(columns, kind):
        return jax.ShapeDtypeStruct((tokens, columns), kind), pl.BlockSpec((span, columns), lambda i: (i, 0))

    def whole(part):
        return pl.BlockSpec(part.shape, lambda i: (0,) * part.ndim, pipeline_mode=pl.Buffered(1))

    turned = pl.BlockSpec((1, width, span), lambda i: (i, 0, 0))
    tables = pl.BlockSpec((windows, block, block), lambda i: (i, 0, 0))
    outs = [
        (jax.ShapeDtypeStruct((rows, width, span), low), turned),
        by_rows(width, low), by_rows(width, low), by_rows(value_width, low), by_rows(value_width, low),
        by_rows(value_width, low), by_rows(value_width, low),
        (jax.ShapeDtypeStruct((rows * windows, block, block), full), tables),
        by_rows(shared_width, low), by_rows(shared_width, low), by_rows(shared_width, full), by_rows(shared_width, full),
        by_rows(value_width, low), by_rows(width, low), by_rows(width, low), by_rows(width, low),
        by_rows(width, full), by_rows(128, full), by_rows(width, low), by_rows(inner_width, low), by_rows(inner_width, low),
        by_rows(width, full), by_rows(128, full),
    ]
    if deep:
        outs.append((jax.ShapeDtypeStruct((rows, width, span), low), ANYWHERE))
    made = pl.pallas_call(
        partial(token_forward_kernel, sizes, deep),
        grid=(rows,),
        in_specs=[turned, turned, pl.BlockSpec((1, 1, span), lambda i: (i, 0, 0))] + [whole(position), ANYWHERE, ANYWHERE] + [whole(part) for part in vectors] + [ANYWHERE] * bool(deep),
        out_specs=[spec for _, spec in outs],
        out_shape=[shape for shape, _ in outs],
        scratch_shapes=[pltpu.VMEM((span, value_width), full), pltpu.VMEM((span, value_width), full), pltpu.VMEM((span, width), full),
                        pltpu.VMEM((block, block), full)] + ([dma(1), dma(2 * deep), dma(2 * deep)] if deep else [])
        + [pltpu.VMEM(first.shape, low), pltpu.VMEM(second.shape, low), dma(2)],
        compiler_params=(pltpu.CompilerParams(collective_id=3, has_side_effects=True, vmem_limit_bytes=ROOM) if deep
                         else pltpu.CompilerParams(vmem_limit_bytes=ROOM)),
        cost_estimate=pl.CostEstimate(flops=2 * tokens * (first.size + second.size), bytes_accessed=60 * 1024 * 1024, transcendentals=tokens * 8192),
    )(token_input, token_mixed, segments, position, first, second, *vectors, *([cotangent] if deep else []))
    if not deep:
        made = [*made, lax.all_to_all(cotangent, "chan", split_axis=2, concat_axis=1, tiled=True)]
    return made


def small_widths(sizes):
    width, shared_width, value_width, inner_width, block = sizes
    base_width = 2 * width + shared_width + value_width
    return (value_width, base_width, width, inner_width, width) + (shared_width,) * 4 + (width,) * 4 + (block,)


def token_backward_kernel(sizes, deep, *refs):
    refs, (first, second, load_sem) = refs[:-3], refs[-3:]
    loads = [pltpu.make_async_copy(far, near, load_sem.at[at]) for at, (far, near) in enumerate(((refs[1], first), (refs[2], second)))]

    @pl.when(pl.program_id(0) == 0)
    def _():
        start(loads[::-1])

    refs = (refs[0], first, second) + refs[3:]
    if deep:
        layer_blocks, layer_out = refs[22], refs[30]
        local_sem, send_sem, recv_sem = refs[34:37]
        refs = refs[:22] + refs[23:30] + refs[31:34]
        here = Place(deep)
        moved = ToChannels(here, layer_blocks, layer_out, send_sem, recv_sem, local_sem.at[0])

        @pl.when(pl.program_id(0) == 0)
        def _():
            here.greet_line()
            moved.begin()
    token_backward_body(sizes, loads, *refs)
    if deep:
        @pl.when(pl.program_id(0) == pl.num_programs(0) - 1)
        def _():
            moved.arrive()
            moved.finish()


def token_backward_body(
    sizes, loads, grad_ref, first, second, gain, norm_gain,
    values, value_slope, reset, reset_back, attention, queries, keys, shared, shared_slope,
    hidden_back, gate_back, gate, normal_one, scale_one, inner_slope, normal_two, scale_two,
    mixed_out, direct_out, back_outer, back_inner, back_base, back_value,
    small, row_values, back_attended, score_sum,
):
    width, shared_width, value_width, inner_width, block = sizes
    low = jnp.bfloat16
    base_at = value_width
    reset_at = width + shared_width
    direct_at = reset_at + value_width
    base_width = direct_at + width
    hidden_at = base_at + base_width
    scale = shared_width ** (-0.5)
    (value_sum, base_sum, attn_sum, hidden_sum, output_sum, query_gain, key_gain, query_shift, key_shift,
     gain_one, gain_two, shift_one, shift_two, position_sum) = parts_of(small, small_widths(sizes))

    @pl.when(pl.program_id(0) == 0)
    def _():
        small[...] = jnp.zeros_like(small)
        score_sum[...] = jnp.zeros_like(score_sum)

    def total(part):
        return jnp.sum(part, axis=0, keepdims=True)

    grads = grad_ref[0].astype(jnp.float32).T
    normal = normal_two[...]
    gain_two[...] += total(grads * normal)
    shift_two[...] += total(grads)
    back_two = normalize_back(grads * norm_gain[1:2, :], normal, scale_two[:, :1])
    row_values[...] = back_two
    output_sum[...] += total(back_two)
    back_outer[...] = back_two.astype(low)

    wait_first(loads[1])

    def inner_piece(at):
        columns = pl.ds(at, PIECE)
        back = (times_turned(back_outer[...], second[columns, pl.ds(width, width)]) * inner_slope[:, columns].astype(jnp.float32)).astype(low)
        back_inner[:, columns] = back
        hidden_sum[:, columns] += total(back.astype(jnp.float32))

    over_pieces(inner_width, inner_piece)

    wait_first(loads[0])

    def normed_piece(at):
        columns = pl.ds(at, PIECE)
        row_values[:, columns] += times_turned(back_inner[...], first[columns, pl.ds(hidden_at, inner_width)])

    over_pieces(width, normed_piece)
    back_normed = row_values[...]
    normal = normal_one[...]
    gain_one[...] += total(back_normed * normal)
    shift_one[...] += total(back_normed)
    back_one = normalize_back(back_normed * norm_gain[0:1, :], normal, scale_one[:, :1])
    back_hidden = back_one * hidden_back[...].astype(jnp.float32)
    attn_sum[...] += total(back_hidden)
    back_base[:, direct_at:base_width] = back_hidden.astype(low)
    back_base[:, 0:width] = (back_one * gate_back[...].astype(jnp.float32)).astype(low)
    row_values[...] = back_one * (1.0 - gate[...].astype(jnp.float32))

    def mix_piece(at):
        columns = pl.ds(at, PIECE)
        back = times_turned(back_base[:, direct_at:base_width], second[columns, pl.ds(0, width)])
        back_attended[:, columns] = (back * reset[:, columns].astype(jnp.float32)).astype(low)
        back_base[:, pl.ds(reset_at + at, PIECE)] = (back * reset_back[:, columns].astype(jnp.float32)).astype(low)

    over_pieces(value_width, mix_piece)
    for window in range(grads.shape[0] // block):
        rows = pl.ds(window * block, block)
        weights = attention[window]
        back_weights = times_turned(back_attended[rows, :], values[rows, :])
        back_scores = (weights * (back_weights - jnp.sum(weights * back_weights, axis=-1, keepdims=True))).astype(low)
        score_sum[...] += back_scores.astype(jnp.float32)
        back_queries = times(back_scores, keys[rows, :]) * scale
        back_keys = turned_times(back_scores, queries[rows, :]) * scale
        shared_rows = shared[rows, :]
        query_gain[...] += total(back_queries * shared_rows)
        key_gain[...] += total(back_keys * shared_rows)
        query_shift[...] += total(back_queries)
        key_shift[...] += total(back_keys)
        back_shared = back_queries * gain[0:1, :] + back_keys * gain[1:2, :]
        back_base[rows, width:reset_at] = (back_shared * shared_slope[rows, :]).astype(low)
        weights_turned = weights.T.astype(low)

        def value_piece(at):
            columns = pl.ds(at, PIECE)
            back = times(weights_turned, back_attended[rows, columns]) * value_slope[rows, columns].astype(jnp.float32)
            back_value[rows, columns] = back.astype(low)

        over_pieces(value_width, value_piece)
    value_sum[...] += total(back_value[...].astype(jnp.float32))
    base_sum[...] += total(back_base[...].astype(jnp.float32))

    def out_piece(at):
        rows = pl.ds(at, PIECE)
        mixed_out[0, rows, :] = times_turned(first[rows, pl.ds(base_at, base_width)], back_base[...]).astype(low)
        direct_out[0, rows, :] = (times_turned(first[rows, pl.ds(0, value_width)], back_value[...]) + row_values[:, rows].T).astype(low)

    over_pieces(width, out_piece)

    @pl.when(pl.program_id(0) == pl.num_programs(0) - 1)
    def _():
        position_sum[...] = total(shear(score_sum[...], -1))


def token_backward(token_grad, first, second, gain, norm_gain, kept, sizes, layer_blocks, deep):
    rows, width, span = token_grad.shape
    _, shared_width, value_width, inner_width, block = sizes
    tokens = rows * span
    low, full = jnp.bfloat16, jnp.float32
    base_width = 2 * width + shared_width + value_width

    def by_rows(columns, kind):
        return jax.ShapeDtypeStruct((tokens, columns), kind), pl.BlockSpec((span, columns), lambda i: (i, 0))

    def whole(part):
        return pl.BlockSpec(part.shape, lambda i: (0,) * len(part.shape), pipeline_mode=pl.Buffered(1))

    def sums(*shape):
        return jax.ShapeDtypeStruct(shape, full), pl.BlockSpec(shape, lambda i: (0, 0))

    def rows_of(part):
        if part.ndim == 3:
            return pl.BlockSpec((span // block, block, block), lambda i: (i, 0, 0))
        return pl.BlockSpec((span, part.shape[1]), lambda i: (i, 0))

    turned = pl.BlockSpec((1, width, span), lambda i: (i, 0, 0))
    outs = [
        (jax.ShapeDtypeStruct((rows, width, span), low), turned), (jax.ShapeDtypeStruct((rows, width, span), low), turned),
        by_rows(width, low), by_rows(inner_width, low), by_rows(base_width, low), by_rows(value_width, low),
        sums(1, sum(small_widths(sizes))),
    ]
    if deep:
        outs.append((jax.ShapeDtypeStruct((rows, width // (2 * deep), span * 2 * deep), low), ANYWHERE))
    made = pl.pallas_call(
        partial(token_backward_kernel, sizes, deep),
        grid=(rows,),
        in_specs=[turned, ANYWHERE, ANYWHERE, whole(gain), whole(norm_gain)] + [rows_of(part) for part in kept] + [ANYWHERE] * bool(deep),
        out_specs=[spec for _, spec in outs],
        out_shape=[shape for shape, _ in outs],
        scratch_shapes=[pltpu.VMEM((span, width), full), pltpu.VMEM((span, value_width), low), pltpu.VMEM((block, block), full)]
        + ([dma(1), dma(2 * deep), dma(2 * deep)] if deep else []) + [pltpu.VMEM(first.shape, low), pltpu.VMEM(second.shape, low), dma(2)],
        compiler_params=(pltpu.CompilerParams(collective_id=4, has_side_effects=True, vmem_limit_bytes=ROOM) if deep
                         else pltpu.CompilerParams(vmem_limit_bytes=ROOM)),
        cost_estimate=pl.CostEstimate(flops=2 * tokens * (first.size + second.size), bytes_accessed=60 * 1024 * 1024, transcendentals=0),
    )(token_grad, first, second, gain, norm_gain, *kept, *([layer_blocks] if deep else []))
    if not deep:
        made = [*made, lax.all_to_all(layer_blocks, "chan", split_axis=1, concat_axis=2, tiled=True)]
    return made


def contract_rows(left, right):
    return lax.dot_general(
        left, right, (((0,), (0,)), ((), ())), preferred_element_type=jnp.float32
    )


def shards(
    inputs,
    cotangent,
    doc_lengths,
    ema_logits,
    ema_mixing,
    ema_skip,
    value_weight,
    base_weight,
    attn_weight,
    hidden_weight,
    output_weight,
    value_bias,
    base_bias,
    attn_bias,
    hidden_bias,
    output_bias,
    query_key_gain,
    query_key_shift,
    position_bias,
    norm_gain,
    norm_bias,
):
    row_count, chan_count, seq_length = inputs.shape
    group_count = lax.axis_size("chan")
    width = chan_count * group_count
    span_local = seq_length // group_count
    length_block = position_bias.shape[0]
    shared_width = query_key_gain.shape[1]
    value_width = value_bias.shape[0]
    keep, keep_next = keep_tables(doc_lengths, seq_length)
    compact = ema_table(ema_logits, ema_mixing, ema_skip)
    on_four = lax.axis_size("row") == 4 and group_count == 8
    devices, deep = lax.axis_size("row") * group_count, group_count // 2
    exchange = partial(forward_exchange, devices=devices, deep=deep) if on_four else plain_forward
    first, second, token_input, token_mixed, pre_mix = exchange(
        [value_weight, base_weight, hidden_weight], [attn_weight, output_weight], inputs, keep, compact
    )
    first, second = first.reshape(width, -1), second.reshape(value_width, -1)
    base_width = base_bias.shape[0]
    local_pos = lax.axis_index("chan") * span_local + jnp.arange(span_local, dtype=jnp.int32)
    segments = jax.vmap(segment_ids, (0, None))(doc_lengths, local_pos).astype(jnp.float32)[:, None]
    turned_bias = jnp.roll(position_bias[::-1], 1)[None]
    sizes = (width, shared_width, value_width, hidden_bias.shape[0], length_block)
    vectors = [value_bias, base_bias, attn_bias, hidden_bias, output_bias, query_key_gain, query_key_shift, norm_gain, norm_bias]
    reach = deep if on_four else 0
    (
        layer_blocks,
        input_rows,
        mixed_rows,
        values,
        value_slope,
        reset,
        reset_back,
        attention,
        queries,
        keys,
        shared,
        shared_slope,
        mixed_att,
        hidden_back,
        gate_back,
        gate,
        normal_one,
        scale_one,
        normed_low,
        activated,
        inner_slope,
        normal_two,
        scale_two,
        token_grad,
    ) = token_forward(token_input, token_mixed, segments, turned_bias, first, second, vectors, sizes, cotangent, reach)
    kept = [values, value_slope, reset, reset_back, attention, queries, keys, shared, shared_slope]
    kept += [hidden_back, gate_back, gate, normal_one, scale_one, inner_slope, normal_two, scale_two]
    (
        back_mixed_blocks,
        back_direct_blocks,
        back_outer,
        back_inner,
        back_base,
        back_value,
        small,
        layer_out,
    ) = token_backward(token_grad, first, second, query_key_gain, norm_gain, kept, sizes, layer_blocks, reach)
    back_proj = back_base[:, base_width - width :]
    grad_output_weight = contract_rows(activated, back_outer)
    grad_hidden_weight = contract_rows(normed_low, back_inner)
    grad_attn_weight = contract_rows(mixed_att, back_proj)
    grad_value_weight = contract_rows(input_rows, back_value)
    grad_base_weight = contract_rows(mixed_rows, back_base)
    def owners(terms):
        return terms.astype(jnp.bfloat16).reshape(devices, -1, terms.shape[1])

    exchange = partial(backward_exchange, deep=deep) if on_four else plain_backward
    owner_value, owner_base, owner_hidden, owner_attn, owner_output, small, grad_ema, direct, sums, skips = exchange(
        [owners(grad_value_weight), owners(grad_base_weight), owners(grad_hidden_weight)],
        [owners(grad_attn_weight), owners(grad_output_weight)],
        small,
        inputs,
        pre_mix,
        back_mixed_blocks,
        back_direct_blocks,
        keep,
        keep_next,
        compact,
    )
    grad_inputs = grad_ema + direct.astype(jnp.float32)
    states = sums.shape[0] // 2
    grad_logits, grad_mixing, grad_skip = ema_grads(
        sums[:states], sums[states:], skips, ema_logits, ema_mixing, row_count, chan_count
    )
    offset, summed = 0, []
    for count, size in ((1, value_width), (1, base_width), (1, width), (1, hidden_bias.shape[0]), (1, width),
                        (2, shared_width), (2, shared_width), (2, width), (2, width), (1, length_block)):
        part = small[0, offset : offset + count * size]
        summed.append(part if count == 1 else part.reshape(count, size))
        offset += count * size
    summed.insert(7, jnp.roll(summed.pop()[::-1], 1))
    return (
        layer_out,
        grad_inputs,
        grad_logits,
        grad_mixing,
        grad_skip,
        owner_value,
        owner_base,
        owner_attn,
        owner_hidden,
        owner_output,
        *summed,
    )


def solution(mesh):
    in_specs = (
        P("row", "chan", None),
        P("row", "chan", None),
        P("row", None),
        P(None, "chan", None),
        P(None, "chan", None),
        P("chan"),
        P(("row", "chan"), None),
        P(("row", "chan"), None),
        P(("row", "chan"), None),
        P(("row", "chan"), None),
        P(("row", "chan"), None),
        P(),
        P(),
        P(),
        P(),
        P(),
        P(),
        P(),
        P(),
        P(),
        P(),
    )
    out_specs = (
        P("row", "chan", None),
        P("row", "chan", None),
        P(None, "chan", None),
        P(None, "chan", None),
        P("chan"),
        P(("row", "chan"), None),
        P(("row", "chan"), None),
        P(("row", "chan"), None),
        P(("row", "chan"), None),
        P(("row", "chan"), None),
        P(),
        P(),
        P(),
        P(),
        P(),
        P(),
        P(),
        P(),
        P(),
        P(),
    )
    return jax.shard_map(shards, mesh=mesh, in_specs=in_specs, out_specs=out_specs, check_vma=False)
```

```python
from functools import partial

import jax
import jax.numpy as jnp
from jax import lax
from jax.experimental import pallas as pl
from jax.experimental.pallas import tpu as pltpu
from jax.sharding import PartitionSpec as P

HIGH = lax.Precision.HIGHEST
EPSILON = 1e-05
MASKED = -1e30


LANES = 128
STEPS = 16
MESH = pl.DeviceIdType.MESH


def pad_rows(block):
    short = LANES - block.shape[0]
    if short == 0:
        return block
    return jnp.concatenate([block, jnp.zeros((short, block.shape[1]), block.dtype)], axis=0)


def spread(block, slots, row, rows):
    turned = pad_rows(block).T
    slots[pl.ds(row, LANES, stride=2 * rows), :] = turned
    slots[pl.ds(row + rows, LANES, stride=2 * rows), :] = turned


def gather(slots, row, rows, chans):
    first = slots[pl.ds(row, LANES, stride=2 * rows), :]
    second = slots[pl.ds(row + rows, LANES, stride=2 * rows), :]
    return (first + second).T[:chans]


def tile_of(ref, tile):
    return ref.at[:, :, pl.ds(pl.multiple_of(tile * LANES, LANES), LANES)]


def lanes_of(ref, tile):
    return ref[:, pl.ds(pl.multiple_of(tile * LANES, LANES), LANES)]


def slot_at(step, tall):
    return pl.ds(pl.multiple_of(step * tall, tall), tall)


TABLE_ROWS = 40


def fill_tables(compact, decay_ref, gain_ref, skip_row_ref):
    halves, tall, _ = decay_ref.shape
    upper = lax.broadcasted_iota(jnp.int32, (tall, LANES), 0) < tall // 2
    for target, at in ((decay_ref, 0), (gain_ref, 2 * halves)):
        for n in range(halves):
            low, high = compact[at + n : at + n + 1, :], compact[at + halves + n : at + halves + n + 1, :]
            target[n] = jnp.where(upper, jnp.broadcast_to(low, (tall, LANES)), jnp.broadcast_to(high, (tall, LANES)))
    skip = compact[4 * halves : 4 * halves + 1, :]
    skip_row_ref[...] = jnp.where(upper, jnp.broadcast_to(skip, (tall, LANES)), 0.0)


def average_tile(x_tile, keep_tile, decay_ref, gain_ref, skip_row_ref, pre_tile, mixed_tile, slots, state):
    rows, chans, _ = x_tile.shape
    halves = decay_ref.shape[0]
    tall = 2 * rows
    for row in range(rows):
        spread(x_tile[row].astype(jnp.float32), slots, row, rows)

    def group(step, carry):
        keeping, states = carry
        states = list(states)
        for inner in range(STEPS):
            at = slot_at(step * STEPS + inner, tall)
            value = slots[at, :]
            keep = jnp.broadcast_to(keeping[:, inner : inner + 1], (tall, LANES))
            total = skip_row_ref[...] * value
            for n in range(halves):
                states[n] = (decay_ref[n] * keep) * states[n] + gain_ref[n] * value
                total = total + states[n]
            slots[at, :] = total
        return pltpu.roll(keeping, LANES - STEPS, axis=1), tuple(states)

    start = tuple(state[n] for n in range(halves))
    _, states = lax.fori_loop(0, LANES // STEPS, group, (keep_tile, start))
    for n in range(halves):
        state[n] = states[n]
    for row in range(rows):
        pre = gather(slots, row, rows, chans)
        if pre_tile is not None:
            pre_tile[row] = pre
        mixed_tile[row] = (pre * jax.nn.sigmoid(pre)).astype(jnp.bfloat16)


def back_tile_of(back_slots, tile, tall):
    return back_slots.at[pl.ds(pl.multiple_of(tile * (LANES * tall), LANES * tall), LANES * tall), :]


def weigh_tile(x_tile, pre_tile, back_mixed_tile, keep_tile, decay_ref, skip_sum, slots, back_tile, state, powers, weight_sum, power_sum):
    rows = x_tile.shape[0]
    halves = decay_ref.shape[0]
    tall = 2 * rows
    for row in range(rows):
        values = x_tile[row].astype(jnp.float32)
        pre = pre_tile[row]
        logistic = jax.nn.sigmoid(pre)
        back = back_mixed_tile[row].astype(jnp.float32) * (logistic * (1.0 + pre * (1.0 - logistic)))
        skip_sum[...] += back * values
        spread(values, slots, row, rows)
        spread(back, back_tile, row, rows)

    def group(step, carry):
        keeping, states, derived, weights, sums = (carry[0], *map(list, carry[1:]))
        for inner in range(STEPS):
            at = slot_at(step * STEPS + inner, tall)
            value = slots[at, :]
            back = back_tile[at, :]
            keep = jnp.broadcast_to(keeping[:, inner : inner + 1], (tall, LANES))
            for n in range(halves):
                decay = decay_ref[n] * keep
                derived[n] = decay * (derived[n] + states[n])
                states[n] = decay * states[n] + value
                weights[n] = weights[n] + back * states[n]
                sums[n] = sums[n] + back * derived[n]
        return pltpu.roll(keeping, LANES - STEPS, axis=1), tuple(states), tuple(derived), tuple(weights), tuple(sums)

    refs = (state, powers, weight_sum, power_sum)
    start = tuple(tuple(ref[n] for n in range(halves)) for ref in refs)
    out = lax.fori_loop(0, LANES // STEPS, group, (keep_tile, *start))
    for ref, values in zip(refs, out[1:]):
        for n in range(halves):
            ref[n] = values[n]


def adjoint_tile(next_tile, decay_ref, gain_ref, skip_row_ref, grad_tile, slots, back_tile, state):
    rows, chans, _ = grad_tile.shape
    halves = decay_ref.shape[0]
    tall = 2 * rows

    def group(step, carry):
        keeping, states = carry
        states = list(states)
        for inner in range(STEPS):
            at = slot_at(LANES - 1 - step * STEPS - inner, tall)
            back = back_tile[at, :]
            keep = jnp.broadcast_to(keeping[:, LANES - 1 - inner : LANES - inner], (tall, LANES))
            total = skip_row_ref[...] * back
            for n in range(halves):
                states[n] = (decay_ref[n] * keep) * states[n] + back
                total = total + gain_ref[n] * states[n]
            slots[at, :] = total
        return pltpu.roll(keeping, STEPS, axis=1), tuple(states)

    start = tuple(state[n] for n in range(halves))
    _, states = lax.fori_loop(0, LANES // STEPS, group, (next_tile, start))
    for n in range(halves):
        state[n] = states[n]
    for row in range(rows):
        grad_tile[row] = gather(slots, row, rows, chans)


class Place:
    def __init__(self, deep):
        self.deep = deep
        row, chan = lax.axis_index("row"), lax.axis_index("chan")
        self.y, self.core = row // 2, row % 2
        self.z, self.x = chan // 2, chan % 2
        self.row, self.chan = row, chan

    def owner(self, z, x, y, core):
        return (y * 2 + core) * (2 * self.deep) + z * 2 + x

    def over_core(self):
        return (self.row + 1 - 2 * self.core, self.chan)

    def over_x(self):
        return (self.row, self.chan + 1 - 2 * self.x)

    def over_y(self):
        return (self.row + 2 - 4 * self.y, self.chan)

    def at_z(self, z):
        return (self.row, z * 2 + self.x)

    def at_chan(self, step):
        chan = (self.chan + step) % (2 * self.deep)
        return chan, (self.row, chan)

    def greet(self):
        barrier = pltpu.get_barrier_semaphore()
        others = [self.over_core(), self.over_y()]
        others += [self.at_chan(step)[1] for step in range(1, 2 * self.deep)]
        for other in others:
            pl.semaphore_signal(barrier, inc=1, device_id=other, device_id_type=MESH)
        pl.semaphore_wait(barrier, len(others))

    def greet_line(self):
        barrier = pltpu.get_barrier_semaphore()
        for step in range(1, 2 * self.deep):
            pl.semaphore_signal(barrier, inc=1, device_id=self.at_chan(step)[1], device_id_type=MESH)
        pl.semaphore_wait(barrier, 2 * self.deep - 1)


def remote(source, target, send, recv, device):
    return pltpu.make_async_remote_copy(src_ref=source, dst_ref=target, send_sem=send, recv_sem=recv,
                                        device_id=device, device_id_type=MESH)


def start(copies):
    for copy in copies:
        copy.start()


class ToTokens:
    def __init__(self, here, source, target, send, recv, keep):
        self.here, self.source, self.target = here, source, target
        self.send, self.recv, self.keep = send, recv, keep
        self.chans, self.span = source.shape[1], target.shape[2]

    def block(self, chan):
        return self.source.at[:, :, pl.ds(pl.multiple_of(chan * self.span, LANES), self.span)]

    def spot(self, chan):
        return self.target.at[:, pl.ds(pl.multiple_of(chan * self.chans, 8), self.chans), :]

    def own(self):
        return pltpu.make_async_copy(self.block(self.here.chan), self.spot(self.here.chan), self.keep)

    def out(self, chan):
        return remote(self.block(chan), self.spot(self.here.chan), self.send.at[chan], self.recv.at[self.here.chan], (self.here.row, chan))

    def arrival(self, chan):
        return remote(self.block(chan), self.spot(chan), self.send.at[chan], self.recv.at[chan], (self.here.row, chan))

    def begin_same(self):
        for step in range(2, 2 * self.here.deep, 2):
            self.out(self.here.at_chan(step)[0]).start()
        self.own().start()

    def begin_cross(self):
        for step in range(1, 2 * self.here.deep, 2):
            self.out(self.here.at_chan(step)[0]).start()

    def begin(self):
        self.begin_cross()
        self.begin_same()

    def begin_one(self, chan):
        @pl.when(chan == self.here.chan)
        def _():
            self.own().start()

        @pl.when(chan != self.here.chan)
        def _():
            self.out(chan).start()

    def arrive(self):
        self.own().wait()
        for step in range(1, 2 * self.here.deep):
            self.arrival(self.here.at_chan(step)[0]).wait_recv()

    def finish(self):
        for step in range(1, 2 * self.here.deep):
            self.out(self.here.at_chan(step)[0]).wait_send()


class ToChannels(ToTokens):
    def __init__(self, here, source, target, send, recv, keep):
        super().__init__(here, source, target, send, recv, keep)
        self.chans, self.span = target.shape[1], source.shape[2]

    def block(self, chan):
        return self.source.at[:, pl.ds(pl.multiple_of(chan * self.chans, 8), self.chans), :]

    def spot(self, chan):
        return self.target.at[:, :, pl.ds(pl.multiple_of(chan * self.span, LANES), self.span)]


def forward_kernel(deep, groups, *refs):
    total = sum(groups)
    forward_body(deep, groups, refs[:total], *refs[total:])


def forward_body(deep, groups, shards_in, x_ref, keep_ref, compact_ref,
                   first_full, second_full, token_x, token_mixed, pre_ref,
                   first, second, mixed, slots, state, decay_ref, gain_ref, skip_row_ref, local_sem, send_z, send_x, send_y, send_d, send_core, recv_z, recv_x, recv_y, recv_d, recv_core,
                   a_send, a_recv, b_send, b_recv):
    count = 2
    mine, full = (first, second), (first_full, second_full)
    here = Place(deep)
    z, x, y, core = here.z, here.x, here.y, here.core
    me = here.owner(z, x, y, core)
    layers = range(deep)

    def piece(which, at, device, send, recv, source=None):
        spot = full[which].at[at]
        return remote(spot if source is None else source, spot, send, recv, device)

    def to_core(at, slot, source=False):
        return [piece(which, at, here.over_core(), send_core.at[which, slot], recv_core.at[which, slot],
                      mine[which] if source else None) for which in range(count)]

    def own_x(k, source=False):
        at = here.owner(k, x, y, core)
        return [piece(which, at, here.over_x(), send_x.at[which, k], recv_x.at[which, k],
                      mine[which] if source else None) for which in range(count)]

    def own_y(k, source=False):
        at = here.owner(k, x, y, core)
        return [piece(which, at, here.over_y(), send_y.at[which, k], recv_y.at[which, k],
                      mine[which] if source else None) for which in range(count)]

    def column(k, source=False):
        start(own_x(k, source))
        start(own_y(k, source))
        start(to_core(here.owner(k, x, y, core), k, source))

    def along(k, to, side, source=False):
        at = here.owner(k, x, y, core)
        return [piece(which, at, here.at_z(to), send_z.at[which, k, side], recv_z.at[which, k],
                      mine[which] if source else None) for which in range(count)]

    via_x = 1

    def onward_y(k):
        at = here.owner(k, 1 - x, y, core)
        return [piece(which, at, here.over_y(), send_d.at[which, k], recv_d.at[which, k]) for which in range(count)]

    def onward_x(k):
        at = here.owner(k, x, 1 - y, core)
        return [piece(which, at, here.over_x(), send_d.at[which, k], recv_d.at[which, k]) for which in range(count)]

    def wait_from(at, recv, k, device):
        for which in range(count):
            piece(which, at, device, send_x.at[which, 0], recv.at[which, k]).wait_recv()

    def sides(distance):
        return [z] if distance == 0 else [z - distance, z + distance]

    def neighbours(distance):
        for k in sides(distance):
            @pl.when((k >= 0) & (k < deep))
            def _():
                at = here.owner(k, 1 - x, y, core)
                wait_from(at, recv_x, k, here.over_x())

                @pl.when(k >= via_x)
                def _():
                    start(onward_y(k))
                start(to_core(at, deep + k))
                at = here.owner(k, x, 1 - y, core)
                wait_from(at, recv_y, k, here.over_y())

                @pl.when(k < via_x)
                def _():
                    start(onward_x(k))
                start(to_core(at, 2 * deep + k))

    def layer_step(distance):
        for side, k in enumerate(sides(distance)):
            @pl.when((k >= 0) & (k < deep))
            def _():
                to = z + 1 if side == 0 else z - 1
                wait_from(here.owner(k, x, y, core), recv_z, k, here.at_z(z))

                @pl.when((to >= 0) & (to < deep))
                def _():
                    start(along(k, to, 1 - side))
                column(k)

    at_shard = 0
    for target, size in zip(mine, groups):
        offset = 0
        for shard in shards_in[at_shard : at_shard + size]:
            target[:, pl.ds(offset, shard.shape[1])] = shard[...].astype(jnp.bfloat16)
            offset += shard.shape[1]
        at_shard += size
    here.greet()
    tokens_x = ToTokens(here, x_ref, token_x, a_send, a_recv, local_sem.at[2])
    tokens_mixed = ToTokens(here, mixed, token_mixed, b_send, b_recv, local_sem.at[3])
    local = [pltpu.make_async_copy(mine[which], full[which].at[me], local_sem.at[which]) for which in range(count)]
    start(local)
    for side, to in ((0, z - 1), (1, z + 1)):
        @pl.when((to >= 0) & (to < deep))
        def _():
            start(along(z, to, side, True))
    column(z, True)
    fill_tables(compact_ref, decay_ref, gain_ref, skip_row_ref)
    state[...] = jnp.zeros_like(state)
    tiles = x_ref.shape[2] // LANES
    each = tokens_x.span // LANES

    def tile_step(tile, carry):
        average_tile(tile_of(x_ref, tile), lanes_of(keep_ref, tile), decay_ref, gain_ref, skip_row_ref,
                     tile_of(pre_ref, tile), tile_of(mixed, tile), slots, state)

        @pl.when(tile == 5)
        def _():
            layer_step(1)

        @pl.when(tile == 8)
        def _():
            neighbours(0)

        @pl.when(tile == 12)
        def _():
            layer_step(2)

        @pl.when(tile == 15)
        def _():
            layer_step(3)
            tokens_x.begin()
        return carry

    lax.fori_loop(0, tiles, tile_step, 0)
    tokens_mixed.begin()
    neighbours(1)
    neighbours(2)
    neighbours(deep - 1)
    for k in layers:
        at = here.owner(k, 1 - x, 1 - y, core)
        wait_from(at, recv_d, k, here.over_y())
        start(to_core(at, 3 * deep + k))
    for copy in local:
        copy.wait()
    tokens_x.arrive()
    tokens_mixed.arrive()
    for slot, (flip_x, flip_y) in enumerate(((0, 0), (1, 0), (0, 1), (1, 1))):
        for k in layers:
            at = here.owner(k, x + flip_x * (1 - 2 * x), y + flip_y * (1 - 2 * y), 1 - core)
            for copy in to_core(at, slot * deep + k):
                copy.wait_recv()
                copy.wait_send()
    for k in layers:
        for copy in own_x(k) + own_y(k) + (onward_x(k) if k < via_x else onward_y(k)):
            copy.wait_send()
        for side, valid in ((0, (k >= z) & (z > 0)), (1, (k <= z) & (z < deep - 1))):
            @pl.when(valid)
            def _():
                for copy in along(k, z, side):
                    copy.wait_send()
    tokens_x.finish()
    tokens_mixed.finish()


LAYER_TIMES = ((3, 11), (0, 12), (2, 16), (1, 20))
LAYER_GAP = 4


def backward_kernel(deep, groups, *refs):
    total = sum(groups)
    sources = refs[:total]
    (small, x_ref, pre_ref, mixed_rows, direct_rows, keep_ref, next_ref, compact_ref) = refs[total : total + 8]
    refs = refs[total + 8 :]
    outs, (small_out, grad_ref, direct, sums_out, skips_out) = refs[:total], refs[total : total + 5]
    rest = refs[total + 5 :]
    held, from_core, from_d, from_x, from_y, from_z = (rest[2 * i : 2 * i + 2] for i in range(6))
    (small_sum, small_pair, small_deep, load_sem, core_send, core_recv, d_send, d_recv, x_send, x_recv, y_send, y_recv,
     z_send, z_recv, small_send, small_recv, back_mixed, slots, back_slots, state, powers, sums, sums_pair,
     skips, skips_pair,     local_sem, a_send, a_recv, b_send, b_recv, sums_send, sums_recv, decay_ref, gain_ref, skip_row_ref) = rest[12:]
    here = Place(deep)
    z, x, y, core = here.z, here.x, here.y, here.core
    rows, chans, length = x_ref.shape
    halves = decay_ref.shape[0]
    tall = 2 * rows
    tiles = length // LANES
    wide = []
    first = 0
    for which, size in enumerate(groups):
        offset = 0
        for source in sources[first : first + size]:
            wide.append((which, source, offset, source.shape[2]))
            offset += source.shape[2]
        first += size

    def begin(index, carry):
        slot = 4 * deep - 1 - index
        k, flips = slot % deep, slot // deep
        to_x = x + (flips % 2) * (1 - 2 * x)
        to_y = y + (flips // 2) * (1 - 2 * y)
        own, other = here.owner(k, to_x, to_y, core), here.owner(k, to_x, to_y, 1 - core)
        for which, source, offset, width in wide:
            pltpu.make_async_copy(source.at[own], held[which].at[slot, :, pl.ds(offset, width)], load_sem.at[which, slot]).start()
            remote(source.at[other], from_core[which].at[slot, :, pl.ds(offset, width)],
                   core_send.at[which, slot], core_recv.at[which, slot], here.over_core()).start()
        return carry

    def ready(slot):
        for which in range(2):
            spot = held[which].at[slot]
            pltpu.make_async_copy(spot, spot, load_sem.at[which, slot]).wait()
            remote(spot, from_core[which].at[slot], core_send.at[which, slot], core_recv.at[which, slot], here.over_core()).wait_recv()
            held[which][slot] = held[which][slot] + from_core[which][slot]

    via_x = 1

    def send_d(which, k):
        device = here.over_x() if k < via_x else here.over_y()
        return remote(held[which].at[3 * deep + k], from_d[which].at[k], d_send.at[which, k], d_recv.at[which, k], device)

    def send_x(which, k):
        return remote(held[which].at[deep + k], from_x[which].at[k], x_send.at[which, k], x_recv.at[which, k], here.over_x())

    def send_y(which, k):
        return remote(held[which].at[2 * deep + k], from_y[which].at[k], y_send.at[which, k], y_recv.at[which, k], here.over_y())

    def send_right(which, k):
        return remote(held[which].at[k], from_z[which].at[k], z_send.at[which, k], z_recv.at[which, k], here.at_z(z + 1))

    def send_left(which, k):
        slot = jnp.where(z - 1 == k, deep, k)
        return remote(held[which].at[k], from_z[which].at[slot], z_send.at[which, k], z_recv.at[which, slot], here.at_z(z - 1))

    def from_right(which, k, slot):
        return remote(held[which].at[k], from_z[which].at[slot], z_send.at[which, k], z_recv.at[which, slot], here.at_z(z + 1))

    def send_small(stage):
        device = (here.over_core(), here.over_y(), here.over_x())[stage]
        return remote(small_sum.at[stage], small_pair.at[stage], small_send.at[stage], small_recv.at[stage], device)

    def send_small_deep(step):
        return remote(small_deep.at[z], small_deep.at[z], small_send.at[3 + step], small_recv.at[3 + step],
                      here.at_z((z + step) % deep))

    def send_sums(stage):
        device = (here.over_core(), here.over_y())[stage]
        return [remote(sums.at[stage], sums_pair.at[stage], sums_send.at[0, stage], sums_recv.at[0, stage], device),
                remote(skips.at[stage], skips_pair.at[stage], sums_send.at[1, stage], sums_recv.at[1, stage], device)]

    def sums_step(stage):
        for copy in send_sums(stage):
            copy.wait_recv()
        sums[stage + 1] = sums[stage] + sums_pair[stage]
        skips[stage + 1] = skips[stage] + skips_pair[stage]

    here.greet()
    mixed_back = ToChannels(here, mixed_rows, back_mixed, a_send, a_recv, local_sem.at[0])
    direct_back = ToChannels(here, direct_rows, direct, b_send, b_recv, local_sem.at[1])
    mixed_back.begin()
    small_sum[0] = small[...]
    send_small(0).start()
    lax.fori_loop(0, 4 * deep, begin, 0)

    def small_step(stage):
        send_small(stage).wait_recv()
        small_sum[stage + 1] = small_sum[stage] + small_pair[stage]
        if stage < 2:
            send_small(stage + 1).start()

    def diagonal(k):
        ready(3 * deep + k)
        for which in range(2):
            send_d(which, k).start()

    def side(slot, send, k, waits):
        ready(slot * deep + k)
        for which in range(2):
            if waits:
                send_d(which, k).wait_recv()
                held[which][slot * deep + k] = held[which][slot * deep + k] + from_d[which][k]
            send(which, k).start()

    def x_side(k):
        side(1, send_x, k, k >= via_x)

    def y_side(k):
        side(2, send_y, k, k < via_x)

    diagonal(3)
    small_step(0)
    y_side(3)
    diagonal(0)
    x_side(0)
    diagonal(2)
    diagonal(1)
    small_step(1)
    direct_back.begin_same()
    x_side(3)
    y_side(0)
    y_side(2)
    x_side(2)
    y_side(1)
    for k in range(deep):
        ready(k)
    x_side(1)
    small_step(2)
    small_deep[z] = small_sum[3]
    for step in range(1, deep):
        send_small_deep(step).start()

    fill_tables(compact_ref, decay_ref, gain_ref, skip_row_ref)
    state[...] = jnp.zeros_like(state)
    powers[...] = jnp.zeros_like(powers)
    sums[0] = jnp.zeros_like(sums[0])
    skips[0] = jnp.zeros_like(skips[0])
    own_sums = sums.at[0]
    weight_sum, power_sum = own_sums.at[pl.ds(0, halves)], own_sums.at[pl.ds(halves, halves)]
    mixed_back.arrive()
    direct_back.begin_cross()

    def layer_sums(k):
        for which in range(2):
            send_x(which, k).wait_recv()
            send_y(which, k).wait_recv()
            held[which][k] = (held[which][k].astype(jnp.float32) + from_x[which][k].astype(jnp.float32)
                              + from_y[which][k].astype(jnp.float32)).astype(jnp.bfloat16)

    def layer_step(k):
        layer_sums(k)

        @pl.when(k > z)
        def _():
            for which in range(2):
                @pl.when(z > 0)
                def _():
                    send_right(which, k).wait_recv()
                    held[which][k] = held[which][k] + from_z[which][k]
                send_right(which, k).start()

        @pl.when(k < z)
        def _():
            for which in range(2):
                @pl.when(z < deep - 1)
                def _():
                    from_right(which, k, k).wait_recv()
                    held[which][k] = held[which][k] + from_z[which][k]
                send_left(which, k).start()

    def layer_steps(index):
        for k, base in LAYER_TIMES:
            hop = jnp.where(k > z, z, deep - 1 - z)

            @pl.when((index == base + LAYER_GAP * hop) & (k != z))
            def _():
                layer_step(k)

    def weigh_step(tile, carry):
        weigh_tile(tile_of(x_ref, tile), tile_of(pre_ref, tile), tile_of(back_mixed, tile), lanes_of(keep_ref, tile), decay_ref,
                   skips.at[0], slots, back_tile_of(back_slots, tile, tall), state, powers, weight_sum, power_sum)
        layer_steps(tile)
        return carry

    lax.fori_loop(0, tiles, weigh_step, 0)
    for copy in send_sums(0):
        copy.start()
    state[...] = jnp.zeros_like(state)

    def adjoint_step(step, carry):
        tile = tiles - 1 - step
        adjoint_tile(lanes_of(next_ref, tile), decay_ref, gain_ref, skip_row_ref, tile_of(grad_ref, tile),
                     slots, back_tile_of(back_slots, tile, tall), state)
        layer_steps(tiles + step)

        @pl.when(step == tiles // 2)
        def _():
            sums_step(0)
            for copy in send_sums(1):
                copy.start()
        return carry

    lax.fori_loop(0, tiles, adjoint_step, 0)
    layer_sums(z)
    sums_step(1)
    sums_out[...] = sums[2]
    skips_out[...] = skips[2]
    for which in range(2):
        @pl.when(z > 0)
        def _():
            send_right(which, z).wait_recv()

        @pl.when(z < deep - 1)
        def _():
            from_right(which, z, deep).wait_recv()
    for out, (which, _, offset, width) in zip(outs, wide):
        columns = pl.ds(offset, width)
        out[...] = held[which][z, :, columns].astype(jnp.float32)

        @pl.when(z > 0)
        def _():
            out[...] += from_z[which][z, :, columns].astype(jnp.float32)

        @pl.when(z < deep - 1)
        def _():
            out[...] += from_z[which][deep, :, columns].astype(jnp.float32)
    direct_back.arrive()
    for step in range(1, deep):
        origin = (z + deep - step) % deep
        remote(small_deep.at[origin], small_deep.at[origin], small_send.at[3 + step], small_recv.at[3 + step], here.at_z(origin)).wait_recv()
    added = small_deep[0]
    for k in range(1, deep):
        added = added + small_deep[k]
    small_out[...] = added
    for stage in range(3):
        send_small(stage).wait_send()
    for stage in range(2):
        for copy in send_sums(stage):
            copy.wait_send()
    for step in range(1, deep):
        send_small_deep(step).wait_send()
    mixed_back.finish()
    direct_back.finish()
    for which in range(2):
        for slot in range(4 * deep):
            remote(held[which].at[slot], from_core[which].at[slot], core_send.at[which, slot], core_recv.at[which, slot], here.over_core()).wait_send()
        for k in range(deep):
            send_d(which, k).wait_send()
            send_x(which, k).wait_send()
            send_y(which, k).wait_send()

            @pl.when(k > z)
            def _():
                send_right(which, k).wait_send()

            @pl.when(k < z)
            def _():
                send_left(which, k).wait_send()


def ema_parts(logits, mixing):
    damping = jax.nn.sigmoid(logits[0])
    decay = 1.0 - damping * jax.nn.sigmoid(logits[1])
    return damping, decay, damping * mixing[0]


def document_ends(lengths):
    count = lengths.shape[1]
    earlier = jnp.tril(jnp.ones((count, count), jnp.int32))
    return jnp.sum(lengths[:, None, :] * earlier[None], axis=2)


def keep_tables(lengths, length):
    begins = document_ends(lengths)
    positions = jnp.arange(length, dtype=jnp.int32)

    def continues(at):
        hit = jnp.any(at[None, :, None] == begins[:, None, :], axis=2) | ((at == 0) | (at == length))[None]
        return jnp.tile(1.0 - hit.astype(jnp.float32), (2, 1))

    return continues(positions), continues(positions + 1)


def lane_sums(sums, rows, chans):
    count = sums.shape[0]
    return jnp.sum(sums.reshape(count, 2, rows, LANES), axis=2)[:, :, :chans].transpose(2, 1, 0).reshape(chans, 2 * count)


def ema_table(logits, mixing, skip):
    _, decay, gain = ema_parts(logits, mixing)
    rows = jnp.concatenate([decay.T, (gain * mixing[1]).T, skip[None]], axis=0)
    return jnp.pad(rows, ((0, TABLE_ROWS - rows.shape[0]), (0, LANES - rows.shape[1])))


def ema_grads(weight, power, skips, logits, mixing, rows, chans):
    damping, decay, gain = ema_parts(logits, mixing)
    weight = lane_sums(weight, rows, chans)
    back_decay = gain * mixing[1] * lane_sums(power, rows, chans) / decay
    other = jax.nn.sigmoid(logits[1])
    back_damping = weight * mixing[0] * mixing[1] - back_decay * other
    grad_logits = jnp.stack([back_damping * damping * (1.0 - damping), -back_decay * damping * other * (1.0 - other)])
    grad_mixing = jnp.stack([damping * mixing[1] * weight, gain * weight])
    return grad_logits, grad_mixing, jnp.sum(skips, axis=1)


def dma(*shape):
    return pltpu.SemaphoreType.DMA(shape)


ANYWHERE = pl.BlockSpec(memory_space=pl.ANY)
NEAR = pl.BlockSpec(memory_space=pltpu.VMEM)
ROOM = 60 * 1024 * 1024


def forward_exchange(first, second, values, keep, compact, devices, deep):
    rows, chans, length = values.shape
    shapes = [(group[0].shape[0], sum(part.shape[1] for part in group)) for group in (first, second)]
    low, full = jnp.bfloat16, jnp.float32
    half, tall = (TABLE_ROWS - 8) // 4, 2 * rows
    tokens = (rows, chans * 2 * deep, length // (2 * deep))
    table = pltpu.VMEM((half, tall, LANES), full)
    return pl.pallas_call(
        partial(forward_kernel, deep, (len(first), len(second))),
        in_specs=[NEAR] * (len(first) + len(second) + 3),
        out_specs=[ANYWHERE] * 4 + [NEAR],
        out_shape=[jax.ShapeDtypeStruct((devices,) + shape, low) for shape in shapes]
        + [jax.ShapeDtypeStruct(tokens, low), jax.ShapeDtypeStruct(tokens, low), jax.ShapeDtypeStruct(values.shape, full)],
        scratch_shapes=[pltpu.VMEM(shape, low) for shape in shapes]
        + [pltpu.VMEM(values.shape, low), pltpu.VMEM((LANES * tall, LANES), full), table, table, table, pltpu.VMEM((tall, LANES), full),
           dma(4), dma(2, deep, 2), dma(2, deep), dma(2, deep), dma(2, deep), dma(2, 4 * deep),
           dma(2, deep), dma(2, deep), dma(2, deep), dma(2, deep), dma(2, 4 * deep)] + [dma(2 * deep)] * 4,
        compiler_params=pltpu.CompilerParams(collective_id=1, has_side_effects=True, vmem_limit_bytes=ROOM),
        cost_estimate=pl.CostEstimate(flops=values.size * 160, bytes_accessed=48 * 1024 * 1024, transcendentals=values.size),
    )(*first, *second, values, keep, compact)


def backward_exchange(first, second, small, values, pre, mixed_rows, direct_rows, keep, keep_next, compact, deep):
    rows, chans, length = values.shape
    half, tall = (TABLE_ROWS - 8) // 4, 2 * rows
    shapes = [(group[0].shape[1], sum(part.shape[2] for part in group)) for group in (first, second)]
    scratch = []
    for count in (4 * deep, 4 * deep, deep, deep, deep, deep + 1):
        scratch += [pltpu.VMEM((count,) + shape, jnp.bfloat16) for shape in shapes]
    scratch += [pltpu.VMEM((4,) + small.shape, jnp.float32), pltpu.VMEM((3,) + small.shape, jnp.float32),
                pltpu.VMEM((deep,) + small.shape, jnp.float32)]
    scratch += [dma(2, 4 * deep)] * 3 + [dma(2, deep)] * 6 + [dma(2, deep), dma(2, deep + 1)] + [dma(3 + deep)] * 2
    scratch += [pltpu.VMEM(values.shape, jnp.bfloat16)]
    scratch += [pltpu.VMEM((LANES * tall, LANES), jnp.float32), pltpu.VMEM((length * tall, LANES), jnp.float32)]
    scratch += [pltpu.VMEM((half, tall, LANES), jnp.float32)] * 2
    scratch += [pltpu.VMEM((3, 2 * half, tall, LANES), jnp.float32), pltpu.VMEM((2, 2 * half, tall, LANES), jnp.float32)]
    scratch += [pltpu.VMEM((3, chans, LANES), jnp.float32), pltpu.VMEM((2, chans, LANES), jnp.float32)]
    scratch += [dma(2)] + [dma(2 * deep)] * 4 + [dma(2, 2)] * 2
    scratch += [pltpu.VMEM((half, tall, LANES), jnp.float32)] * 2 + [pltpu.VMEM((tall, LANES), jnp.float32)]
    return pl.pallas_call(
        partial(backward_kernel, deep, (len(first), len(second))),
        in_specs=[ANYWHERE] * (len(first) + len(second)) + [NEAR] * 3 + [ANYWHERE] * 2 + [NEAR] * 3,
        out_specs=[NEAR] * (len(first) + len(second) + 2) + [ANYWHERE] + [NEAR] * 2,
        out_shape=[jax.ShapeDtypeStruct(part.shape[1:], jnp.float32) for part in (*first, *second)]
        + [jax.ShapeDtypeStruct(small.shape, jnp.float32), jax.ShapeDtypeStruct(values.shape, jnp.float32),
           jax.ShapeDtypeStruct(values.shape, jnp.bfloat16),
           jax.ShapeDtypeStruct((2 * half, tall, LANES), jnp.float32), jax.ShapeDtypeStruct((chans, LANES), jnp.float32)],
        scratch_shapes=scratch,
        compiler_params=pltpu.CompilerParams(collective_id=2, has_side_effects=True, vmem_limit_bytes=ROOM),
        cost_estimate=pl.CostEstimate(flops=values.size * 240, bytes_accessed=64 * 1024 * 1024, transcendentals=values.size),
    )(*first, *second, small, values, pre, mixed_rows, direct_rows, keep, keep_next, compact)


def plain_forward_kernel(x_ref, keep_ref, compact_ref, pre_ref, mixed_ref, slots, state, decay_ref, gain_ref, skip_row_ref):
    @pl.when(pl.program_id(0) == 0)
    def _():
        state[...] = jnp.zeros_like(state)
        fill_tables(compact_ref, decay_ref, gain_ref, skip_row_ref)

    average_tile(x_ref, keep_ref[...], decay_ref, gain_ref, skip_row_ref, pre_ref, mixed_ref, slots, state)


def plain_backward_kernel(x_ref, pre_ref, back_ref, keep_ref, next_ref, compact_ref, grad_ref, sums_ref, skips_ref,
                          slots, back_slots, state, powers, decay_ref, gain_ref, skip_row_ref):
    halves, tall, _ = decay_ref.shape
    tiles = pl.num_programs(0) // 2
    index = pl.program_id(0)

    @pl.when(index == 0)
    def _():
        fill_tables(compact_ref, decay_ref, gain_ref, skip_row_ref)
        state[...] = jnp.zeros_like(state)
        powers[...] = jnp.zeros_like(powers)
        sums_ref[...] = jnp.zeros_like(sums_ref)
        skips_ref[...] = jnp.zeros_like(skips_ref)

    @pl.when(index < tiles)
    def _():
        weigh_tile(x_ref, pre_ref, back_ref, keep_ref[...], decay_ref, skips_ref, slots, back_tile_of(back_slots, index, tall),
                   state, powers, sums_ref.at[pl.ds(0, halves)], sums_ref.at[pl.ds(halves, halves)])

    @pl.when(index == tiles)
    def _():
        state[...] = jnp.zeros_like(state)

    @pl.when(index >= tiles)
    def _():
        adjoint_tile(next_ref[...], decay_ref, gain_ref, skip_row_ref, grad_ref, slots,
                     back_tile_of(back_slots, 2 * tiles - 1 - index, tall), state)


def gathered(part):
    return lax.all_gather(part, ("row", "chan"), axis=0)


def plain_forward(first, second, values, keep, compact):
    rows, chans, length = values.shape
    half, tall = (TABLE_ROWS - 8) // 4, 2 * rows
    first, second = (jnp.concatenate([part.astype(jnp.bfloat16) for part in group], axis=1) for group in (first, second))
    block = pl.BlockSpec((rows, chans, LANES), lambda i: (0, 0, i))
    table = pl.BlockSpec((TABLE_ROWS, LANES), lambda i: (0, 0))
    spread_tables = [pltpu.VMEM((half, tall, LANES), jnp.float32)] * 2 + [pltpu.VMEM((tall, LANES), jnp.float32)]
    pre, mixed = pl.pallas_call(
        plain_forward_kernel,
        grid=(length // LANES,),
        in_specs=[block, pl.BlockSpec((tall, LANES), lambda i: (0, i)), table],
        out_specs=[block, block],
        out_shape=[jax.ShapeDtypeStruct(values.shape, jnp.float32), jax.ShapeDtypeStruct(values.shape, jnp.bfloat16)],
        scratch_shapes=[pltpu.VMEM((LANES * tall, LANES), jnp.float32), pltpu.VMEM((half, tall, LANES), jnp.float32)] + spread_tables,
    )(values, keep, compact)
    moved = [lax.all_to_all(part, "chan", split_axis=2, concat_axis=1, tiled=True) for part in (values, mixed)]
    return gathered(first), gathered(second), *moved, pre


def plain_backward(first, second, small, values, pre, mixed_rows, direct_rows, keep, keep_next, compact):
    rows, chans, length = values.shape
    back, direct = [lax.all_to_all(part, "chan", split_axis=1, concat_axis=2, tiled=True) for part in (mixed_rows, direct_rows)]
    half, tall = (TABLE_ROWS - 8) // 4, 2 * rows
    tiles = length // LANES
    ahead = pl.BlockSpec((rows, chans, LANES), lambda i: (0, 0, jnp.minimum(i, tiles - 1)))
    behind = pl.BlockSpec((rows, chans, LANES), lambda i: (0, 0, jnp.minimum(tiles - 1, 2 * tiles - 1 - i)))
    table = pl.BlockSpec((TABLE_ROWS, LANES), lambda i: (0, 0))
    spread_tables = [pltpu.VMEM((half, tall, LANES), jnp.float32)] * 2 + [pltpu.VMEM((tall, LANES), jnp.float32)]
    grads, sums, skips = pl.pallas_call(
        plain_backward_kernel,
        grid=(2 * tiles,),
        in_specs=[ahead] * 3 + [pl.BlockSpec((tall, LANES), lambda i: (0, jnp.minimum(i, tiles - 1))),
                                pl.BlockSpec((tall, LANES), lambda i: (0, jnp.minimum(tiles - 1, 2 * tiles - 1 - i))),
                                table],
        out_specs=[behind, pl.BlockSpec((2 * half, tall, LANES), lambda i: (0, 0, 0)), pl.BlockSpec((chans, LANES), lambda i: (0, 0))],
        out_shape=[jax.ShapeDtypeStruct(values.shape, jnp.float32), jax.ShapeDtypeStruct((2 * half, tall, LANES), jnp.float32),
                   jax.ShapeDtypeStruct((chans, LANES), jnp.float32)],
        scratch_shapes=[pltpu.VMEM((LANES * tall, LANES), jnp.float32), pltpu.VMEM((length * tall, LANES), jnp.float32)]
        + [pltpu.VMEM((half, tall, LANES), jnp.float32)] * 2 + spread_tables,
        compiler_params=pltpu.CompilerParams(vmem_limit_bytes=ROOM),
    )(values, pre, back, keep, keep_next, compact)
    sums, skips, small = lax.psum((sums, skips), "row") + (lax.psum(small, ("row", "chan")),)
    owned = [
        lax.psum_scatter(part, ("row", "chan"), scatter_dimension=0, tiled=True)[0].astype(jnp.float32) for part in (*first, *second)
    ]
    return *owned, small, grads, direct, sums, skips


PIECE = 256


def over_pieces(width, body):
    for at in range(0, width, PIECE):
        body(at)


def times(left, right):
    return jnp.dot(left, right, preferred_element_type=jnp.float32)


def times_turned(left, right):
    return lax.dot_general(left, right, (((1,), (1,)), ((), ())), preferred_element_type=jnp.float32)


def turned_times(left, right):
    return lax.dot_general(left, right, (((0,), (0,)), ((), ())), preferred_element_type=jnp.float32)


def silu_and_slope(values):
    logistic = jax.nn.sigmoid(values)
    return values * logistic, logistic * (1.0 + values * (1.0 - logistic))


def normalize(values):
    center = jnp.mean(values, axis=-1, keepdims=True)
    centered = values - center
    scale = lax.rsqrt(jnp.mean(centered * centered, axis=-1, keepdims=True) + EPSILON)
    return centered * scale, scale


def normalize_back(grads, normal, scale):
    return (grads - jnp.mean(grads, axis=-1, keepdims=True) - normal * jnp.mean(grads * normal, axis=-1, keepdims=True)) * scale


def shear(table, step):
    side = table.shape[1]
    index = lax.broadcasted_iota(jnp.int32, table.shape, 0)
    bit = 1
    while bit < side:
        table = jnp.where((index // bit) % 2 == 1, pltpu.roll(table, bit if step == 1 else side - bit, axis=1), table)
        bit *= 2
    return table


def row_of(ref, at, size):
    return ref[pl.ds(at, size)].reshape(1, size)


def wait_first(load):
    @pl.when(pl.program_id(0) == 0)
    def _():
        load.wait()


def parts_of(ref, widths):
    made, offset = [], 0
    for width in widths:
        made.append(ref.at[:, pl.ds(offset, width)])
        offset += width
    return made


def token_forward_kernel(sizes, deep, *refs):
    width, shared_width, value_width, inner_width, block = sizes
    input_ref, mixed_ref, segments_ref, position_ref, first_far, second_far = refs[:6]
    value_bias, base_bias, attn_bias, hidden_bias, output_bias, gain, shift, norm_gain, norm_bias = refs[6:15]
    refs = refs[4:]
    refs, (first, second, load_sem) = refs[:-3], refs[-3:]
    loads = [pltpu.make_async_copy(far, near, load_sem.at[at]) for at, (far, near) in enumerate(((first_far, first), (second_far, second)))]

    @pl.when(pl.program_id(0) == 0)
    def _():
        start(loads)
    if deep:
        cotangent, token_grad = refs[11], refs[35]
        local_sem, send_sem, recv_sem = refs[40:43]
        refs = refs[12:35] + refs[36:40]
        here = Place(deep)
        moved = ToTokens(here, cotangent, token_grad, send_sem, recv_sem, local_sem.at[0])

        @pl.when(pl.program_id(0) == 0)
        def _():
            here.greet_line()
            moved.begin()
    else:
        refs = refs[11:]
    token_forward_body(sizes, loads, input_ref, mixed_ref, segments_ref, position_ref, first, second, value_bias, base_bias, attn_bias,
                       hidden_bias, output_bias, gain, shift, norm_gain, norm_bias, *refs)
    if deep:
        @pl.when(pl.program_id(0) == pl.num_programs(0) - 1)
        def _():
            moved.arrive()
            moved.finish()


def token_forward_body(
    sizes, loads, input_ref, mixed_ref, segments_ref, position_ref, first, second, value_bias, base_bias, attn_bias, hidden_bias, output_bias,
    gain, shift, norm_gain, norm_bias,
    layer_ref, x_rows, mixed_rows, values, value_slope, reset, reset_back, attention, queries, keys, shared, shared_slope,
    mixed_att, hidden_back, gate_back, gate, normal_one, scale_one, normed_low, activated, inner_slope, normal_two, scale_two,
    reset_slope, wide, row_values, table,
):
    width, shared_width, value_width, inner_width, block = sizes
    low = jnp.bfloat16
    base_at = value_width
    reset_at = width + shared_width
    direct_at = reset_at + value_width
    hidden_at = base_at + direct_at + width

    @pl.when(pl.program_id(0) == 0)
    def _():
        table[...] = shear(jnp.broadcast_to(row_of(position_ref, 0, block), (block, block)), 1).T

    x_float = input_ref[0].astype(jnp.float32).T
    row_values[...] = x_float
    x_rows[...] = x_float.astype(low)
    mixed_rows[...] = mixed_ref[0].astype(jnp.float32).T.astype(low)

    wait_first(loads[0])

    def value_piece(at):
        out, slope = silu_and_slope(times(x_rows[...], first[:, pl.ds(at, PIECE)]) + row_of(value_bias, at, PIECE))
        values[:, pl.ds(at, PIECE)] = out.astype(low)
        value_slope[:, pl.ds(at, PIECE)] = slope.astype(low)

    over_pieces(value_width, value_piece)

    def base(at, size):
        return times(mixed_rows[...], first[:, pl.ds(base_at + at, size)]) + row_of(base_bias, at, size)

    shared_value, slope = silu_and_slope(base(width, shared_width))
    shared[...] = shared_value
    shared_slope[...] = slope
    queries[...] = (shared_value * gain[0:1, :] + shift[0:1, :]).astype(low)
    keys[...] = (shared_value * gain[1:2, :] + shift[1:2, :]).astype(low)

    def reset_piece(at):
        out, slope = silu_and_slope(base(reset_at + at, PIECE))
        reset[:, pl.ds(at, PIECE)] = out.astype(low)
        wide[:, pl.ds(at, PIECE)] = out
        reset_slope[:, pl.ds(at, PIECE)] = slope

    over_pieces(value_width, reset_piece)
    for window in range(x_rows.shape[0] // block):
        rows = pl.ds(window * block, block)
        across = jnp.broadcast_to(segments_ref[0, :, pl.ds(window * block, block)], (block, block))
        earlier = lax.broadcasted_iota(jnp.int32, (block, block), 0) >= lax.broadcasted_iota(jnp.int32, (block, block), 1)
        allowed = earlier & (across == across.T)
        scores = times_turned(queries[rows, :], keys[rows, :]) * shared_width ** (-0.5) + table[...]
        scores = jnp.where(allowed, scores, MASKED)
        raised = jnp.exp(scores - jnp.max(scores, axis=-1, keepdims=True))
        weights = raised / jnp.sum(raised, axis=-1, keepdims=True)
        attention[window] = weights
        weights_low = weights.astype(low)

        def attended_piece(at):
            columns = pl.ds(at, PIECE)
            attended = times(weights_low, values[rows, columns])
            mixed_att[rows, columns] = (attended * wide[rows, columns]).astype(low)
            reset_back[rows, columns] = (attended * reset_slope[rows, columns]).astype(low)

        over_pieces(value_width, attended_piece)

    wait_first(loads[1])

    def hidden_piece(at):
        columns = pl.ds(at, PIECE)
        update = jax.nn.sigmoid(base(at, PIECE))
        pre = base(direct_at + at, PIECE) + times(mixed_att[...], second[:, columns]) + row_of(attn_bias, at, PIECE)
        hidden, slope = silu_and_slope(pre)
        value = row_values[:, columns]
        change = hidden - value
        gate[:, columns] = update.astype(low)
        hidden_back[:, columns] = (update * slope).astype(low)
        gate_back[:, columns] = (change * update * (1.0 - update)).astype(low)
        row_values[:, columns] = value + update * change

    over_pieces(width, hidden_piece)
    normal, scale = normalize(row_values[...])
    normal_one[...] = normal
    scale_one[...] = jnp.broadcast_to(scale, scale_one.shape)
    normed = normal * norm_gain[0:1, :] + norm_bias[0:1, :]
    normed_low[...] = normed.astype(low)
    row_values[...] = normed

    def inner_piece(at):
        columns = pl.ds(at, PIECE)
        out, slope = silu_and_slope(times(normed_low[...], first[:, pl.ds(hidden_at + at, PIECE)]) + row_of(hidden_bias, at, PIECE))
        activated[:, columns] = out.astype(low)
        inner_slope[:, columns] = slope.astype(low)

    over_pieces(inner_width, inner_piece)

    def outer_piece(at):
        columns = pl.ds(at, PIECE)
        row_values[:, columns] += times(activated[...], second[:, pl.ds(width + at, PIECE)]) + row_of(output_bias, at, PIECE)

    over_pieces(width, outer_piece)
    normal, scale = normalize(row_values[...])
    normal_two[...] = normal
    scale_two[...] = jnp.broadcast_to(scale, scale_two.shape)
    layer_ref[0] = (normal * norm_gain[1:2, :] + norm_bias[1:2, :]).T.astype(low)


def token_forward(token_input, token_mixed, segments, position, first, second, vectors, sizes, cotangent, deep):
    rows, width, span = token_input.shape
    _, shared_width, value_width, inner_width, block = sizes
    tokens = rows * span
    low, full = jnp.bfloat16, jnp.float32
    windows = span // block

    def by_rows(columns, kind):
        return jax.ShapeDtypeStruct((tokens, columns), kind), pl.BlockSpec((span, columns), lambda i: (i, 0))

    def whole(part):
        return pl.BlockSpec(part.shape, lambda i: (0,) * part.ndim, pipeline_mode=pl.Buffered(1))

    turned = pl.BlockSpec((1, width, span), lambda i: (i, 0, 0))
    tables = pl.BlockSpec((windows, block, block), lambda i: (i, 0, 0))
    outs = [
        (jax.ShapeDtypeStruct((rows, width, span), low), turned),
        by_rows(width, low), by_rows(width, low), by_rows(value_width, low), by_rows(value_width, low),
        by_rows(value_width, low), by_rows(value_width, low),
        (jax.ShapeDtypeStruct((rows * windows, block, block), full), tables),
        by_rows(shared_width, low), by_rows(shared_width, low), by_rows(shared_width, full), by_rows(shared_width, full),
        by_rows(value_width, low), by_rows(width, low), by_rows(width, low), by_rows(width, low),
        by_rows(width, full), by_rows(128, full), by_rows(width, low), by_rows(inner_width, low), by_rows(inner_width, low),
        by_rows(width, full), by_rows(128, full),
    ]
    if deep:
        outs.append((jax.ShapeDtypeStruct((rows, width, span), low), ANYWHERE))
    made = pl.pallas_call(
        partial(token_forward_kernel, sizes, deep),
        grid=(rows,),
        in_specs=[turned, turned, pl.BlockSpec((1, 1, span), lambda i: (i, 0, 0))] + [whole(position), ANYWHERE, ANYWHERE] + [whole(part) for part in vectors] + [ANYWHERE] * bool(deep),
        out_specs=[spec for _, spec in outs],
        out_shape=[shape for shape, _ in outs],
        scratch_shapes=[pltpu.VMEM((span, value_width), full), pltpu.VMEM((span, value_width), full), pltpu.VMEM((span, width), full),
                        pltpu.VMEM((block, block), full)] + ([dma(1), dma(2 * deep), dma(2 * deep)] if deep else [])
        + [pltpu.VMEM(first.shape, low), pltpu.VMEM(second.shape, low), dma(2)],
        compiler_params=(pltpu.CompilerParams(collective_id=3, has_side_effects=True, vmem_limit_bytes=ROOM) if deep
                         else pltpu.CompilerParams(vmem_limit_bytes=ROOM)),
        cost_estimate=pl.CostEstimate(flops=2 * tokens * (first.size + second.size), bytes_accessed=60 * 1024 * 1024, transcendentals=tokens * 8192),
    )(token_input, token_mixed, segments, position, first, second, *vectors, *([cotangent] if deep else []))
    if not deep:
        made = [*made, lax.all_to_all(cotangent, "chan", split_axis=2, concat_axis=1, tiled=True)]
    return made


def small_widths(sizes):
    width, shared_width, value_width, inner_width, block = sizes
    base_width = 2 * width + shared_width + value_width
    return (value_width, base_width, width, inner_width, width) + (shared_width,) * 4 + (width,) * 4 + (block,)


def token_backward_kernel(sizes, deep, *refs):
    refs, (first, second, load_sem) = refs[:-3], refs[-3:]
    loads = [pltpu.make_async_copy(far, near, load_sem.at[at]) for at, (far, near) in enumerate(((refs[1], first), (refs[2], second)))]

    @pl.when(pl.program_id(0) == 0)
    def _():
        start(loads[::-1])

    refs = (refs[0], first, second) + refs[3:]
    if deep:
        layer_blocks, layer_out = refs[22], refs[30]
        local_sem, send_sem, recv_sem = refs[34:37]
        refs = refs[:22] + refs[23:30] + refs[31:34]
        here = Place(deep)
        moved = ToChannels(here, layer_blocks, layer_out, send_sem, recv_sem, local_sem.at[0])

        @pl.when(pl.program_id(0) == 0)
        def _():
            here.greet_line()
            moved.begin()
    token_backward_body(sizes, loads, *refs)
    if deep:
        @pl.when(pl.program_id(0) == pl.num_programs(0) - 1)
        def _():
            moved.arrive()
            moved.finish()


def token_backward_body(
    sizes, loads, grad_ref, first, second, gain, norm_gain,
    values, value_slope, reset, reset_back, attention, queries, keys, shared, shared_slope,
    hidden_back, gate_back, gate, normal_one, scale_one, inner_slope, normal_two, scale_two,
    mixed_out, direct_out, back_outer, back_inner, back_base, back_value,
    small, row_values, back_attended, score_sum,
):
    width, shared_width, value_width, inner_width, block = sizes
    low = jnp.bfloat16
    base_at = value_width
    reset_at = width + shared_width
    direct_at = reset_at + value_width
    base_width = direct_at + width
    hidden_at = base_at + base_width
    scale = shared_width ** (-0.5)
    (value_sum, base_sum, attn_sum, hidden_sum, output_sum, query_gain, key_gain, query_shift, key_shift,
     gain_one, gain_two, shift_one, shift_two, position_sum) = parts_of(small, small_widths(sizes))

    @pl.when(pl.program_id(0) == 0)
    def _():
        small[...] = jnp.zeros_like(small)
        score_sum[...] = jnp.zeros_like(score_sum)

    def total(part):
        return jnp.sum(part, axis=0, keepdims=True)

    grads = grad_ref[0].astype(jnp.float32).T
    normal = normal_two[...]
    gain_two[...] += total(grads * normal)
    shift_two[...] += total(grads)
    back_two = normalize_back(grads * norm_gain[1:2, :], normal, scale_two[:, :1])
    row_values[...] = back_two
    output_sum[...] += total(back_two)
    back_outer[...] = back_two.astype(low)

    wait_first(loads[1])

    def inner_piece(at):
        columns = pl.ds(at, PIECE)
        back = (times_turned(back_outer[...], second[columns, pl.ds(width, width)]) * inner_slope[:, columns].astype(jnp.float32)).astype(low)
        back_inner[:, columns] = back
        hidden_sum[:, columns] += total(back.astype(jnp.float32))

    over_pieces(inner_width, inner_piece)

    wait_first(loads[0])

    def normed_piece(at):
        columns = pl.ds(at, PIECE)
        row_values[:, columns] += times_turned(back_inner[...], first[columns, pl.ds(hidden_at, inner_width)])

    over_pieces(width, normed_piece)
    back_normed = row_values[...]
    normal = normal_one[...]
    gain_one[...] += total(back_normed * normal)
    shift_one[...] += total(back_normed)
    back_one = normalize_back(back_normed * norm_gain[0:1, :], normal, scale_one[:, :1])
    back_hidden = back_one * hidden_back[...].astype(jnp.float32)
    attn_sum[...] += total(back_hidden)
    back_base[:, direct_at:base_width] = back_hidden.astype(low)
    back_base[:, 0:width] = (back_one * gate_back[...].astype(jnp.float32)).astype(low)
    row_values[...] = back_one * (1.0 - gate[...].astype(jnp.float32))

    def mix_piece(at):
        columns = pl.ds(at, PIECE)
        back = times_turned(back_base[:, direct_at:base_width], second[columns, pl.ds(0, width)])
        back_attended[:, columns] = (back * reset[:, columns].astype(jnp.float32)).astype(low)
        back_base[:, pl.ds(reset_at + at, PIECE)] = (back * reset_back[:, columns].astype(jnp.float32)).astype(low)

    over_pieces(value_width, mix_piece)
    for window in range(grads.shape[0] // block):
        rows = pl.ds(window * block, block)
        weights = attention[window]
        back_weights = times_turned(back_attended[rows, :], values[rows, :])
        back_scores = (weights * (back_weights - jnp.sum(weights * back_weights, axis=-1, keepdims=True))).astype(low)
        score_sum[...] += back_scores.astype(jnp.float32)
        back_queries = times(back_scores, keys[rows, :]) * scale
        back_keys = turned_times(back_scores, queries[rows, :]) * scale
        shared_rows = shared[rows, :]
        query_gain[...] += total(back_queries * shared_rows)
        key_gain[...] += total(back_keys * shared_rows)
        query_shift[...] += total(back_queries)
        key_shift[...] += total(back_keys)
        back_shared = back_queries * gain[0:1, :] + back_keys * gain[1:2, :]
        back_base[rows, width:reset_at] = (back_shared * shared_slope[rows, :]).astype(low)
        weights_turned = weights.T.astype(low)

        def value_piece(at):
            columns = pl.ds(at, PIECE)
            back = times(weights_turned, back_attended[rows, columns]) * value_slope[rows, columns].astype(jnp.float32)
            back_value[rows, columns] = back.astype(low)

        over_pieces(value_width, value_piece)
    value_sum[...] += total(back_value[...].astype(jnp.float32))
    base_sum[...] += total(back_base[...].astype(jnp.float32))

    def out_piece(at):
        rows = pl.ds(at, PIECE)
        mixed_out[0, rows, :] = times_turned(first[rows, pl.ds(base_at, base_width)], back_base[...]).astype(low)
        direct_out[0, rows, :] = (times_turned(first[rows, pl.ds(0, value_width)], back_value[...]) + row_values[:, rows].T).astype(low)

    over_pieces(width, out_piece)

    @pl.when(pl.program_id(0) == pl.num_programs(0) - 1)
    def _():
        position_sum[...] = total(shear(score_sum[...].T, -1))


def token_backward(token_grad, first, second, gain, norm_gain, kept, sizes, layer_blocks, deep):
    rows, width, span = token_grad.shape
    _, shared_width, value_width, inner_width, block = sizes
    tokens = rows * span
    low, full = jnp.bfloat16, jnp.float32
    base_width = 2 * width + shared_width + value_width

    def by_rows(columns, kind):
        return jax.ShapeDtypeStruct((tokens, columns), kind), pl.BlockSpec((span, columns), lambda i: (i, 0))

    def whole(part):
        return pl.BlockSpec(part.shape, lambda i: (0,) * len(part.shape), pipeline_mode=pl.Buffered(1))

    def sums(*shape):
        return jax.ShapeDtypeStruct(shape, full), pl.BlockSpec(shape, lambda i: (0, 0))

    def rows_of(part):
        if part.ndim == 3:
            return pl.BlockSpec((span // block, block, block), lambda i: (i, 0, 0))
        return pl.BlockSpec((span, part.shape[1]), lambda i: (i, 0))

    turned = pl.BlockSpec((1, width, span), lambda i: (i, 0, 0))
    outs = [
        (jax.ShapeDtypeStruct((rows, width, span), low), turned), (jax.ShapeDtypeStruct((rows, width, span), low), turned),
        by_rows(width, low), by_rows(inner_width, low), by_rows(base_width, low), by_rows(value_width, low),
        sums(1, sum(small_widths(sizes))),
    ]
    if deep:
        outs.append((jax.ShapeDtypeStruct((rows, width // (2 * deep), span * 2 * deep), low), ANYWHERE))
    made = pl.pallas_call(
        partial(token_backward_kernel, sizes, deep),
        grid=(rows,),
        in_specs=[turned, ANYWHERE, ANYWHERE, whole(gain), whole(norm_gain)] + [rows_of(part) for part in kept] + [ANYWHERE] * bool(deep),
        out_specs=[spec for _, spec in outs],
        out_shape=[shape for shape, _ in outs],
        scratch_shapes=[pltpu.VMEM((span, width), full), pltpu.VMEM((span, value_width), low), pltpu.VMEM((block, block), full)]
        + ([dma(1), dma(2 * deep), dma(2 * deep)] if deep else []) + [pltpu.VMEM(first.shape, low), pltpu.VMEM(second.shape, low), dma(2)],
        compiler_params=(pltpu.CompilerParams(collective_id=4, has_side_effects=True, vmem_limit_bytes=ROOM) if deep
                         else pltpu.CompilerParams(vmem_limit_bytes=ROOM)),
        cost_estimate=pl.CostEstimate(flops=2 * tokens * (first.size + second.size), bytes_accessed=60 * 1024 * 1024, transcendentals=0),
    )(token_grad, first, second, gain, norm_gain, *kept, *([layer_blocks] if deep else []))
    if not deep:
        made = [*made, lax.all_to_all(layer_blocks, "chan", split_axis=1, concat_axis=2, tiled=True)]
    return made


def contract_rows(left, right):
    return lax.dot_general(
        left, right, (((0,), (0,)), ((), ())), preferred_element_type=jnp.float32
    )


def shards(
    inputs,
    cotangent,
    doc_lengths,
    ema_logits,
    ema_mixing,
    ema_skip,
    value_weight,
    base_weight,
    attn_weight,
    hidden_weight,
    output_weight,
    value_bias,
    base_bias,
    attn_bias,
    hidden_bias,
    output_bias,
    query_key_gain,
    query_key_shift,
    position_bias,
    norm_gain,
    norm_bias,
):
    row_count, chan_count, seq_length = inputs.shape
    group_count = lax.axis_size("chan")
    width = chan_count * group_count
    span_local = seq_length // group_count
    length_block = position_bias.shape[0]
    shared_width = query_key_gain.shape[1]
    value_width = value_bias.shape[0]
    keep, keep_next = keep_tables(doc_lengths, seq_length)
    compact = ema_table(ema_logits, ema_mixing, ema_skip)
    on_four = lax.axis_size("row") == 4 and group_count == 8
    devices, deep = lax.axis_size("row") * group_count, group_count // 2
    exchange = partial(forward_exchange, devices=devices, deep=deep) if on_four else plain_forward
    first, second, token_input, token_mixed, pre_mix = exchange(
        [value_weight, base_weight, hidden_weight], [attn_weight, output_weight], inputs, keep, compact
    )
    first, second = first.reshape(width, -1), second.reshape(value_width, -1)
    base_width = base_bias.shape[0]
    local_pos = lax.axis_index("chan") * span_local + jnp.arange(span_local, dtype=jnp.int32)
    passed = local_pos[None, :, None] >= document_ends(doc_lengths)[:, None, :]
    segments = jnp.sum(passed.astype(jnp.float32), axis=2)[:, None]
    sizes = (width, shared_width, value_width, hidden_bias.shape[0], length_block)
    vectors = [value_bias, base_bias, attn_bias, hidden_bias, output_bias, query_key_gain, query_key_shift, norm_gain, norm_bias]
    reach = deep if on_four else 0
    (
        layer_blocks,
        input_rows,
        mixed_rows,
        values,
        value_slope,
        reset,
        reset_back,
        attention,
        queries,
        keys,
        shared,
        shared_slope,
        mixed_att,
        hidden_back,
        gate_back,
        gate,
        normal_one,
        scale_one,
        normed_low,
        activated,
        inner_slope,
        normal_two,
        scale_two,
        token_grad,
    ) = token_forward(token_input, token_mixed, segments, position_bias, first, second, vectors, sizes, cotangent, reach)
    kept = [values, value_slope, reset, reset_back, attention, queries, keys, shared, shared_slope]
    kept += [hidden_back, gate_back, gate, normal_one, scale_one, inner_slope, normal_two, scale_two]
    (
        back_mixed_blocks,
        back_direct_blocks,
        back_outer,
        back_inner,
        back_base,
        back_value,
        small,
        layer_out,
    ) = token_backward(token_grad, first, second, query_key_gain, norm_gain, kept, sizes, layer_blocks, reach)
    back_proj = back_base[:, base_width - width :]
    grad_output_weight = contract_rows(activated, back_outer)
    grad_hidden_weight = contract_rows(normed_low, back_inner)
    grad_attn_weight = contract_rows(mixed_att, back_proj)
    grad_value_weight = contract_rows(input_rows, back_value)
    grad_base_weight = contract_rows(mixed_rows, back_base)
    def owners(terms):
        return terms.astype(jnp.bfloat16).reshape(devices, -1, terms.shape[1])

    exchange = partial(backward_exchange, deep=deep) if on_four else plain_backward
    owner_value, owner_base, owner_hidden, owner_attn, owner_output, small, grad_ema, direct, sums, skips = exchange(
        [owners(grad_value_weight), owners(grad_base_weight), owners(grad_hidden_weight)],
        [owners(grad_attn_weight), owners(grad_output_weight)],
        small,
        inputs,
        pre_mix,
        back_mixed_blocks,
        back_direct_blocks,
        keep,
        keep_next,
        compact,
    )
    grad_inputs = grad_ema + direct.astype(jnp.float32)
    states = sums.shape[0] // 2
    grad_logits, grad_mixing, grad_skip = ema_grads(
        sums[:states], sums[states:], skips, ema_logits, ema_mixing, row_count, chan_count
    )
    offset, summed = 0, []
    for count, size in ((1, value_width), (1, base_width), (1, width), (1, hidden_bias.shape[0]), (1, width),
                        (2, shared_width), (2, shared_width), (2, width), (2, width), (1, length_block)):
        part = small[0, offset : offset + count * size]
        summed.append(part if count == 1 else part.reshape(count, size))
        offset += count * size
    summed.insert(7, summed.pop())
    return (
        layer_out,
        grad_inputs,
        grad_logits,
        grad_mixing,
        grad_skip,
        owner_value,
        owner_base,
        owner_attn,
        owner_hidden,
        owner_output,
        *summed,
    )


def solution(mesh):
    in_specs = (
        P("row", "chan", None),
        P("row", "chan", None),
        P("row", None),
        P(None, "chan", None),
        P(None, "chan", None),
        P("chan"),
        P(("row", "chan"), None),
        P(("row", "chan"), None),
        P(("row", "chan"), None),
        P(("row", "chan"), None),
        P(("row", "chan"), None),
        P(),
        P(),
        P(),
        P(),
        P(),
        P(),
        P(),
        P(),
        P(),
        P(),
    )
    out_specs = (
        P("row", "chan", None),
        P("row", "chan", None),
        P(None, "chan", None),
        P(None, "chan", None),
        P("chan"),
        P(("row", "chan"), None),
        P(("row", "chan"), None),
        P(("row", "chan"), None),
        P(("row", "chan"), None),
        P(("row", "chan"), None),
        P(),
        P(),
        P(),
        P(),
        P(),
        P(),
        P(),
        P(),
        P(),
        P(),
    )
    return jax.shard_map(shards, mesh=mesh, in_specs=in_specs, out_specs=out_specs, check_vma=False)
```
